32 devices in a mesh: dp: 2 (over y), fsdp: 16 (over z, x, core).
Axes of the slice: x: 2, y: 2, z: 4, core: 2. Of those that a mesh axis runs over, the one named last changes fastest.
Arguments:
- hidden: bfloat16 [32, 1024, 768], P(('dp', 'fsdp')), may hold values from -6 to 6
- cotangent: bfloat16 [32, 1024, 768], P(('dp', 'fsdp')), may hold values from -6 to 6
- lengths: int32 [32], P(('dp', 'fsdp')), may hold values from 34 to 1024, as said below
- thought_start: int32 [32], P(('dp', 'fsdp')), may hold values from 30 to 380, as said below
- first_gain: bfloat16 [768], P(('dp', 'fsdp')), may hold values from 0.5 to 1.5
- first_bias: bfloat16 [768], P(('dp', 'fsdp')), may hold values from -1 to 1
- project_weight: bfloat16 [768, 2304], P(('dp', 'fsdp')), may hold values from -0.21875 to 0.21875
- project_bias: bfloat16 [1536], P(('dp', 'fsdp')), may hold values from -1 to 1
- output_weight: bfloat16 [768, 768], P(('dp', 'fsdp')), may hold values from -0.625 to 0.625
- output_bias: bfloat16 [768], P(('dp', 'fsdp')), may hold values from -1 to 1
- second_gain: bfloat16 [768], P(('dp', 'fsdp')), may hold values from 0.5 to 1.5
- second_bias: bfloat16 [768], P(('dp', 'fsdp')), may hold values from -1 to 1
- expand_weight: bfloat16 [768, 3072], P(('dp', 'fsdp')), may hold values from -0.21875 to 0.21875
- expand_bias: bfloat16 [3072], P(('dp', 'fsdp')), may hold values from -1 to 1
- contract_weight: bfloat16 [3072, 768], P(('dp', 'fsdp')), may hold values from -0.109375 to 0.109375
- contract_bias: bfloat16 [768], P(('dp', 'fsdp')), may hold values from -1 to 1
Outputs:
- final_hidden: float32 [32, 1024, 768], P(('dp', 'fsdp'))
- hidden_grad: float32 [32, 1024, 768], P(('dp', 'fsdp'))
- first_gain_grad: float32 [768], P(('dp', 'fsdp'))
- first_bias_grad: float32 [768], P(('dp', 'fsdp'))
- project_weight_grad: float32 [768, 2304], P(('dp', 'fsdp'))
- project_bias_grad: float32 [1536], P(('dp', 'fsdp'))
- output_weight_grad: float32 [768, 768], P(('dp', 'fsdp'))
- output_bias_grad: float32 [768], P(('dp', 'fsdp'))
- second_gain_grad: float32 [768], P(('dp', 'fsdp'))
- second_bias_grad: float32 [768], P(('dp', 'fsdp'))
- expand_weight_grad: float32 [768, 3072], P(('dp', 'fsdp'))
- expand_bias_grad: float32 [3072], P(('dp', 'fsdp'))
- contract_weight_grad: float32 [3072, 768], P(('dp', 'fsdp'))
- contract_bias_grad: float32 [768], P(('dp', 'fsdp'))
The draws below stay inside these ranges and needn't reach their ends.
Inputs may be any that keep to these rules, and one draw needn't show every extreme that they name: Row r holds thought_start[r] question tokens, then 3 latent thoughts, then at least one answer token; positions from lengths[r] on are padding; some row has length 1024. `thought_start`: both ends of the range occur in every draw.
All inputs are finite; a program needn't handle non-finite values.
Results may differ from the reference program's by a relative error of at most 0.012.
Values may be sent and summed in bfloat16 or wider, within the bound.
A program may use at most 320 MiB of HBM per device.

```python
import jax
import jax.numpy as jnp
from jax import lax

D = 768
HEADS = 12
FF = 3072
SEQ = 1024
PASSES = 4
THOUGHTS = 3
QUEST_MIN = 30
QUEST_MAX = 380
ROWS = 32


def draw_together(key):
    start_key = jax.random.fold_in(key, 101)
    answer_key = jax.random.fold_in(key, 202)
    starts = jax.random.randint(start_key, (ROWS,), QUEST_MIN, QUEST_MAX + 1)
    starts = starts.at[0].set(QUEST_MIN).at[ROWS - 1].set(QUEST_MAX)
    room = SEQ - THOUGHTS - starts
    answer = 1 + jax.random.randint(answer_key, (ROWS,), 0, 16777216) % room
    lengths = (starts + THOUGHTS + answer).at[0].set(SEQ)
    return (starts.astype(jnp.int32), lengths.astype(jnp.int32))


def draw_lengths(key, part):
    return draw_together(key)[1]


def draw_thought_start(key, part):
    return draw_together(key)[0]


def shard_levels(key, dims, shards, least, largest):
    loudness = 1.0
    for position, blocks in shards:
        steps = jax.random.uniform(jax.random.fold_in(jax.random.fold_in(key, 6), position), (blocks,), jnp.float32, least / len(shards), largest / len(shards))
        loudness = loudness * jnp.repeat(jnp.exp(steps), dims[position] // blocks).reshape((-1,) + (1,) * (len(dims) - 1 - position))
    return loudness


def noise(rng, dims, scale, limit, shards=(), dtype=jnp.bfloat16):
    values = scale * jax.random.normal(rng, dims, jnp.float32)
    if shards:
        values = values * shard_levels(rng, dims, shards, -0.22, 0.18)
    return jnp.clip(values, -limit, limit).astype(dtype)


def setup_inputs(seed: int = 0) -> dict:
    key_list = jax.random.split(jax.random.key(seed), 17)
    hidden = noise(key_list[0], (ROWS, SEQ, D), 1.0, 6.0, ((0, 32),))
    cotangent = noise(key_list[1], (ROWS, SEQ, D), 1.0, 6.0, ((0, 32),))
    lengths = draw_lengths(jax.random.fold_in(key_list[16], 71), 0)
    thought_start = draw_thought_start(jax.random.fold_in(key_list[16], 71), 0)
    first_gain = jnp.clip(1.0 + 0.1 * jax.random.normal(key_list[4], (D,), jnp.float32), 0.5, 1.5).astype(jnp.bfloat16)
    first_bias = noise(key_list[5], (D,), 0.2, 1.0, ((0, 32),))
    project_weight = noise(key_list[6], (D, 3 * D), D ** -0.5, 0.21875, ((0, 32),))
    project_bias = noise(key_list[7], (2 * D,), 0.2, 1.0, ((0, 32),))
    output_weight = noise(key_list[8], (D, D), (D // 8) ** -0.5, 0.625, ((0, 32),))
    output_bias = noise(key_list[9], (D,), 0.2, 1.0, ((0, 32),))
    second_gain = jnp.clip(1.0 + 0.1 * jax.random.normal(key_list[10], (D,), jnp.float32), 0.5, 1.5).astype(jnp.bfloat16)
    second_bias = noise(key_list[11], (D,), 0.2, 1.0, ((0, 32),))
    expand_weight = noise(key_list[12], (D, FF), D ** -0.5, 0.21875, ((0, 32),))
    expand_bias = noise(key_list[13], (FF,), 0.2, 1.0, ((0, 32),))
    contract_weight = noise(key_list[14], (FF, D), FF ** -0.5, 0.109375, ((0, 32),))
    contract_bias = noise(key_list[15], (D,), 0.2, 1.0, ((0, 32),))
    return dict(hidden=hidden, cotangent=cotangent, lengths=lengths, thought_start=thought_start, first_gain=first_gain, first_bias=first_bias, project_weight=project_weight, project_bias=project_bias, output_weight=output_weight, output_bias=output_bias, second_gain=second_gain, second_bias=second_bias, expand_weight=expand_weight, expand_bias=expand_bias, contract_weight=contract_weight, contract_bias=contract_bias)


@jax.custom_vjp
def low(v):
    return lax.optimization_barrier(v.astype(jnp.bfloat16)).astype(jnp.float32)

@jax.custom_vjp
def low_back(v):
    return v

def low_keep(v):
    return (low(v), None)

def low_pass(kept, grad):
    return (grad,)

def back_keep(v):
    return (v, None)

def back_low(kept, grad):
    return (low(grad),)
low.defvjp(low_keep, low_pass)
low_back.defvjp(back_keep, back_low)
EPSILON = 1e-05
NEG_FILL = -1e+30
HIGHEST = lax.Precision.HIGHEST

def layer_norm(value, gain, shift):
    center = value - lax.optimization_barrier(jnp.mean(value, axis=-1, keepdims=True))
    spread = lax.optimization_barrier(jnp.mean(center * center, axis=-1, keepdims=True))
    return center * lax.rsqrt(spread + EPSILON) * gain + shift

def attend_one(operands):
    query, keys, values, length = operands
    seq = keys.shape[0]
    scale = float(query.shape[-1]) ** (-0.5)
    score = low_back(jnp.einsum('qd,kd->qk', query, keys, precision=HIGHEST) * scale)
    query_pos = lax.broadcasted_iota(jnp.int32, (seq, seq), 0)
    key_pos = lax.broadcasted_iota(jnp.int32, (seq, seq), 1)
    allowed = (key_pos <= query_pos) & (key_pos < length) | (key_pos == query_pos)
    prob = low(jax.nn.softmax(jnp.where(allowed, score, NEG_FILL), axis=-1))
    return jnp.einsum('qk,kd->qd', prob, values, precision=HIGHEST)

def block_forward(params, inputs, lengths):
    first_gain, first_bias, project_weight, project_bias, output_weight, output_bias, second_gain, second_bias, expand_weight, expand_bias, contract_weight, contract_bias = params
    groups, seq, width = inputs.shape
    head_size = width // HEADS
    flat = inputs.reshape(groups * seq, width)
    normed = low(layer_norm(flat, first_gain, first_bias))
    full_bias = jnp.concatenate([project_bias[:width], jnp.zeros((width,), jnp.float32), project_bias[width:]])
    mixed = low(low_back(jnp.dot(normed, project_weight, precision=HIGHEST) + full_bias))
    parts = mixed.reshape(groups, seq, 3, HEADS, head_size).transpose(2, 0, 3, 1, 4)
    parts = parts.reshape(3, groups * HEADS, seq, head_size)
    repeated = jnp.repeat(lengths, HEADS)
    context = lax.map(jax.checkpoint(attend_one), (parts[0], parts[1], parts[2], repeated))
    context = context.reshape(groups, HEADS, seq, head_size).transpose(0, 2, 1, 3).reshape(groups * seq, width)
    attended = low(low_back(context))
    resid = flat + low_back(jnp.dot(attended, output_weight, precision=HIGHEST) + output_bias)
    normed_two = low(layer_norm(resid, second_gain, second_bias))
    pre = low_back(jnp.dot(normed_two, expand_weight, precision=HIGHEST) + expand_bias)
    active = low(jax.nn.gelu(pre, approximate=True))
    branch = low_back(jnp.dot(active, contract_weight, precision=HIGHEST) + contract_bias)
    return (resid + branch).reshape(groups, seq, width)

def coconut(params, inputs, lengths, starts):
    groups, seq, width = inputs.shape
    positions = lax.broadcasted_iota(jnp.int32, (groups, seq), 1)
    current = inputs
    result = block_forward(params, current, lengths)
    for step in range(1, PASSES):
        place = starts + (step - 1)
        chosen = (positions == (place - 1)[:, None])[..., None]
        source = lax.optimization_barrier(jnp.sum(jnp.where(chosen, result, 0.0), axis=1, keepdims=True))
        current = jnp.where((positions == place[:, None])[..., None], source, current)
        result = block_forward(params, current, lengths)
    valid = (positions < lengths[:, None]).astype(jnp.float32)
    return result * valid[..., None]

def reference(hidden, cotangent, lengths, thought_start, first_gain, first_bias, project_weight, project_bias, output_weight, output_bias, second_gain, second_bias, expand_weight, expand_bias, contract_weight, contract_bias):
    params = (first_gain.astype(jnp.float32), first_bias.astype(jnp.float32), project_weight.astype(jnp.float32), project_bias.astype(jnp.float32), output_weight.astype(jnp.float32), output_bias.astype(jnp.float32), second_gain.astype(jnp.float32), second_bias.astype(jnp.float32), expand_weight.astype(jnp.float32), expand_bias.astype(jnp.float32), contract_weight.astype(jnp.float32), contract_bias.astype(jnp.float32))
    total_rows, seq, width = hidden.shape
    group = 4
    count = total_rows // group
    grouped = (hidden.reshape(count, group, seq, width), cotangent.reshape(count, group, seq, width), lengths.reshape(count, group), thought_start.reshape(count, group))

    def one_group(totals, operands):
        inputs, upstream, group_lengths, group_starts = operands

        def forward(weights, values):
            return coconut(weights, values, group_lengths, group_starts)
        result, pull = jax.vjp(forward, params, inputs.astype(jnp.float32))
        weight_grads, input_grads = pull(upstream.astype(jnp.float32))
        totals = jax.tree.map(jnp.add, totals, weight_grads)
        return (totals, (result, input_grads))
    zeros = tuple((jnp.zeros_like(weight) for weight in params))
    totals, (result, input_grads) = lax.scan(one_group, zeros, grouped)
    return (result.reshape(total_rows, seq, width), input_grads.reshape(total_rows, seq, width), totals[0], totals[1], totals[2], totals[3], totals[4], totals[5], totals[6], totals[7], totals[8], totals[9], totals[10], totals[11])
```

```python
import jax
import jax.numpy as jnp
from jax import lax
from jax.sharding import PartitionSpec as P

HEADS = 12
THOUGHTS = 3
PREFIX = 384

EPSILON = 1e-05
NEG_FILL = -1e30
AXES = ("dp", "fsdp")
F32 = jnp.float32
BF16 = jnp.bfloat16


def dot(left, right):
    return jnp.dot(left, right, preferred_element_type=F32)


def dot_t(left, right):
    return jnp.einsum("nf,df->nd", left, right, preferred_element_type=F32)


def dot_g(left, right):
    return jnp.einsum("nd,ne->de", left, right, preferred_element_type=F32)


def norm_parts(value):
    center = value - jnp.mean(value, axis=-1, keepdims=True)
    inv = lax.rsqrt(jnp.mean(center * center, axis=-1, keepdims=True) + EPSILON)
    return center * inv, inv


def norm_back(grad, hat, inv, gain):
    scaled = grad * gain
    return inv * (
        scaled
        - jnp.mean(scaled, axis=-1, keepdims=True)
        - hat * jnp.mean(scaled * hat, axis=-1, keepdims=True)
    )


def smooth_gelu(value):
    return jax.nn.gelu(value, approximate=True)


def gelu_slope(value):
    root = 0.7978845608028654
    inner = jnp.tanh(root * (value + 0.044715 * value * value * value))
    return 0.5 * (1.0 + inner) + 0.5 * value * (1.0 - inner * inner) * root * (
        1.0 + 3 * 0.044715 * value * value
    )


def allowed_keys(start, count, key_count, length):
    query_pos = start + lax.broadcasted_iota(jnp.int32, (count, key_count), 0)
    key_pos = lax.broadcasted_iota(jnp.int32, (count, key_count), 1)
    return (key_pos <= query_pos) & (key_pos < length) | (key_pos == query_pos)


def attend_forward(query, keys, values, length, block):
    seq = keys.shape[1]
    scale = float(query.shape[-1]) ** (-0.5)
    results = []
    log_parts = []
    for start in range(0, seq, block):
        stop = start + block
        score = (
            jnp.einsum(
                "hqd,hkd->hqk",
                query[:, start:stop],
                keys[:, :stop],
                preferred_element_type=F32,
            )
            * scale
        )
        score = jnp.where(allowed_keys(start, block, stop, length)[None], score, NEG_FILL)
        peak = jnp.max(score, axis=-1, keepdims=True)
        expo = jnp.exp(score - peak)
        total = jnp.sum(expo, axis=-1, keepdims=True)
        weights = (expo / total).astype(BF16)
        results.append(
            jnp.einsum("hqk,hkd->hqd", weights, values[:, :stop], preferred_element_type=F32)
        )
        log_parts.append(peak[..., 0] + jnp.log(total[..., 0]))
    return (jnp.concatenate(results, 1), jnp.concatenate(log_parts, 1))


def attend_backward(query, keys, values, upstream, log_total, length, block):
    seq = keys.shape[1]
    scale = float(query.shape[-1]) ** (-0.5)
    keys_sum = jnp.zeros(keys.shape, F32)
    values_sum = jnp.zeros(values.shape, F32)
    query_parts = []
    for start in range(0, seq, block):
        stop = start + block
        query_block = query[:, start:stop]
        upstream_block = upstream[:, start:stop]
        keys_block = keys[:, :stop]
        score = (
            jnp.einsum("hqd,hkd->hqk", query_block, keys_block, preferred_element_type=F32) * scale
        )
        score = jnp.where(allowed_keys(start, block, stop, length)[None], score, NEG_FILL)
        prob = jnp.exp(score - log_total[:, start:stop, None])
        values_sum = values_sum.at[:, :stop].add(
            jnp.einsum(
                "hqk,hqd->hkd", prob.astype(BF16), upstream_block, preferred_element_type=F32
            )
        )
        prob_grad = jnp.einsum(
            "hqd,hkd->hqk", upstream_block, values[:, :stop], preferred_element_type=F32
        )
        score_grad = prob * (prob_grad - jnp.sum(prob * prob_grad, axis=-1, keepdims=True))
        score_grad = score_grad.astype(BF16)
        query_parts.append(
            jnp.einsum("hqk,hkd->hqd", score_grad, keys_block, preferred_element_type=F32) * scale
        )
        keys_sum = keys_sum.at[:, :stop].add(
            jnp.einsum("hqk,hqd->hkd", score_grad, query_block, preferred_element_type=F32) * scale
        )
    return (jnp.concatenate(query_parts, 1), keys_sum, values_sum)


def to_heads(flat):
    return flat.reshape(flat.shape[0], HEADS, flat.shape[1] // HEADS).transpose(1, 0, 2)


def from_heads(heads):
    return heads.transpose(1, 0, 2).reshape(heads.shape[1], -1)


def take_row(array, place):
    return lax.dynamic_slice(array, (place, 0), (1, array.shape[1]))


def put_row(array, row, place):
    return lax.dynamic_update_slice(array, row.astype(array.dtype), (place, 0))


def add_row(array, row, place):
    return put_row(array, take_row(array, place) + row, place)


def row_probs(q_row, keys, place):
    width = keys.shape[1]
    heads = q_row.reshape(HEADS, width // HEADS)
    key_heads = keys.reshape(keys.shape[0], HEADS, width // HEADS)
    score = jnp.einsum("hd,khd->hk", heads, key_heads, preferred_element_type=F32) * 0.125
    key_pos = lax.broadcasted_iota(jnp.int32, score.shape, 1)
    score = jnp.where(key_pos <= place, score, NEG_FILL)
    peak = jnp.max(score, axis=-1, keepdims=True)
    expo = jnp.exp(score - peak)
    return expo / jnp.sum(expo, axis=-1, keepdims=True)


def gathered(value):
    return lax.all_gather(value, AXES, axis=0, tiled=True)


def scattered(value):
    return lax.psum_scatter(value, AXES, scatter_dimension=0, tiled=True)


def per_device(
    hidden,
    cotangent,
    lengths,
    thought_start,
    first_gain,
    first_bias,
    project_weight,
    project_bias,
    output_weight,
    output_bias,
    second_gain,
    second_bias,
    expand_weight,
    expand_bias,
    contract_weight,
    contract_bias,
):
    _, seq, width = hidden.shape
    dim = width // HEADS
    start = thought_start[0]
    length = lengths[0]
    Wp = gathered(project_weight)
    Wo = gathered(output_weight)
    We = gathered(expand_weight)
    Wc = gathered(contract_weight)
    g1 = gathered(first_gain).astype(F32)[None]
    b1 = gathered(first_bias).astype(F32)[None]
    bp = gathered(project_bias).astype(F32)
    bp = jnp.concatenate([bp[:width], jnp.zeros((width,), F32), bp[width:]])[None]
    bo = gathered(output_bias).astype(F32)[None]
    g2 = gathered(second_gain).astype(F32)[None]
    b2 = gathered(second_bias).astype(F32)[None]
    be = gathered(expand_bias).astype(F32)[None]
    bc = gathered(contract_bias).astype(F32)[None]

    def project(rows):
        normed = (norm_parts(rows)[0] * g1 + b1).astype(BF16)
        return (dot(normed, Wp) + bp).astype(BF16)

    def after_attention(rows, context):
        resid = rows + (dot(context, Wo) + bo)
        normed = (norm_parts(resid)[0] * g2 + b2).astype(BF16)
        pre = dot(normed, We) + be
        active = smooth_gelu(pre).astype(BF16)
        return resid, normed, pre, active, resid + (dot(active, Wc) + bc)

    x = hidden[0].astype(F32)
    mixed = project(x)
    keys = mixed[:PREFIX, width : 2 * width]
    values = mixed[:PREFIX, 2 * width :]
    x_row = take_row(x, start - 1)
    mixed_row = take_row(mixed, start - 1)
    for step in range(THOUGHTS):
        place = start + (step - 1)
        prob = row_probs(mixed_row[:, :width], keys, place).astype(BF16)
        context = jnp.einsum(
            "hk,khd->hd", prob, values.reshape(PREFIX, HEADS, dim), preferred_element_type=F32
        )
        context = context.reshape(1, width).astype(BF16)
        x_row = after_attention(x_row, context)[-1]
        mixed_row = project(x_row)
        x = put_row(x, x_row, place + 1)
        mixed = put_row(mixed, mixed_row, place + 1)
        keys = put_row(keys, mixed_row[:, width : 2 * width], place + 1)
        values = put_row(values, mixed_row[:, 2 * width :], place + 1)

    query_heads = to_heads(mixed[:, :width])
    key_heads = to_heads(mixed[:, width : 2 * width])
    value_heads = to_heads(mixed[:, 2 * width :])
    context, log_total = attend_forward(query_heads, key_heads, value_heads, length, 512)
    context = from_heads(context).astype(BF16)
    resid, normed_two, pre, active, result = after_attention(x, context)
    valid = lax.broadcasted_iota(jnp.int32, (seq, 1), 0) < length
    final = jnp.where(valid, result, 0.0)

    dout = jnp.where(valid, cotangent[0], 0)
    slope = gelu_slope(pre)
    resid_hat, resid_inv = norm_parts(resid)
    dz = dout
    df = (dot_t(dz, Wc) * slope).astype(BF16)
    dc = dot_t(df, We)
    dh = dout.astype(F32) + norm_back(dc, resid_hat, resid_inv, g2)
    dy = dh.astype(BF16)
    dctx = dot_t(dy, Wo).astype(BF16)
    dq, dk, dv = attend_backward(
        query_heads, key_heads, value_heads, to_heads(dctx), log_total, length, 512
    )
    dmixed = jnp.concatenate([from_heads(dq), from_heads(dk), from_heads(dv)], 1)

    x_hat, x_inv = norm_parts(x)

    def input_back(dmixed_row, place):
        da_row = dot_t(dmixed_row.astype(BF16), Wp)
        return norm_back(da_row, take_row(x_hat, place), take_row(x_inv, place), g1)

    scale = 0.125
    for step in reversed(range(THOUGHTS)):
        place = start + (step - 1)
        g_row = take_row(dh, place + 1) + input_back(take_row(dmixed, place + 1), place + 1)
        dz_row = g_row.astype(BF16)
        df_row = (dot_t(dz_row, Wc) * take_row(slope, place)).astype(BF16)
        dc_row = dot_t(df_row, We)
        dh_row = g_row + norm_back(dc_row, take_row(resid_hat, place), take_row(resid_inv, place), g2)
        dy_row = dh_row.astype(BF16)
        dctx_row = dot_t(dy_row, Wo).astype(BF16)
        mixed_row = take_row(mixed, place)
        prob = row_probs(mixed_row[:, :width], keys, place)
        dctx_heads = dctx_row.reshape(HEADS, dim)
        query_row = mixed_row[:, :width].reshape(HEADS, dim)
        dprob = jnp.einsum(
            "hd,khd->hk",
            dctx_heads,
            values.reshape(PREFIX, HEADS, dim),
            preferred_element_type=F32,
        )
        dscore = prob * (dprob - jnp.sum(prob * dprob, axis=-1, keepdims=True))
        dscore = dscore.astype(BF16)
        dq_row = (
            jnp.einsum(
                "hk,khd->hd",
                dscore,
                keys.reshape(PREFIX, HEADS, dim),
                preferred_element_type=F32,
            )
            * scale
        )
        dk_extra = dscore.astype(F32).T[:, :, None] * (query_row.astype(F32) * scale)[None]
        dv_extra = prob.astype(BF16).astype(F32).T[:, :, None] * dctx_heads.astype(F32)[None]
        extra = jnp.concatenate(
            [
                jnp.zeros((PREFIX, width), F32),
                dk_extra.reshape(PREFIX, width),
                dv_extra.reshape(PREFIX, width),
            ],
            1,
        )
        dmixed = dmixed.at[:PREFIX].add(extra)
        dmixed = add_row(
            dmixed,
            jnp.concatenate([dq_row.reshape(1, width), jnp.zeros((1, 2 * width), F32)], 1),
            place,
        )
        dz = add_row(dz, dz_row, place)
        df = add_row(df, df_row, place)
        dc = add_row(dc, dc_row, place)
        dh = add_row(dh, dh_row, place)
        dy = add_row(dy, dy_row, place)

    dmixed = dmixed.astype(BF16)
    da = dot_t(dmixed, Wp)
    dx = dh + norm_back(da, x_hat, x_inv, g1)
    position = lax.broadcasted_iota(jnp.int32, (seq, 1), 0)
    is_thought = (position >= start) & (position < start + THOUGHTS)
    hidden_grad = jnp.where(is_thought, 0.0, dx)

    normed = (x_hat * g1 + b1).astype(BF16)

    def column_sum(value):
        return jnp.sum(value, axis=0, dtype=F32)

    column = column_sum(dmixed)
    grads = (
        column_sum(da * x_hat),
        column_sum(da),
        dot_g(normed, dmixed).astype(BF16),
        jnp.concatenate([column[:width], column[2 * width :]]),
        dot_g(context, dy).astype(BF16),
        column_sum(dy),
        column_sum(dc * resid_hat),
        column_sum(dc),
        dot_g(normed_two, df).astype(BF16),
        column_sum(df),
        dot_g(active, dz).astype(BF16),
        column_sum(dz),
    )
    grads = tuple(scattered(grad).astype(F32) for grad in grads)
    return (final[None], hidden_grad[None]) + grads


def solution(mesh):
    rows = P(AXES, None, None)
    flat = P(AXES)
    square = P(AXES, None)
    params = (flat, flat, square, flat, square, flat, flat, flat, square, flat, square, flat)
    return jax.shard_map(
        per_device,
        mesh=mesh,
        in_specs=(rows, rows, flat, flat) + params,
        out_specs=(rows, rows) + params,
        check_vma=False,
    )
```

```python
import functools

import jax
import jax.numpy as jnp
from jax import lax
from jax.experimental import pallas as pl
from jax.experimental.pallas import tpu as pltpu
from jax.sharding import PartitionSpec as P

HEADS = 12
THOUGHTS = 3
PREFIX = 384

EPSILON = 1e-05
NEG_FILL = -1e30
F32 = jnp.float32
BF16 = jnp.bfloat16


AXES = ("dp", "fsdp")
ANY = pl.BlockSpec(memory_space=pl.ANY)
DMA = pltpu.SemaphoreType.DMA


class Place:
    def __init__(self, rows, depths, sides):
        self.rows, self.depths, self.sides = rows, depths, sides
        self.row = lax.axis_index("dp")
        flat = lax.axis_index("fsdp")
        self.depth = flat // (sides * 2)
        self.side = flat // 2 % sides
        self.core = flat % 2

    def index(self, row, depth, side, core):
        return row * (self.depths * self.sides * 2) + (depth * self.sides + side) * 2 + core

    def device(self, row, depth, side, core):
        return {"dp": row, "fsdp": (depth * self.sides + side) * 2 + core}


def gather_kernel(rows, depths, sides, count, *refs):
    shards, fulls = refs[:count], refs[count : 2 * count]
    send_sem, recv_sem, pair_send, pair_recv, own_sem = refs[2 * count :]
    at = Place(rows, depths, sides)
    dev = dict(device_id_type=pl.DeviceIdType.MESH)

    barrier = pltpu.get_barrier_semaphore()
    peers = []
    for k in range(1, depths):
        peers.append(at.device(at.row, (at.depth + k) % depths, at.side, at.core))
    for k in range(1, sides):
        peers.append(at.device(at.row, at.depth, (at.side + k) % sides, at.core))
    for k in range(1, rows):
        peers.append(at.device((at.row + k) % rows, at.depth, at.side, at.core))
    peers.append(at.device(at.row, at.depth, at.side, 1 - at.core))
    for peer in peers:
        pl.semaphore_signal(barrier, inc=1, device_id=peer, **dev)
    pl.semaphore_wait(barrier, len(peers))

    def run(core):
        sends = []

        def index(row, depth, side):
            return at.index(row, depth, side, core)

        def send(w, source, shard, peer, slot):
            copy = pltpu.make_async_remote_copy(
                src_ref=source,
                dst_ref=fulls[w].at[shard],
                send_sem=send_sem.at[w, slot],
                recv_sem=recv_sem.at[w, shard],
                device_id=peer,
                **dev,
            )
            copy.start()
            sends.append(copy)

        def arrive(w, shard):
            pltpu.make_async_remote_copy(
                src_ref=fulls[w].at[shard],
                dst_ref=fulls[w].at[shard],
                send_sem=send_sem.at[w, 0],
                recv_sem=recv_sem.at[w, shard],
                device_id=peers[0],
                **dev,
            ).wait_recv()

        def to_pair(w, source, shard):
            copy = pltpu.make_async_remote_copy(
                src_ref=source,
                dst_ref=fulls[w].at[shard],
                send_sem=pair_send.at[w, shard // 2],
                recv_sem=pair_recv.at[w, shard // 2],
                device_id=at.device(at.row, at.depth, at.side, 1 - core),
                **dev,
            )
            copy.start()
            sends.append(copy)

        slots = [0] * count

        def slot(w):
            slots[w] += 1
            return slots[w] - 1

        second_size, third_size = (sides, rows) if core == 0 else (rows, sides)

        def spot(second, third):
            return (third, second) if core == 0 else (second, third)

        mine = (at.side, at.row) if core == 0 else (at.row, at.side)

        def forward_second(w, source, depth):
            row, side = spot(*mine)
            for k in range(1, second_size):
                r, s = spot((mine[0] + k) % second_size, mine[1])
                send(w, source, index(row, depth, side), at.device(r, at.depth, s, core), slot(w))

        def forward_third(w, source, depth, second):
            row, side = spot(second, mine[1])
            for k in range(1, third_size):
                r, s = spot(mine[0], (mine[1] + k) % third_size)
                send(w, source, index(row, depth, side), at.device(r, at.depth, s, core), slot(w))

        own = []
        for w in range(count):
            me = index(at.row, at.depth, at.side)
            for k in range(1, depths):
                send(w, shards[w], me, at.device(at.row, (at.depth + k) % depths, at.side, core), slot(w))
            forward_second(w, shards[w], at.depth)
            forward_third(w, shards[w], at.depth, mine[0])
            to_pair(w, shards[w], me)
            copy = pltpu.make_async_copy(shards[w], fulls[w].at[me], own_sem.at[w])
            copy.start()
            own.append(copy)

        def stage_one(w):
            for k in range(1, depths):
                depth = (at.depth - k) % depths
                shard = index(at.row, depth, at.side)
                arrive(w, shard)
                forward_second(w, fulls[w].at[shard], depth)
                forward_third(w, fulls[w].at[shard], depth, mine[0])
                to_pair(w, fulls[w].at[shard], shard)

        def stage_two(w):
            for k in range(1, second_size):
                second = (mine[0] - k) % second_size
                for d in range(depths):
                    depth = (at.depth - d) % depths
                    shard = index(spot(second, mine[1])[0], depth, spot(second, mine[1])[1])
                    arrive(w, shard)
                    forward_third(w, fulls[w].at[shard], depth, second)
                    to_pair(w, fulls[w].at[shard], shard)

        def stage_three(w):
            for k in range(1, third_size):
                third = (mine[1] - k) % third_size
                for s in range(second_size):
                    second = (mine[0] - s) % second_size
                    for d in range(depths):
                        depth = (at.depth - d) % depths
                        row, side = spot(second, third)
                        shard = index(row, depth, side)
                        arrive(w, shard)
                        to_pair(w, fulls[w].at[shard], shard)

        for step in range(count + 2):
            if step < count:
                stage_one(step)
            if 0 <= step - 1 < count:
                stage_two(step - 1)
            if 0 <= step - 2 < count:
                stage_three(step - 2)

        for w in range(count):
            for row in range(rows):
                for depth in range(depths):
                    for side in range(sides):
                        shard = at.index(row, depth, side, 1 - core)
                        pltpu.make_async_remote_copy(
                            src_ref=fulls[w].at[shard],
                            dst_ref=fulls[w].at[shard],
                            send_sem=pair_send.at[w, shard // 2],
                            recv_sem=pair_recv.at[w, shard // 2],
                            device_id=peers[0],
                            **dev,
                        ).wait_recv()
        for copy in own:
            copy.wait()
        for copy in sends:
            copy.wait_send()

    for core in range(2):

        @pl.when(at.core == core)
        def _():
            run(core)


def gather_all(mesh_shape, shards, collective_id=0):
    rows, inner = mesh_shape["dp"], mesh_shape["fsdp"]
    depths = 4
    sides = inner // (2 * depths)
    total = rows * inner
    count = len(shards)
    sent = (depths - 1) + depths * (max(rows, sides) - 1) + depths * sides * (rows - 1) + depths * rows * (sides - 1)
    return pl.pallas_call(
        functools.partial(gather_kernel, rows, depths, sides, count),
        out_shape=[jax.ShapeDtypeStruct((total,) + s.shape, s.dtype) for s in shards],
        in_specs=[ANY] * count,
        out_specs=[ANY] * count,
        scratch_shapes=[
            DMA((count, sent)),
            DMA((count, total)),
            DMA((count, total // 2)),
            DMA((count, total // 2)),
            DMA((count,)),
        ],
        compiler_params=pltpu.CompilerParams(collective_id=collective_id, has_side_effects=True),
        name="gather_weights",
    )(*shards)


def scatter_kernel(rows, depths, sides, count, *refs):
    parts, outs = refs[:count], refs[count : 2 * count]
    scratch = refs[2 * count :]
    held, pair, third_in, second_in, depth_in = (scratch[i * count : (i + 1) * count] for i in range(5))
    (own_sem, pair_send, pair_recv, third_send, third_recv, second_send, second_recv, depth_send, depth_recv) = scratch[
        5 * count :
    ]
    at = Place(rows, depths, sides)
    dev = dict(device_id_type=pl.DeviceIdType.MESH)

    barrier = pltpu.get_barrier_semaphore()
    peers = []
    for k in range(1, depths):
        peers.append(at.device(at.row, (at.depth + k) % depths, at.side, at.core))
    for k in range(1, sides):
        peers.append(at.device(at.row, at.depth, (at.side + k) % sides, at.core))
    for k in range(1, rows):
        peers.append(at.device((at.row + k) % rows, at.depth, at.side, at.core))
    peers.append(at.device(at.row, at.depth, at.side, 1 - at.core))
    for peer in peers:
        pl.semaphore_signal(barrier, inc=1, device_id=peer, **dev)
    pl.semaphore_wait(barrier, len(peers))

    def run(core):
        second_size, third_size = (sides, rows) if core == 0 else (rows, sides)
        my_second, my_third = (at.side, at.row) if core == 0 else (at.row, at.side)

        def unit(second, third, depth):
            row, side = (third, second) if core == 0 else (second, third)
            return (row * depths + depth) * sides + side

        def device(second, third, depth):
            row, side = (third, second) if core == 0 else (second, third)
            return at.device(row, depth, side, core)

        def remote(source, target, send, recv, peer):
            return pltpu.make_async_remote_copy(
                src_ref=source, dst_ref=target, send_sem=send, recv_sem=recv, device_id=peer, **dev
            )

        sibling = at.device(at.row, at.depth, at.side, 1 - core)

        def pair_copy(w, u):
            return remote(
                parts[w].at[u, 1 - core], pair[w].at[u], pair_send.at[w], pair_recv.at[w, u], sibling
            )

        def own_copy(w):
            return pltpu.make_async_copy(parts[w].at[:, core], held[w], own_sem.at[w])

        def third_copy(w, u, k, q, peer):
            return remote(
                held[w].at[u],
                third_in[w].at[k - 1, q],
                third_send.at[w, k - 1, q],
                third_recv.at[w, k - 1, q],
                peer,
            )

        def second_copy(w, u, k, q, peer):
            return remote(
                held[w].at[u],
                second_in[w].at[k - 1, q],
                second_send.at[w, k - 1, q],
                second_recv.at[w, k - 1, q],
                peer,
            )

        def depth_copy(w, u, k, peer):
            return remote(
                held[w].at[u], depth_in[w].at[k - 1], depth_send.at[w, k - 1], depth_recv.at[w, k - 1], peer
            )

        def loop(size, body):
            lax.fori_loop(0, size, lambda i, c: (body(i), c)[1], 0)

        def each_unit(visit):
            other_second, other_third = third_size, second_size
            far = my_second
            for k in list(range(1, other_third)) + [0]:
                def inner(q, k=k):
                    second, third = q // depths, (far + k) % other_third
                    row, side = (second, third) if core == 0 else (third, second)
                    visit((row * depths + q % depths) * sides + side)
                loop(other_second * depths, inner)

        for w in range(count):
            each_unit(lambda u, w=w: pair_copy(w, u).start())
            own_copy(w).start()

        def add_pair(w, u):
            pair_copy(w, u).wait_recv()
            held[w][u] = held[w][u] + pair[w][u]

        def stage_third(w):
            own_copy(w).wait()
            for k in list(range(1, third_size)) + [0]:
                third = (my_third + k) % third_size

                def inner(q, k=k, third=third):
                    second, depth = q // depths, q % depths
                    u = unit(second, third, depth)
                    add_pair(w, u)
                    if k:
                        third_copy(w, u, k, q, device(my_second, third, at.depth)).start()

                loop(second_size * depths, inner)

        def stage_second(w):
            for k in list(range(1, second_size)) + [0]:
                second = (my_second + k) % second_size

                def inner(depth, k=k, second=second):
                    u = unit(second, my_third, depth)
                    for j in range(1, third_size):
                        third_copy(w, u, j, second * depths + depth, sibling).wait_recv()
                        held[w][u] = held[w][u] + third_in[w][j - 1, second * depths + depth]
                    if k:
                        second_copy(w, u, k, depth, device(second, my_third, at.depth)).start()

                loop(depths, inner)

        def stage_depth(w):
            for k in list(range(1, depths)) + [0]:
                depth = (at.depth + k) % depths
                u = unit(my_second, my_third, depth)
                for j in range(1, second_size):
                    second_copy(w, u, j, depth, sibling).wait_recv()
                    held[w][u] = held[w][u] + second_in[w][j - 1, depth]
                if k:
                    depth_copy(w, u, k, device(my_second, my_third, depth)).start()

        def stage_last(w):
            u = unit(my_second, my_third, at.depth)
            total = held[w][u].astype(jnp.float32)
            for k in range(1, depths):
                depth_copy(w, u, k, sibling).wait_recv()
                total = total + depth_in[w][k - 1].astype(jnp.float32)
            outs[w][...] = total

        for step in range(count + 3):
            for lag, stage in enumerate((stage_third, stage_second, stage_depth, stage_last)):
                if 0 <= step - lag < count:
                    stage(step - lag)

        for w in range(count):
            remote(pair[w], pair[w], pair_send.at[w], pair_recv.at[w, 0], sibling).wait_send()
            for k in range(1, third_size):
                loop(second_size * depths, lambda q, w=w, k=k: third_copy(w, 0, k, q, sibling).wait_send())
            for k in range(1, second_size):
                loop(depths, lambda q, w=w, k=k: second_copy(w, 0, k, q, sibling).wait_send())
            for k in range(1, depths):
                depth_copy(w, 0, k, sibling).wait_send()

    for core in range(2):

        @pl.when(at.core == core)
        def _():
            run(core)


def scatter_all(mesh_shape, parts, collective_id=1):
    rows, inner = mesh_shape["dp"], mesh_shape["fsdp"]
    depths = 4
    sides = inner // (2 * depths)
    total = rows * inner
    half = total // 2
    count = len(parts)
    if rows == sides:
        thirds, seconds = (rows - 1, sides * depths), (sides - 1, depths)
    else:
        wide = max(rows, sides)
        thirds, seconds = (wide - 1, wide * depths), (wide - 1, depths)
    scratch = []
    for lead in ((half,), (half,), thirds, seconds, (depths - 1,)):
        scratch += [pltpu.VMEM(lead + p.shape[1:], p.dtype) for p in parts]
    parts = [p.reshape((half, 2) + p.shape[1:]) for p in parts]
    sems = [
        (), (), (half,), thirds, thirds, seconds, seconds, (depths - 1,), (depths - 1,),
    ]
    return pl.pallas_call(
        functools.partial(scatter_kernel, rows, depths, sides, count),
        out_shape=[jax.ShapeDtypeStruct(p.shape[2:], jnp.float32) for p in parts],
        in_specs=[ANY] * count,
        out_specs=[pl.BlockSpec(memory_space=pltpu.VMEM)] * count,
        scratch_shapes=scratch + [DMA((count,) + s) for s in sems],
        compiler_params=pltpu.CompilerParams(
            collective_id=collective_id, has_side_effects=True, vmem_limit_bytes=60 * 2**20
        ),
        name="scatter_grads",
    )(*parts)


def dot(left, right):
    return jnp.dot(left, right, preferred_element_type=F32)


def dot_t(left, right):
    return jnp.einsum("nf,df->nd", left, right, preferred_element_type=F32)


def dot_g(left, right):
    return jnp.einsum("nd,ne->de", left, right, preferred_element_type=F32)


def norm_parts(value):
    center = value - jnp.mean(value, axis=-1, keepdims=True)
    inv = lax.rsqrt(jnp.mean(center * center, axis=-1, keepdims=True) + EPSILON)
    return center * inv, inv


def norm_back(grad, hat, inv, gain):
    scaled = grad * gain
    return inv * (
        scaled
        - jnp.mean(scaled, axis=-1, keepdims=True)
        - hat * jnp.mean(scaled * hat, axis=-1, keepdims=True)
    )


def smooth_gelu(value):
    return jax.nn.gelu(value, approximate=True)


def gelu_slope(value):
    root = 0.7978845608028654
    inner = jnp.tanh(root * (value + 0.044715 * value * value * value))
    return 0.5 * (1.0 + inner) + 0.5 * value * (1.0 - inner * inner) * root * (
        1.0 + 3 * 0.044715 * value * value
    )


def allowed_keys(start, count, key_count, length):
    query_pos = start + lax.broadcasted_iota(jnp.int32, (count, key_count), 0)
    key_pos = lax.broadcasted_iota(jnp.int32, (count, key_count), 1)
    return (key_pos <= query_pos) & (key_pos < length) | (key_pos == query_pos)


def attend_forward(query, keys, values, length, block):
    seq = keys.shape[1]
    scale = float(query.shape[-1]) ** (-0.5)
    results = []
    log_parts = []
    for start in range(0, seq, block):
        stop = start + block
        score = (
            jnp.einsum(
                "hqd,hkd->hqk",
                query[:, start:stop],
                keys[:, :stop],
                preferred_element_type=F32,
            )
            * scale
        )
        score = jnp.where(allowed_keys(start, block, stop, length)[None], score, NEG_FILL)
        peak = jnp.max(score, axis=-1, keepdims=True)
        expo = jnp.exp(score - peak)
        total = jnp.sum(expo, axis=-1, keepdims=True)
        weights = (expo / total).astype(BF16)
        results.append(
            jnp.einsum("hqk,hkd->hqd", weights, values[:, :stop], preferred_element_type=F32)
        )
        log_parts.append(peak[..., 0] + jnp.log(total[..., 0]))
    return (jnp.concatenate(results, 1), jnp.concatenate(log_parts, 1))


def attend_backward(query, keys, values, upstream, log_total, length, block):
    seq = keys.shape[1]
    scale = float(query.shape[-1]) ** (-0.5)
    keys_sum = jnp.zeros(keys.shape, F32)
    values_sum = jnp.zeros(values.shape, F32)
    query_parts = []
    for start in range(0, seq, block):
        stop = start + block
        query_block = query[:, start:stop]
        upstream_block = upstream[:, start:stop]
        keys_block = keys[:, :stop]
        score = (
            jnp.einsum("hqd,hkd->hqk", query_block, keys_block, preferred_element_type=F32) * scale
        )
        score = jnp.where(allowed_keys(start, block, stop, length)[None], score, NEG_FILL)
        prob = jnp.exp(score - log_total[:, start:stop, None])
        values_sum = values_sum.at[:, :stop].add(
            jnp.einsum(
                "hqk,hqd->hkd", prob.astype(BF16), upstream_block, preferred_element_type=F32
            )
        )
        prob_grad = jnp.einsum(
            "hqd,hkd->hqk", upstream_block, values[:, :stop], preferred_element_type=F32
        )
        score_grad = prob * (prob_grad - jnp.sum(prob * prob_grad, axis=-1, keepdims=True))
        score_grad = score_grad.astype(BF16)
        query_parts.append(
            jnp.einsum("hqk,hkd->hqd", score_grad, keys_block, preferred_element_type=F32) * scale
        )
        keys_sum = keys_sum.at[:, :stop].add(
            jnp.einsum("hqk,hqd->hkd", score_grad, query_block, preferred_element_type=F32) * scale
        )
    return (jnp.concatenate(query_parts, 1), keys_sum, values_sum)


def to_heads(flat):
    return flat.reshape(flat.shape[0], HEADS, flat.shape[1] // HEADS).transpose(1, 0, 2)


def from_heads(heads):
    return heads.transpose(1, 0, 2).reshape(heads.shape[1], -1)


def take_row(array, place):
    return lax.dynamic_slice(array, (place, 0), (1, array.shape[1]))


def put_row(array, row, place):
    return lax.dynamic_update_slice(array, row.astype(array.dtype), (place, 0))


def add_row(array, row, place):
    return put_row(array, take_row(array, place) + row, place)


def row_probs(q_row, keys, place):
    width = keys.shape[1]
    heads = q_row.reshape(HEADS, width // HEADS)
    key_heads = keys.reshape(keys.shape[0], HEADS, width // HEADS)
    score = jnp.einsum("hd,khd->hk", heads, key_heads, preferred_element_type=F32) * 0.125
    key_pos = lax.broadcasted_iota(jnp.int32, score.shape, 1)
    score = jnp.where(key_pos <= place, score, NEG_FILL)
    peak = jnp.max(score, axis=-1, keepdims=True)
    expo = jnp.exp(score - peak)
    return expo / jnp.sum(expo, axis=-1, keepdims=True)


def pack(vectors, total):
    joined = jnp.concatenate([v.reshape(total, -1) for v in vectors], 1)
    fill = -joined.shape[1] % 128
    return jnp.pad(joined, ((0, 0), (0, fill)))[:, None]


def unpack(packed, sizes):
    flat = packed.reshape(-1, packed.shape[-1])
    out, at = [], 0
    for size in sizes:
        out.append(flat[:, at : at + size].reshape(-1))
        at += size
    return out


def per_device(
    mesh_shape,
    hidden,
    cotangent,
    lengths,
    thought_start,
    first_gain,
    first_bias,
    project_weight,
    project_bias,
    output_weight,
    output_bias,
    second_gain,
    second_bias,
    expand_weight,
    expand_bias,
    contract_weight,
    contract_bias,
):
    _, seq, width = hidden.shape
    dim = width // HEADS
    start = thought_start[0]
    length = lengths[0]
    total = mesh_shape["dp"] * mesh_shape["fsdp"]
    vectors = (
        first_gain,
        first_bias,
        project_bias,
        output_bias,
        second_gain,
        second_bias,
        expand_bias,
        contract_bias,
    )
    sizes = [v.shape[0] for v in vectors]
    full = gather_all(
        mesh_shape,
        (pack(vectors, 1)[0], project_weight, output_weight, expand_weight, contract_weight),
    )
    vectors = [v.astype(F32)[None] for v in unpack(full[0], sizes)]
    g1, b1, bp, bo, g2, b2, be, bc = vectors
    bp = jnp.concatenate([bp[:, :width], jnp.zeros((1, width), F32), bp[:, width:]], 1)
    Wp, Wo, We, Wc = (w.reshape(-1, w.shape[-1]) for w in full[1:])

    def project(rows):
        normed = (norm_parts(rows)[0] * g1 + b1).astype(BF16)
        return (dot(normed, Wp) + bp).astype(BF16)

    def after_attention(rows, context):
        resid = rows + (dot(context, Wo) + bo)
        normed = (norm_parts(resid)[0] * g2 + b2).astype(BF16)
        pre = dot(normed, We) + be
        active = smooth_gelu(pre).astype(BF16)
        return resid, normed, pre, active, resid + (dot(active, Wc) + bc)

    x = hidden[0].astype(F32)
    mixed = project(x)
    keys = mixed[:PREFIX, width : 2 * width]
    values = mixed[:PREFIX, 2 * width :]
    x_row = take_row(x, start - 1)
    mixed_row = take_row(mixed, start - 1)
    for step in range(THOUGHTS):
        place = start + (step - 1)
        prob = row_probs(mixed_row[:, :width], keys, place).astype(BF16)
        context = jnp.einsum(
            "hk,khd->hd", prob, values.reshape(PREFIX, HEADS, dim), preferred_element_type=F32
        )
        context = context.reshape(1, width).astype(BF16)
        x_row = after_attention(x_row, context)[-1]
        mixed_row = project(x_row)
        x = put_row(x, x_row, place + 1)
        mixed = put_row(mixed, mixed_row, place + 1)
        keys = put_row(keys, mixed_row[:, width : 2 * width], place + 1)
        values = put_row(values, mixed_row[:, 2 * width :], place + 1)

    query_heads = to_heads(mixed[:, :width])
    key_heads = to_heads(mixed[:, width : 2 * width])
    value_heads = to_heads(mixed[:, 2 * width :])
    context, log_total = attend_forward(query_heads, key_heads, value_heads, length, 512)
    context = from_heads(context).astype(BF16)
    resid, normed_two, pre, active, result = after_attention(x, context)
    valid = lax.broadcasted_iota(jnp.int32, (seq, 1), 0) < length
    final = jnp.where(valid, result, 0.0)

    dout = jnp.where(valid, cotangent[0], 0)
    slope = gelu_slope(pre)
    resid_hat, resid_inv = norm_parts(resid)
    dz = dout
    df = (dot_t(dz, Wc) * slope).astype(BF16)
    dc = dot_t(df, We)
    dh = dout.astype(F32) + norm_back(dc, resid_hat, resid_inv, g2)
    dy = dh.astype(BF16)
    dctx = dot_t(dy, Wo).astype(BF16)
    dq, dk, dv = attend_backward(
        query_heads, key_heads, value_heads, to_heads(dctx), log_total, length, 512
    )
    dmixed = jnp.concatenate([from_heads(dq), from_heads(dk), from_heads(dv)], 1)

    x_hat, x_inv = norm_parts(x)

    def input_back(dmixed_row, place):
        da_row = dot_t(dmixed_row.astype(BF16), Wp)
        return norm_back(da_row, take_row(x_hat, place), take_row(x_inv, place), g1)

    scale = 0.125
    for step in reversed(range(THOUGHTS)):
        place = start + (step - 1)
        g_row = take_row(dh, place + 1) + input_back(take_row(dmixed, place + 1), place + 1)
        dz_row = g_row.astype(BF16)
        df_row = (dot_t(dz_row, Wc) * take_row(slope, place)).astype(BF16)
        dc_row = dot_t(df_row, We)
        dh_row = g_row + norm_back(dc_row, take_row(resid_hat, place), take_row(resid_inv, place), g2)
        dy_row = dh_row.astype(BF16)
        dctx_row = dot_t(dy_row, Wo).astype(BF16)
        mixed_row = take_row(mixed, place)
        prob = row_probs(mixed_row[:, :width], keys, place)
        dctx_heads = dctx_row.reshape(HEADS, dim)
        query_row = mixed_row[:, :width].reshape(HEADS, dim)
        dprob = jnp.einsum(
            "hd,khd->hk",
            dctx_heads,
            values.reshape(PREFIX, HEADS, dim),
            preferred_element_type=F32,
        )
        dscore = prob * (dprob - jnp.sum(prob * dprob, axis=-1, keepdims=True))
        dscore = dscore.astype(BF16)
        dq_row = (
            jnp.einsum(
                "hk,khd->hd",
                dscore,
                keys.reshape(PREFIX, HEADS, dim),
                preferred_element_type=F32,
            )
            * scale
        )
        dk_extra = dscore.astype(F32).T[:, :, None] * (query_row.astype(F32) * scale)[None]
        dv_extra = prob.astype(BF16).astype(F32).T[:, :, None] * dctx_heads.astype(F32)[None]
        extra = jnp.concatenate(
            [
                jnp.zeros((PREFIX, width), F32),
                dk_extra.reshape(PREFIX, width),
                dv_extra.reshape(PREFIX, width),
            ],
            1,
        )
        dmixed = dmixed.at[:PREFIX].add(extra)
        dmixed = add_row(
            dmixed,
            jnp.concatenate([dq_row.reshape(1, width), jnp.zeros((1, 2 * width), F32)], 1),
            place,
        )
        dz = add_row(dz, dz_row, place)
        df = add_row(df, df_row, place)
        dc = add_row(dc, dc_row, place)
        dh = add_row(dh, dh_row, place)
        dy = add_row(dy, dy_row, place)

    dmixed = dmixed.astype(BF16)
    da = dot_t(dmixed, Wp)
    dx = dh + norm_back(da, x_hat, x_inv, g1)
    position = lax.broadcasted_iota(jnp.int32, (seq, 1), 0)
    is_thought = (position >= start) & (position < start + THOUGHTS)
    hidden_grad = jnp.where(is_thought, 0.0, dx)

    normed = (x_hat * g1 + b1).astype(BF16)

    def column_sum(value):
        return jnp.sum(value, axis=0, dtype=F32)

    column = column_sum(dmixed)
    small = (
        column_sum(da * x_hat),
        column_sum(da),
        jnp.concatenate([column[:width], column[2 * width :]]),
        column_sum(dy),
        column_sum(dc * resid_hat),
        column_sum(dc),
        column_sum(df),
        column_sum(dz),
    )
    large = (
        dot_g(normed, dmixed),
        dot_g(context, dy),
        dot_g(normed_two, df),
        dot_g(active, dz),
    )
    parts = [pack(small, total)]
    for grad in large:
        parts.append(grad.astype(BF16).reshape(total, grad.shape[0] // total, grad.shape[1]))
    small, dWp, dWo, dWe, dWc = scatter_all(mesh_shape, parts)
    dg1, db1, dbp, dbo, dg2, db2, dbe, dbc = unpack(small, sizes)
    return (final[None], hidden_grad[None], dg1, db1, dWp, dbp, dWo, dbo, dg2, db2, dWe, dbe, dWc, dbc)


def solution(mesh):
    rows = P(AXES, None, None)
    flat = P(AXES)
    square = P(AXES, None)
    params = (flat, flat, square, flat, square, flat, flat, flat, square, flat, square, flat)
    return jax.shard_map(
        functools.partial(per_device, dict(mesh.shape)),
        mesh=mesh,
        in_specs=(rows, rows, flat, flat) + params,
        out_specs=(rows, rows) + params,
        check_vma=False,
    )
```

```python
import functools

import jax
import jax.numpy as jnp
from jax import lax
from jax.experimental import pallas as pl
from jax.experimental.pallas import tpu as pltpu
from jax.sharding import PartitionSpec as P

HEADS = 12
THOUGHTS = 3
PREFIX = 384
TILE = 256

EPSILON = 1e-05
NEG_FILL = -1e30
F32 = jnp.float32
BF16 = jnp.bfloat16
VMEM_LIMIT = 62 * 2**20


AXES = ("dp", "fsdp")
ANY = pl.BlockSpec(memory_space=pl.ANY)
DMA = pltpu.SemaphoreType.DMA


class Place:
    def __init__(self, rows, depths, sides):
        self.rows, self.depths, self.sides = rows, depths, sides
        self.row = lax.axis_index("dp")
        flat = lax.axis_index("fsdp")
        self.depth = flat // (sides * 2)
        self.side = flat // 2 % sides
        self.core = flat % 2

    def index(self, row, depth, side, core):
        return row * (self.depths * self.sides * 2) + (depth * self.sides + side) * 2 + core

    def device(self, row, depth, side, core):
        return {"dp": row, "fsdp": (depth * self.sides + side) * 2 + core}


def gather_kernel(rows, depths, sides, count, *refs):
    shards, fulls = refs[:count], refs[count : 2 * count]
    send_sem, recv_sem, pair_send, pair_recv, own_sem = refs[2 * count :]
    at = Place(rows, depths, sides)
    dev = dict(device_id_type=pl.DeviceIdType.MESH)

    barrier = pltpu.get_barrier_semaphore()
    peers = []
    for k in range(1, depths):
        peers.append(at.device(at.row, (at.depth + k) % depths, at.side, at.core))
    for k in range(1, sides):
        peers.append(at.device(at.row, at.depth, (at.side + k) % sides, at.core))
    for k in range(1, rows):
        peers.append(at.device((at.row + k) % rows, at.depth, at.side, at.core))
    peers.append(at.device(at.row, at.depth, at.side, 1 - at.core))
    for peer in peers:
        pl.semaphore_signal(barrier, inc=1, device_id=peer, **dev)
    pl.semaphore_wait(barrier, len(peers))

    def run(core):
        sends = []

        def index(row, depth, side):
            return at.index(row, depth, side, core)

        def send(w, source, shard, peer, slot):
            copy = pltpu.make_async_remote_copy(
                src_ref=source,
                dst_ref=fulls[w].at[shard],
                send_sem=send_sem.at[w, slot],
                recv_sem=recv_sem.at[w, shard],
                device_id=peer,
                **dev,
            )
            copy.start()
            sends.append(copy)

        def arrive(w, shard):
            pltpu.make_async_remote_copy(
                src_ref=fulls[w].at[shard],
                dst_ref=fulls[w].at[shard],
                send_sem=send_sem.at[w, 0],
                recv_sem=recv_sem.at[w, shard],
                device_id=peers[0],
                **dev,
            ).wait_recv()

        def to_pair(w, source, shard):
            copy = pltpu.make_async_remote_copy(
                src_ref=source,
                dst_ref=fulls[w].at[shard],
                send_sem=pair_send.at[w, shard // 2],
                recv_sem=pair_recv.at[w, shard // 2],
                device_id=at.device(at.row, at.depth, at.side, 1 - core),
                **dev,
            )
            copy.start()
            sends.append(copy)

        slots = [0] * count

        def slot(w):
            slots[w] += 1
            return slots[w] - 1

        second_size, third_size = (sides, rows) if core == 0 else (rows, sides)

        def spot(second, third):
            return (third, second) if core == 0 else (second, third)

        mine = (at.side, at.row) if core == 0 else (at.row, at.side)

        def forward_second(w, source, depth):
            row, side = spot(*mine)
            for k in range(1, second_size):
                r, s = spot((mine[0] + k) % second_size, mine[1])
                send(w, source, index(row, depth, side), at.device(r, at.depth, s, core), slot(w))

        def forward_third(w, source, depth, second):
            row, side = spot(second, mine[1])
            for k in range(1, third_size):
                r, s = spot(mine[0], (mine[1] + k) % third_size)
                send(w, source, index(row, depth, side), at.device(r, at.depth, s, core), slot(w))

        own = []
        for w in range(count):
            me = index(at.row, at.depth, at.side)
            for k in range(1, depths):
                send(w, shards[w], me, at.device(at.row, (at.depth + k) % depths, at.side, core), slot(w))
            forward_second(w, shards[w], at.depth)
            forward_third(w, shards[w], at.depth, mine[0])
            to_pair(w, shards[w], me)
            copy = pltpu.make_async_copy(shards[w], fulls[w].at[me], own_sem.at[w])
            copy.start()
            own.append(copy)

        def stage_one(w):
            for k in range(1, depths):
                depth = (at.depth - k) % depths
                shard = index(at.row, depth, at.side)
                arrive(w, shard)
                forward_second(w, fulls[w].at[shard], depth)
                forward_third(w, fulls[w].at[shard], depth, mine[0])
                to_pair(w, fulls[w].at[shard], shard)

        def stage_two(w):
            for k in range(1, second_size):
                second = (mine[0] - k) % second_size
                for d in range(depths):
                    depth = (at.depth - d) % depths
                    shard = index(spot(second, mine[1])[0], depth, spot(second, mine[1])[1])
                    arrive(w, shard)
                    forward_third(w, fulls[w].at[shard], depth, second)
                    to_pair(w, fulls[w].at[shard], shard)

        def stage_three(w):
            for k in range(1, third_size):
                third = (mine[1] - k) % third_size
                for s in range(second_size):
                    second = (mine[0] - s) % second_size
                    for d in range(depths):
                        depth = (at.depth - d) % depths
                        row, side = spot(second, third)
                        shard = index(row, depth, side)
                        arrive(w, shard)
                        to_pair(w, fulls[w].at[shard], shard)

        for step in range(count + 2):
            if step < count:
                stage_one(step)
            if 0 <= step - 1 < count:
                stage_two(step - 1)
            if 0 <= step - 2 < count:
                stage_three(step - 2)

        for w in range(count):
            for row in range(rows):
                for depth in range(depths):
                    for side in range(sides):
                        shard = at.index(row, depth, side, 1 - core)
                        pltpu.make_async_remote_copy(
                            src_ref=fulls[w].at[shard],
                            dst_ref=fulls[w].at[shard],
                            send_sem=pair_send.at[w, shard // 2],
                            recv_sem=pair_recv.at[w, shard // 2],
                            device_id=peers[0],
                            **dev,
                        ).wait_recv()
        for copy in own:
            copy.wait()
        for copy in sends:
            copy.wait_send()

    for core in range(2):

        @pl.when(at.core == core)
        def _():
            run(core)


def gather_all(mesh_shape, shards, collective_id=0):
    rows, inner = mesh_shape["dp"], mesh_shape["fsdp"]
    depths = 4
    sides = inner // (2 * depths)
    total = rows * inner
    count = len(shards)
    sent = (depths - 1) + depths * (max(rows, sides) - 1) + depths * sides * (rows - 1) + depths * rows * (sides - 1)
    return pl.pallas_call(
        functools.partial(gather_kernel, rows, depths, sides, count),
        out_shape=[jax.ShapeDtypeStruct((total,) + s.shape, s.dtype) for s in shards],
        in_specs=[ANY] * count,
        out_specs=[ANY] * count,
        scratch_shapes=[
            DMA((count, sent)),
            DMA((count, total)),
            DMA((count, total // 2)),
            DMA((count, total // 2)),
            DMA((count,)),
        ],
        compiler_params=pltpu.CompilerParams(collective_id=collective_id, has_side_effects=True),
        name="gather_weights",
    )(*shards)


def scatter_kernel(rows, depths, sides, count, *refs):
    parts, outs = refs[:count], refs[count : 2 * count]
    scratch = refs[2 * count :]
    held, pair, third_in, second_in, depth_in = (scratch[i * count : (i + 1) * count] for i in range(5))
    (own_sem, pair_send, pair_recv, third_send, third_recv, second_send, second_recv, depth_send, depth_recv) = scratch[
        5 * count :
    ]
    at = Place(rows, depths, sides)
    dev = dict(device_id_type=pl.DeviceIdType.MESH)

    barrier = pltpu.get_barrier_semaphore()
    peers = []
    for k in range(1, depths):
        peers.append(at.device(at.row, (at.depth + k) % depths, at.side, at.core))
    for k in range(1, sides):
        peers.append(at.device(at.row, at.depth, (at.side + k) % sides, at.core))
    for k in range(1, rows):
        peers.append(at.device((at.row + k) % rows, at.depth, at.side, at.core))
    peers.append(at.device(at.row, at.depth, at.side, 1 - at.core))
    for peer in peers:
        pl.semaphore_signal(barrier, inc=1, device_id=peer, **dev)
    pl.semaphore_wait(barrier, len(peers))

    def run(core):
        second_size, third_size = (sides, rows) if core == 0 else (rows, sides)
        my_second, my_third = (at.side, at.row) if core == 0 else (at.row, at.side)

        def unit(second, third, depth):
            row, side = (third, second) if core == 0 else (second, third)
            return (row * depths + depth) * sides + side

        def device(second, third, depth):
            row, side = (third, second) if core == 0 else (second, third)
            return at.device(row, depth, side, core)

        def remote(source, target, send, recv, peer):
            return pltpu.make_async_remote_copy(
                src_ref=source, dst_ref=target, send_sem=send, recv_sem=recv, device_id=peer, **dev
            )

        sibling = at.device(at.row, at.depth, at.side, 1 - core)

        def pair_copy(w, u):
            return remote(
                parts[w].at[u, 1 - core], pair[w].at[u], pair_send.at[w], pair_recv.at[w, u], sibling
            )

        def own_copy(w):
            return pltpu.make_async_copy(parts[w].at[:, core], held[w], own_sem.at[w])

        def third_copy(w, u, k, q, peer):
            return remote(
                held[w].at[u],
                third_in[w].at[k - 1, q],
                third_send.at[w, k - 1, q],
                third_recv.at[w, k - 1, q],
                peer,
            )

        def second_copy(w, u, k, q, peer):
            return remote(
                held[w].at[u],
                second_in[w].at[k - 1, q],
                second_send.at[w, k - 1, q],
                second_recv.at[w, k - 1, q],
                peer,
            )

        def depth_copy(w, u, k, peer):
            return remote(
                held[w].at[u], depth_in[w].at[k - 1], depth_send.at[w, k - 1], depth_recv.at[w, k - 1], peer
            )

        def loop(size, body):
            lax.fori_loop(0, size, lambda i, c: (body(i), c)[1], 0)

        def each_unit(visit):
            other_second, other_third = third_size, second_size
            far = my_second
            for k in list(range(1, other_third)) + [0]:
                def inner(q, k=k):
                    second, third = q // depths, (far + k) % other_third
                    row, side = (second, third) if core == 0 else (third, second)
                    visit((row * depths + q % depths) * sides + side)
                loop(other_second * depths, inner)

        for w in range(count):
            each_unit(lambda u, w=w: pair_copy(w, u).start())
            own_copy(w).start()

        def add_pair(w, u):
            pair_copy(w, u).wait_recv()
            held[w][u] = held[w][u] + pair[w][u]

        def stage_third(w):
            own_copy(w).wait()
            for k in list(range(1, third_size)) + [0]:
                third = (my_third + k) % third_size

                def inner(q, k=k, third=third):
                    second, depth = q // depths, q % depths
                    u = unit(second, third, depth)
                    add_pair(w, u)
                    if k:
                        third_copy(w, u, k, q, device(my_second, third, at.depth)).start()

                loop(second_size * depths, inner)

        def stage_second(w):
            for k in list(range(1, second_size)) + [0]:
                second = (my_second + k) % second_size

                def inner(depth, k=k, second=second):
                    u = unit(second, my_third, depth)
                    for j in range(1, third_size):
                        third_copy(w, u, j, second * depths + depth, sibling).wait_recv()
                        held[w][u] = held[w][u] + third_in[w][j - 1, second * depths + depth]
                    if k:
                        second_copy(w, u, k, depth, device(second, my_third, at.depth)).start()

                loop(depths, inner)

        def stage_depth(w):
            for k in list(range(1, depths)) + [0]:
                depth = (at.depth + k) % depths
                u = unit(my_second, my_third, depth)
                for j in range(1, second_size):
                    second_copy(w, u, j, depth, sibling).wait_recv()
                    held[w][u] = held[w][u] + second_in[w][j - 1, depth]
                if k:
                    depth_copy(w, u, k, device(my_second, my_third, depth)).start()

        def stage_last(w):
            u = unit(my_second, my_third, at.depth)
            total = held[w][u].astype(jnp.float32)
            for k in range(1, depths):
                depth_copy(w, u, k, sibling).wait_recv()
                total = total + depth_in[w][k - 1].astype(jnp.float32)
            outs[w][...] = total

        for step in range(count + 3):
            for lag, stage in enumerate((stage_third, stage_second, stage_depth, stage_last)):
                if 0 <= step - lag < count:
                    stage(step - lag)

        for w in range(count):
            remote(pair[w], pair[w], pair_send.at[w], pair_recv.at[w, 0], sibling).wait_send()
            for k in range(1, third_size):
                loop(second_size * depths, lambda q, w=w, k=k: third_copy(w, 0, k, q, sibling).wait_send())
            for k in range(1, second_size):
                loop(depths, lambda q, w=w, k=k: second_copy(w, 0, k, q, sibling).wait_send())
            for k in range(1, depths):
                depth_copy(w, 0, k, sibling).wait_send()

    for core in range(2):

        @pl.when(at.core == core)
        def _():
            run(core)


def scatter_all(mesh_shape, parts, collective_id=1):
    rows, inner = mesh_shape["dp"], mesh_shape["fsdp"]
    depths = 4
    sides = inner // (2 * depths)
    total = rows * inner
    half = total // 2
    count = len(parts)
    if rows == sides:
        thirds, seconds = (rows - 1, sides * depths), (sides - 1, depths)
    else:
        wide = max(rows, sides)
        thirds, seconds = (wide - 1, wide * depths), (wide - 1, depths)
    scratch = []
    for lead in ((half,), (half,), thirds, seconds, (depths - 1,)):
        scratch += [pltpu.VMEM(lead + p.shape[1:], p.dtype) for p in parts]
    parts = [p.reshape((half, 2) + p.shape[1:]) for p in parts]
    sems = [
        (), (), (half,), thirds, thirds, seconds, seconds, (depths - 1,), (depths - 1,),
    ]
    return pl.pallas_call(
        functools.partial(scatter_kernel, rows, depths, sides, count),
        out_shape=[jax.ShapeDtypeStruct(p.shape[2:], jnp.float32) for p in parts],
        in_specs=[ANY] * count,
        out_specs=[pl.BlockSpec(memory_space=pltpu.VMEM)] * count,
        scratch_shapes=scratch + [DMA((count,) + s) for s in sems],
        compiler_params=pltpu.CompilerParams(
            collective_id=collective_id, has_side_effects=True, vmem_limit_bytes=60 * 2**20
        ),
        name="scatter_grads",
    )(*parts)


def dot(left, right):
    return jnp.dot(left, right, preferred_element_type=F32)


def dot_nt(left, right):
    return lax.dot_general(left, right, (((1,), (1,)), ((), ())), preferred_element_type=F32)


def dot_tn(left, right):
    return lax.dot_general(left, right, (((0,), (0,)), ((), ())), preferred_element_type=F32)


def norm_parts(value):
    center = value - jnp.mean(value, axis=-1, keepdims=True)
    inv = lax.rsqrt(jnp.mean(center * center, axis=-1, keepdims=True) + EPSILON)
    return center * inv, inv


def norm_back(grad, hat, inv, gain):
    scaled = grad * gain
    return inv * (
        scaled
        - jnp.mean(scaled, axis=-1, keepdims=True)
        - hat * jnp.mean(scaled * hat, axis=-1, keepdims=True)
    )


GELU_ROOT = 0.7978845608028654


def gelu_parts(value):
    square = value * value
    inner = jnp.tanh(GELU_ROOT * value * (1.0 + 0.044715 * square))
    half = 0.5 * (1.0 + inner)
    slope = half + 0.5 * value * (1.0 - inner * inner) * (GELU_ROOT + 3 * 0.044715 * GELU_ROOT * square)
    return value * half, slope


def iota(shape, axis):
    return lax.broadcasted_iota(jnp.int32, shape, axis)


def wide(row):
    return jnp.broadcast_to(row, (16, row.shape[1])).astype(BF16)


def head_mask(width):
    return iota((16, width), 1) // (width // HEADS) == iota((16, width), 0)


def spread(row, mask):
    return jnp.where(mask, jnp.broadcast_to(row.astype(F32), mask.shape), 0.0).astype(BF16)


def collect(rows, mask):
    return jnp.sum(jnp.where(mask, rows, 0.0), axis=0, keepdims=True)


def row_softmax(spread_query, keys, place):
    score = dot_nt(spread_query, keys) * 0.125
    score = jnp.where(iota(score.shape, 1) <= place, score, NEG_FILL)
    expo = jnp.exp(score - jnp.max(score, axis=-1, keepdims=True))
    return expo / jnp.sum(expo, axis=-1, keepdims=True)


def pick_rows(first, array):
    chosen = iota((16, array.shape[0]), 1) == first + iota((16, array.shape[0]), 0)
    return dot(chosen.astype(F32).astype(BF16), array)


def think_kernel(
    start_ref, x_in, mixed_in, wp_ref, wo_ref, we_ref, wc_ref,
    g1_ref, b1_ref, bp_ref, bo_ref, g2_ref, b2_ref, be_ref, bc_ref, x_ref, mixed_ref,
):
    width = x_in.shape[1]
    start = start_ref[0]
    mask = head_mask(width)
    row_pos = iota((PREFIX, 1), 0)
    x_ref[...] = x_in[...]
    mixed_ref[...] = mixed_in[...]
    x_row = x_ref[pl.ds(start - 1, 1), :]
    query = pick_rows(start - 1, mixed_ref[:, :width])[0:1]
    for step in range(THOUGHTS):
        place = start - 1 + step
        prob = row_softmax(spread(query, mask), mixed_ref[:, width : 2 * width], place)
        context = collect(dot(prob.astype(BF16), mixed_ref[:, 2 * width :]), mask)
        resid = x_row + (dot(wide(context), wo_ref[...])[0:1] + bo_ref[...])
        normed = norm_parts(resid)[0] * g2_ref[...] + b2_ref[...]
        pre = dot(wide(normed), we_ref[...])[0:1] + be_ref[...]
        active = gelu_parts(pre)[0]
        x_row = resid + (dot(wide(active), wc_ref[...])[0:1] + bc_ref[...])
        normed = norm_parts(x_row)[0] * g1_ref[...] + b1_ref[...]
        mixed_row = dot(wide(normed), wp_ref[...])[0:1] + bp_ref[...]
        query = mixed_row[:, :width].astype(BF16)
        x_ref[pl.ds(place + 1, 1), :] = x_row
        here = row_pos == place + 1
        mixed_ref[...] = jnp.where(here, mixed_row, mixed_ref[...].astype(F32)).astype(BF16)


def smem():
    return pl.BlockSpec(memory_space=pltpu.SMEM)


def whole(array):
    return pl.BlockSpec(array.shape, lambda *_: (0,) * array.ndim, pipeline_mode=pl.Buffered(1))


def prefix_block(array):
    return pl.BlockSpec((PREFIX, array.shape[1]), lambda *_: (0, 0), pipeline_mode=pl.Buffered(1))


def params(semantics=("arbitrary",)):
    return pltpu.CompilerParams(dimension_semantics=semantics, vmem_limit_bytes=VMEM_LIMIT)


def think(start, x, mixed, weights, vectors):
    operands = (x, mixed) + weights + vectors
    return pl.pallas_call(
        think_kernel,
        grid=(1,),
        out_shape=[jax.ShapeDtypeStruct(x.shape, F32), jax.ShapeDtypeStruct(mixed.shape, BF16)],
        in_specs=[smem(), prefix_block(x), prefix_block(mixed)] + [whole(a) for a in operands[2:]],
        out_specs=[prefix_block(x), prefix_block(mixed)],
        input_output_aliases={1: 0, 2: 1},
        compiler_params=params(),
        name="think",
    )(start, *operands)


def attend_kernel(query_ref, key_ref, value_ref, context_ref, log_ref):
    seq, lanes = query_ref.shape
    half = lanes // 2
    first_head = iota((TILE, lanes), 1) < half
    values_t = value_ref[...].T
    for start in range(0, seq, TILE):
        stop = start + TILE
        query = query_ref[start:stop]
        outs = []
        for head in range(2):
            own = first_head if head == 0 else jnp.logical_not(first_head)
            masked = jnp.where(own, query.astype(F32) * 0.125, 0.0).astype(BF16)
            score = dot_nt(key_ref[:stop], masked)
            hidden = iota((TILE, TILE), 0) > iota((TILE, TILE), 1)
            last = jnp.where(hidden, NEG_FILL, score[start:])
            score = jnp.concatenate([score[:start], last], 0) if start else last
            peak = jnp.max(score, axis=0, keepdims=True)
            expo = jnp.exp(score - peak)
            total = jnp.sum(expo, axis=0, keepdims=True)
            prob = (expo * (1.0 / total)).astype(BF16)
            outs.append(dot(values_t[:, :stop], prob)[head * half : (head + 1) * half])
            log_ref[head : head + 1, start:stop] = peak + jnp.log(total)
        context_ref[start:stop] = jnp.concatenate(outs, 0).T.astype(BF16)


def pair_spec(seq, offset, lanes=128):
    return pl.BlockSpec((seq, lanes), lambda i: (0, offset + i))


def attend(mixed):
    seq, width = mixed.shape[0], mixed.shape[1] // 3
    pairs = HEADS // 2
    return pl.pallas_call(
        attend_kernel,
        grid=(pairs,),
        out_shape=[jax.ShapeDtypeStruct((seq, width), BF16), jax.ShapeDtypeStruct((pairs, 2, seq), F32)],
        in_specs=[pair_spec(seq, 0), pair_spec(seq, pairs), pair_spec(seq, 2 * pairs)],
        out_specs=[pair_spec(seq, 0), pl.BlockSpec((None, 2, seq), lambda i: (i, 0, 0))],
        compiler_params=params(),
        name="attend",
    )(mixed, mixed, mixed)


def attend_back_kernel(query_ref, key_ref, value_ref, up_ref, log_ref, dq_ref, dk_ref, dv_ref, dk_sum, dv_sum):
    seq, lanes = query_ref.shape
    half = lanes // 2
    first_head = iota((TILE, lanes), 1) < half
    keys_t = key_ref[...].T
    for start in reversed(range(0, seq, TILE)):
        stop = start + TILE
        query = query_ref[start:stop].astype(F32) * 0.125
        upstream = up_ref[start:stop].astype(F32)
        outs = []
        for head in range(2):
            own = first_head if head == 0 else jnp.logical_not(first_head)
            masked = jnp.where(own, query, 0.0).astype(BF16)
            up_masked = jnp.where(own, upstream, 0.0).astype(BF16)
            score = dot_nt(key_ref[:stop], masked)
            hidden = iota((TILE, TILE), 0) > iota((TILE, TILE), 1)
            last = jnp.where(hidden, NEG_FILL, score[start:])
            score = jnp.concatenate([score[:start], last], 0) if start else last
            prob = jnp.exp(score - log_ref[head : head + 1, start:stop])
            prob_grad = dot_nt(value_ref[:stop], up_masked)
            inner = jnp.sum(prob * prob_grad, axis=0, keepdims=True)
            score_grad = (prob * (prob_grad - inner)).astype(BF16)
            dv = dot(prob.astype(BF16), up_masked)
            dk = dot(score_grad, masked)
            if stop == seq and head == 0:
                dv_sum[...] = dv
                dk_sum[...] = dk
            else:
                dv_sum[:stop] += dv
                dk_sum[:stop] += dk
            outs.append(dot(keys_t[:, :stop], score_grad)[head * half : (head + 1) * half])
        dq_ref[start:stop] = (jnp.concatenate(outs, 0).T * 0.125).astype(BF16)
    dk_ref[...] = dk_sum[...].astype(BF16)
    dv_ref[...] = dv_sum[...].astype(BF16)


def attend_back(mixed, upstream, log_total):
    seq, width = upstream.shape
    pairs = HEADS // 2
    out = jax.ShapeDtypeStruct((seq, width), BF16)
    return pl.pallas_call(
        attend_back_kernel,
        grid=(pairs,),
        out_shape=[out, out, out],
        in_specs=[
            pair_spec(seq, 0),
            pair_spec(seq, pairs),
            pair_spec(seq, 2 * pairs),
            pair_spec(seq, 0),
            pl.BlockSpec((None, 2, seq), lambda i: (i, 0, 0)),
        ],
        out_specs=[pair_spec(seq, 0)] * 3,
        scratch_shapes=[pltpu.VMEM((seq, 128), F32), pltpu.VMEM((seq, 128), F32)],
        compiler_params=params(),
        name="attend_back",
    )(mixed, mixed, mixed, upstream, log_total)


def feed_kernel(
    length_ref, context_ref, x_ref, cot_ref, wo_ref, we_ref, wc_ref, bo_ref, g2_ref, b2_ref, be_ref, bc_ref,
    final_ref, resid_ref, normed_ref, active_ref, dz_ref, df_ref, dh_ref, dctx_ref, sums_ref,
):
    rows, width = x_ref.shape
    inner = we_ref.shape[1]
    valid = pl.program_id(0) * rows + iota((rows, 1), 0) < length_ref[0]
    resid = x_ref[...] + (dot(context_ref[...], wo_ref[...]) + bo_ref[...])
    resid_ref[...] = resid
    hat, inv = norm_parts(resid)
    normed = (hat * g2_ref[...] + b2_ref[...]).astype(BF16)
    normed_ref[...] = normed
    dout = jnp.where(valid, cot_ref[...].astype(F32), 0.0)
    dz = dout.astype(BF16)
    dz_ref[...] = dz
    total = jnp.zeros((rows, width), F32)
    dc = jnp.zeros((rows, width), F32)
    for at in range(0, inner, width):
        part = slice(at, at + width)
        value, slope = gelu_parts(dot(normed, we_ref[:, part]) + be_ref[:, part])
        value = value.astype(BF16)
        active_ref[:, part] = value
        total = total + dot(value, wc_ref[part])
        df = (dot_nt(dz, wc_ref[part]) * slope).astype(BF16)
        df_ref[:, part] = df
        dc = dc + dot_nt(df, we_ref[:, part])
    final_ref[...] = jnp.where(valid, resid + (total + bc_ref[...]), 0.0)
    dh = dout + norm_back(dc, hat, inv, g2_ref[...])
    dh_ref[...] = dh
    dctx_ref[...] = dot_nt(dh.astype(BF16), wo_ref[...]).astype(BF16)

    @pl.when(pl.program_id(0) == 0)
    def _():
        sums_ref[...] = jnp.zeros_like(sums_ref)

    sums_ref[0:1] += jnp.sum(dc * hat, axis=0, keepdims=True)
    sums_ref[1:2] += jnp.sum(dc, axis=0, keepdims=True)


def row_block(columns):
    return pl.BlockSpec((TILE, columns), lambda i: (i, 0))


def feed(length, context, x, cotangent, weights, vectors):
    seq, width = x.shape
    inner = weights[1].shape[1]
    shape = lambda n, t: jax.ShapeDtypeStruct((seq, n), t)
    outs = [
        (width, F32), (width, F32), (width, BF16), (inner, BF16), (width, BF16), (inner, BF16), (width, F32), (width, BF16),
    ]
    fixed = weights + vectors
    return pl.pallas_call(
        feed_kernel,
        grid=(seq // TILE,),
        out_shape=[shape(*o) for o in outs] + [jax.ShapeDtypeStruct((8, width), F32)],
        in_specs=[smem()] + [row_block(width)] * 3 + [whole(a) for a in fixed],
        out_specs=[row_block(o[0]) for o in outs] + [pl.BlockSpec((8, width), lambda i: (0, 0))],
        compiler_params=params(),
        name="feed",
    )(length, context, x, cotangent, *fixed)


def reflect_kernel(
    start_ref, x_ref, mixed_ref, resid_ref, dh_in, dq_in, dk_in, dv_in, dz_in, df_in,
    wp_ref, wo_ref, we_ref, wc_ref, g1_ref, g2_ref, b2_ref, be_ref, sums_in,
    dh_ref, dq_ref, dk_ref, dv_ref, dz_ref, df_ref, sums_ref,
):
    width = x_ref.shape[1]
    start = start_ref[0]
    mask = head_mask(width)
    row_pos = iota((PREFIX, 1), 0)
    for source, target in ((dh_in, dh_ref), (dz_in, dz_ref), (df_in, df_ref), (sums_in, sums_ref)):
        target[...] = source[...]
    main = [pick_rows(start, ref[...]) for ref in (dq_in, dk_in, dv_in)]
    queries = pick_rows(start - 1, mixed_ref[:, :width])
    places = [start - 1 + step for step in range(THOUGHTS)]
    resid = jnp.concatenate([resid_ref[pl.ds(p, 1), :] for p in places] + [jnp.zeros((13, width), F32)], 0)
    resid_hat, resid_inv = norm_parts(resid)
    normed = (resid_hat * g2_ref[...] + b2_ref[...]).astype(BF16)
    slopes = gelu_parts(dot(normed, we_ref[...]) + be_ref[...])[1]
    scores, spreads, probs, ups = [], [], [], []
    dq_add = jnp.zeros((1, width), F32)
    for step in reversed(range(THOUGHTS)):
        place = places[step]
        dq_row = main[0][step : step + 1] + dq_add
        dk_row, dv_row = main[1][step : step + 1], main[2][step : step + 1]
        for score, query, prob, up in zip(scores, spreads, probs, ups):
            chosen = iota(score.shape, 1) == place + 1
            share = jnp.sum(jnp.where(chosen, score.astype(F32), 0.0), axis=1, keepdims=True)
            dk_row = dk_row + 0.125 * jnp.sum(share * query.astype(F32), axis=0, keepdims=True)
            share = jnp.sum(jnp.where(chosen, prob.astype(F32), 0.0), axis=1, keepdims=True)
            dv_row = dv_row + jnp.sum(share * up.astype(F32), axis=0, keepdims=True)
        x_hat, x_inv = norm_parts(x_ref[pl.ds(place + 1, 1), :])
        da = (
            dot_nt(wide(dq_row), wp_ref[:, :width])
            + dot_nt(wide(dk_row), wp_ref[:, width : 2 * width])
            + dot_nt(wide(dv_row), wp_ref[:, 2 * width :])
        )
        dz = dh_ref[pl.ds(place + 1, 1), :] + norm_back(da[0:1], x_hat, x_inv, g1_ref[...])
        df = dot_nt(wide(dz), wc_ref[...])[0:1] * slopes[step : step + 1]
        dc = dot_nt(wide(df), we_ref[...])[0:1]
        hat, inv = resid_hat[step : step + 1], resid_inv[step : step + 1]
        dh = dz + norm_back(dc, hat, inv, g2_ref[...])
        sums_ref[0:1] += dc * hat
        sums_ref[1:2] += dc
        dctx = dot_nt(wide(dh), wo_ref[...])[0:1]
        query, up = spread(queries[step : step + 1], mask), spread(dctx, mask)
        prob = row_softmax(query, mixed_ref[:, width : 2 * width], place)
        prob_grad = dot_nt(up, mixed_ref[:, 2 * width :])
        score = prob * (prob_grad - jnp.sum(prob * prob_grad, axis=-1, keepdims=True))
        score = score.astype(BF16)
        dq_add = collect(dot(score, mixed_ref[:, width : 2 * width]), mask) * 0.125
        scores.append(score)
        spreads.append(query)
        probs.append(prob.astype(BF16))
        ups.append(up)
        here = row_pos == place
        dh_ref[pl.ds(place, 1), :] += dh
        dz_ref[...] = jnp.where(here, dz_ref[...].astype(F32) + dz, dz_ref[...].astype(F32)).astype(BF16)
        df_ref[...] = jnp.where(here, df_ref[...].astype(F32) + df, df_ref[...].astype(F32)).astype(BF16)
        if step == THOUGHTS - 1:
            dq_ref[...] = dq_in[...]
        dq_ref[...] = jnp.where(here, dq_ref[...].astype(F32) + dq_add, dq_ref[...].astype(F32)).astype(BF16)
    stack = lambda parts: jnp.concatenate(parts, 0)
    dk = dot_tn(stack(scores), stack(spreads)) * 0.125
    dv = dot_tn(stack(probs), stack(ups))
    dk_ref[...] = (dk_in[...].astype(F32) + dk).astype(BF16)
    dv_ref[...] = (dv_in[...].astype(F32) + dv).astype(BF16)


def reflect(start, fixed, changed, weights, vectors, sums):
    operands = fixed + changed + weights + vectors + (sums,)
    blocks = [prefix_block(a) for a in fixed + changed]
    first = 1 + len(fixed)
    return pl.pallas_call(
        reflect_kernel,
        grid=(1,),
        out_shape=[jax.ShapeDtypeStruct(a.shape, a.dtype) for a in changed + (sums,)],
        in_specs=[smem()] + blocks + [whole(a) for a in weights + vectors + (sums,)],
        out_specs=[prefix_block(a) for a in changed] + [whole(sums)],
        input_output_aliases={first + i: i for i in range(len(changed))} | {len(operands): len(changed)},
        compiler_params=params(),
        name="reflect",
    )(start, *operands)


def pack(vectors, total):
    joined = jnp.concatenate([v.reshape(total, -1) for v in vectors], 1)
    fill = -joined.shape[1] % 128
    return jnp.pad(joined, ((0, 0), (0, fill)))[:, None]


def unpack(packed, sizes):
    flat = packed.reshape(-1, packed.shape[-1])
    out, at = [], 0
    for size in sizes:
        out.append(flat[:, at : at + size].reshape(-1))
        at += size
    return out


def per_device(
    mesh_shape,
    hidden,
    cotangent,
    lengths,
    thought_start,
    first_gain,
    first_bias,
    project_weight,
    project_bias,
    output_weight,
    output_bias,
    second_gain,
    second_bias,
    expand_weight,
    expand_bias,
    contract_weight,
    contract_bias,
):
    _, seq, width = hidden.shape
    total = mesh_shape["dp"] * mesh_shape["fsdp"]
    vectors = (
        first_gain,
        first_bias,
        project_bias,
        output_bias,
        second_gain,
        second_bias,
        expand_bias,
        contract_bias,
    )
    sizes = [v.shape[0] for v in vectors]
    full = gather_all(
        mesh_shape,
        (pack(vectors, 1)[0], project_weight, output_weight, expand_weight, contract_weight),
    )
    vectors = [v.astype(F32)[None] for v in unpack(full[0], sizes)]
    g1, b1, bp, bo, g2, b2, be, bc = vectors
    bp = jnp.concatenate([bp[:, :width], jnp.zeros((1, width), F32), bp[:, width:]], 1)
    Wp, Wo, We, Wc = (w.reshape(-1, w.shape[-1]) for w in full[1:])

    x = hidden[0].astype(F32)
    mixed = (dot((norm_parts(x)[0] * g1 + b1).astype(BF16), Wp) + bp).astype(BF16)
    x, mixed = think(thought_start, x, mixed, (Wp, Wo, We, Wc), (g1, b1, bp, bo, g2, b2, be, bc))
    context, log_total = attend(mixed)
    final, resid, normed_two, active, dz, df, dh, dctx, sums = feed(
        lengths, context, x, cotangent[0], (Wo, We, Wc), (bo, g2, b2, be, bc)
    )
    dq, dk, dv = attend_back(mixed, dctx, log_total)
    dh, dq, dk, dv, dz, df, sums = reflect(
        thought_start, (x, mixed, resid), (dh, dq, dk, dv, dz, df), (Wp, Wo, We, Wc), (g1, g2, b2, be), sums
    )
    dy = dh.astype(BF16)
    x_hat, x_inv = norm_parts(x)
    normed = (x_hat * g1 + b1).astype(BF16)
    dmixed = jnp.concatenate([dq, dk, dv], 1)
    da = dot_nt(dmixed, Wp)
    dx = dh + norm_back(da, x_hat, x_inv, g1)
    position = iota((seq, 1), 0)
    is_thought = (position >= thought_start[0]) & (position < thought_start[0] + THOUGHTS)
    hidden_grad = jnp.where(is_thought, 0.0, dx)

    def column_sum(value):
        return jnp.sum(value, axis=0, dtype=F32)

    column = column_sum(dmixed)
    small = (
        column_sum(da * x_hat),
        column_sum(da),
        jnp.concatenate([column[:width], column[2 * width :]]),
        column_sum(dy),
        sums[0],
        sums[1],
        column_sum(df),
        column_sum(dz),
    )
    large = (
        dot_tn(normed, dmixed),
        dot_tn(context, dy),
        dot_tn(normed_two, df),
        dot_tn(active, dz),
    )
    parts = [pack(small, total)]
    for grad in large:
        parts.append(grad.astype(BF16).reshape(total, grad.shape[0] // total, grad.shape[1]))
    small, dWp, dWo, dWe, dWc = scatter_all(mesh_shape, parts)
    dg1, db1, dbp, dbo, dg2, db2, dbe, dbc = unpack(small, sizes)
    return (final[None], hidden_grad[None], dg1, db1, dWp, dbp, dWo, dbo, dg2, db2, dWe, dbe, dWc, dbc)


def solution(mesh):
    rows = P(AXES, None, None)
    flat = P(AXES)
    square = P(AXES, None)
    specs = (flat, flat, square, flat, square, flat, flat, flat, square, flat, square, flat)
    return jax.shard_map(
        functools.partial(per_device, dict(mesh.shape)),
        mesh=mesh,
        in_specs=(rows, rows, flat, flat) + specs,
        out_specs=(rows, rows) + specs,
        check_vma=False,
    )
```

```python
import functools

import jax
import jax.numpy as jnp
from jax import lax
from jax.experimental import pallas as pl
from jax.experimental.pallas import tpu as pltpu
from jax.sharding import PartitionSpec as P

HEADS = 12
THOUGHTS = 3
PREFIX = 384
TILE = 256

EPSILON = 1e-05
NEG_FILL = -1e30
F32 = jnp.float32
BF16 = jnp.bfloat16
VMEM_LIMIT = 62 * 2**20


AXES = ("dp", "fsdp")
ANY = pl.BlockSpec(memory_space=pl.ANY)
DMA = pltpu.SemaphoreType.DMA


class Place:
    def __init__(self, rows, depths, sides):
        self.rows, self.depths, self.sides = rows, depths, sides
        self.row = lax.axis_index("dp")
        flat = lax.axis_index("fsdp")
        self.depth = flat // (sides * 2)
        self.side = flat // 2 % sides
        self.core = flat % 2

    def index(self, row, depth, side, core):
        return row * (self.depths * self.sides * 2) + (depth * self.sides + side) * 2 + core

    def device(self, row, depth, side, core):
        return {"dp": row, "fsdp": (depth * self.sides + side) * 2 + core}


def gather_kernel(rows, depths, sides, count, *refs):
    shards, fulls = refs[:count], refs[count : 2 * count]
    send_sem, recv_sem, pair_send, pair_recv, own_sem = refs[2 * count :]
    at = Place(rows, depths, sides)
    dev = dict(device_id_type=pl.DeviceIdType.MESH)

    barrier = pltpu.get_barrier_semaphore()
    peers = []
    for k in range(1, depths):
        peers.append(at.device(at.row, (at.depth + k) % depths, at.side, at.core))
    for k in range(1, sides):
        peers.append(at.device(at.row, at.depth, (at.side + k) % sides, at.core))
    for k in range(1, rows):
        peers.append(at.device((at.row + k) % rows, at.depth, at.side, at.core))
    peers.append(at.device(at.row, at.depth, at.side, 1 - at.core))
    for peer in peers:
        pl.semaphore_signal(barrier, inc=1, device_id=peer, **dev)
    pl.semaphore_wait(barrier, len(peers))

    def run(core):
        sends = []

        def index(row, depth, side):
            return at.index(row, depth, side, core)

        def send(w, source, shard, peer, slot):
            copy = pltpu.make_async_remote_copy(
                src_ref=source,
                dst_ref=fulls[w].at[shard],
                send_sem=send_sem.at[w, slot],
                recv_sem=recv_sem.at[w, shard],
                device_id=peer,
                **dev,
            )
            copy.start()
            sends.append(copy)

        def arrive(w, shard):
            pltpu.make_async_remote_copy(
                src_ref=fulls[w].at[shard],
                dst_ref=fulls[w].at[shard],
                send_sem=send_sem.at[w, 0],
                recv_sem=recv_sem.at[w, shard],
                device_id=peers[0],
                **dev,
            ).wait_recv()

        def to_pair(w, source, shard):
            copy = pltpu.make_async_remote_copy(
                src_ref=source,
                dst_ref=fulls[w].at[shard],
                send_sem=pair_send.at[w, shard // 2],
                recv_sem=pair_recv.at[w, shard // 2],
                device_id=at.device(at.row, at.depth, at.side, 1 - core),
                **dev,
            )
            copy.start()
            sends.append(copy)

        slots = [0] * count

        def slot(w):
            slots[w] += 1
            return slots[w] - 1

        second_size, third_size = (sides, rows) if core == 0 else (rows, sides)

        def spot(second, third):
            return (third, second) if core == 0 else (second, third)

        mine = (at.side, at.row) if core == 0 else (at.row, at.side)

        def forward_second(w, source, depth):
            row, side = spot(*mine)
            for k in range(1, second_size):
                r, s = spot((mine[0] + k) % second_size, mine[1])
                send(w, source, index(row, depth, side), at.device(r, at.depth, s, core), slot(w))

        def forward_third(w, source, depth, second):
            row, side = spot(second, mine[1])
            for k in range(1, third_size):
                r, s = spot(mine[0], (mine[1] + k) % third_size)
                send(w, source, index(row, depth, side), at.device(r, at.depth, s, core), slot(w))

        own = []
        for w in range(count):
            me = index(at.row, at.depth, at.side)
            for k in range(1, depths):
                send(w, shards[w], me, at.device(at.row, (at.depth + k) % depths, at.side, core), slot(w))
            forward_second(w, shards[w], at.depth)
            forward_third(w, shards[w], at.depth, mine[0])
            to_pair(w, shards[w], me)
            copy = pltpu.make_async_copy(shards[w], fulls[w].at[me], own_sem.at[w])
            copy.start()
            own.append(copy)

        def stage_one(w):
            for k in range(1, depths):
                depth = (at.depth - k) % depths
                shard = index(at.row, depth, at.side)
                arrive(w, shard)
                forward_second(w, fulls[w].at[shard], depth)
                forward_third(w, fulls[w].at[shard], depth, mine[0])
                to_pair(w, fulls[w].at[shard], shard)

        def stage_two(w):
            for k in range(1, second_size):
                second = (mine[0] - k) % second_size
                for d in range(depths):
                    depth = (at.depth - d) % depths
                    shard = index(spot(second, mine[1])[0], depth, spot(second, mine[1])[1])
                    arrive(w, shard)
                    forward_third(w, fulls[w].at[shard], depth, second)
                    to_pair(w, fulls[w].at[shard], shard)

        def stage_three(w):
            for k in range(1, third_size):
                third = (mine[1] - k) % third_size
                for s in range(second_size):
                    second = (mine[0] - s) % second_size
                    for d in range(depths):
                        depth = (at.depth - d) % depths
                        row, side = spot(second, third)
                        shard = index(row, depth, side)
                        arrive(w, shard)
                        to_pair(w, fulls[w].at[shard], shard)

        for step in range(count + 2):
            if step < count:
                stage_one(step)
            if 0 <= step - 1 < count:
                stage_two(step - 1)
            if 0 <= step - 2 < count:
                stage_three(step - 2)

        for w in range(count):
            for row in range(rows):
                for depth in range(depths):
                    for side in range(sides):
                        shard = at.index(row, depth, side, 1 - core)
                        pltpu.make_async_remote_copy(
                            src_ref=fulls[w].at[shard],
                            dst_ref=fulls[w].at[shard],
                            send_sem=pair_send.at[w, shard // 2],
                            recv_sem=pair_recv.at[w, shard // 2],
                            device_id=peers[0],
                            **dev,
                        ).wait_recv()
        for copy in own:
            copy.wait()
        for copy in sends:
            copy.wait_send()

    for core in range(2):

        @pl.when(at.core == core)
        def _():
            run(core)


def gather_all(mesh_shape, shards, collective_id=0):
    rows, inner = mesh_shape["dp"], mesh_shape["fsdp"]
    depths = 4
    sides = inner // (2 * depths)
    total = rows * inner
    count = len(shards)
    sent = (depths - 1) + depths * (max(rows, sides) - 1) + depths * sides * (rows - 1) + depths * rows * (sides - 1)
    return pl.pallas_call(
        functools.partial(gather_kernel, rows, depths, sides, count),
        out_shape=[jax.ShapeDtypeStruct((total,) + s.shape, s.dtype) for s in shards],
        in_specs=[ANY] * count,
        out_specs=[ANY] * count,
        scratch_shapes=[
            DMA((count, sent)),
            DMA((count, total)),
            DMA((count, total // 2)),
            DMA((count, total // 2)),
            DMA((count,)),
        ],
        compiler_params=pltpu.CompilerParams(collective_id=collective_id, has_side_effects=True),
        name="gather_weights",
    )(*shards)


def scatter_kernel(rows, depths, sides, count, *refs):
    parts, outs = refs[:count], refs[count : 2 * count]
    scratch = refs[2 * count :]
    held, pair, third_in, second_in, depth_in = (scratch[i * count : (i + 1) * count] for i in range(5))
    (own_sem, pair_send, pair_recv, third_send, third_recv, second_send, second_recv, depth_send, depth_recv) = scratch[
        5 * count :
    ]
    at = Place(rows, depths, sides)
    dev = dict(device_id_type=pl.DeviceIdType.MESH)

    barrier = pltpu.get_barrier_semaphore()
    peers = []
    for k in range(1, depths):
        peers.append(at.device(at.row, (at.depth + k) % depths, at.side, at.core))
    for k in range(1, sides):
        peers.append(at.device(at.row, at.depth, (at.side + k) % sides, at.core))
    for k in range(1, rows):
        peers.append(at.device((at.row + k) % rows, at.depth, at.side, at.core))
    peers.append(at.device(at.row, at.depth, at.side, 1 - at.core))
    for peer in peers:
        pl.semaphore_signal(barrier, inc=1, device_id=peer, **dev)
    pl.semaphore_wait(barrier, len(peers))

    def run(core):
        second_size, third_size = (sides, rows) if core == 0 else (rows, sides)
        my_second, my_third = (at.side, at.row) if core == 0 else (at.row, at.side)

        def unit(second, third, depth):
            row, side = (third, second) if core == 0 else (second, third)
            return (row * depths + depth) * sides + side

        def device(second, third, depth):
            row, side = (third, second) if core == 0 else (second, third)
            return at.device(row, depth, side, core)

        def remote(source, target, send, recv, peer):
            return pltpu.make_async_remote_copy(
                src_ref=source, dst_ref=target, send_sem=send, recv_sem=recv, device_id=peer, **dev
            )

        sibling = at.device(at.row, at.depth, at.side, 1 - core)

        def pair_copy(w, u):
            return remote(
                parts[w].at[u, 1 - core], pair[w].at[u], pair_send.at[w], pair_recv.at[w, u], sibling
            )

        def own_copy(w):
            return pltpu.make_async_copy(parts[w].at[:, core], held[w], own_sem.at[w])

        def third_copy(w, u, k, q, peer):
            return remote(
                held[w].at[u],
                third_in[w].at[k - 1, q],
                third_send.at[w, k - 1, q],
                third_recv.at[w, k - 1, q],
                peer,
            )

        def second_copy(w, u, k, q, peer):
            return remote(
                held[w].at[u],
                second_in[w].at[k - 1, q],
                second_send.at[w, k - 1, q],
                second_recv.at[w, k - 1, q],
                peer,
            )

        def depth_copy(w, u, k, peer):
            return remote(
                held[w].at[u], depth_in[w].at[k - 1], depth_send.at[w, k - 1], depth_recv.at[w, k - 1], peer
            )

        def loop(size, body):
            lax.fori_loop(0, size, lambda i, c: (body(i), c)[1], 0)

        def each_unit(visit):
            other_second, other_third = third_size, second_size
            far = my_second
            for k in list(range(1, other_third)) + [0]:
                def inner(q, k=k):
                    second, third = q // depths, (far + k) % other_third
                    row, side = (second, third) if core == 0 else (third, second)
                    visit((row * depths + q % depths) * sides + side)
                loop(other_second * depths, inner)

        for w in range(count):
            each_unit(lambda u, w=w: pair_copy(w, u).start())
            own_copy(w).start()

        def add_pair(w, u):
            pair_copy(w, u).wait_recv()
            held[w][u] = held[w][u] + pair[w][u]

        def stage_third(w):
            own_copy(w).wait()
            for k in list(range(1, third_size)) + [0]:
                third = (my_third + k) % third_size

                def inner(q, k=k, third=third):
                    second, depth = q // depths, q % depths
                    u = unit(second, third, depth)
                    add_pair(w, u)
                    if k:
                        third_copy(w, u, k, q, device(my_second, third, at.depth)).start()

                loop(second_size * depths, inner)

        def stage_second(w):
            for k in list(range(1, second_size)) + [0]:
                second = (my_second + k) % second_size

                def inner(depth, k=k, second=second):
                    u = unit(second, my_third, depth)
                    for j in range(1, third_size):
                        third_copy(w, u, j, second * depths + depth, sibling).wait_recv()
                        held[w][u] = held[w][u] + third_in[w][j - 1, second * depths + depth]
                    if k:
                        second_copy(w, u, k, depth, device(second, my_third, at.depth)).start()

                loop(depths, inner)

        def stage_depth(w):
            for k in list(range(1, depths)) + [0]:
                depth = (at.depth + k) % depths
                u = unit(my_second, my_third, depth)
                for j in range(1, second_size):
                    second_copy(w, u, j, depth, sibling).wait_recv()
                    held[w][u] = held[w][u] + second_in[w][j - 1, depth]
                if k:
                    depth_copy(w, u, k, device(my_second, my_third, depth)).start()

        def stage_last(w):
            u = unit(my_second, my_third, at.depth)
            total = held[w][u].astype(jnp.float32)
            for k in range(1, depths):
                depth_copy(w, u, k, sibling).wait_recv()
                total = total + depth_in[w][k - 1].astype(jnp.float32)
            outs[w][...] = total

        for step in range(count + 3):
            for lag, stage in enumerate((stage_third, stage_second, stage_depth, stage_last)):
                if 0 <= step - lag < count:
                    stage(step - lag)

        for w in range(count):
            remote(pair[w], pair[w], pair_send.at[w], pair_recv.at[w, 0], sibling).wait_send()
            for k in range(1, third_size):
                loop(second_size * depths, lambda q, w=w, k=k: third_copy(w, 0, k, q, sibling).wait_send())
            for k in range(1, second_size):
                loop(depths, lambda q, w=w, k=k: second_copy(w, 0, k, q, sibling).wait_send())
            for k in range(1, depths):
                depth_copy(w, 0, k, sibling).wait_send()

    for core in range(2):

        @pl.when(at.core == core)
        def _():
            run(core)


def scatter_all(mesh_shape, parts, collective_id=1):
    rows, inner = mesh_shape["dp"], mesh_shape["fsdp"]
    depths = 4
    sides = inner // (2 * depths)
    total = rows * inner
    half = total // 2
    count = len(parts)
    if rows == sides:
        thirds, seconds = (rows - 1, sides * depths), (sides - 1, depths)
    else:
        wide = max(rows, sides)
        thirds, seconds = (wide - 1, wide * depths), (wide - 1, depths)
    scratch = []
    for lead in ((half,), (half,), thirds, seconds, (depths - 1,)):
        scratch += [pltpu.VMEM(lead + p.shape[1:], p.dtype) for p in parts]
    parts = [p.reshape((half, 2) + p.shape[1:]) for p in parts]
    sems = [
        (), (), (half,), thirds, thirds, seconds, seconds, (depths - 1,), (depths - 1,),
    ]
    return pl.pallas_call(
        functools.partial(scatter_kernel, rows, depths, sides, count),
        out_shape=[jax.ShapeDtypeStruct(p.shape[2:], jnp.float32) for p in parts],
        in_specs=[ANY] * count,
        out_specs=[pl.BlockSpec(memory_space=pltpu.VMEM)] * count,
        scratch_shapes=scratch + [DMA((count,) + s) for s in sems],
        compiler_params=pltpu.CompilerParams(
            collective_id=collective_id, has_side_effects=True, vmem_limit_bytes=60 * 2**20
        ),
        name="scatter_grads",
    )(*parts)


def dot(left, right):
    return jnp.dot(left, right, preferred_element_type=F32)


def dot_nt(left, right):
    return lax.dot_general(left, right, (((1,), (1,)), ((), ())), preferred_element_type=F32)


def dot_tn(left, right):
    return lax.dot_general(left, right, (((0,), (0,)), ((), ())), preferred_element_type=F32)


def norm_parts(value):
    center = value - jnp.mean(value, axis=-1, keepdims=True)
    inv = lax.rsqrt(jnp.mean(center * center, axis=-1, keepdims=True) + EPSILON)
    return center * inv, inv


def norm_back(grad, hat, inv, gain):
    scaled = grad * gain
    return inv * (
        scaled
        - jnp.mean(scaled, axis=-1, keepdims=True)
        - hat * jnp.mean(scaled * hat, axis=-1, keepdims=True)
    )


GELU_ROOT = 0.7978845608028654


def gelu_parts(value):
    square = value * value
    inner = jnp.tanh(GELU_ROOT * value * (1.0 + 0.044715 * square))
    half = 0.5 * (1.0 + inner)
    slope = half + 0.5 * value * (1.0 - inner * inner) * (GELU_ROOT + 3 * 0.044715 * GELU_ROOT * square)
    return value * half, slope


def iota(shape, axis):
    return lax.broadcasted_iota(jnp.int32, shape, axis)


def wide(row):
    return jnp.broadcast_to(row, (16, row.shape[1])).astype(BF16)


def head_mask(width):
    return iota((16, width), 1) // (width // HEADS) == iota((16, width), 0)


def spread(row, mask):
    return jnp.where(mask, jnp.broadcast_to(row.astype(F32), mask.shape), 0.0).astype(BF16)


def collect(rows, mask):
    return jnp.sum(jnp.where(mask, rows, 0.0), axis=0, keepdims=True)


def row_softmax(spread_query, keys, place):
    score = dot_nt(spread_query, keys) * 0.125
    score = jnp.where(iota(score.shape, 1) <= place, score, NEG_FILL)
    expo = jnp.exp(score - jnp.max(score, axis=-1, keepdims=True))
    return expo / jnp.sum(expo, axis=-1, keepdims=True)


def pick_rows(first, array):
    chosen = iota((16, array.shape[0]), 1) == first + iota((16, array.shape[0]), 0)
    return dot(chosen.astype(F32).astype(BF16), array)


VECTORS = ("g1", "b1", "bp", "bo", "g2", "b2", "be", "bc")


class Vectors:
    def __init__(self, ref, width):
        self.ref, self.width = ref, width
        self.sizes = dict(bp=3 * width, be=4 * width)

    def __getattr__(self, name):
        return self.ref[VECTORS.index(name) : VECTORS.index(name) + 1, : self.sizes.get(name, self.width)]


def spread_vectors(pieces, sizes, width, vec_ref):
    count, offset = pieces.shape[0], 0
    vec_ref[...] = jnp.zeros_like(vec_ref)
    for row, (name, size) in enumerate(zip(VECTORS, sizes)):
        low, high = offset // 128 * 128, -(-(offset + size) // 128) * 128
        length = count * size
        lane = iota((1, length), 1)
        pick = iota((high - low, length), 0) == lane % size + (offset - low)
        tiled = dot(pieces[:, low:high], pick.astype(F32).astype(BF16))
        line = jnp.sum(jnp.where(iota((count, length), 0) == lane // size, tiled, 0.0), axis=0, keepdims=True)
        if name == "bp":
            vec_ref[row : row + 1, :width] = line[:, :width]
            vec_ref[row : row + 1, 2 * width : 3 * width] = line[:, width:]
        else:
            vec_ref[row : row + 1, :length] = line
        offset += size


def fetch(sources, targets, sems):
    copies = [pltpu.make_async_copy(s, t, sems.at[i]) for i, (s, t) in enumerate(zip(sources, targets))]
    for copy in copies:
        copy.start()
    return copies


def aligned(place):
    return pl.multiple_of(place // 16 * 16, 16)


def think_kernel(
    sizes, start_ref, hidden_ref, pieces_ref, wp_hbm, wo_hbm, we_hbm, wc_hbm,
    x_ref, mixed_ref, vec_ref, wp_ref, wo_ref, we_ref, wc_ref, sems,
):
    seq, width = hidden_ref.shape
    copies = fetch((wp_hbm, wo_hbm, we_hbm, wc_hbm), (wp_ref, wo_ref, we_ref, wc_ref), sems)
    spread_vectors(pieces_ref[:, 0, :], sizes, width, vec_ref)
    vec = Vectors(vec_ref, width)
    start = start_ref[0]
    copies[0].wait()
    for at in range(0, seq, TILE):
        part = slice(at, at + TILE)
        x = hidden_ref[part].astype(F32)
        x_ref[part] = x
        normed = (norm_parts(x)[0] * vec.g1 + vec.b1).astype(BF16)
        mixed_ref[part] = (dot(normed, wp_ref[...]) + vec.bp).astype(BF16)
    mask = head_mask(width)
    x_row = x_ref[pl.ds(start - 1, 1), :]
    query = pick_rows(start - 1, mixed_ref[:PREFIX, :width])[0:1]
    for copy in copies[1:]:
        copy.wait()
    for step in range(THOUGHTS):
        place = start - 1 + step
        prob = row_softmax(spread(query, mask), mixed_ref[:PREFIX, width : 2 * width], place)
        context = collect(dot(prob.astype(BF16), mixed_ref[:PREFIX, 2 * width :]), mask)
        resid = x_row + (dot(wide(context), wo_ref[...])[0:1] + vec.bo)
        normed = norm_parts(resid)[0] * vec.g2 + vec.b2
        pre = dot(wide(normed), we_ref[...])[0:1] + vec.be
        active = gelu_parts(pre)[0]
        x_row = resid + (dot(wide(active), wc_ref[...])[0:1] + vec.bc)
        normed = norm_parts(x_row)[0] * vec.g1 + vec.b1
        mixed_row = dot(wide(normed), wp_ref[...])[0:1] + vec.bp
        query = mixed_row[:, :width].astype(BF16)
        x_ref[pl.ds(place + 1, 1), :] = x_row
        window = pl.ds(aligned(place + 1), 16)
        here = aligned(place + 1) + iota((16, 1), 0) == place + 1
        mixed_ref[window, :] = jnp.where(here, mixed_row, mixed_ref[window, :].astype(F32)).astype(BF16)


def smem():
    return pl.BlockSpec(memory_space=pltpu.SMEM)


def whole(array):
    return pl.BlockSpec(array.shape, lambda *_: (0,) * array.ndim, pipeline_mode=pl.Buffered(1))


def prefix_block(array):
    return pl.BlockSpec((PREFIX, array.shape[1]), lambda *_: (0, 0), pipeline_mode=pl.Buffered(1))


def params(semantics=("arbitrary",)):
    return pltpu.CompilerParams(dimension_semantics=semantics, vmem_limit_bytes=VMEM_LIMIT)


def in_hbm():
    return pl.BlockSpec(memory_space=pl.ANY)


def weight_scratch(weights):
    return [pltpu.VMEM(w.shape, w.dtype) for w in weights] + [DMA((len(weights),))]


def think(start, hidden, pieces, sizes, weights):
    seq, width = hidden.shape
    outs = [
        jax.ShapeDtypeStruct((seq, width), F32),
        jax.ShapeDtypeStruct((seq, 3 * width), BF16),
        jax.ShapeDtypeStruct((8, weights[2].shape[1]), F32),
    ]
    return pl.pallas_call(
        functools.partial(think_kernel, sizes),
        grid=(1,),
        out_shape=outs,
        in_specs=[smem(), whole(hidden), whole(pieces)] + [in_hbm() for _ in weights],
        out_specs=[whole(o) for o in outs],
        scratch_shapes=weight_scratch(weights),
        compiler_params=params(),
        name="think",
    )(start, hidden, pieces, *weights)


def attend_kernel(query_ref, key_ref, value_ref, context_ref, log_ref):
    seq, lanes = query_ref.shape
    half = lanes // 2
    first_head = iota((TILE, lanes), 1) < half
    values_t = value_ref[...].T
    for start in range(0, seq, TILE):
        stop = start + TILE
        query = query_ref[start:stop]
        outs = []
        for head in range(2):
            own = first_head if head == 0 else jnp.logical_not(first_head)
            masked = jnp.where(own, query.astype(F32) * 0.125, 0.0).astype(BF16)
            score = dot_nt(key_ref[:stop], masked)
            hidden = iota((TILE, TILE), 0) > iota((TILE, TILE), 1)
            last = jnp.where(hidden, NEG_FILL, score[start:])
            score = jnp.concatenate([score[:start], last], 0) if start else last
            peak = jnp.max(score, axis=0, keepdims=True)
            expo = jnp.exp(score - peak)
            total = jnp.sum(expo, axis=0, keepdims=True)
            prob = (expo * (1.0 / total)).astype(BF16)
            outs.append(dot(values_t[:, :stop], prob)[head * half : (head + 1) * half])
            log_ref[head : head + 1, start:stop] = peak + jnp.log(total)
        context_ref[start:stop] = jnp.concatenate(outs, 0).T.astype(BF16)


def pair_spec(seq, offset, lanes=128):
    return pl.BlockSpec((seq, lanes), lambda i: (0, offset + i))


def attend(mixed):
    seq, width = mixed.shape[0], mixed.shape[1] // 3
    pairs = HEADS // 2
    return pl.pallas_call(
        attend_kernel,
        grid=(pairs,),
        out_shape=[jax.ShapeDtypeStruct((seq, width), BF16), jax.ShapeDtypeStruct((pairs, 2, seq), F32)],
        in_specs=[pair_spec(seq, 0), pair_spec(seq, pairs), pair_spec(seq, 2 * pairs)],
        out_specs=[pair_spec(seq, 0), pl.BlockSpec((None, 2, seq), lambda i: (i, 0, 0))],
        compiler_params=params(),
        name="attend",
    )(mixed, mixed, mixed)


def attend_back_kernel(query_ref, key_ref, value_ref, up_ref, log_ref, dq_ref, dk_ref, dv_ref, dk_sum, dv_sum):
    seq, lanes = query_ref.shape
    half = lanes // 2
    first_head = iota((TILE, lanes), 1) < half
    keys_t = key_ref[...].T
    for start in reversed(range(0, seq, TILE)):
        stop = start + TILE
        query = query_ref[start:stop].astype(F32) * 0.125
        upstream = up_ref[start:stop].astype(F32)
        outs = []
        for head in range(2):
            own = first_head if head == 0 else jnp.logical_not(first_head)
            masked = jnp.where(own, query, 0.0).astype(BF16)
            up_masked = jnp.where(own, upstream, 0.0).astype(BF16)
            score = dot_nt(key_ref[:stop], masked)
            hidden = iota((TILE, TILE), 0) > iota((TILE, TILE), 1)
            last = jnp.where(hidden, NEG_FILL, score[start:])
            score = jnp.concatenate([score[:start], last], 0) if start else last
            prob = jnp.exp(score - log_ref[head : head + 1, start:stop])
            prob_grad = dot_nt(value_ref[:stop], up_masked)
            inner = jnp.sum(prob * prob_grad, axis=0, keepdims=True)
            score_grad = (prob * (prob_grad - inner)).astype(BF16)
            dv = dot(prob.astype(BF16), up_masked)
            dk = dot(score_grad, masked)
            if stop == seq and head == 0:
                dv_sum[...] = dv
                dk_sum[...] = dk
            else:
                dv_sum[:stop] += dv
                dk_sum[:stop] += dk
            outs.append(dot(keys_t[:, :stop], score_grad)[head * half : (head + 1) * half])
        dq_ref[start:stop] = (jnp.concatenate(outs, 0).T * 0.125).astype(BF16)
    dk_ref[...] = dk_sum[...].astype(BF16)
    dv_ref[...] = dv_sum[...].astype(BF16)


def attend_back(mixed, upstream, log_total):
    seq, width = upstream.shape
    pairs = HEADS // 2
    out = jax.ShapeDtypeStruct((seq, width), BF16)
    return pl.pallas_call(
        attend_back_kernel,
        grid=(pairs,),
        out_shape=[out, out, out],
        in_specs=[
            pair_spec(seq, 0),
            pair_spec(seq, pairs),
            pair_spec(seq, 2 * pairs),
            pair_spec(seq, 0),
            pl.BlockSpec((None, 2, seq), lambda i: (i, 0, 0)),
        ],
        out_specs=[pair_spec(seq, 0)] * 3,
        scratch_shapes=[pltpu.VMEM((seq, 128), F32), pltpu.VMEM((seq, 128), F32)],
        compiler_params=params(),
        name="attend_back",
    )(mixed, mixed, mixed, upstream, log_total)


def feed_kernel(
    length_ref, context_ref, x_ref, cot_ref, wo_ref, we_ref, wc_ref, vec_ref,
    final_ref, resid_ref, normed_ref, active_ref, dz_ref, df_ref, dh_ref, dctx_ref, sums_ref,
):
    rows, width = x_ref.shape
    inner = we_ref.shape[1]
    vec = Vectors(vec_ref, width)
    be = vec.be
    valid = pl.program_id(0) * rows + iota((rows, 1), 0) < length_ref[0]
    resid = x_ref[...] + (dot(context_ref[...], wo_ref[...]) + vec.bo)
    resid_ref[...] = resid
    hat, inv = norm_parts(resid)
    normed = (hat * vec.g2 + vec.b2).astype(BF16)
    normed_ref[...] = normed
    dout = jnp.where(valid, cot_ref[...].astype(F32), 0.0)
    dz = dout.astype(BF16)
    dz_ref[...] = dz
    total = jnp.zeros((rows, width), F32)
    dc = jnp.zeros((rows, width), F32)
    for at in range(0, inner, width):
        part = slice(at, at + width)
        value, slope = gelu_parts(dot(normed, we_ref[:, part]) + be[:, part])
        value = value.astype(BF16)
        active_ref[:, part] = value
        total = total + dot(value, wc_ref[part])
        df = (dot_nt(dz, wc_ref[part]) * slope).astype(BF16)
        df_ref[:, part] = df
        dc = dc + dot_nt(df, we_ref[:, part])
    final_ref[...] = jnp.where(valid, resid + (total + vec.bc), 0.0)
    dh = dout + norm_back(dc, hat, inv, vec.g2)
    dh_ref[...] = dh
    dctx_ref[...] = dot_nt(dh.astype(BF16), wo_ref[...]).astype(BF16)

    @pl.when(pl.program_id(0) == 0)
    def _():
        sums_ref[...] = jnp.zeros_like(sums_ref)

    sums_ref[0:1] += jnp.sum(dc * hat, axis=0, keepdims=True)
    sums_ref[1:2] += jnp.sum(dc, axis=0, keepdims=True)


def row_block(columns):
    return pl.BlockSpec((TILE, columns), lambda i: (i, 0))


def feed(length, context, x, cotangent, weights, vec):
    seq, width = x.shape
    inner = weights[1].shape[1]
    shape = lambda n, t: jax.ShapeDtypeStruct((seq, n), t)
    outs = [
        (width, F32), (width, F32), (width, BF16), (inner, BF16), (width, BF16), (inner, BF16), (width, F32), (width, BF16),
    ]
    fixed = weights + (vec,)
    return pl.pallas_call(
        feed_kernel,
        grid=(seq // TILE,),
        out_shape=[shape(*o) for o in outs] + [jax.ShapeDtypeStruct((8, width), F32)],
        in_specs=[smem()] + [row_block(width)] * 3 + [whole(a) for a in fixed],
        out_specs=[row_block(o[0]) for o in outs] + [pl.BlockSpec((8, width), lambda i: (0, 0))],
        compiler_params=params(),
        name="feed",
    )(length, context, x, cotangent, *fixed)


def tall(row):
    return jnp.concatenate([jnp.broadcast_to(row[i : i + 1], (16, row.shape[1])) for i in range(THOUGHTS)], 0)


def reflect_kernel(
    start_ref, x_ref, mixed_ref, resid_ref, context_ref, log_ref, vec_ref, wp_hbm, wc_hbm, we_hbm, wo_hbm,
    dh_in, dctx_in, dz_hbm, df_hbm, sums_in,
    dh_ref, dctx_ref, dz_out, df_out, sums_ref,
    wp_ref, wc_ref, we_ref, wo_ref, sems, dz_ref, df_ref, edge_sems,
):
    seq, width = context_ref.shape
    copies = fetch((wp_hbm, wc_hbm, we_hbm, wo_hbm), (wp_ref, wc_ref, we_ref, wo_ref), sems)
    start = start_ref[0]
    base = aligned(start - 1)
    edge = pl.ds(base, 32)
    loads = fetch((dz_hbm.at[edge], df_hbm.at[edge]), (dz_ref, df_ref), edge_sems)
    vec = Vectors(vec_ref, width)
    mask = head_mask(width)
    masks = jnp.concatenate([mask] * THOUGHTS, 0)
    dh_ref[...] = dh_in[...]
    dctx_ref[...] = dctx_in[...]
    sums_ref[...] = sums_in[...]
    queries, keys, values = (mixed_ref.at[:, i * width : (i + 1) * width] for i in range(3))
    first_keys, first_values = keys.at[:PREFIX], values.at[:PREFIX]

    def split(rows):
        picked = jnp.where(masks, rows, 0.0)
        return jnp.concatenate(
            [jnp.sum(picked[16 * i : 16 * i + 16], axis=0, keepdims=True) for i in range(THOUGHTS)], 0
        )

    def spread_all(rows):
        return jnp.where(masks, tall(rows), 0.0).astype(BF16)

    later = iota((16, seq), 1)
    logs = jnp.concatenate([log_ref[i] for i in range(HEADS // 2)] + [jnp.zeros((4, seq), F32)], 0)
    product = dctx_in[...].astype(F32) * context_ref[...].astype(F32)
    high = product.astype(BF16)
    ones = mask.astype(F32).astype(BF16)
    delta = dot_nt(ones, high) + dot_nt(ones, (product - high.astype(F32)).astype(BF16))
    key_rows = spread_all(pick_rows(start, first_keys[...]))
    value_rows = spread_all(pick_rows(start, first_values[...]))
    score = dot_nt(key_rows, queries[...])
    prob_grad = dot_nt(value_rows, dctx_in[...])
    probs, grads = [], []
    for i in range(THOUGHTS):
        part = slice(16 * i, 16 * i + 16)
        prob = jnp.where(later >= start + i, jnp.exp(0.125 * score[part] - logs), 0.0)
        probs.append(prob.astype(BF16))
        grads.append((prob * (prob_grad[part] - delta)).astype(BF16))
    main_dk = split(dot(jnp.concatenate(grads, 0), queries[...])) * 0.125
    main_dv = split(dot(jnp.concatenate(probs, 0), dctx_in[...]))

    def row_back(query, up, place):
        score = dot_nt(query, first_keys[...]) * 0.125
        score = jnp.where(iota(score.shape, 1) <= place, score, NEG_FILL)
        expo = jnp.exp(score - jnp.max(score, axis=-1, keepdims=True))
        prob = expo / jnp.sum(expo, axis=-1, keepdims=True)
        prob_grad = dot_nt(up, first_values[...])
        grad = (prob * (prob_grad - jnp.sum(prob * prob_grad, axis=-1, keepdims=True))).astype(BF16)
        return prob.astype(BF16), grad, dot(grad, first_keys[...]) * 0.125

    places = start + iota((16 * THOUGHTS, 1), 0) // 16
    up = spread_all(pick_rows(start, dctx_in[:PREFIX]))
    main_dq = split(row_back(spread_all(pick_rows(start, queries[:PREFIX])), up, places)[2])

    query_rows = pick_rows(start - 1, queries[:PREFIX])
    rows = [start - 1 + step for step in range(THOUGHTS)]
    resid = jnp.concatenate([resid_ref[pl.ds(p, 1), :] for p in rows] + [jnp.zeros((13, width), F32)], 0)
    resid_hat, resid_inv = norm_parts(resid)
    normed = (resid_hat * vec.g2 + vec.b2).astype(BF16)
    for copy in loads:
        copy.wait()
    copies[2].wait()
    slopes = gelu_parts(dot(normed, we_ref[...]) + vec.be)[1]
    for i in (0, 1, 3):
        copies[i].wait()
    scores, spreads, probs, ups = [], [], [], []
    dq_add = jnp.zeros((1, width), F32)
    for step in reversed(range(THOUGHTS)):
        place = rows[step]
        dq_row = main_dq[step : step + 1] + dq_add
        dk_row, dv_row = main_dk[step : step + 1], main_dv[step : step + 1]
        for score, query, prob, up in zip(scores, spreads, probs, ups):
            chosen = iota(score.shape, 1) == place + 1
            share = jnp.sum(jnp.where(chosen, score.astype(F32), 0.0), axis=1, keepdims=True)
            dk_row = dk_row + 0.125 * jnp.sum(share * query.astype(F32), axis=0, keepdims=True)
            share = jnp.sum(jnp.where(chosen, prob.astype(F32), 0.0), axis=1, keepdims=True)
            dv_row = dv_row + jnp.sum(share * up.astype(F32), axis=0, keepdims=True)
        x_hat, x_inv = norm_parts(x_ref[pl.ds(place + 1, 1), :])
        da = dot_nt(wide(jnp.concatenate([dq_row, dk_row, dv_row], 1)), wp_ref[...])
        dz = dh_ref[pl.ds(place + 1, 1), :] + norm_back(da[0:1], x_hat, x_inv, vec.g1)
        df = dot_nt(wide(dz), wc_ref[...])[0:1] * slopes[step : step + 1]
        dc = dot_nt(wide(df), we_ref[...])[0:1]
        hat, inv = resid_hat[step : step + 1], resid_inv[step : step + 1]
        dh = dz + norm_back(dc, hat, inv, vec.g2)
        sums_ref[0:1] += dc * hat
        sums_ref[1:2] += dc
        dctx = dot_nt(wide(dh), wo_ref[...])[0:1]
        query, up = spread(query_rows[step : step + 1], mask), spread(dctx, mask)
        prob, score, dq = row_back(query, up, place)
        dq_add = collect(dq, mask)
        scores.append(score)
        spreads.append(query)
        probs.append(prob)
        ups.append(up)
        dh_ref[pl.ds(place, 1), :] += dh
        here = base + iota((32, 1), 0) == place
        for target, row in ((dz_ref, dz), (df_ref, df)):
            target[...] = (target[...].astype(F32) + jnp.where(here, row, 0.0)).astype(BF16)
        dctx_ref[edge, :] = (dctx_ref[edge, :].astype(F32) + jnp.where(here, dctx, 0.0)).astype(BF16)
    for copy in fetch((dz_ref, df_ref), (dz_out.at[edge], df_out.at[edge]), edge_sems):
        copy.wait()


def reflect(start, x, mixed, resid, context, log_total, vec, weights, dh, dctx, dz, df, sums):
    changed = (dh, dctx, dz, df, sums)
    operands = (x, mixed, resid, context, log_total, vec) + weights + changed
    specs = [prefix_block(x), whole(mixed), prefix_block(resid), whole(context), whole(log_total), whole(vec)]
    specs += [in_hbm() for _ in weights]
    changed_specs = [prefix_block(dh), whole(dctx), in_hbm(), in_hbm(), whole(sums)]
    first = 1 + len(specs)
    return pl.pallas_call(
        reflect_kernel,
        grid=(1,),
        out_shape=[jax.ShapeDtypeStruct(a.shape, a.dtype) for a in changed],
        in_specs=[smem()] + specs + changed_specs,
        out_specs=changed_specs,
        input_output_aliases={first + i: i for i in range(len(changed))},
        scratch_shapes=weight_scratch(weights)
        + [pltpu.VMEM((32, dz.shape[1]), BF16), pltpu.VMEM((32, df.shape[1]), BF16), DMA((2,))],
        compiler_params=params(),
        name="reflect",
    )(start, *operands)


def pack(vectors, total):
    joined = jnp.concatenate([v.reshape(total, -1) for v in vectors], 1)
    fill = -joined.shape[1] % 128
    return jnp.pad(joined, ((0, 0), (0, fill)))[:, None]


def unpack(packed, sizes):
    flat = packed.reshape(-1, packed.shape[-1])
    out, at = [], 0
    for size in sizes:
        out.append(flat[:, at : at + size].reshape(-1))
        at += size
    return out


def per_device(
    mesh_shape,
    hidden,
    cotangent,
    lengths,
    thought_start,
    first_gain,
    first_bias,
    project_weight,
    project_bias,
    output_weight,
    output_bias,
    second_gain,
    second_bias,
    expand_weight,
    expand_bias,
    contract_weight,
    contract_bias,
):
    _, seq, width = hidden.shape
    total = mesh_shape["dp"] * mesh_shape["fsdp"]
    vectors = (
        first_gain,
        first_bias,
        project_bias,
        output_bias,
        second_gain,
        second_bias,
        expand_bias,
        contract_bias,
    )
    sizes = [v.shape[0] for v in vectors]
    full = gather_all(
        mesh_shape,
        (pack(vectors, 1)[0], project_weight, output_weight, expand_weight, contract_weight),
    )
    Wp, Wo, We, Wc = (w.reshape(-1, w.shape[-1]) for w in full[1:])

    x, mixed, vec = think(thought_start, hidden[0], full[0], sizes, (Wp, Wo, We, Wc))
    context, log_total = attend(mixed)
    final, resid, normed_two, active, dz, df, dh, dctx, sums = feed(
        lengths, context, x, cotangent[0], (Wo, We, Wc), vec
    )
    dh, dctx, dz, df, sums = reflect(
        thought_start, x, mixed, resid, context, log_total, vec, (Wp, Wc, We, Wo), dh, dctx, dz, df, sums
    )
    dq, dk, dv = attend_back(mixed, dctx, log_total)
    g1, b1 = vec[0:1, :width], vec[1:2, :width]
    dy = dh.astype(BF16)
    x_hat, x_inv = norm_parts(x)
    normed = (x_hat * g1 + b1).astype(BF16)
    dmixed = jnp.concatenate([dq, dk, dv], 1)
    da = dot_nt(dmixed, Wp)
    dx = dh + norm_back(da, x_hat, x_inv, g1)
    position = iota((seq, 1), 0)
    is_thought = (position >= thought_start[0]) & (position < thought_start[0] + THOUGHTS)
    hidden_grad = jnp.where(is_thought, 0.0, dx)

    def column_sum(value):
        return jnp.sum(value, axis=0, dtype=F32)

    column = column_sum(dmixed)
    small = (
        column_sum(da * x_hat),
        column_sum(da),
        jnp.concatenate([column[:width], column[2 * width :]]),
        column_sum(dy),
        sums[0],
        sums[1],
        column_sum(df),
        column_sum(dz),
    )
    large = (
        dot_tn(normed, dmixed),
        dot_tn(context, dy),
        dot_tn(normed_two, df),
        dot_tn(active, dz),
    )
    parts = [pack(small, total)]
    for grad in large:
        parts.append(grad.astype(BF16).reshape(total, grad.shape[0] // total, grad.shape[1]))
    small, dWp, dWo, dWe, dWc = scatter_all(mesh_shape, parts)
    dg1, db1, dbp, dbo, dg2, db2, dbe, dbc = unpack(small, sizes)
    return (final[None], hidden_grad[None], dg1, db1, dWp, dbp, dWo, dbo, dg2, db2, dWe, dbe, dWc, dbc)


def solution(mesh):
    rows = P(AXES, None, None)
    flat = P(AXES)
    square = P(AXES, None)
    specs = (flat, flat, square, flat, square, flat, flat, flat, square, flat, square, flat)
    return jax.shard_map(
        functools.partial(per_device, dict(mesh.shape)),
        mesh=mesh,
        in_specs=(rows, rows, flat, flat) + specs,
        out_specs=(rows, rows) + specs,
        check_vma=False,
    )
```

```python
import functools

import jax
import jax.numpy as jnp
from jax import lax
from jax.experimental import pallas as pl
from jax.experimental.pallas import tpu as pltpu
from jax.sharding import PartitionSpec as P

HEADS = 12
THOUGHTS = 3
PREFIX = 384
TILE = 256

EPSILON = 1e-05
NEG_FILL = -1e30
F32 = jnp.float32
BF16 = jnp.bfloat16
VMEM_LIMIT = 62 * 2**20


AXES = ("dp", "fsdp")
ANY = pl.BlockSpec(memory_space=pl.ANY)
DMA = pltpu.SemaphoreType.DMA


class Place:
    def __init__(self, rows, depths, sides):
        self.rows, self.depths, self.sides = rows, depths, sides
        self.row = lax.axis_index("dp")
        flat = lax.axis_index("fsdp")
        self.depth = flat // (sides * 2)
        self.side = flat // 2 % sides
        self.core = flat % 2

    def index(self, row, depth, side, core):
        return row * (self.depths * self.sides * 2) + (depth * self.sides + side) * 2 + core

    def device(self, row, depth, side, core):
        return {"dp": row, "fsdp": (depth * self.sides + side) * 2 + core}


def gather_kernel(rows, depths, sides, count, *refs):
    shards, fulls = refs[:count], refs[count : 2 * count]
    send_sem, recv_sem, pair_send, pair_recv, own_sem = refs[2 * count :]
    at = Place(rows, depths, sides)
    dev = dict(device_id_type=pl.DeviceIdType.MESH)

    barrier = pltpu.get_barrier_semaphore()
    peers = []
    for k in range(1, depths):
        peers.append(at.device(at.row, (at.depth + k) % depths, at.side, at.core))
    for k in range(1, sides):
        peers.append(at.device(at.row, at.depth, (at.side + k) % sides, at.core))
    for k in range(1, rows):
        peers.append(at.device((at.row + k) % rows, at.depth, at.side, at.core))
    peers.append(at.device(at.row, at.depth, at.side, 1 - at.core))
    for peer in peers:
        pl.semaphore_signal(barrier, inc=1, device_id=peer, **dev)
    pl.semaphore_wait(barrier, len(peers))

    def run(core):
        sends = []

        def index(row, depth, side):
            return at.index(row, depth, side, core)

        def send(w, source, shard, peer, slot):
            copy = pltpu.make_async_remote_copy(
                src_ref=source,
                dst_ref=fulls[w].at[shard],
                send_sem=send_sem.at[w, slot],
                recv_sem=recv_sem.at[w, shard],
                device_id=peer,
                **dev,
            )
            copy.start()
            sends.append(copy)

        def arrive(w, shard):
            pltpu.make_async_remote_copy(
                src_ref=fulls[w].at[shard],
                dst_ref=fulls[w].at[shard],
                send_sem=send_sem.at[w, 0],
                recv_sem=recv_sem.at[w, shard],
                device_id=peers[0],
                **dev,
            ).wait_recv()

        def to_pair(w, source, shard):
            copy = pltpu.make_async_remote_copy(
                src_ref=source,
                dst_ref=fulls[w].at[shard],
                send_sem=pair_send.at[w, shard // 2],
                recv_sem=pair_recv.at[w, shard // 2],
                device_id=at.device(at.row, at.depth, at.side, 1 - core),
                **dev,
            )
            copy.start()
            sends.append(copy)

        slots = [0] * count

        def slot(w):
            slots[w] += 1
            return slots[w] - 1

        second_size, third_size = (sides, rows) if core == 0 else (rows, sides)

        def spot(second, third):
            return (third, second) if core == 0 else (second, third)

        mine = (at.side, at.row) if core == 0 else (at.row, at.side)

        def forward_second(w, source, depth):
            row, side = spot(*mine)
            for k in range(1, second_size):
                r, s = spot((mine[0] + k) % second_size, mine[1])
                send(w, source, index(row, depth, side), at.device(r, at.depth, s, core), slot(w))

        def forward_third(w, source, depth, second):
            row, side = spot(second, mine[1])
            for k in range(1, third_size):
                r, s = spot(mine[0], (mine[1] + k) % third_size)
                send(w, source, index(row, depth, side), at.device(r, at.depth, s, core), slot(w))

        own = []
        for w in range(count):
            me = index(at.row, at.depth, at.side)
            for k in range(1, depths):
                send(w, shards[w], me, at.device(at.row, (at.depth + k) % depths, at.side, core), slot(w))
            forward_second(w, shards[w], at.depth)
            forward_third(w, shards[w], at.depth, mine[0])
            to_pair(w, shards[w], me)
            copy = pltpu.make_async_copy(shards[w], fulls[w].at[me], own_sem.at[w])
            copy.start()
            own.append(copy)

        def stage_one(w):
            for k in range(1, depths):
                depth = (at.depth - k) % depths
                shard = index(at.row, depth, at.side)
                arrive(w, shard)
                forward_second(w, fulls[w].at[shard], depth)
                forward_third(w, fulls[w].at[shard], depth, mine[0])
                to_pair(w, fulls[w].at[shard], shard)

        def stage_two(w):
            for k in range(1, second_size):
                second = (mine[0] - k) % second_size
                for d in range(depths):
                    depth = (at.depth - d) % depths
                    shard = index(spot(second, mine[1])[0], depth, spot(second, mine[1])[1])
                    arrive(w, shard)
                    forward_third(w, fulls[w].at[shard], depth, second)
                    to_pair(w, fulls[w].at[shard], shard)

        def stage_three(w):
            for k in range(1, third_size):
                third = (mine[1] - k) % third_size
                for s in range(second_size):
                    second = (mine[0] - s) % second_size
                    for d in range(depths):
                        depth = (at.depth - d) % depths
                        row, side = spot(second, third)
                        shard = index(row, depth, side)
                        arrive(w, shard)
                        to_pair(w, fulls[w].at[shard], shard)

        for step in range(count + 2):
            if step < count:
                stage_one(step)
            if 0 <= step - 1 < count:
                stage_two(step - 1)
            if 0 <= step - 2 < count:
                stage_three(step - 2)

        for w in range(count):
            for row in range(rows):
                for depth in range(depths):
                    for side in range(sides):
                        shard = at.index(row, depth, side, 1 - core)
                        pltpu.make_async_remote_copy(
                            src_ref=fulls[w].at[shard],
                            dst_ref=fulls[w].at[shard],
                            send_sem=pair_send.at[w, shard // 2],
                            recv_sem=pair_recv.at[w, shard // 2],
                            device_id=peers[0],
                            **dev,
                        ).wait_recv()
        for copy in own:
            copy.wait()
        for copy in sends:
            copy.wait_send()

    for core in range(2):

        @pl.when(at.core == core)
        def _():
            run(core)


def gather_all(mesh_shape, shards, collective_id=0):
    rows, inner = mesh_shape["dp"], mesh_shape["fsdp"]
    depths = 4
    sides = inner // (2 * depths)
    total = rows * inner
    count = len(shards)
    sent = (depths - 1) + depths * (max(rows, sides) - 1) + depths * sides * (rows - 1) + depths * rows * (sides - 1)
    return pl.pallas_call(
        functools.partial(gather_kernel, rows, depths, sides, count),
        out_shape=[jax.ShapeDtypeStruct((total,) + s.shape, s.dtype) for s in shards],
        in_specs=[ANY] * count,
        out_specs=[ANY] * count,
        scratch_shapes=[
            DMA((count, sent)),
            DMA((count, total)),
            DMA((count, total // 2)),
            DMA((count, total // 2)),
            DMA((count,)),
        ],
        compiler_params=pltpu.CompilerParams(collective_id=collective_id, has_side_effects=True),
        name="gather_weights",
    )(*shards)


def scatter_kernel(rows, depths, sides, count, *refs):
    parts, outs = refs[:count], refs[count : 2 * count]
    scratch = refs[2 * count :]
    held, pair, third_in, second_in, depth_in = (scratch[i * count : (i + 1) * count] for i in range(5))
    (own_sem, pair_send, pair_recv, third_send, third_recv, second_send, second_recv, depth_send, depth_recv) = scratch[
        5 * count :
    ]
    at = Place(rows, depths, sides)
    dev = dict(device_id_type=pl.DeviceIdType.MESH)

    barrier = pltpu.get_barrier_semaphore()
    peers = []
    for k in range(1, depths):
        peers.append(at.device(at.row, (at.depth + k) % depths, at.side, at.core))
    for k in range(1, sides):
        peers.append(at.device(at.row, at.depth, (at.side + k) % sides, at.core))
    for k in range(1, rows):
        peers.append(at.device((at.row + k) % rows, at.depth, at.side, at.core))
    peers.append(at.device(at.row, at.depth, at.side, 1 - at.core))
    for peer in peers:
        pl.semaphore_signal(barrier, inc=1, device_id=peer, **dev)
    pl.semaphore_wait(barrier, len(peers))

    def run(core):
        second_size, third_size = (sides, rows) if core == 0 else (rows, sides)
        my_second, my_third = (at.side, at.row) if core == 0 else (at.row, at.side)

        def unit(second, third, depth):
            row, side = (third, second) if core == 0 else (second, third)
            return (row * depths + depth) * sides + side

        def device(second, third, depth):
            row, side = (third, second) if core == 0 else (second, third)
            return at.device(row, depth, side, core)

        def remote(source, target, send, recv, peer):
            return pltpu.make_async_remote_copy(
                src_ref=source, dst_ref=target, send_sem=send, recv_sem=recv, device_id=peer, **dev
            )

        sibling = at.device(at.row, at.depth, at.side, 1 - core)

        def pair_copy(w, u):
            return remote(
                parts[w].at[u, 1 - core], pair[w].at[u], pair_send.at[w], pair_recv.at[w, u], sibling
            )

        def own_copy(w):
            return pltpu.make_async_copy(parts[w].at[:, core], held[w], own_sem.at[w])

        def third_copy(w, u, k, q, peer):
            return remote(
                held[w].at[u],
                third_in[w].at[k - 1, q],
                third_send.at[w, k - 1, q],
                third_recv.at[w, k - 1, q],
                peer,
            )

        def second_copy(w, u, k, q, peer):
            return remote(
                held[w].at[u],
                second_in[w].at[k - 1, q],
                second_send.at[w, k - 1, q],
                second_recv.at[w, k - 1, q],
                peer,
            )

        def depth_copy(w, u, k, peer):
            return remote(
                held[w].at[u], depth_in[w].at[k - 1], depth_send.at[w, k - 1], depth_recv.at[w, k - 1], peer
            )

        def loop(size, body):
            lax.fori_loop(0, size, lambda i, c: (body(i), c)[1], 0)

        def each_unit(visit):
            other_second, other_third = third_size, second_size
            far = my_second
            for k in list(range(1, other_third)) + [0]:
                def inner(q, k=k):
                    second, third = q // depths, (far + k) % other_third
                    row, side = (second, third) if core == 0 else (third, second)
                    visit((row * depths + q % depths) * sides + side)
                loop(other_second * depths, inner)

        for w in range(count):
            each_unit(lambda u, w=w: pair_copy(w, u).start())
            own_copy(w).start()

        def add_pair(w, u):
            pair_copy(w, u).wait_recv()
            held[w][u] = held[w][u] + pair[w][u]

        def stage_third(w):
            own_copy(w).wait()
            for k in list(range(1, third_size)) + [0]:
                third = (my_third + k) % third_size

                def inner(q, k=k, third=third):
                    second, depth = q // depths, q % depths
                    u = unit(second, third, depth)
                    add_pair(w, u)
                    if k:
                        third_copy(w, u, k, q, device(my_second, third, at.depth)).start()

                loop(second_size * depths, inner)

        def stage_second(w):
            for k in list(range(1, second_size)) + [0]:
                second = (my_second + k) % second_size

                def inner(depth, k=k, second=second):
                    u = unit(second, my_third, depth)
                    for j in range(1, third_size):
                        third_copy(w, u, j, second * depths + depth, sibling).wait_recv()
                        held[w][u] = held[w][u] + third_in[w][j - 1, second * depths + depth]
                    if k:
                        second_copy(w, u, k, depth, device(second, my_third, at.depth)).start()

                loop(depths, inner)

        def stage_depth(w):
            for k in list(range(1, depths)) + [0]:
                depth = (at.depth + k) % depths
                u = unit(my_second, my_third, depth)
                for j in range(1, second_size):
                    second_copy(w, u, j, depth, sibling).wait_recv()
                    held[w][u] = held[w][u] + second_in[w][j - 1, depth]
                if k:
                    depth_copy(w, u, k, device(my_second, my_third, depth)).start()

        def stage_last(w):
            u = unit(my_second, my_third, at.depth)
            total = held[w][u].astype(jnp.float32)
            for k in range(1, depths):
                depth_copy(w, u, k, sibling).wait_recv()
                total = total + depth_in[w][k - 1].astype(jnp.float32)
            outs[w][...] = total

        for step in range(count + 3):
            for lag, stage in enumerate((stage_third, stage_second, stage_depth, stage_last)):
                if 0 <= step - lag < count:
                    stage(step - lag)

        for w in range(count):
            remote(pair[w], pair[w], pair_send.at[w], pair_recv.at[w, 0], sibling).wait_send()
            for k in range(1, third_size):
                loop(second_size * depths, lambda q, w=w, k=k: third_copy(w, 0, k, q, sibling).wait_send())
            for k in range(1, second_size):
                loop(depths, lambda q, w=w, k=k: second_copy(w, 0, k, q, sibling).wait_send())
            for k in range(1, depths):
                depth_copy(w, 0, k, sibling).wait_send()

    for core in range(2):

        @pl.when(at.core == core)
        def _():
            run(core)


def scatter_all(mesh_shape, parts, collective_id=1):
    rows, inner = mesh_shape["dp"], mesh_shape["fsdp"]
    depths = 4
    sides = inner // (2 * depths)
    total = rows * inner
    half = total // 2
    count = len(parts)
    if rows == sides:
        thirds, seconds = (rows - 1, sides * depths), (sides - 1, depths)
    else:
        wide = max(rows, sides)
        thirds, seconds = (wide - 1, wide * depths), (wide - 1, depths)
    scratch = []
    for lead in ((half,), (half,), thirds, seconds, (depths - 1,)):
        scratch += [pltpu.VMEM(lead + p.shape[1:], p.dtype) for p in parts]
    parts = [p.reshape((half, 2) + p.shape[1:]) for p in parts]
    sems = [
        (), (), (half,), thirds, thirds, seconds, seconds, (depths - 1,), (depths - 1,),
    ]
    return pl.pallas_call(
        functools.partial(scatter_kernel, rows, depths, sides, count),
        out_shape=[jax.ShapeDtypeStruct(p.shape[2:], jnp.float32) for p in parts],
        in_specs=[ANY] * count,
        out_specs=[pl.BlockSpec(memory_space=pltpu.VMEM)] * count,
        scratch_shapes=scratch + [DMA((count,) + s) for s in sems],
        compiler_params=pltpu.CompilerParams(
            collective_id=collective_id, has_side_effects=True, vmem_limit_bytes=60 * 2**20
        ),
        name="scatter_grads",
    )(*parts)


def dot(left, right):
    return jnp.dot(left, right, preferred_element_type=F32)


def dot_nt(left, right):
    return lax.dot_general(left, right, (((1,), (1,)), ((), ())), preferred_element_type=F32)


def dot_tn(left, right):
    return lax.dot_general(left, right, (((0,), (0,)), ((), ())), preferred_element_type=F32)


def norm_parts(value):
    center = value - jnp.mean(value, axis=-1, keepdims=True)
    inv = lax.rsqrt(jnp.mean(center * center, axis=-1, keepdims=True) + EPSILON)
    return center * inv, inv


def norm_back(grad, hat, inv, gain):
    scaled = grad * gain
    return inv * (
        scaled
        - jnp.mean(scaled, axis=-1, keepdims=True)
        - hat * jnp.mean(scaled * hat, axis=-1, keepdims=True)
    )


GELU_ROOT = 0.7978845608028654


def gelu_parts(value):
    square = value * value
    inner = jnp.tanh(GELU_ROOT * value * (1.0 + 0.044715 * square))
    half = 0.5 * (1.0 + inner)
    slope = half + 0.5 * value * (1.0 - inner * inner) * (GELU_ROOT + 3 * 0.044715 * GELU_ROOT * square)
    return value * half, slope


def iota(shape, axis):
    return lax.broadcasted_iota(jnp.int32, shape, axis)


def wide(row):
    return jnp.broadcast_to(row, (16, row.shape[1])).astype(BF16)


def head_mask(width):
    return iota((16, width), 1) // (width // HEADS) == iota((16, width), 0)


def spread(row, mask):
    return jnp.where(mask, jnp.broadcast_to(row.astype(F32), mask.shape), 0.0).astype(BF16)


def collect(rows, mask):
    return jnp.sum(jnp.where(mask, rows, 0.0), axis=0, keepdims=True)


def row_softmax(spread_query, keys, place):
    score = dot_nt(spread_query, keys) * 0.125
    score = jnp.where(iota(score.shape, 1) <= place, score, NEG_FILL)
    expo = jnp.exp(score - jnp.max(score, axis=-1, keepdims=True))
    return expo / jnp.sum(expo, axis=-1, keepdims=True)


def pick_rows(first, array):
    chosen = iota((16, array.shape[0]), 1) == first + iota((16, array.shape[0]), 0)
    return dot(chosen.astype(F32).astype(BF16), array)


VECTORS = ("g1", "b1", "bp", "bo", "g2", "b2", "be", "bc")


class Vectors:
    def __init__(self, ref, width):
        self.ref, self.width = ref, width
        self.sizes = dict(bp=3 * width, be=4 * width)

    def __getattr__(self, name):
        return self.ref[VECTORS.index(name) : VECTORS.index(name) + 1, : self.sizes.get(name, self.width)]


def spread_vectors(pieces, sizes, width, vec_ref):
    count, offset = pieces.shape[0], 0
    vec_ref[...] = jnp.zeros_like(vec_ref)
    for row, (name, size) in enumerate(zip(VECTORS, sizes)):
        low, high = offset // 128 * 128, -(-(offset + size) // 128) * 128
        length = count * size
        lane = iota((1, length), 1)
        pick = iota((high - low, length), 0) == lane % size + (offset - low)
        tiled = dot(pieces[:, low:high], pick.astype(F32).astype(BF16))
        line = jnp.sum(jnp.where(iota((count, length), 0) == lane // size, tiled, 0.0), axis=0, keepdims=True)
        if name == "bp":
            vec_ref[row : row + 1, :width] = line[:, :width]
            vec_ref[row : row + 1, 2 * width : 3 * width] = line[:, width:]
        else:
            vec_ref[row : row + 1, :length] = line
        offset += size


def fetch(sources, targets, sems):
    copies = [pltpu.make_async_copy(s, t, sems.at[i]) for i, (s, t) in enumerate(zip(sources, targets))]
    for copy in copies:
        copy.start()
    return copies


def aligned(place):
    return pl.multiple_of(place // 16 * 16, 16)


def think_kernel(
    sizes, start_ref, hidden_ref, pieces_ref, wp_hbm, wo_hbm, we_hbm, wc_hbm,
    x_ref, mixed_ref, normed_ref, vec_ref, wp_ref, wo_ref, we_ref, wc_ref, sems,
):
    seq, width = hidden_ref.shape
    copies = fetch((wp_hbm, wo_hbm, we_hbm, wc_hbm), (wp_ref, wo_ref, we_ref, wc_ref), sems)
    spread_vectors(pieces_ref[:, 0, :], sizes, width, vec_ref)
    vec = Vectors(vec_ref, width)
    start = start_ref[0]
    copies[0].wait()
    for at in range(0, seq, TILE):
        part = slice(at, at + TILE)
        x = hidden_ref[part].astype(F32)
        x_ref[part] = x
        normed = (norm_parts(x)[0] * vec.g1 + vec.b1).astype(BF16)
        normed_ref[part] = normed
        mixed_ref[part] = (dot(normed, wp_ref[...]) + vec.bp).astype(BF16)
    mask = head_mask(width)
    x_row = x_ref[pl.ds(start - 1, 1), :]
    query = pick_rows(start - 1, mixed_ref[:PREFIX, :width])[0:1]
    for copy in copies[1:]:
        copy.wait()
    for step in range(THOUGHTS):
        place = start - 1 + step
        prob = row_softmax(spread(query, mask), mixed_ref[:PREFIX, width : 2 * width], place)
        context = collect(dot(prob.astype(BF16), mixed_ref[:PREFIX, 2 * width :]), mask)
        resid = x_row + (dot(wide(context), wo_ref[...])[0:1] + vec.bo)
        normed = norm_parts(resid)[0] * vec.g2 + vec.b2
        pre = dot(wide(normed), we_ref[...])[0:1] + vec.be
        active = gelu_parts(pre)[0]
        x_row = resid + (dot(wide(active), wc_ref[...])[0:1] + vec.bc)
        normed = norm_parts(x_row)[0] * vec.g1 + vec.b1
        mixed_row = dot(wide(normed), wp_ref[...])[0:1] + vec.bp
        query = mixed_row[:, :width].astype(BF16)
        x_ref[pl.ds(place + 1, 1), :] = x_row
        window = pl.ds(aligned(place + 1), 16)
        here = aligned(place + 1) + iota((16, 1), 0) == place + 1
        for target, row in ((mixed_ref, mixed_row), (normed_ref, normed)):
            target[window, :] = jnp.where(here, row, target[window, :].astype(F32)).astype(BF16)


def smem():
    return pl.BlockSpec(memory_space=pltpu.SMEM)


def whole(array):
    return pl.BlockSpec(array.shape, lambda *_: (0,) * array.ndim, pipeline_mode=pl.Buffered(1))


def prefix_block(array):
    return pl.BlockSpec((PREFIX, array.shape[1]), lambda *_: (0, 0), pipeline_mode=pl.Buffered(1))


def params(semantics=("arbitrary",)):
    return pltpu.CompilerParams(dimension_semantics=semantics, vmem_limit_bytes=VMEM_LIMIT)


def in_hbm():
    return pl.BlockSpec(memory_space=pl.ANY)


def weight_scratch(weights):
    return [pltpu.VMEM(w.shape, w.dtype) for w in weights] + [DMA((len(weights),))]


def think(start, hidden, pieces, sizes, weights):
    seq, width = hidden.shape
    outs = [
        jax.ShapeDtypeStruct((seq, width), F32),
        jax.ShapeDtypeStruct((seq, 3 * width), BF16),
        jax.ShapeDtypeStruct((seq, width), BF16),
        jax.ShapeDtypeStruct((8, weights[2].shape[1]), F32),
    ]
    return pl.pallas_call(
        functools.partial(think_kernel, sizes),
        grid=(1,),
        out_shape=outs,
        in_specs=[smem(), whole(hidden), whole(pieces)] + [in_hbm() for _ in weights],
        out_specs=[whole(o) for o in outs],
        scratch_shapes=weight_scratch(weights),
        compiler_params=params(),
        name="think",
    )(start, hidden, pieces, *weights)


def attend_kernel(query_ref, key_ref, value_ref, context_ref, log_ref):
    seq, lanes = query_ref.shape
    half = lanes // 2
    first_head = iota((TILE, lanes), 1) < half
    values_t = value_ref[...].T
    for start in range(0, seq, TILE):
        stop = start + TILE
        query = query_ref[start:stop]
        outs = []
        for head in range(2):
            own = first_head if head == 0 else jnp.logical_not(first_head)
            masked = jnp.where(own, query.astype(F32) * 0.125, 0.0).astype(BF16)
            score = dot_nt(key_ref[:stop], masked)
            hidden = iota((TILE, TILE), 0) > iota((TILE, TILE), 1)
            last = jnp.where(hidden, NEG_FILL, score[start:])
            score = jnp.concatenate([score[:start], last], 0) if start else last
            peak = jnp.max(score, axis=0, keepdims=True)
            expo = jnp.exp(score - peak)
            total = jnp.sum(expo, axis=0, keepdims=True)
            prob = (expo * (1.0 / total)).astype(BF16)
            outs.append(dot(values_t[:, :stop], prob)[head * half : (head + 1) * half])
            log_ref[head : head + 1, start:stop] = peak + jnp.log(total)
        context_ref[start:stop] = jnp.concatenate(outs, 0).T.astype(BF16)


def pair_spec(seq, offset, lanes=128):
    return pl.BlockSpec((seq, lanes), lambda i: (0, offset + i))


def attend(mixed):
    seq, width = mixed.shape[0], mixed.shape[1] // 3
    pairs = HEADS // 2
    return pl.pallas_call(
        attend_kernel,
        grid=(pairs,),
        out_shape=[jax.ShapeDtypeStruct((seq, width), BF16), jax.ShapeDtypeStruct((pairs, 2, seq), F32)],
        in_specs=[pair_spec(seq, 0), pair_spec(seq, pairs), pair_spec(seq, 2 * pairs)],
        out_specs=[pair_spec(seq, 0), pl.BlockSpec((None, 2, seq), lambda i: (i, 0, 0))],
        compiler_params=params(),
        name="attend",
    )(mixed, mixed, mixed)


def attend_back_kernel(query_ref, key_ref, value_ref, up_ref, log_ref, dq_ref, dk_ref, dv_ref, dk_sum, dv_sum):
    seq, lanes = query_ref.shape
    half = lanes // 2
    first_head = iota((TILE, lanes), 1) < half
    keys_t = key_ref[...].T
    for start in reversed(range(0, seq, TILE)):
        stop = start + TILE
        query = query_ref[start:stop].astype(F32) * 0.125
        upstream = up_ref[start:stop].astype(F32)
        outs = []
        for head in range(2):
            own = first_head if head == 0 else jnp.logical_not(first_head)
            masked = jnp.where(own, query, 0.0).astype(BF16)
            up_masked = jnp.where(own, upstream, 0.0).astype(BF16)
            score = dot_nt(key_ref[:stop], masked)
            hidden = iota((TILE, TILE), 0) > iota((TILE, TILE), 1)
            last = jnp.where(hidden, NEG_FILL, score[start:])
            score = jnp.concatenate([score[:start], last], 0) if start else last
            prob = jnp.exp(score - log_ref[head : head + 1, start:stop])
            prob_grad = dot_nt(value_ref[:stop], up_masked)
            inner = jnp.sum(prob * prob_grad, axis=0, keepdims=True)
            score_grad = (prob * (prob_grad - inner)).astype(BF16)
            dv = dot(prob.astype(BF16), up_masked)
            dk = dot(score_grad, masked)
            if stop == seq and head == 0:
                dv_sum[...] = dv
                dk_sum[...] = dk
            else:
                dv_sum[:stop] += dv
                dk_sum[:stop] += dk
            outs.append(dot(keys_t[:, :stop], score_grad)[head * half : (head + 1) * half])
        dq_ref[start:stop] = (jnp.concatenate(outs, 0).T * 0.125).astype(BF16)
    dk_ref[...] = dk_sum[...].astype(BF16)
    dv_ref[...] = dv_sum[...].astype(BF16)


def attend_back(mixed, upstream, log_total):
    seq, width = upstream.shape
    pairs = HEADS // 2
    out = jax.ShapeDtypeStruct((seq, width), BF16)
    return pl.pallas_call(
        attend_back_kernel,
        grid=(pairs,),
        out_shape=[out, out, out],
        in_specs=[
            pair_spec(seq, 0),
            pair_spec(seq, pairs),
            pair_spec(seq, 2 * pairs),
            pair_spec(seq, 0),
            pl.BlockSpec((None, 2, seq), lambda i: (i, 0, 0)),
        ],
        out_specs=[pair_spec(seq, 0)] * 3,
        scratch_shapes=[pltpu.VMEM((seq, 128), F32), pltpu.VMEM((seq, 128), F32)],
        compiler_params=params(),
        name="attend_back",
    )(mixed, mixed, mixed, upstream, log_total)


def feed_kernel(
    length_ref, context_ref, x_ref, cot_ref, wo_ref, we_ref, wc_ref, vec_ref,
    final_ref, resid_ref, normed_ref, active_ref, dz_ref, df_ref, dh_ref, dctx_ref, sums_ref,
):
    rows, width = x_ref.shape
    inner = we_ref.shape[1]
    vec = Vectors(vec_ref, width)
    be = vec.be
    valid = pl.program_id(0) * rows + iota((rows, 1), 0) < length_ref[0]
    resid = x_ref[...] + (dot(context_ref[...], wo_ref[...]) + vec.bo)
    resid_ref[...] = resid
    hat, inv = norm_parts(resid)
    normed = (hat * vec.g2 + vec.b2).astype(BF16)
    normed_ref[...] = normed
    dout = jnp.where(valid, cot_ref[...].astype(F32), 0.0)
    dz = dout.astype(BF16)
    dz_ref[...] = dz
    total = jnp.zeros((rows, width), F32)
    dc = jnp.zeros((rows, width), F32)
    for at in range(0, inner, width):
        part = slice(at, at + width)
        value, slope = gelu_parts(dot(normed, we_ref[:, part]) + be[:, part])
        value = value.astype(BF16)
        active_ref[:, part] = value
        total = total + dot(value, wc_ref[part])
        df = (dot_nt(dz, wc_ref[part]) * slope).astype(BF16)
        df_ref[:, part] = df
        dc = dc + dot_nt(df, we_ref[:, part])
    final_ref[...] = jnp.where(valid, resid + (total + vec.bc), 0.0)
    dh = dout + norm_back(dc, hat, inv, vec.g2)
    dh_ref[...] = dh
    dctx_ref[...] = dot_nt(dh.astype(BF16), wo_ref[...]).astype(BF16)

    @pl.when(pl.program_id(0) == 0)
    def _():
        sums_ref[...] = jnp.zeros_like(sums_ref)

    sums_ref[0:1] += jnp.sum(dc * hat, axis=0, keepdims=True)
    sums_ref[1:2] += jnp.sum(dc, axis=0, keepdims=True)


def row_block(columns):
    return pl.BlockSpec((TILE, columns), lambda i: (i, 0))


def feed(length, context, x, cotangent, weights, vec):
    seq, width = x.shape
    inner = weights[1].shape[1]
    shape = lambda n, t: jax.ShapeDtypeStruct((seq, n), t)
    outs = [
        (width, F32), (width, F32), (width, BF16), (inner, BF16), (width, BF16), (inner, BF16), (width, F32), (width, BF16),
    ]
    fixed = weights + (vec,)
    return pl.pallas_call(
        feed_kernel,
        grid=(seq // TILE,),
        out_shape=[shape(*o) for o in outs] + [jax.ShapeDtypeStruct((8, width), F32)],
        in_specs=[smem()] + [row_block(width)] * 3 + [whole(a) for a in fixed],
        out_specs=[row_block(o[0]) for o in outs] + [pl.BlockSpec((8, width), lambda i: (0, 0))],
        compiler_params=params(),
        name="feed",
    )(length, context, x, cotangent, *fixed)


def tall(row):
    return jnp.concatenate([jnp.broadcast_to(row[i : i + 1], (16, row.shape[1])) for i in range(THOUGHTS)], 0)


def reflect_kernel(
    start_ref, x_ref, mixed_ref, resid_ref, context_ref, log_ref, vec_ref, wp_hbm, wc_hbm, we_hbm, wo_hbm,
    dh_in, dctx_in, dz_hbm, df_hbm, sums_in,
    dh_ref, dctx_ref, dz_out, df_out, sums_ref,
    wp_ref, wc_ref, we_ref, wo_ref, sems, dz_ref, df_ref, edge_sems,
):
    seq, width = context_ref.shape
    copies = fetch((wp_hbm, wc_hbm, we_hbm, wo_hbm), (wp_ref, wc_ref, we_ref, wo_ref), sems)
    start = start_ref[0]
    base = aligned(start - 1)
    edge = pl.ds(base, 32)
    loads = fetch((dz_hbm.at[edge], df_hbm.at[edge]), (dz_ref, df_ref), edge_sems)
    vec = Vectors(vec_ref, width)
    mask = head_mask(width)
    masks = jnp.concatenate([mask] * THOUGHTS, 0)
    dh_ref[...] = dh_in[...]
    dctx_ref[...] = dctx_in[...]
    sums_ref[...] = sums_in[...]
    queries, keys, values = (mixed_ref.at[:, i * width : (i + 1) * width] for i in range(3))
    first_keys, first_values = keys.at[:PREFIX], values.at[:PREFIX]

    def split(rows):
        picked = jnp.where(masks, rows, 0.0)
        return jnp.concatenate(
            [jnp.sum(picked[16 * i : 16 * i + 16], axis=0, keepdims=True) for i in range(THOUGHTS)], 0
        )

    def spread_all(rows):
        return jnp.where(masks, tall(rows), 0.0).astype(BF16)

    later = iota((16, seq), 1)
    logs = jnp.concatenate([log_ref[i] for i in range(HEADS // 2)] + [jnp.zeros((4, seq), F32)], 0)
    product = dctx_in[...].astype(F32) * context_ref[...].astype(F32)
    high = product.astype(BF16)
    ones = mask.astype(F32).astype(BF16)
    delta = dot_nt(ones, high) + dot_nt(ones, (product - high.astype(F32)).astype(BF16))
    key_rows = spread_all(pick_rows(start, first_keys[...]))
    value_rows = spread_all(pick_rows(start, first_values[...]))
    score = dot_nt(key_rows, queries[...])
    prob_grad = dot_nt(value_rows, dctx_in[...])
    probs, grads = [], []
    for i in range(THOUGHTS):
        part = slice(16 * i, 16 * i + 16)
        prob = jnp.where(later >= start + i, jnp.exp(0.125 * score[part] - logs), 0.0)
        probs.append(prob.astype(BF16))
        grads.append((prob * (prob_grad[part] - delta)).astype(BF16))
    main_dk = split(dot(jnp.concatenate(grads, 0), queries[...])) * 0.125
    main_dv = split(dot(jnp.concatenate(probs, 0), dctx_in[...]))

    def row_back(query, up, place):
        score = dot_nt(query, first_keys[...]) * 0.125
        score = jnp.where(iota(score.shape, 1) <= place, score, NEG_FILL)
        expo = jnp.exp(score - jnp.max(score, axis=-1, keepdims=True))
        prob = expo / jnp.sum(expo, axis=-1, keepdims=True)
        prob_grad = dot_nt(up, first_values[...])
        grad = (prob * (prob_grad - jnp.sum(prob * prob_grad, axis=-1, keepdims=True))).astype(BF16)
        return prob.astype(BF16), grad, dot(grad, first_keys[...]) * 0.125

    places = start + iota((16 * THOUGHTS, 1), 0) // 16
    up = spread_all(pick_rows(start, dctx_in[:PREFIX]))
    main_dq = split(row_back(spread_all(pick_rows(start, queries[:PREFIX])), up, places)[2])

    query_rows = pick_rows(start - 1, queries[:PREFIX])
    rows = [start - 1 + step for step in range(THOUGHTS)]
    resid = jnp.concatenate([resid_ref[pl.ds(p, 1), :] for p in rows] + [jnp.zeros((13, width), F32)], 0)
    resid_hat, resid_inv = norm_parts(resid)
    normed = (resid_hat * vec.g2 + vec.b2).astype(BF16)
    for copy in loads:
        copy.wait()
    copies[2].wait()
    slopes = gelu_parts(dot(normed, we_ref[...]) + vec.be)[1]
    for i in (0, 1, 3):
        copies[i].wait()
    scores, spreads, probs, ups = [], [], [], []
    dq_add = jnp.zeros((1, width), F32)
    for step in reversed(range(THOUGHTS)):
        place = rows[step]
        dq_row = main_dq[step : step + 1] + dq_add
        dk_row, dv_row = main_dk[step : step + 1], main_dv[step : step + 1]
        for score, query, prob, up in zip(scores, spreads, probs, ups):
            chosen = iota(score.shape, 1) == place + 1
            share = jnp.sum(jnp.where(chosen, score.astype(F32), 0.0), axis=1, keepdims=True)
            dk_row = dk_row + 0.125 * jnp.sum(share * query.astype(F32), axis=0, keepdims=True)
            share = jnp.sum(jnp.where(chosen, prob.astype(F32), 0.0), axis=1, keepdims=True)
            dv_row = dv_row + jnp.sum(share * up.astype(F32), axis=0, keepdims=True)
        x_hat, x_inv = norm_parts(x_ref[pl.ds(place + 1, 1), :])
        da = dot_nt(wide(jnp.concatenate([dq_row, dk_row, dv_row], 1)), wp_ref[...])
        dz = dh_ref[pl.ds(place + 1, 1), :] + norm_back(da[0:1], x_hat, x_inv, vec.g1)
        df = dot_nt(wide(dz), wc_ref[...])[0:1] * slopes[step : step + 1]
        dc = dot_nt(wide(df), we_ref[...])[0:1]
        hat, inv = resid_hat[step : step + 1], resid_inv[step : step + 1]
        dh = dz + norm_back(dc, hat, inv, vec.g2)
        sums_ref[0:1] += dc * hat
        sums_ref[1:2] += dc
        dctx = dot_nt(wide(dh), wo_ref[...])[0:1]
        query, up = spread(query_rows[step : step + 1], mask), spread(dctx, mask)
        prob, score, dq = row_back(query, up, place)
        dq_add = collect(dq, mask)
        scores.append(score)
        spreads.append(query)
        probs.append(prob)
        ups.append(up)
        dh_ref[pl.ds(place, 1), :] += dh
        here = base + iota((32, 1), 0) == place
        for target, row in ((dz_ref, dz), (df_ref, df)):
            target[...] = (target[...].astype(F32) + jnp.where(here, row, 0.0)).astype(BF16)
        dctx_ref[edge, :] = (dctx_ref[edge, :].astype(F32) + jnp.where(here, dctx, 0.0)).astype(BF16)
    for copy in fetch((dz_ref, df_ref), (dz_out.at[edge], df_out.at[edge]), edge_sems):
        copy.wait()


def reflect(start, x, mixed, resid, context, log_total, vec, weights, dh, dctx, dz, df, sums):
    changed = (dh, dctx, dz, df, sums)
    operands = (x, mixed, resid, context, log_total, vec) + weights + changed
    specs = [prefix_block(x), whole(mixed), prefix_block(resid), whole(context), whole(log_total), whole(vec)]
    specs += [in_hbm() for _ in weights]
    changed_specs = [prefix_block(dh), whole(dctx), in_hbm(), in_hbm(), whole(sums)]
    first = 1 + len(specs)
    return pl.pallas_call(
        reflect_kernel,
        grid=(1,),
        out_shape=[jax.ShapeDtypeStruct(a.shape, a.dtype) for a in changed],
        in_specs=[smem()] + specs + changed_specs,
        out_specs=changed_specs,
        input_output_aliases={first + i: i for i in range(len(changed))},
        scratch_shapes=weight_scratch(weights)
        + [pltpu.VMEM((32, dz.shape[1]), BF16), pltpu.VMEM((32, df.shape[1]), BF16), DMA((2,))],
        compiler_params=params(),
        name="reflect",
    )(start, *operands)


class Refs:
    def __init__(self, names, refs):
        self.__dict__.update(zip(names, refs))


MESH = dict(device_id_type=pl.DeviceIdType.MESH)


class Stream:
    def __init__(self, at, side_first, name, refs):
        self.at, self.side_first = at, side_first
        for field in STREAM_FIELDS:
            setattr(self, field, getattr(refs, name + "_" + field))
        self.sizes = (at.rows, at.sides) if side_first else (at.sides, at.rows)
        self.mine = (at.row, at.side) if side_first else (at.side, at.row)
        self.sent = []

    def spot(self, second, third):
        return (second, third) if self.side_first else (third, second)

    def unit(self, second, third, depth):
        row, side = self.spot(second, third)
        return (row * self.at.depths + depth) * self.at.sides + side

    def remote(self, source, target, send, recv, peer):
        return pltpu.make_async_remote_copy(
            src_ref=source, dst_ref=target, send_sem=send, recv_sem=recv, device_id=peer, **MESH
        )

    def sibling(self):
        return self.at.device(self.at.row, self.at.depth, self.at.side, 1 - self.at.core)

    def pair_copy(self, u, source):
        return self.remote(source, self.pair.at[u], self.pair_send.at[u], self.pair_recv.at[u], self.sibling())

    def third_copy(self, u, k, q):
        peer = self.at.device(*self.place(self.mine[0], (self.mine[1] + k) % self.sizes[1], self.at.depth))
        return self.remote(
            self.held.at[u], self.third.at[k - 1, q], self.third_send.at[k - 1, q], self.third_recv.at[k - 1, q], peer
        )

    def second_copy(self, u, k, depth):
        peer = self.at.device(*self.place((self.mine[0] + k) % self.sizes[0], self.mine[1], self.at.depth))
        return self.remote(
            self.held.at[u],
            self.second.at[k - 1, depth],
            self.second_send.at[k - 1, depth],
            self.second_recv.at[k - 1, depth],
            peer,
        )

    def depth_copy(self, u, k):
        peer = self.at.device(*self.place(*self.mine, (self.at.depth + k) % self.at.depths))
        return self.remote(
            self.held.at[u], self.depth.at[k - 1], self.depth_send.at[k - 1], self.depth_recv.at[k - 1], peer
        )

    def place(self, second, third, depth):
        row, side = self.spot(second, third)
        return row, depth, side, self.at.core

    def third_step(self, k, q, source):
        depths = self.at.depths
        u = self.unit(q // depths, (self.mine[1] + k) % self.sizes[1], q % depths)
        own = source(u)
        self.pair_copy(u, own).wait_recv()
        self.held[u] = own[...] + self.pair[u]
        if k:
            self.third_copy(u, k, q).start()

    def second_step(self, depth):
        for k in list(range(1, self.sizes[0])) + [0]:
            second = (self.mine[0] + k) % self.sizes[0]
            u = self.unit(second, self.mine[1], depth)
            q = second * self.at.depths + depth
            for j in range(1, self.sizes[1]):
                self.third_copy(u, j, q).wait_recv()
                self.held[u] = self.held[u] + self.third[j - 1, q]
            if k:
                self.second_copy(u, k, depth).start()

    def depth_step(self, k):
        depth = (self.at.depth + k) % self.at.depths
        u = self.unit(*self.mine, depth)
        for j in range(1, self.sizes[0]):
            self.second_copy(u, j, depth).wait_recv()
            self.held[u] = self.held[u] + self.second[j - 1, depth]
        if k:
            self.depth_copy(u, k).start()

    def total(self):
        u = self.unit(*self.mine, self.at.depth)
        total = self.held[u].astype(F32)
        for k in range(1, self.at.depths):
            self.depth_copy(u, k).wait_recv()
            total = total + self.depth[k - 1].astype(F32)
        return total

    def drain(self):
        count = self.sizes[0] * self.at.depths
        for k in range(1, self.sizes[1]):
            loop(count, lambda q, k=k: self.third_copy(0, k, q).wait_send())
        for k in range(1, self.sizes[0]):
            loop(self.at.depths, lambda d, k=k: self.second_copy(0, k, d).wait_send())
        for k in range(1, self.at.depths):
            self.depth_copy(0, k).wait_send()


def loop(size, body):
    lax.fori_loop(0, size, lambda i, c: (body(i), c)[1], 0)


STREAM_FIELDS = (
    "held", "pair", "third", "second", "depth",
    "pair_send", "pair_recv", "third_send", "third_recv", "second_send", "second_recv", "depth_send", "depth_recv",
)


def stream_scratch(rows, depths, sides, side_first, shape):
    second, third = (rows, sides) if side_first else (sides, rows)
    half = rows * depths * sides
    leads = ((half,), (half,), (third - 1, second * depths), (second - 1, depths), (depths - 1,))
    buffers = [pltpu.VMEM(lead + shape, BF16) for lead in leads]
    sems = [DMA((half,)), DMA((half,))] + [DMA(lead) for lead in leads[2:] for _ in range(2)]
    return buffers + sems


STREAMS = (("con", False), ("ex0", True), ("ex1", True), ("out", False), ("pr0", True), ("pr1", False))


def finish_kernel(mesh_shape, sizes, names, *refs):
    r = Refs(names, refs)
    rows, inner = mesh_shape["dp"], mesh_shape["fsdp"]
    depths = 4
    sides = inner // (2 * depths)
    total = rows * inner
    half = total // 2
    at = Place(rows, depths, sides)
    seq, width = r.dz.shape
    group = width // 2
    core = at.core
    me = at.row * inner + lax.axis_index("fsdp")
    piece = width // total
    vec = Vectors(r.vec, width)

    copies = {}

    def load(key, source, target, sem):
        copies[key] = pltpu.make_async_copy(source, target, sem)
        copies[key].start()

    def ready(key):
        copies.pop(key).wait()

    chunks = [(k, d) for k in list(range(1, rows)) + [0] for d in range(depths)]
    span = sides * 2 * piece * 4

    def load_active(i):
        k, d = chunks[i]
        first = ((at.row + k) % rows * depths + d) * span
        columns = pl.ds(pl.multiple_of(first, 128), span)
        load(("act", i), r.active.at[:, columns], r.act.at[i % 2], r.act_sem.at[i % 2])

    load_active(0)
    load("df0", r.df.at[:, : 2 * width], r.dfs.at[0], r.df_sem.at[0])
    load_active(1)
    load("df1", r.df.at[:, 2 * width :], r.dfs.at[1], r.df_sem.at[1])
    load("dh", r.dh, r.dhv, r.dh_sem)

    def load_pair(p):
        slot = p % 2
        for i in range(3):
            columns = pl.ds(i * width + p * 128, 128)
            load(("pair", p, i), r.mixed.at[:, columns], r.qkv.at[slot, i], r.qkv_sem.at[slot, i])
        load(("pair", p, 3), r.dctx.at[:, pl.ds(p * 128, 128)], r.qkv.at[slot, 3], r.qkv_sem.at[slot, 3])

    barrier = pltpu.get_barrier_semaphore()

    def other(k):
        index = (me + k) % total
        return {"dp": index // inner, "fsdp": index % inner}

    loop(total - 1, lambda i: pl.semaphore_signal(barrier, inc=1, device_id=other(i + 1), **MESH))
    pl.semaphore_wait(barrier, total - 1)

    streams = {name: Stream(at, side_first, name, r) for name, side_first in STREAMS}
    con = streams["con"]
    ones = jnp.ones((16, seq), BF16)
    sums = {}

    def chunk(i):
        ready(("act", i))
        slot = i % 3
        if i >= 3:
            con_sent(i - 3)
        grad = dot_tn(r.act[i % 2], r.dz[...])
        if i + 2 < len(chunks):
            load_active(i + 2)
        r.con_stage[slot] = grad.reshape(sides, 2, 4 * piece, width).astype(BF16)
        for side in range(sides):
            con.pair_copy(con_unit(i, side), r.con_stage.at[slot, side, 1 - core]).start()

    def con_unit(i, side):
        k, d = chunks[i]
        return ((at.row + k) % rows * depths + d) * sides + side

    def con_sent(i):
        for side in range(sides):
            con.pair_copy(con_unit(i, side), r.con_stage.at[i % 3, side, 1 - core]).wait_send()

    def con_third(i):
        k, d = chunks[i]
        for side in range(sides):
            con.third_step(k, side * depths + d, lambda u: r.con_stage.at[i % 3, side, core])

    slots = {}

    def square(name, left, right):
        columns = right.shape[1]
        slot = len(slots) % 2
        previous = [n for n, s in slots.items() if s == slot]
        if previous:
            stage_sent(previous[-1])
        slots[name] = slot
        quarter = width // 4
        for part in range(4):
            grad = dot_tn(left[:, part * quarter : (part + 1) * quarter], right[...])
            target = r.stage.at[slot, part * half // 4 : (part + 1) * half // 4, :, :, :columns]
            target[...] = grad.reshape(half // 4, 2, piece, columns).astype(BF16)
        stream = streams[name]
        for k in list(range(1, stream.sizes[1])) + [0]:

            def start(q):
                u = stream.unit(q // depths, (other_third + k) % stream.sizes[1], q % depths)
                stream.pair_copy(u, stage_at(name, u, 1 - core, columns)).start()

            other_third = stream.mine[1]
            loop(stream.sizes[0] * depths, start)

    def stage_at(name, u, which, columns):
        return r.stage.at[slots[name], u, which, :, :columns]

    def columns_of(name):
        return streams[name].held.shape[-1]

    def stage_sent(name):
        stream = streams[name]
        loop(half, lambda u: stream.pair_copy(u, stage_at(name, u, 1 - core, columns_of(name))).wait_send())

    def square_third(name, far):
        stream = streams[name]
        for k in range(1, stream.sizes[1]) if far else [0]:
            loop(
                stream.sizes[0] * depths,
                lambda q, k=k: stream.third_step(k, q, lambda u: stage_at(name, u, core, columns_of(name))),
            )

    def expand(e):
        ready("df%d" % e)
        square("ex%d" % e, r.normed, r.dfs.at[e])
        sums["be%d" % e] = dot(ones, r.dfs[e])[0:1]

    def output():
        ready("dh")
        r.dy[...] = r.dhv[...].astype(BF16)
        square("out", r.context, r.dy)
        sums["bo"] = dot(ones, r.dy[...])[0:1]
        sums["bc"] = dot(ones, r.dz[...])[0:1]

    hidden_keys = iota((TILE, TILE), 0) > iota((TILE, TILE), 1)
    first_head = iota((TILE, 128), 1) < 64

    def pair_target(p):
        return r.dfs.at[p // 3], p % 3 * 128

    def attend_block(p, block):
        slot, last = p % 2, seq // TILE - 1
        if block == last:
            for i in range(4):
                ready(("pair", p, i))
            if p + 1 < HEADS // 2:
                load_pair(p + 1)
            r.keys_t[...] = r.qkv[slot, 1].T
        query_ref, key_ref, value_ref, up_ref = (r.qkv.at[slot, i] for i in range(4))
        start, stop = block * TILE, block * TILE + TILE
        query = query_ref[start:stop].astype(F32) * 0.125
        upstream = up_ref[start:stop].astype(F32)
        outs = []
        for head in range(2):
            own = first_head if head == 0 else jnp.logical_not(first_head)
            masked = jnp.where(own, query, 0.0).astype(BF16)
            up_masked = jnp.where(own, upstream, 0.0).astype(BF16)
            score = dot_nt(key_ref[:stop], masked)
            edge = jnp.where(hidden_keys, NEG_FILL, score[start:])
            score = jnp.concatenate([score[:start], edge], 0) if start else edge
            prob = jnp.exp(score - r.logs[p, head : head + 1, start:stop])
            prob_grad = dot_nt(value_ref[:stop], up_masked)
            mean = jnp.sum(prob * prob_grad, axis=0, keepdims=True)
            score_grad = (prob * (prob_grad - mean)).astype(BF16)
            dv = dot(prob.astype(BF16), up_masked)
            dk = dot(score_grad, masked)
            if block == last and head == 0:
                r.dv_sum[...] = dv
                r.dk_sum[...] = dk
            else:
                r.dv_sum[:stop] += dv
                r.dk_sum[:stop] += dk
            outs.append(dot(r.keys_t[:, :stop], score_grad)[head * 64 : (head + 1) * 64])
        target, column = pair_target(p)
        target[start:stop, column : column + 128] = (jnp.concatenate(outs, 0).T * 0.125).astype(BF16)
        if block == 0:
            target[:, group + column : group + column + 128] = r.dk_sum[...].astype(BF16)
            target[:, 2 * group + column : 2 * group + column + 128] = r.dv_sum[...].astype(BF16)

    def project(g):
        right = r.dfs.at[g, :, : 3 * group]
        square("pr%d" % g, r.first_normed, right)
        sums["bp%d" % g] = dot(ones, right[...])[0:1]

    def load_tile(i):
        load(("x", i), r.x.at[pl.ds(i * TILE, TILE)], r.xs.at[i % 2], r.x_sem.at[i % 2])

    def tile(i):
        ready(("x", i))
        part = slice(i * TILE, i * TILE + TILE)
        da = jnp.zeros((TILE, width), F32)
        for g in range(2):
            for n in range(3):
                columns = slice(n * width + g * group, n * width + (g + 1) * group)
                da = da + dot_nt(r.dfs[g, part, n * group : (n + 1) * group], r.wpv[:, columns])
        hat, inv = norm_parts(r.xs[i % 2])
        if i + 2 < seq // TILE:
            load_tile(i + 2)
        position = i * TILE + iota((TILE, 1), 0)
        kept = (position < r.start[0]) | (position >= r.start[0] + THOUGHTS)
        if i >= 2:
            ready(("dx", i - 2))
        r.dxs[i % 2] = jnp.where(kept, r.dhv[part] + norm_back(da, hat, inv, vec.g1), 0.0)
        load(("dx", i), r.dxs.at[i % 2], r.hidden_grad.at[pl.ds(i * TILE, TILE)], r.dx_sem.at[i % 2])
        gain, bias = jnp.sum(da * hat, axis=0, keepdims=True), jnp.sum(da, axis=0, keepdims=True)
        sums["g1"] = gain if i == 0 else sums["g1"] + gain
        sums["b1"] = bias if i == 0 else sums["b1"] + bias

    def small_start():
        group_of = lambda n: jnp.concatenate([sums["bp%d" % g][:, n * group : (n + 1) * group] for g in range(2)], 1)
        lines = dict(
            g1=sums["g1"], b1=sums["b1"], bp=jnp.concatenate([group_of(0), group_of(2)], 1), bo=sums["bo"],
            g2=r.sums[0:1], b2=r.sums[1:2], be=jnp.concatenate([sums["be0"], sums["be1"]], 1), bc=sums["bc"],
        )
        offset = 0
        r.small_part[...] = jnp.zeros_like(r.small_part)
        for name, size in zip(VECTORS, sizes):
            low, high = offset // 128 * 128, -(-(offset + size) // 128) * 128
            length = total * size
            lane = iota((1, length), 1)
            pick = (iota((high - low, length), 0) == lane % size + (offset - low)).astype(F32).astype(BF16)
            rest = jnp.where(iota((total, length), 0) == lane // size, lines[name], 0.0)
            pieces = jnp.zeros((total, high - low), F32)
            for _ in range(3):
                rounded = rest.astype(BF16)
                pieces = pieces + dot_nt(rounded, pick)
                rest = rest - rounded.astype(F32)
            r.small_part[:, 0, low:high] += pieces
            offset += size
        loop(total - 1, lambda i: small_copy(i + 1).start())

    def small_copy(k):
        return pltpu.make_async_remote_copy(
            src_ref=r.small_part.at[(me + k) % total],
            dst_ref=r.small_in.at[k - 1],
            send_sem=r.small_send.at[k - 1],
            recv_sem=r.small_recv.at[k - 1],
            device_id=other(k),
            **MESH,
        )

    def small_end():
        loop(total - 1, lambda i: small_copy(i + 1).wait_recv())
        received = r.small_in[...]
        r.small_out[...] = r.small_part[me] + jnp.sum(received[: total - 1], axis=0)

    ex0, ex1, out, pr0, pr1 = (streams[n] for n in ("ex0", "ex1", "out", "pr0", "pr1"))
    far = (rows - 1) * depths
    load_pair(0)
    for i in range(far):
        chunk(i)
        if i:
            con_third(i - 1)
    expand(0)
    con_third(far - 1)
    chunk(far)
    square_third("ex0", True)
    for i in range(far + 1, far + depths):
        chunk(i)
        con_third(i - 1)
    expand(1)
    con_third(far + depths - 1)
    square_third("ex0", False)
    con.second_step(0)
    output()
    square_third("ex1", True)
    load("wp", r.wp, r.wpv, r.wp_sem)

    steps = [
        [lambda: square_third("ex1", False)],
        [lambda: square_third("out", True), lambda: con.second_step(1)],
        [lambda: square_third("out", False), lambda: ex0.second_step(0)],
        [lambda: ex0.second_step(1)],
        [lambda: con.second_step(2), lambda: ex0.second_step(2)],
        [lambda: ex0.second_step(3)],
        [lambda: ex1.second_step(0)],
        [lambda: con.second_step(3)],
        [lambda: ex1.second_step(1)],
        [lambda: con.depth_step(1), lambda: con.depth_step(2)],
        [lambda: ex0.depth_step(1), lambda: ex0.depth_step(2), lambda: ex1.second_step(2)],
        [lambda: ex0.depth_step(3), lambda: ex0.depth_step(0)],
        [lambda: square_third("pr0", True), lambda: con.depth_step(3), lambda: con.depth_step(0)],
        [lambda: ex1.second_step(3)],
        [lambda: square_third("pr0", False), lambda: out.second_step(0), lambda: out.second_step(1)],
        [lambda: out.second_step(2), lambda: out.second_step(3)],
        [lambda: ex1.depth_step(1), lambda: ex1.depth_step(2)],
        [lambda: ex1.depth_step(3), lambda: ex1.depth_step(0)],
        [lambda: out.depth_step(1), lambda: out.depth_step(2)],
        [lambda: out.depth_step(3), lambda: out.depth_step(0)],
        [lambda: pr0.second_step(0)],
        [lambda: pr0.second_step(1)],
        [lambda: pr0.second_step(2)],
        [lambda: pr0.second_step(3)],
    ]
    blocks = seq // TILE
    for p in range(HEADS // 2):
        for n, block in enumerate(reversed(range(blocks))):
            attend_block(p, block)
            for step in steps[p * blocks + n]:
                step()
        if p == 2:
            project(0)
    load_tile(0)
    load_tile(1)
    project(1)
    for k in (1, 2, 3, 0):
        pr0.depth_step(k)
    square_third("pr1", True)
    ready("wp")
    tile(0)
    square_third("pr1", False)
    r.contract_out[...] = con.total()
    tile(1)
    for depth in range(depths):
        pr1.second_step(depth)
    r.expand_out[:, : 2 * width] = ex0.total()
    tile(2)
    for k in (1, 2, 3, 0):
        pr1.depth_step(k)
    r.expand_out[:, 2 * width :] = ex1.total()
    r.output_out[...] = out.total()
    tile(3)
    small_start()
    for g, stream in enumerate((pr0, pr1)):
        grad = stream.total()
        for n in range(3):
            columns = slice(n * width + g * group, n * width + (g + 1) * group)
            r.project_out[:, columns] = grad[:, n * group : (n + 1) * group]
    small_end()
    ready(("dx", 2))
    ready(("dx", 3))
    for i in range(len(chunks) - 3, len(chunks)):
        con_sent(i)
    for name in list(slots)[-2:]:
        stage_sent(name)
    for stream in streams.values():
        stream.drain()
    loop(total - 1, lambda i: small_copy(i + 1).wait_send())


def finish(mesh_shape, sizes, start, operands):
    rows, inner = mesh_shape["dp"], mesh_shape["fsdp"]
    depths = 4
    sides = inner // (2 * depths)
    total = rows * inner
    half = total // 2
    seq, width = operands["dz"].shape
    piece = width // total
    lanes = -(-sum(sizes) // 128) * 128
    in_vmem = ("dz", "normed", "context", "first_normed", "logs", "vec", "sums")
    outs = dict(
        hidden_grad=(seq, width),
        contract_out=(4 * piece, width),
        expand_out=(piece, 4 * width),
        output_out=(piece, width),
        project_out=(piece, 3 * width),
        small_out=(1, lanes),
    )
    shapes = dict(
        con=(4 * piece, width), ex0=(piece, 2 * width), ex1=(piece, 2 * width), out=(piece, width),
        pr0=(piece, 3 * width // 2), pr1=(piece, 3 * width // 2),
    )
    span = sides * 2 * piece * 4
    scratch = dict(
        act=pltpu.VMEM((2, seq, span), BF16), act_sem=DMA((2,)),
        dfs=pltpu.VMEM((2, seq, 2 * width), BF16), df_sem=DMA((2,)),
        dhv=pltpu.VMEM((seq, width), F32), dh_sem=DMA(()),
        dy=pltpu.VMEM((seq, width), BF16),
        qkv=pltpu.VMEM((2, 4, seq, 128), BF16), qkv_sem=DMA((2, 4)),
        keys_t=pltpu.VMEM((128, seq), BF16),
        dk_sum=pltpu.VMEM((seq, 128), F32), dv_sum=pltpu.VMEM((seq, 128), F32),
        wpv=pltpu.VMEM((width, 3 * width), BF16), wp_sem=DMA(()),
        xs=pltpu.VMEM((2, TILE, width), F32), x_sem=DMA((2,)),
        dxs=pltpu.VMEM((2, TILE, width), F32), dx_sem=DMA((2,)),
        con_stage=pltpu.VMEM((3, sides, 2, 4 * piece, width), BF16),
        stage=pltpu.VMEM((2, half, 2, piece, 2 * width), BF16),
        small_part=pltpu.VMEM((total, 1, lanes), F32), small_in=pltpu.VMEM((total, 1, lanes), F32),
        small_send=DMA((total - 1,)), small_recv=DMA((total - 1,)),
    )
    for name, side_first in STREAMS:
        fields = stream_scratch(rows, depths, sides, side_first, shapes[name])
        scratch.update({name + "_" + f: s for f, s in zip(STREAM_FIELDS, fields)})
    names = ("start",) + tuple(operands) + tuple(outs) + tuple(scratch)
    whole_vmem = pl.BlockSpec(memory_space=pltpu.VMEM)
    return pl.pallas_call(
        functools.partial(finish_kernel, mesh_shape, sizes, names),
        out_shape=[jax.ShapeDtypeStruct(s, F32) for s in outs.values()],
        in_specs=[smem()] + [whole_vmem if n in in_vmem else in_hbm() for n in operands],
        out_specs=[in_hbm()] + [whole_vmem] * 5,
        scratch_shapes=list(scratch.values()),
        compiler_params=pltpu.CompilerParams(collective_id=2, has_side_effects=True, vmem_limit_bytes=63 * 2**20),
        name="finish",
    )(start, *operands.values())


def pack(vectors, total):
    joined = jnp.concatenate([v.reshape(total, -1) for v in vectors], 1)
    fill = -joined.shape[1] % 128
    return jnp.pad(joined, ((0, 0), (0, fill)))[:, None]


def unpack(packed, sizes):
    flat = packed.reshape(-1, packed.shape[-1])
    out, at = [], 0
    for size in sizes:
        out.append(flat[:, at : at + size].reshape(-1))
        at += size
    return out


def per_device(
    mesh_shape,
    hidden,
    cotangent,
    lengths,
    thought_start,
    first_gain,
    first_bias,
    project_weight,
    project_bias,
    output_weight,
    output_bias,
    second_gain,
    second_bias,
    expand_weight,
    expand_bias,
    contract_weight,
    contract_bias,
):
    _, seq, width = hidden.shape
    total = mesh_shape["dp"] * mesh_shape["fsdp"]
    vectors = (
        first_gain,
        first_bias,
        project_bias,
        output_bias,
        second_gain,
        second_bias,
        expand_bias,
        contract_bias,
    )
    sizes = [v.shape[0] for v in vectors]
    full = gather_all(
        mesh_shape,
        (pack(vectors, 1)[0], project_weight, output_weight, expand_weight, contract_weight),
    )
    Wp, Wo, We, Wc = (w.reshape(-1, w.shape[-1]) for w in full[1:])

    x, mixed, normed, vec = think(thought_start, hidden[0], full[0], sizes, (Wp, Wo, We, Wc))
    context, log_total = attend(mixed)
    final, resid, normed_two, active, dz, df, dh, dctx, sums = feed(
        lengths, context, x, cotangent[0], (Wo, We, Wc), vec
    )
    dh, dctx, dz, df, sums = reflect(
        thought_start, x, mixed, resid, context, log_total, vec, (Wp, Wc, We, Wo), dh, dctx, dz, df, sums
    )
    if width // total % 8 == 0:
        operands = dict(
            dz=dz, normed=normed_two, context=context, first_normed=normed, logs=log_total, vec=vec, sums=sums,
            active=active, df=df, dh=dh, mixed=mixed, dctx=dctx, x=x, wp=Wp,
        )
        hidden_grad, dWc, dWe, dWo, dWp, small = finish(mesh_shape, sizes, thought_start, operands)
        dg1, db1, dbp, dbo, dg2, db2, dbe, dbc = unpack(small, sizes)
        return (final[None], hidden_grad[None], dg1, db1, dWp, dbp, dWo, dbo, dg2, db2, dWe, dbe, dWc, dbc)
    dq, dk, dv = attend_back(mixed, dctx, log_total)
    g1 = vec[0:1, :width]
    dy = dh.astype(BF16)
    x_hat, x_inv = norm_parts(x)
    dmixed = jnp.concatenate([dq, dk, dv], 1)
    da = dot_nt(dmixed, Wp)
    dx = dh + norm_back(da, x_hat, x_inv, g1)
    position = iota((seq, 1), 0)
    is_thought = (position >= thought_start[0]) & (position < thought_start[0] + THOUGHTS)
    hidden_grad = jnp.where(is_thought, 0.0, dx)

    def column_sum(value):
        return jnp.sum(value, axis=0, dtype=F32)

    column = column_sum(dmixed)
    small = (
        column_sum(da * x_hat),
        column_sum(da),
        jnp.concatenate([column[:width], column[2 * width :]]),
        column_sum(dy),
        sums[0],
        sums[1],
        column_sum(df),
        column_sum(dz),
    )
    large = (
        dot_tn(normed, dmixed),
        dot_tn(context, dy),
        dot_tn(normed_two, df),
        dot_tn(active, dz),
    )
    parts = [pack(small, total)]
    for grad in large:
        parts.append(grad.astype(BF16).reshape(total, grad.shape[0] // total, grad.shape[1]))
    small, dWp, dWo, dWe, dWc = scatter_all(mesh_shape, parts)
    dg1, db1, dbp, dbo, dg2, db2, dbe, dbc = unpack(small, sizes)
    return (final[None], hidden_grad[None], dg1, db1, dWp, dbp, dWo, dbo, dg2, db2, dWe, dbe, dWc, dbc)


def solution(mesh):
    rows = P(AXES, None, None)
    flat = P(AXES)
    square = P(AXES, None)
    specs = (flat, flat, square, flat, square, flat, flat, flat, square, flat, square, flat)
    return jax.shard_map(
        functools.partial(per_device, dict(mesh.shape)),
        mesh=mesh,
        in_specs=(rows, rows, flat, flat) + specs,
        out_specs=(rows, rows) + specs,
        check_vma=False,
    )
```

```python
import functools

import jax
import jax.numpy as jnp
from jax import lax
from jax.experimental import pallas as pl
from jax.experimental.pallas import tpu as pltpu
from jax.sharding import PartitionSpec as P

HEADS = 12
THOUGHTS = 3
PREFIX = 384
TILE = 256

EPSILON = 1e-05
NEG_FILL = -1e30
F32 = jnp.float32
BF16 = jnp.bfloat16
VMEM_LIMIT = 62 * 2**20


AXES = ("dp", "fsdp")
ANY = pl.BlockSpec(memory_space=pl.ANY)
DMA = pltpu.SemaphoreType.DMA


class Place:
    def __init__(self, rows, depths, sides):
        self.rows, self.depths, self.sides = rows, depths, sides
        self.row = lax.axis_index("dp")
        flat = lax.axis_index("fsdp")
        self.depth = flat // (sides * 2)
        self.side = flat // 2 % sides
        self.core = flat % 2

    def index(self, row, depth, side, core):
        return row * (self.depths * self.sides * 2) + (depth * self.sides + side) * 2 + core

    def device(self, row, depth, side, core):
        return {"dp": row, "fsdp": (depth * self.sides + side) * 2 + core}


def gather_kernel(rows, depths, sides, count, *refs):
    shards, fulls = refs[:count], refs[count : 2 * count]
    send_sem, recv_sem, pair_send, pair_recv, own_sem = refs[2 * count :]
    at = Place(rows, depths, sides)
    dev = dict(device_id_type=pl.DeviceIdType.MESH)

    barrier = pltpu.get_barrier_semaphore()
    peers = []
    for k in range(1, depths):
        peers.append(at.device(at.row, (at.depth + k) % depths, at.side, at.core))
    for k in range(1, sides):
        peers.append(at.device(at.row, at.depth, (at.side + k) % sides, at.core))
    for k in range(1, rows):
        peers.append(at.device((at.row + k) % rows, at.depth, at.side, at.core))
    peers.append(at.device(at.row, at.depth, at.side, 1 - at.core))
    for peer in peers:
        pl.semaphore_signal(barrier, inc=1, device_id=peer, **dev)
    pl.semaphore_wait(barrier, len(peers))

    def run(core):
        sends = []

        def index(row, depth, side):
            return at.index(row, depth, side, core)

        def send(w, source, shard, peer, slot):
            copy = pltpu.make_async_remote_copy(
                src_ref=source,
                dst_ref=fulls[w].at[shard],
                send_sem=send_sem.at[w, slot],
                recv_sem=recv_sem.at[w, shard],
                device_id=peer,
                **dev,
            )
            copy.start()
            sends.append(copy)

        def arrive(w, shard):
            pltpu.make_async_remote_copy(
                src_ref=fulls[w].at[shard],
                dst_ref=fulls[w].at[shard],
                send_sem=send_sem.at[w, 0],
                recv_sem=recv_sem.at[w, shard],
                device_id=peers[0],
                **dev,
            ).wait_recv()

        def to_pair(w, source, shard):
            copy = pltpu.make_async_remote_copy(
                src_ref=source,
                dst_ref=fulls[w].at[shard],
                send_sem=pair_send.at[w, shard // 2],
                recv_sem=pair_recv.at[w, shard // 2],
                device_id=at.device(at.row, at.depth, at.side, 1 - core),
                **dev,
            )
            copy.start()
            sends.append(copy)

        slots = [0] * count

        def slot(w):
            slots[w] += 1
            return slots[w] - 1

        second_size, third_size = (sides, rows) if core == 0 else (rows, sides)

        def spot(second, third):
            return (third, second) if core == 0 else (second, third)

        mine = (at.side, at.row) if core == 0 else (at.row, at.side)

        def forward_second(w, source, depth):
            row, side = spot(*mine)
            for k in range(1, second_size):
                r, s = spot((mine[0] + k) % second_size, mine[1])
                send(w, source, index(row, depth, side), at.device(r, at.depth, s, core), slot(w))

        def forward_third(w, source, depth, second):
            row, side = spot(second, mine[1])
            for k in range(1, third_size):
                r, s = spot(mine[0], (mine[1] + k) % third_size)
                send(w, source, index(row, depth, side), at.device(r, at.depth, s, core), slot(w))

        own = []
        for w in range(count):
            me = index(at.row, at.depth, at.side)
            for k in range(1, depths):
                send(w, shards[w], me, at.device(at.row, (at.depth + k) % depths, at.side, core), slot(w))
            forward_second(w, shards[w], at.depth)
            forward_third(w, shards[w], at.depth, mine[0])
            to_pair(w, shards[w], me)
            copy = pltpu.make_async_copy(shards[w], fulls[w].at[me], own_sem.at[w])
            copy.start()
            own.append(copy)

        def stage_one(w):
            for k in range(1, depths):
                depth = (at.depth - k) % depths
                shard = index(at.row, depth, at.side)
                arrive(w, shard)
                forward_second(w, fulls[w].at[shard], depth)
                forward_third(w, fulls[w].at[shard], depth, mine[0])
                to_pair(w, fulls[w].at[shard], shard)

        def stage_two(w):
            for k in range(1, second_size):
                second = (mine[0] - k) % second_size
                for d in range(depths):
                    depth = (at.depth - d) % depths
                    shard = index(spot(second, mine[1])[0], depth, spot(second, mine[1])[1])
                    arrive(w, shard)
                    forward_third(w, fulls[w].at[shard], depth, second)
                    to_pair(w, fulls[w].at[shard], shard)

        def stage_three(w):
            for k in range(1, third_size):
                third = (mine[1] - k) % third_size
                for s in range(second_size):
                    second = (mine[0] - s) % second_size
                    for d in range(depths):
                        depth = (at.depth - d) % depths
                        row, side = spot(second, third)
                        shard = index(row, depth, side)
                        arrive(w, shard)
                        to_pair(w, fulls[w].at[shard], shard)

        for step in range(count + 2):
            if step < count:
                stage_one(step)
            if 0 <= step - 1 < count:
                stage_two(step - 1)
            if 0 <= step - 2 < count:
                stage_three(step - 2)

        for w in range(count):
            for row in range(rows):
                for depth in range(depths):
                    for side in range(sides):
                        shard = at.index(row, depth, side, 1 - core)
                        pltpu.make_async_remote_copy(
                            src_ref=fulls[w].at[shard],
                            dst_ref=fulls[w].at[shard],
                            send_sem=pair_send.at[w, shard // 2],
                            recv_sem=pair_recv.at[w, shard // 2],
                            device_id=peers[0],
                            **dev,
                        ).wait_recv()
        for copy in own:
            copy.wait()
        for copy in sends:
            copy.wait_send()

    for core in range(2):

        @pl.when(at.core == core)
        def _():
            run(core)


def gather_all(mesh_shape, shards, collective_id=0):
    rows, inner = mesh_shape["dp"], mesh_shape["fsdp"]
    depths = 4
    sides = inner // (2 * depths)
    total = rows * inner
    count = len(shards)
    sent = (depths - 1) + depths * (max(rows, sides) - 1) + depths * sides * (rows - 1) + depths * rows * (sides - 1)
    return pl.pallas_call(
        functools.partial(gather_kernel, rows, depths, sides, count),
        out_shape=[jax.ShapeDtypeStruct((total,) + s.shape, s.dtype) for s in shards],
        in_specs=[ANY] * count,
        out_specs=[ANY] * count,
        scratch_shapes=[
            DMA((count, sent)),
            DMA((count, total)),
            DMA((count, total // 2)),
            DMA((count, total // 2)),
            DMA((count,)),
        ],
        compiler_params=pltpu.CompilerParams(collective_id=collective_id, has_side_effects=True),
        name="gather_weights",
    )(*shards)


def scatter_kernel(rows, depths, sides, count, *refs):
    parts, outs = refs[:count], refs[count : 2 * count]
    scratch = refs[2 * count :]
    held, pair, third_in, second_in, depth_in = (scratch[i * count : (i + 1) * count] for i in range(5))
    (own_sem, pair_send, pair_recv, third_send, third_recv, second_send, second_recv, depth_send, depth_recv) = scratch[
        5 * count :
    ]
    at = Place(rows, depths, sides)
    dev = dict(device_id_type=pl.DeviceIdType.MESH)

    barrier = pltpu.get_barrier_semaphore()
    peers = []
    for k in range(1, depths):
        peers.append(at.device(at.row, (at.depth + k) % depths, at.side, at.core))
    for k in range(1, sides):
        peers.append(at.device(at.row, at.depth, (at.side + k) % sides, at.core))
    for k in range(1, rows):
        peers.append(at.device((at.row + k) % rows, at.depth, at.side, at.core))
    peers.append(at.device(at.row, at.depth, at.side, 1 - at.core))
    for peer in peers:
        pl.semaphore_signal(barrier, inc=1, device_id=peer, **dev)
    pl.semaphore_wait(barrier, len(peers))

    def run(core):
        second_size, third_size = (sides, rows) if core == 0 else (rows, sides)
        my_second, my_third = (at.side, at.row) if core == 0 else (at.row, at.side)

        def unit(second, third, depth):
            row, side = (third, second) if core == 0 else (second, third)
            return (row * depths + depth) * sides + side

        def device(second, third, depth):
            row, side = (third, second) if core == 0 else (second, third)
            return at.device(row, depth, side, core)

        def remote(source, target, send, recv, peer):
            return pltpu.make_async_remote_copy(
                src_ref=source, dst_ref=target, send_sem=send, recv_sem=recv, device_id=peer, **dev
            )

        sibling = at.device(at.row, at.depth, at.side, 1 - core)

        def pair_copy(w, u):
            return remote(
                parts[w].at[u, 1 - core], pair[w].at[u], pair_send.at[w], pair_recv.at[w, u], sibling
            )

        def own_copy(w):
            return pltpu.make_async_copy(parts[w].at[:, core], held[w], own_sem.at[w])

        def third_copy(w, u, k, q, peer):
            return remote(
                held[w].at[u],
                third_in[w].at[k - 1, q],
                third_send.at[w, k - 1, q],
                third_recv.at[w, k - 1, q],
                peer,
            )

        def second_copy(w, u, k, q, peer):
            return remote(
                held[w].at[u],
                second_in[w].at[k - 1, q],
                second_send.at[w, k - 1, q],
                second_recv.at[w, k - 1, q],
                peer,
            )

        def depth_copy(w, u, k, peer):
            return remote(
                held[w].at[u], depth_in[w].at[k - 1], depth_send.at[w, k - 1], depth_recv.at[w, k - 1], peer
            )

        def loop(size, body):
            lax.fori_loop(0, size, lambda i, c: (body(i), c)[1], 0)

        def each_unit(visit):
            other_second, other_third = third_size, second_size
            far = my_second
            for k in list(range(1, other_third)) + [0]:
                def inner(q, k=k):
                    second, third = q // depths, (far + k) % other_third
                    row, side = (second, third) if core == 0 else (third, second)
                    visit((row * depths + q % depths) * sides + side)
                loop(other_second * depths, inner)

        for w in range(count):
            each_unit(lambda u, w=w: pair_copy(w, u).start())
            own_copy(w).start()

        def add_pair(w, u):
            pair_copy(w, u).wait_recv()
            held[w][u] = held[w][u] + pair[w][u]

        def stage_third(w):
            own_copy(w).wait()
            for k in list(range(1, third_size)) + [0]:
                third = (my_third + k) % third_size

                def inner(q, k=k, third=third):
                    second, depth = q // depths, q % depths
                    u = unit(second, third, depth)
                    add_pair(w, u)
                    if k:
                        third_copy(w, u, k, q, device(my_second, third, at.depth)).start()

                loop(second_size * depths, inner)

        def stage_second(w):
            for k in list(range(1, second_size)) + [0]:
                second = (my_second + k) % second_size

                def inner(depth, k=k, second=second):
                    u = unit(second, my_third, depth)
                    for j in range(1, third_size):
                        third_copy(w, u, j, second * depths + depth, sibling).wait_recv()
                        held[w][u] = held[w][u] + third_in[w][j - 1, second * depths + depth]
                    if k:
                        second_copy(w, u, k, depth, device(second, my_third, at.depth)).start()

                loop(depths, inner)

        def stage_depth(w):
            for k in list(range(1, depths)) + [0]:
                depth = (at.depth + k) % depths
                u = unit(my_second, my_third, depth)
                for j in range(1, second_size):
                    second_copy(w, u, j, depth, sibling).wait_recv()
                    held[w][u] = held[w][u] + second_in[w][j - 1, depth]
                if k:
                    depth_copy(w, u, k, device(my_second, my_third, depth)).start()

        def stage_last(w):
            u = unit(my_second, my_third, at.depth)
            total = held[w][u].astype(jnp.float32)
            for k in range(1, depths):
                depth_copy(w, u, k, sibling).wait_recv()
                total = total + depth_in[w][k - 1].astype(jnp.float32)
            outs[w][...] = total

        for step in range(count + 3):
            for lag, stage in enumerate((stage_third, stage_second, stage_depth, stage_last)):
                if 0 <= step - lag < count:
                    stage(step - lag)

        for w in range(count):
            remote(pair[w], pair[w], pair_send.at[w], pair_recv.at[w, 0], sibling).wait_send()
            for k in range(1, third_size):
                loop(second_size * depths, lambda q, w=w, k=k: third_copy(w, 0, k, q, sibling).wait_send())
            for k in range(1, second_size):
                loop(depths, lambda q, w=w, k=k: second_copy(w, 0, k, q, sibling).wait_send())
            for k in range(1, depths):
                depth_copy(w, 0, k, sibling).wait_send()

    for core in range(2):

        @pl.when(at.core == core)
        def _():
            run(core)


def scatter_all(mesh_shape, parts, collective_id=1):
    rows, inner = mesh_shape["dp"], mesh_shape["fsdp"]
    depths = 4
    sides = inner // (2 * depths)
    total = rows * inner
    half = total // 2
    count = len(parts)
    if rows == sides:
        thirds, seconds = (rows - 1, sides * depths), (sides - 1, depths)
    else:
        wide = max(rows, sides)
        thirds, seconds = (wide - 1, wide * depths), (wide - 1, depths)
    scratch = []
    for lead in ((half,), (half,), thirds, seconds, (depths - 1,)):
        scratch += [pltpu.VMEM(lead + p.shape[1:], p.dtype) for p in parts]
    parts = [p.reshape((half, 2) + p.shape[1:]) for p in parts]
    sems = [
        (), (), (half,), thirds, thirds, seconds, seconds, (depths - 1,), (depths - 1,),
    ]
    return pl.pallas_call(
        functools.partial(scatter_kernel, rows, depths, sides, count),
        out_shape=[jax.ShapeDtypeStruct(p.shape[2:], jnp.float32) for p in parts],
        in_specs=[ANY] * count,
        out_specs=[pl.BlockSpec(memory_space=pltpu.VMEM)] * count,
        scratch_shapes=scratch + [DMA((count,) + s) for s in sems],
        compiler_params=pltpu.CompilerParams(
            collective_id=collective_id, has_side_effects=True, vmem_limit_bytes=60 * 2**20
        ),
        name="scatter_grads",
    )(*parts)


def dot(left, right):
    return jnp.dot(left, right, preferred_element_type=F32)


def dot_nt(left, right):
    return lax.dot_general(left, right, (((1,), (1,)), ((), ())), preferred_element_type=F32)


def dot_tn(left, right):
    return lax.dot_general(left, right, (((0,), (0,)), ((), ())), preferred_element_type=F32)


def norm_parts(value):
    center = value - jnp.mean(value, axis=-1, keepdims=True)
    inv = lax.rsqrt(jnp.mean(center * center, axis=-1, keepdims=True) + EPSILON)
    return center * inv, inv


def norm_back(grad, hat, inv, gain):
    scaled = grad * gain
    return inv * (
        scaled
        - jnp.mean(scaled, axis=-1, keepdims=True)
        - hat * jnp.mean(scaled * hat, axis=-1, keepdims=True)
    )


GELU_ROOT = 0.7978845608028654


def gelu_parts(value):
    square = value * value
    inner = jnp.tanh(GELU_ROOT * value * (1.0 + 0.044715 * square))
    half = 0.5 * (1.0 + inner)
    slope = half + 0.5 * value * (1.0 - inner * inner) * (GELU_ROOT + 3 * 0.044715 * GELU_ROOT * square)
    return value * half, slope


def iota(shape, axis):
    return lax.broadcasted_iota(jnp.int32, shape, axis)


def wide(row):
    return jnp.broadcast_to(row, (16, row.shape[1])).astype(BF16)


def head_mask(width):
    return iota((16, width), 1) // (width // HEADS) == iota((16, width), 0)


def spread(row, mask):
    return jnp.where(mask, jnp.broadcast_to(row.astype(F32), mask.shape), 0.0).astype(BF16)


def collect(rows, mask):
    return jnp.sum(jnp.where(mask, rows, 0.0), axis=0, keepdims=True)


def row_softmax(spread_query, keys, place):
    score = dot_nt(spread_query, keys) * 0.125
    score = jnp.where(iota(score.shape, 1) <= place, score, NEG_FILL)
    expo = jnp.exp(score - jnp.max(score, axis=-1, keepdims=True))
    return expo / jnp.sum(expo, axis=-1, keepdims=True)


def pick_rows(first, array):
    chosen = iota((16, array.shape[0]), 1) == first + iota((16, array.shape[0]), 0)
    return dot(chosen.astype(F32).astype(BF16), array)


VECTORS = ("g1", "b1", "bp", "bo", "g2", "b2", "be", "bc")


class Vectors:
    def __init__(self, ref, width):
        self.ref, self.width = ref, width
        self.sizes = dict(bp=3 * width, be=4 * width)

    def __getattr__(self, name):
        return self.ref[VECTORS.index(name) : VECTORS.index(name) + 1, : self.sizes.get(name, self.width)]


def spread_vectors(pieces, sizes, width, vec_ref):
    count, offset = pieces.shape[0], 0
    vec_ref[...] = jnp.zeros_like(vec_ref)
    for row, (name, size) in enumerate(zip(VECTORS, sizes)):
        low, high = offset // 128 * 128, -(-(offset + size) // 128) * 128
        length = count * size
        lane = iota((1, length), 1)
        pick = iota((high - low, length), 0) == lane % size + (offset - low)
        tiled = dot(pieces[:, low:high], pick.astype(F32).astype(BF16))
        line = jnp.sum(jnp.where(iota((count, length), 0) == lane // size, tiled, 0.0), axis=0, keepdims=True)
        if name == "bp":
            vec_ref[row : row + 1, :width] = line[:, :width]
            vec_ref[row : row + 1, 2 * width : 3 * width] = line[:, width:]
        else:
            vec_ref[row : row + 1, :length] = line
        offset += size


def fetch(sources, targets, sems):
    copies = [pltpu.make_async_copy(s, t, sems.at[i]) for i, (s, t) in enumerate(zip(sources, targets))]
    for copy in copies:
        copy.start()
    return copies


def aligned(place):
    return pl.multiple_of(place // 16 * 16, 16)


def think_kernel(
    sizes, start_ref, hidden_ref, pieces_ref, wp_hbm, wo_hbm, we_hbm, wc_hbm,
    x_ref, mixed_ref, normed_ref, vec_ref, wp_ref, wo_ref, we_ref, wc_ref, sems,
):
    seq, width = hidden_ref.shape
    copies = fetch((wp_hbm, wo_hbm, we_hbm, wc_hbm), (wp_ref, wo_ref, we_ref, wc_ref), sems)
    spread_vectors(pieces_ref[:, 0, :], sizes, width, vec_ref)
    vec = Vectors(vec_ref, width)
    start = start_ref[0]
    copies[0].wait()
    for at in range(0, seq, TILE):
        part = slice(at, at + TILE)
        x = hidden_ref[part].astype(F32)
        x_ref[part] = x
        normed = (norm_parts(x)[0] * vec.g1 + vec.b1).astype(BF16)
        normed_ref[part] = normed
        mixed_ref[part] = (dot(normed, wp_ref[...]) + vec.bp).astype(BF16)
    mask = head_mask(width)
    x_row = x_ref[pl.ds(start - 1, 1), :]
    query = pick_rows(start - 1, mixed_ref[:PREFIX, :width])[0:1]
    for copy in copies[1:]:
        copy.wait()
    for step in range(THOUGHTS):
        place = start - 1 + step
        prob = row_softmax(spread(query, mask), mixed_ref[:PREFIX, width : 2 * width], place)
        context = collect(dot(prob.astype(BF16), mixed_ref[:PREFIX, 2 * width :]), mask)
        resid = x_row + (dot(wide(context), wo_ref[...])[0:1] + vec.bo)
        normed = norm_parts(resid)[0] * vec.g2 + vec.b2
        pre = dot(wide(normed), we_ref[...])[0:1] + vec.be
        active = gelu_parts(pre)[0]
        x_row = resid + (dot(wide(active), wc_ref[...])[0:1] + vec.bc)
        normed = norm_parts(x_row)[0] * vec.g1 + vec.b1
        mixed_row = dot(wide(normed), wp_ref[...])[0:1] + vec.bp
        query = mixed_row[:, :width].astype(BF16)
        x_ref[pl.ds(place + 1, 1), :] = x_row
        window = pl.ds(aligned(place + 1), 16)
        here = aligned(place + 1) + iota((16, 1), 0) == place + 1
        for target, row in ((mixed_ref, mixed_row), (normed_ref, normed)):
            target[window, :] = jnp.where(here, row, target[window, :].astype(F32)).astype(BF16)


def smem():
    return pl.BlockSpec(memory_space=pltpu.SMEM)


def whole(array):
    return pl.BlockSpec(array.shape, lambda *_: (0,) * array.ndim, pipeline_mode=pl.Buffered(1))


def prefix_block(array):
    return pl.BlockSpec((PREFIX, array.shape[1]), lambda *_: (0, 0), pipeline_mode=pl.Buffered(1))


def params(semantics=("arbitrary",)):
    return pltpu.CompilerParams(dimension_semantics=semantics, vmem_limit_bytes=VMEM_LIMIT)


def in_hbm():
    return pl.BlockSpec(memory_space=pl.ANY)


def weight_scratch(weights):
    return [pltpu.VMEM(w.shape, w.dtype) for w in weights] + [DMA((len(weights),))]


def think(start, hidden, pieces, sizes, weights):
    seq, width = hidden.shape
    outs = [
        jax.ShapeDtypeStruct((seq, width), F32),
        jax.ShapeDtypeStruct((seq, 3 * width), BF16),
        jax.ShapeDtypeStruct((seq, width), BF16),
        jax.ShapeDtypeStruct((8, weights[2].shape[1]), F32),
    ]
    return pl.pallas_call(
        functools.partial(think_kernel, sizes),
        grid=(1,),
        out_shape=outs,
        in_specs=[smem(), whole(hidden), whole(pieces)] + [in_hbm() for _ in weights],
        out_specs=[whole(o) for o in outs],
        scratch_shapes=weight_scratch(weights),
        compiler_params=params(),
        name="think",
    )(start, hidden, pieces, *weights)


def attend_kernel(query_ref, key_ref, value_ref, context_ref, log_ref):
    seq, lanes = query_ref.shape
    half, block = lanes // 2, seq // 2
    first_head = iota((block, lanes), 1) < half
    later = iota((block, block), 0) > iota((block, block), 1)
    values_t = value_ref[...].T
    for start in range(0, seq, block):
        stop = start + block
        query = query_ref[start:stop].astype(F32) * 0.125
        scores = []
        for head in range(2):
            own = first_head if head == 0 else jnp.logical_not(first_head)
            score = dot_nt(key_ref[:stop], jnp.where(own, query, 0.0).astype(BF16))
            last = jnp.where(later, NEG_FILL, score[start:])
            scores.append(jnp.concatenate([score[:start], last], 0) if start else last)
        peaks = [jnp.max(score, axis=0, keepdims=True) for score in scores]
        expos = [jnp.exp(score - peak) for score, peak in zip(scores, peaks)]
        totals = [jnp.sum(expo, axis=0, keepdims=True) for expo in expos]
        outs = []
        for head in range(2):
            out = dot(values_t[:, :stop], expos[head].astype(BF16)) * (1.0 / totals[head])
            outs.append(out[head * half : (head + 1) * half])
            log_ref[head : head + 1, start:stop] = peaks[head] + jnp.log(totals[head])
        context_ref[start:stop] = jnp.concatenate(outs, 0).T.astype(BF16)


def pair_spec(seq, offset, lanes=128):
    return pl.BlockSpec((seq, lanes), lambda i: (0, offset + i))


def attend(mixed):
    seq, width = mixed.shape[0], mixed.shape[1] // 3
    pairs = HEADS // 2
    return pl.pallas_call(
        attend_kernel,
        grid=(pairs,),
        out_shape=[jax.ShapeDtypeStruct((seq, width), BF16), jax.ShapeDtypeStruct((pairs, 2, seq), F32)],
        in_specs=[pair_spec(seq, 0), pair_spec(seq, pairs), pair_spec(seq, 2 * pairs)],
        out_specs=[pair_spec(seq, 0), pl.BlockSpec((None, 2, seq), lambda i: (i, 0, 0))],
        compiler_params=params(),
        name="attend",
    )(mixed, mixed, mixed)


def attend_back_kernel(query_ref, key_ref, value_ref, up_ref, log_ref, dq_ref, dk_ref, dv_ref, dk_sum, dv_sum):
    seq, lanes = query_ref.shape
    half = lanes // 2
    first_head = iota((TILE, lanes), 1) < half
    keys_t = key_ref[...].T
    for start in reversed(range(0, seq, TILE)):
        stop = start + TILE
        query = query_ref[start:stop].astype(F32) * 0.125
        upstream = up_ref[start:stop].astype(F32)
        outs = []
        for head in range(2):
            own = first_head if head == 0 else jnp.logical_not(first_head)
            masked = jnp.where(own, query, 0.0).astype(BF16)
            up_masked = jnp.where(own, upstream, 0.0).astype(BF16)
            score = dot_nt(key_ref[:stop], masked)
            hidden = iota((TILE, TILE), 0) > iota((TILE, TILE), 1)
            last = jnp.where(hidden, NEG_FILL, score[start:])
            score = jnp.concatenate([score[:start], last], 0) if start else last
            prob = jnp.exp(score - log_ref[head : head + 1, start:stop])
            prob_grad = dot_nt(value_ref[:stop], up_masked)
            inner = jnp.sum(prob * prob_grad, axis=0, keepdims=True)
            score_grad = (prob * (prob_grad - inner)).astype(BF16)
            dv = dot(prob.astype(BF16), up_masked)
            dk = dot(score_grad, masked)
            if stop == seq and head == 0:
                dv_sum[...] = dv
                dk_sum[...] = dk
            else:
                dv_sum[:stop] += dv
                dk_sum[:stop] += dk
            outs.append(dot(keys_t[:, :stop], score_grad)[head * half : (head + 1) * half])
        dq_ref[start:stop] = (jnp.concatenate(outs, 0).T * 0.125).astype(BF16)
    dk_ref[...] = dk_sum[...].astype(BF16)
    dv_ref[...] = dv_sum[...].astype(BF16)


def attend_back(mixed, upstream, log_total):
    seq, width = upstream.shape
    pairs = HEADS // 2
    out = jax.ShapeDtypeStruct((seq, width), BF16)
    return pl.pallas_call(
        attend_back_kernel,
        grid=(pairs,),
        out_shape=[out, out, out],
        in_specs=[
            pair_spec(seq, 0),
            pair_spec(seq, pairs),
            pair_spec(seq, 2 * pairs),
            pair_spec(seq, 0),
            pl.BlockSpec((None, 2, seq), lambda i: (i, 0, 0)),
        ],
        out_specs=[pair_spec(seq, 0)] * 3,
        scratch_shapes=[pltpu.VMEM((seq, 128), F32), pltpu.VMEM((seq, 128), F32)],
        compiler_params=params(),
        name="attend_back",
    )(mixed, mixed, mixed, upstream, log_total)


def feed_kernel(
    length_ref, context_ref, x_ref, cot_ref, wo_ref, we_ref, wc_ref, vec_ref,
    final_ref, resid_ref, normed_ref, active_ref, dz_ref, df_ref, dh_ref, dctx_ref, sums_ref,
):
    rows, width = x_ref.shape
    inner = we_ref.shape[1]
    vec = Vectors(vec_ref, width)
    be = vec.be
    valid = pl.program_id(0) * rows + iota((rows, 1), 0) < length_ref[0]
    resid = x_ref[...] + (dot(context_ref[...], wo_ref[...]) + vec.bo)
    resid_ref[...] = resid
    hat, inv = norm_parts(resid)
    normed = (hat * vec.g2 + vec.b2).astype(BF16)
    normed_ref[...] = normed
    dout = jnp.where(valid, cot_ref[...].astype(F32), 0.0)
    dz = dout.astype(BF16)
    dz_ref[...] = dz
    total = jnp.zeros((rows, width), F32)
    dc = jnp.zeros((rows, width), F32)
    for at in range(0, inner, width):
        part = slice(at, at + width)
        value, slope = gelu_parts(dot(normed, we_ref[:, part]) + be[:, part])
        value = value.astype(BF16)
        active_ref[:, part] = value
        total = total + dot(value, wc_ref[part])
        df = (dot_nt(dz, wc_ref[part]) * slope).astype(BF16)
        df_ref[:, part] = df
        dc = dc + dot_nt(df, we_ref[:, part])
    final_ref[...] = jnp.where(valid, resid + (total + vec.bc), 0.0)
    dh = dout + norm_back(dc, hat, inv, vec.g2)
    dh_ref[...] = dh
    dctx_ref[...] = dot_nt(dh.astype(BF16), wo_ref[...]).astype(BF16)

    @pl.when(pl.program_id(0) == 0)
    def _():
        sums_ref[...] = jnp.zeros_like(sums_ref)

    sums_ref[0:1] += jnp.sum(dc * hat, axis=0, keepdims=True)
    sums_ref[1:2] += jnp.sum(dc, axis=0, keepdims=True)


def row_block(columns):
    return pl.BlockSpec((TILE, columns), lambda i: (i, 0))


def feed(length, context, x, cotangent, weights, vec):
    seq, width = x.shape
    inner = weights[1].shape[1]
    shape = lambda n, t: jax.ShapeDtypeStruct((seq, n), t)
    outs = [
        (width, F32), (width, F32), (width, BF16), (inner, BF16), (width, BF16), (inner, BF16), (width, F32), (width, BF16),
    ]
    fixed = weights + (vec,)
    return pl.pallas_call(
        feed_kernel,
        grid=(seq // TILE,),
        out_shape=[shape(*o) for o in outs] + [jax.ShapeDtypeStruct((8, width), F32)],
        in_specs=[smem()] + [row_block(width)] * 3 + [whole(a) for a in fixed],
        out_specs=[row_block(o[0]) for o in outs] + [pl.BlockSpec((8, width), lambda i: (0, 0))],
        compiler_params=params(),
        name="feed",
    )(length, context, x, cotangent, *fixed)


def tall(row):
    return jnp.concatenate([jnp.broadcast_to(row[i : i + 1], (16, row.shape[1])) for i in range(THOUGHTS)], 0)


def reflect_kernel(
    start_ref, x_ref, mixed_ref, resid_ref, context_ref, log_ref, vec_ref, wp_hbm, wc_hbm, we_hbm, wo_hbm,
    dh_in, dctx_in, dz_hbm, df_hbm, sums_in,
    dh_ref, dctx_ref, dz_out, df_out, sums_ref,
    wp_ref, wc_ref, we_ref, wo_ref, sems, dz_ref, df_ref, edge_sems,
):
    seq, width = context_ref.shape
    copies = fetch((wp_hbm, wc_hbm, we_hbm, wo_hbm), (wp_ref, wc_ref, we_ref, wo_ref), sems)
    start = start_ref[0]
    base = aligned(start - 1)
    edge = pl.ds(base, 32)
    loads = fetch((dz_hbm.at[edge], df_hbm.at[edge]), (dz_ref, df_ref), edge_sems)
    vec = Vectors(vec_ref, width)
    mask = head_mask(width)
    masks = jnp.concatenate([mask] * THOUGHTS, 0)
    dh_ref[...] = dh_in[...]
    dctx_ref[...] = dctx_in[...]
    sums_ref[...] = sums_in[...]
    queries, keys, values = (mixed_ref.at[:, i * width : (i + 1) * width] for i in range(3))
    first_keys, first_values = keys.at[:PREFIX], values.at[:PREFIX]

    def split(rows):
        picked = jnp.where(masks, rows, 0.0)
        return jnp.concatenate(
            [jnp.sum(picked[16 * i : 16 * i + 16], axis=0, keepdims=True) for i in range(THOUGHTS)], 0
        )

    def spread_all(rows):
        return jnp.where(masks, tall(rows), 0.0).astype(BF16)

    later = iota((16, seq), 1)
    logs = jnp.concatenate([log_ref[i] for i in range(HEADS // 2)] + [jnp.zeros((4, seq), F32)], 0)
    product = dctx_in[...].astype(F32) * context_ref[...].astype(F32)
    high = product.astype(BF16)
    ones = mask.astype(F32).astype(BF16)
    delta = dot_nt(ones, high) + dot_nt(ones, (product - high.astype(F32)).astype(BF16))
    key_rows = spread_all(pick_rows(start, first_keys[...]))
    value_rows = spread_all(pick_rows(start, first_values[...]))
    score = dot_nt(key_rows, queries[...])
    prob_grad = dot_nt(value_rows, dctx_in[...])
    probs, grads = [], []
    for i in range(THOUGHTS):
        part = slice(16 * i, 16 * i + 16)
        prob = jnp.where(later >= start + i, jnp.exp(0.125 * score[part] - logs), 0.0)
        probs.append(prob.astype(BF16))
        grads.append((prob * (prob_grad[part] - delta)).astype(BF16))
    main_dk = split(dot(jnp.concatenate(grads, 0), queries[...])) * 0.125
    main_dv = split(dot(jnp.concatenate(probs, 0), dctx_in[...]))

    def row_back(query, up, place):
        score = dot_nt(query, first_keys[...]) * 0.125
        score = jnp.where(iota(score.shape, 1) <= place, score, NEG_FILL)
        expo = jnp.exp(score - jnp.max(score, axis=-1, keepdims=True))
        prob = expo / jnp.sum(expo, axis=-1, keepdims=True)
        prob_grad = dot_nt(up, first_values[...])
        grad = (prob * (prob_grad - jnp.sum(prob * prob_grad, axis=-1, keepdims=True))).astype(BF16)
        return prob.astype(BF16), grad, dot(grad, first_keys[...]) * 0.125

    places = start + iota((16 * THOUGHTS, 1), 0) // 16
    up = spread_all(pick_rows(start, dctx_in[:PREFIX]))
    main_dq = split(row_back(spread_all(pick_rows(start, queries[:PREFIX])), up, places)[2])

    query_rows = pick_rows(start - 1, queries[:PREFIX])
    rows = [start - 1 + step for step in range(THOUGHTS)]
    resid = jnp.concatenate([resid_ref[pl.ds(p, 1), :] for p in rows] + [jnp.zeros((13, width), F32)], 0)
    resid_hat, resid_inv = norm_parts(resid)
    normed = (resid_hat * vec.g2 + vec.b2).astype(BF16)
    for copy in loads:
        copy.wait()
    copies[2].wait()
    slopes = gelu_parts(dot(normed, we_ref[...]) + vec.be)[1]
    for i in (0, 1, 3):
        copies[i].wait()
    scores, spreads, probs, ups = [], [], [], []
    dq_add = jnp.zeros((1, width), F32)
    for step in reversed(range(THOUGHTS)):
        place = rows[step]
        dq_row = main_dq[step : step + 1] + dq_add
        dk_row, dv_row = main_dk[step : step + 1], main_dv[step : step + 1]
        for score, query, prob, up in zip(scores, spreads, probs, ups):
            chosen = iota(score.shape, 1) == place + 1
            share = jnp.sum(jnp.where(chosen, score.astype(F32), 0.0), axis=1, keepdims=True)
            dk_row = dk_row + 0.125 * jnp.sum(share * query.astype(F32), axis=0, keepdims=True)
            share = jnp.sum(jnp.where(chosen, prob.astype(F32), 0.0), axis=1, keepdims=True)
            dv_row = dv_row + jnp.sum(share * up.astype(F32), axis=0, keepdims=True)
        x_hat, x_inv = norm_parts(x_ref[pl.ds(place + 1, 1), :])
        da = dot_nt(wide(jnp.concatenate([dq_row, dk_row, dv_row], 1)), wp_ref[...])
        dz = dh_ref[pl.ds(place + 1, 1), :] + norm_back(da[0:1], x_hat, x_inv, vec.g1)
        df = dot_nt(wide(dz), wc_ref[...])[0:1] * slopes[step : step + 1]
        dc = dot_nt(wide(df), we_ref[...])[0:1]
        hat, inv = resid_hat[step : step + 1], resid_inv[step : step + 1]
        dh = dz + norm_back(dc, hat, inv, vec.g2)
        sums_ref[0:1] += dc * hat
        sums_ref[1:2] += dc
        dctx = dot_nt(wide(dh), wo_ref[...])[0:1]
        query, up = spread(query_rows[step : step + 1], mask), spread(dctx, mask)
        prob, score, dq = row_back(query, up, place)
        dq_add = collect(dq, mask)
        scores.append(score)
        spreads.append(query)
        probs.append(prob)
        ups.append(up)
        dh_ref[pl.ds(place, 1), :] += dh
        here = base + iota((32, 1), 0) == place
        for target, row in ((dz_ref, dz), (df_ref, df)):
            target[...] = (target[...].astype(F32) + jnp.where(here, row, 0.0)).astype(BF16)
        dctx_ref[edge, :] = (dctx_ref[edge, :].astype(F32) + jnp.where(here, dctx, 0.0)).astype(BF16)
    for copy in fetch((dz_ref, df_ref), (dz_out.at[edge], df_out.at[edge]), edge_sems):
        copy.wait()


def reflect(start, x, mixed, resid, context, log_total, vec, weights, dh, dctx, dz, df, sums):
    changed = (dh, dctx, dz, df, sums)
    operands = (x, mixed, resid, context, log_total, vec) + weights + changed
    specs = [prefix_block(x), whole(mixed), prefix_block(resid), whole(context), whole(log_total), whole(vec)]
    specs += [in_hbm() for _ in weights]
    changed_specs = [prefix_block(dh), whole(dctx), in_hbm(), in_hbm(), whole(sums)]
    first = 1 + len(specs)
    return pl.pallas_call(
        reflect_kernel,
        grid=(1,),
        out_shape=[jax.ShapeDtypeStruct(a.shape, a.dtype) for a in changed],
        in_specs=[smem()] + specs + changed_specs,
        out_specs=changed_specs,
        input_output_aliases={first + i: i for i in range(len(changed))},
        scratch_shapes=weight_scratch(weights)
        + [pltpu.VMEM((32, dz.shape[1]), BF16), pltpu.VMEM((32, df.shape[1]), BF16), DMA((2,))],
        compiler_params=params(),
        name="reflect",
    )(start, *operands)


class Refs:
    def __init__(self, names, refs):
        self.__dict__.update(zip(names, refs))


MESH = dict(device_id_type=pl.DeviceIdType.MESH)


class Stream:
    def __init__(self, at, side_first, name, refs):
        self.at, self.side_first = at, side_first
        for field in STREAM_FIELDS:
            setattr(self, field, getattr(refs, name + "_" + field))
        self.sizes = (at.rows, at.sides) if side_first else (at.sides, at.rows)
        self.mine = (at.row, at.side) if side_first else (at.side, at.row)
        self.sent = []

    def spot(self, second, third):
        return (second, third) if self.side_first else (third, second)

    def unit(self, second, third, depth):
        row, side = self.spot(second, third)
        return (row * self.at.depths + depth) * self.at.sides + side

    def remote(self, source, target, send, recv, peer):
        return pltpu.make_async_remote_copy(
            src_ref=source, dst_ref=target, send_sem=send, recv_sem=recv, device_id=peer, **MESH
        )

    def sibling(self):
        return self.at.device(self.at.row, self.at.depth, self.at.side, 1 - self.at.core)

    def pair_copy(self, u, source):
        return self.remote(source, self.pair.at[u], self.pair_send.at[u], self.pair_recv.at[u], self.sibling())

    def third_copy(self, u, k, q):
        peer = self.at.device(*self.place(self.mine[0], (self.mine[1] + k) % self.sizes[1], self.at.depth))
        return self.remote(
            self.held.at[u], self.third.at[k - 1, q], self.third_send.at[k - 1, q], self.third_recv.at[k - 1, q], peer
        )

    def second_copy(self, u, k, depth):
        peer = self.at.device(*self.place((self.mine[0] + k) % self.sizes[0], self.mine[1], self.at.depth))
        return self.remote(
            self.held.at[u],
            self.second.at[k - 1, depth],
            self.second_send.at[k - 1, depth],
            self.second_recv.at[k - 1, depth],
            peer,
        )

    def depth_copy(self, u, k):
        peer = self.at.device(*self.place(*self.mine, (self.at.depth + k) % self.at.depths))
        return self.remote(
            self.held.at[u], self.depth.at[k - 1], self.depth_send.at[k - 1], self.depth_recv.at[k - 1], peer
        )

    def place(self, second, third, depth):
        row, side = self.spot(second, third)
        return row, depth, side, self.at.core

    def third_step(self, k, j, d, source):
        depths = self.at.depths
        second, depth = (self.mine[0] + j) % self.sizes[0], (self.at.depth + d) % depths
        q = second * depths + depth
        u = self.unit(second, (self.mine[1] + k) % self.sizes[1], depth)
        own = source(u)
        self.pair_copy(u, own).wait_recv()
        self.held[u] = own[...] + self.pair[u]
        if k:
            self.third_copy(u, k, q).start()

    def second_step(self, d):
        depth = (self.at.depth + d) % self.at.depths
        for k in list(range(1, self.sizes[0])) + [0]:
            second = (self.mine[0] + k) % self.sizes[0]
            u = self.unit(second, self.mine[1], depth)
            q = second * self.at.depths + depth
            for j in range(1, self.sizes[1]):
                self.third_copy(u, j, q).wait_recv()
                self.held[u] = self.held[u] + self.third[j - 1, q]
            if k:
                self.second_copy(u, k, depth).start()

    def depth_step(self, k):
        depth = (self.at.depth + k) % self.at.depths
        u = self.unit(*self.mine, depth)
        for j in range(1, self.sizes[0]):
            self.second_copy(u, j, depth).wait_recv()
            self.held[u] = self.held[u] + self.second[j - 1, depth]
        if k:
            self.depth_copy(u, k).start()

    def total(self):
        u = self.unit(*self.mine, self.at.depth)
        total = self.held[u].astype(F32)
        for k in range(1, self.at.depths):
            self.depth_copy(u, k).wait_recv()
            total = total + self.depth[k - 1].astype(F32)
        return total

    def drain(self):
        count = self.sizes[0] * self.at.depths
        for k in range(1, self.sizes[1]):
            loop(count, lambda q, k=k: self.third_copy(0, k, q).wait_send())
        for k in range(1, self.sizes[0]):
            loop(self.at.depths, lambda d, k=k: self.second_copy(0, k, d).wait_send())
        for k in range(1, self.at.depths):
            self.depth_copy(0, k).wait_send()


def loop(size, body):
    lax.fori_loop(0, size, lambda i, c: (body(i), c)[1], 0)


STREAM_FIELDS = (
    "held", "pair", "third", "second", "depth",
    "pair_send", "pair_recv", "third_send", "third_recv", "second_send", "second_recv", "depth_send", "depth_recv",
)


def stream_scratch(rows, depths, sides, side_first, shape):
    second, third = (rows, sides) if side_first else (sides, rows)
    half = rows * depths * sides
    leads = ((half,), (half,), (third - 1, second * depths), (second - 1, depths), (depths - 1,))
    buffers = [pltpu.VMEM(lead + shape, BF16) for lead in leads]
    sems = [DMA((half,)), DMA((half,))] + [DMA(lead) for lead in leads[2:] for _ in range(2)]
    return buffers + sems


STREAMS = (("con", False), ("ex0", True), ("ex1", True), ("out", False), ("pr0", True), ("pr1", False))


FIRST_PAIRS = 4
CHUNK_SLOTS = 4
SCHEDULE = (
    ("chunk", 1, 1), ("chunk", 1, 3), ("square", "ex0"), ("third", "con", 1, 1), ("third", "con", 1, 3),
    ("chunk", 0, 1), ("third", "ex0", 1, 0), ("third", "ex0", 1, 1), ("attn", 0, 0), ("third", "ex0", 0, 0),
    ("third", "ex0", 0, 1), ("attn", 0, 1), ("third", "con", 0, 1), ("chunk", 1, 2), ("chunk", 0, 3), ("attn", 0, 2),
    ("second", "con", 1), ("third", "con", 1, 2), ("square", "ex1"), ("third", "con", 0, 3), ("second", "ex0", 0),
    ("second", "ex0", 1), ("chunk", 1, 0), ("third", "ex1", 1, 0), ("third", "ex1", 1, 1), ("second", "con", 3),
    ("second", "ex0", 2), ("attn", 0, 3), ("third", "ex1", 0, 0), ("second", "ex0", 3), ("attn", 1, 0),
    ("third", "ex1", 0, 1), ("third", "con", 1, 0), ("attn", 1, 1), ("depth", "con", 1), ("attn", 1, 2),
    ("attn", 1, 3), ("attn", 2, 0), ("attn", 2, 1), ("depth", "ex0", 0), ("attn", 2, 2), ("attn", 2, 3),
    ("depth", "ex0", 1), ("attn", 3, 0), ("depth", "ex0", 2), ("attn", 3, 1), ("attn", 3, 2), ("second", "ex1", 0),
    ("depth", "ex0", 3), ("attn", 3, 3), ("square", "pr0"), ("second", "ex1", 1), ("second", "ex1", 2),
    ("second", "ex1", 3), ("attn", 4, 0), ("third", "pr0", 1, 0), ("third", "pr0", 1, 1), ("depth", "con", 3),
    ("third", "pr0", 0, 0), ("depth", "ex1", 0), ("square", "out"), ("third", "pr0", 0, 1), ("depth", "ex1", 1),
    ("third", "out", 1, 0), ("depth", "ex1", 2), ("third", "out", 1, 1), ("depth", "ex1", 3), ("third", "out", 0, 0),
    ("chunk", 0, 2), ("third", "out", 0, 1), ("attn", 4, 1), ("attn", 4, 2), ("third", "con", 0, 2),
    ("second", "con", 2), ("chunk", 0, 0), ("second", "out", 0), ("second", "pr0", 0), ("attn", 4, 3),
    ("second", "out", 1), ("second", "pr0", 1), ("attn", 5, 0), ("third", "con", 0, 0), ("second", "con", 0),
    ("second", "out", 2), ("second", "out", 3), ("second", "pr0", 2), ("attn", 5, 1), ("second", "pr0", 3),
    ("depth", "pr0", 0), ("attn", 5, 2), ("attn", 5, 3), ("depth", "pr0", 1), ("square", "pr1"), ("depth", "con", 2),
    ("depth", "out", 1), ("third", "pr1", 1, 0), ("third", "pr1", 1, 1), ("third", "pr1", 0, 0), ("depth", "out", 0),
    ("depth", "pr0", 2), ("depth", "pr0", 3), ("third", "pr1", 0, 1), ("tile", 0), ("depth", "con", 0), ("tile", 1),
    ("depth", "out", 2), ("second", "pr1", 0), ("depth", "out", 3), ("tile", 2), ("second", "pr1", 1),
    ("second", "pr1", 2), ("second", "pr1", 3), ("depth", "pr1", 0), ("tile", 3), ("depth", "pr1", 1), ("small",),
    ("depth", "pr1", 2), ("depth", "pr1", 3),
)


def finish_kernel(mesh_shape, sizes, names, *refs):
    r = Refs(names, refs)
    rows, inner = mesh_shape["dp"], mesh_shape["fsdp"]
    depths = 4
    sides = inner // (2 * depths)
    total = rows * inner
    half = total // 2
    at = Place(rows, depths, sides)
    seq, width = r.dz.shape
    groups = (FIRST_PAIRS * 128, width - FIRST_PAIRS * 128)
    core = at.core
    me = at.row * inner + lax.axis_index("fsdp")
    piece = width // total
    vec = Vectors(r.vec, width)

    copies = {}

    def load(key, source, target, sem):
        copies[key] = pltpu.make_async_copy(source, target, sem)
        copies[key].start()

    def ready(key):
        copies.pop(key).wait()

    chunks = [step[1:] for step in SCHEDULE if step[0] == "chunk"]
    span = sides * 2 * piece * 4

    def load_active(i):
        k, d = chunks[i]
        first = ((at.row + k) % rows * depths + (at.depth + d) % depths) * span
        columns = pl.ds(pl.multiple_of(first, 128), span)
        load(("act", i), r.active.at[:, columns], r.act.at[i % 2], r.act_sem.at[i % 2])

    load_active(0)
    load_active(1)
    load("normed", r.normed, r.normedv, r.in_sem.at[0])
    load("df0", r.df.at[:, : 2 * width], r.dfs.at[0], r.df_sem.at[0])
    load("df1", r.df.at[:, 2 * width :], r.dfs.at[1], r.df_sem.at[1])
    load("dh", r.dh, r.dhv, r.dh_sem)
    load("context", r.context, r.contextv, r.in_sem.at[1])
    load("first", r.first_normed, r.firstv, r.in_sem.at[2])
    load("wp", r.wp, r.wpv, r.wp_sem)

    def load_pair(p):
        slot = p % 2
        for i in range(3):
            columns = pl.ds(i * width + p * 128, 128)
            load(("pair", p, i), r.mixed.at[:, columns], r.qkv.at[slot, i], r.qkv_sem.at[slot, i])
        load(("pair", p, 3), r.dctx.at[:, pl.ds(p * 128, 128)], r.qkv.at[slot, 3], r.qkv_sem.at[slot, 3])

    load_pair(0)

    barrier = pltpu.get_barrier_semaphore()

    def other(k):
        index = (me + k) % total
        return {"dp": index // inner, "fsdp": index % inner}

    loop(total - 1, lambda i: pl.semaphore_signal(barrier, inc=1, device_id=other(i + 1), **MESH))
    pl.semaphore_wait(barrier, total - 1)

    streams = {name: Stream(at, side_first, name, r) for name, side_first in STREAMS}
    con = streams["con"]
    ones = jnp.ones((16, seq), BF16)
    sums = {}

    def chunk(k, d):
        i = chunks.index((k, d))
        ready(("act", i))
        slot = i % CHUNK_SLOTS
        if i >= CHUNK_SLOTS:
            con_sent(i - CHUNK_SLOTS)
        grad = dot_tn(r.act[i % 2], r.dz[...])
        if i + 2 < len(chunks):
            load_active(i + 2)
        r.con_stage[slot] = grad.reshape(sides, 2, 4 * piece, width).astype(BF16)
        for side in range(sides):
            con.pair_copy(con_unit(i, side), r.con_stage.at[slot, side, 1 - core]).start()

    def con_unit(i, side):
        k, d = chunks[i]
        return ((at.row + k) % rows * depths + (at.depth + d) % depths) * sides + side

    def con_sent(i):
        for side in range(sides):
            con.pair_copy(con_unit(i, side), r.con_stage.at[i % CHUNK_SLOTS, side, 1 - core]).wait_send()

    def con_third(k, d):
        slot = chunks.index((k, d)) % CHUNK_SLOTS
        for j in list(range(1, sides)) + [0]:
            side = (at.side + j) % sides
            con.third_step(k, j, d, lambda u: r.con_stage.at[slot, side, core])

    slots = {}

    def square(name, left, right):
        columns = right.shape[1]
        slot = len(slots) % 2
        previous = [n for n, s in slots.items() if s == slot]
        if previous:
            stage_sent(previous[-1])
        slots[name] = slot
        quarter = width // 4
        for part in range(4):
            grad = dot_tn(left[:, part * quarter : (part + 1) * quarter], right[...])
            target = r.stage.at[slot, part * half // 4 : (part + 1) * half // 4, :, :, :columns]
            target[...] = grad.reshape(half // 4, 2, piece, columns).astype(BF16)
        stream = streams[name]
        for k in list(range(1, stream.sizes[1])) + [0]:
            for j in list(range(1, stream.sizes[0])) + [0]:

                def start(d, k=k, j=j):
                    second, third = ((m + n) % z for m, n, z in zip(stream.mine, (j, k), stream.sizes))
                    u = stream.unit(second, third, (at.depth + d) % depths)
                    stream.pair_copy(u, stage_at(name, u, 1 - core, columns)).start()

                loop(depths, start)

    def stage_at(name, u, which, columns):
        return r.stage.at[slots[name], u, which, :, :columns]

    def columns_of(name):
        return streams[name].held.shape[-1]

    def stage_sent(name):
        stream = streams[name]
        loop(half, lambda u: stream.pair_copy(u, stage_at(name, u, 1 - core, columns_of(name))).wait_send())

    def square_third(name, k, j):
        stream = streams[name]
        source = lambda u: stage_at(name, u, core, columns_of(name))
        loop(depths, lambda d: stream.third_step(k, j, d, source))

    def expand(e):
        if e == 0:
            ready("normed")
        ready("df%d" % e)
        square("ex%d" % e, r.normedv, r.dfs.at[e])
        sums["be%d" % e] = dot(ones, r.dfs[e])[0:1]

    def output():
        ready("dh")
        ready("context")
        r.dy[...] = r.dhv[...].astype(BF16)
        square("out", r.contextv, r.dy)
        sums["bo"] = dot(ones, r.dy[...])[0:1]
        sums["bc"] = dot(ones, r.dz[...])[0:1]

    later = iota((TILE, TILE), 0) > iota((TILE, TILE), 1)
    later = jnp.concatenate([later, later], 1)
    first_head = iota((TILE, 128), 1) < 64

    def two(value):
        parts = [jnp.where(first_head, value, 0.0), jnp.where(first_head, 0.0, value)]
        return jnp.concatenate(parts, 0).astype(BF16)

    def attend_block(p, n):
        block = seq // TILE - 1 - n
        slot = p % 2
        if n == 0:
            for i in range(4):
                ready(("pair", p, i))
            if p + 1 < HEADS // 2:
                load_pair(p + 1)
            r.keys_t[...] = r.qkv[slot, 1].T
        query_ref, key_ref, value_ref, up_ref = (r.qkv.at[slot, i] for i in range(4))
        start, stop = block * TILE, block * TILE + TILE
        query = two(query_ref[start:stop].astype(F32) * 0.125)
        upstream = two(up_ref[start:stop].astype(F32))
        score = dot_nt(key_ref[:stop], query)
        edge = jnp.where(later, NEG_FILL, score[start:])
        score = jnp.concatenate([score[:start], edge], 0) if start else edge
        logs = jnp.concatenate([r.logs[p, 0:1, start:stop], r.logs[p, 1:2, start:stop]], 1)
        prob = jnp.exp(score - logs)
        prob_grad = dot_nt(value_ref[:stop], upstream)
        mean = jnp.sum(prob * prob_grad, axis=0, keepdims=True)
        score_grad = (prob * (prob_grad - mean)).astype(BF16)
        dv = dot(prob.astype(BF16), upstream)
        dk = dot(score_grad, query)
        if n == 0:
            r.dv_sum[...] = dv
            r.dk_sum[...] = dk
        else:
            r.dv_sum[:stop] += dv
            r.dk_sum[:stop] += dk
        out = dot(r.keys_t[:, :stop], score_grad)
        out = jnp.concatenate([out[:64, :TILE], out[64:, TILE:]], 0)
        g = int(p >= FIRST_PAIRS)
        target, group = r.dfs.at[g], groups[g]
        column = (p - g * FIRST_PAIRS) * 128
        target[start:stop, column : column + 128] = (out.T * 0.125).astype(BF16)
        if block == 0:
            target[:, group + column : group + column + 128] = r.dk_sum[...].astype(BF16)
            target[:, 2 * group + column : 2 * group + column + 128] = r.dv_sum[...].astype(BF16)

    def project(g):
        if g == 0:
            ready("first")
        right = r.dfs.at[g, :, : 3 * groups[g]]
        square("pr%d" % g, r.firstv, right)
        sums["bp%d" % g] = dot(ones, right[...])[0:1]

    def project_columns(g, n):
        first = n * width + g * groups[0]
        return slice(first, first + groups[g])

    def load_tile(i):
        load(("x", i), r.x.at[pl.ds(i * TILE, TILE)], r.xs.at[i % 2], r.x_sem.at[i % 2])

    def tile(i):
        if i == 0:
            ready("wp")
            load_tile(0)
            load_tile(1)
        ready(("x", i))
        part = slice(i * TILE, i * TILE + TILE)
        da = jnp.zeros((TILE, width), F32)
        for g in range(2):
            for n in range(3):
                da = da + dot_nt(r.dfs[g, part, n * groups[g] : (n + 1) * groups[g]], r.wpv[:, project_columns(g, n)])
        hat, inv = norm_parts(r.xs[i % 2])
        if i + 2 < seq // TILE:
            load_tile(i + 2)
        position = i * TILE + iota((TILE, 1), 0)
        kept = (position < r.start[0]) | (position >= r.start[0] + THOUGHTS)
        if i >= 2:
            ready(("dx", i - 2))
        r.dxs[i % 2] = jnp.where(kept, r.dhv[part] + norm_back(da, hat, inv, vec.g1), 0.0)
        load(("dx", i), r.dxs.at[i % 2], r.hidden_grad.at[pl.ds(i * TILE, TILE)], r.dx_sem.at[i % 2])
        gain, bias = jnp.sum(da * hat, axis=0, keepdims=True), jnp.sum(da, axis=0, keepdims=True)
        sums["g1"] = gain if i == 0 else sums["g1"] + gain
        sums["b1"] = bias if i == 0 else sums["b1"] + bias

    def small_start():
        group_of = lambda n: jnp.concatenate(
            [sums["bp%d" % g][:, n * groups[g] : (n + 1) * groups[g]] for g in range(2)], 1
        )
        lines = dict(
            g1=sums["g1"], b1=sums["b1"], bp=jnp.concatenate([group_of(0), group_of(2)], 1), bo=sums["bo"],
            g2=r.sums[0:1], b2=r.sums[1:2], be=jnp.concatenate([sums["be0"], sums["be1"]], 1), bc=sums["bc"],
        )
        offset = 0
        r.small_part[...] = jnp.zeros_like(r.small_part)
        for name, size in zip(VECTORS, sizes):
            low, high = offset // 128 * 128, -(-(offset + size) // 128) * 128
            length = total * size
            lane = iota((1, length), 1)
            pick = (iota((high - low, length), 0) == lane % size + (offset - low)).astype(F32).astype(BF16)
            rest = jnp.where(iota((total, length), 0) == lane // size, lines[name], 0.0)
            pieces = jnp.zeros((total, high - low), F32)
            for _ in range(2):
                rounded = rest.astype(BF16)
                pieces = pieces + dot_nt(rounded, pick)
                rest = rest - rounded.astype(F32)
            r.small_part[:, 0, low:high] += pieces
            offset += size
        loop(total - 1, lambda i: small_copy(i + 1).start())

    def small_copy(k):
        return pltpu.make_async_remote_copy(
            src_ref=r.small_part.at[(me + k) % total],
            dst_ref=r.small_in.at[k - 1],
            send_sem=r.small_send.at[k - 1],
            recv_sem=r.small_recv.at[k - 1],
            device_id=other(k),
            **MESH,
        )

    def small_end():
        loop(total - 1, lambda i: small_copy(i + 1).wait_recv())
        received = r.small_in[...]
        r.small_out[...] = r.small_part[me] + jnp.sum(received[: total - 1], axis=0)

    def work(kind, *what):
        if kind == "chunk":
            chunk(*what)
        elif kind == "attn":
            attend_block(*what)
        elif kind == "tile":
            tile(*what)
        elif kind == "small":
            small_start()
        elif kind == "square":
            name = what[0]
            if name == "out":
                output()
            else:
                (expand if name[:2] == "ex" else project)(int(name[2]))
        elif kind == "third":
            name, k, j = what
            if name == "con":
                con_third(k, j)
            else:
                square_third(name, k, 1 - j)
        elif kind == "second":
            streams[what[0]].second_step(what[1])
        else:
            streams[what[0]].depth_step(what[1])

    for step in SCHEDULE:
        work(*step)
    r.contract_out[...] = con.total()
    r.expand_out[:, : 2 * width] = streams["ex0"].total()
    r.expand_out[:, 2 * width :] = streams["ex1"].total()
    r.output_out[...] = streams["out"].total()
    for g in range(2):
        grad = streams["pr%d" % g].total()
        for n in range(3):
            r.project_out[:, project_columns(g, n)] = grad[:, n * groups[g] : (n + 1) * groups[g]]
    small_end()
    ready(("dx", 2))
    ready(("dx", 3))
    for i in range(len(chunks) - CHUNK_SLOTS, len(chunks)):
        con_sent(i)
    for name in list(slots)[-2:]:
        stage_sent(name)
    for stream in streams.values():
        stream.drain()
    loop(total - 1, lambda i: small_copy(i + 1).wait_send())


def finish(mesh_shape, sizes, start, operands):
    rows, inner = mesh_shape["dp"], mesh_shape["fsdp"]
    depths = 4
    sides = inner // (2 * depths)
    total = rows * inner
    half = total // 2
    seq, width = operands["dz"].shape
    piece = width // total
    lanes = -(-sum(sizes) // 128) * 128
    in_vmem = ("dz", "logs", "vec", "sums")
    outs = dict(
        hidden_grad=(seq, width),
        contract_out=(4 * piece, width),
        expand_out=(piece, 4 * width),
        output_out=(piece, width),
        project_out=(piece, 3 * width),
        small_out=(1, lanes),
    )
    shapes = dict(
        con=(4 * piece, width), ex0=(piece, 2 * width), ex1=(piece, 2 * width), out=(piece, width),
        pr0=(piece, 3 * FIRST_PAIRS * 128), pr1=(piece, 3 * (width - FIRST_PAIRS * 128)),
    )
    span = sides * 2 * piece * 4
    scratch = dict(
        act=pltpu.VMEM((2, seq, span), BF16), act_sem=DMA((2,)),
        dfs=pltpu.VMEM((2, seq, 2 * width), BF16), df_sem=DMA((2,)),
        dhv=pltpu.VMEM((seq, width), F32), dh_sem=DMA(()),
        normedv=pltpu.VMEM((seq, width), BF16), contextv=pltpu.VMEM((seq, width), BF16),
        firstv=pltpu.VMEM((seq, width), BF16), in_sem=DMA((3,)),
        dy=pltpu.VMEM((seq, width), BF16),
        qkv=pltpu.VMEM((2, 4, seq, 128), BF16), qkv_sem=DMA((2, 4)),
        keys_t=pltpu.VMEM((128, seq), BF16),
        dk_sum=pltpu.VMEM((seq, 128), F32), dv_sum=pltpu.VMEM((seq, 128), F32),
        wpv=pltpu.VMEM((width, 3 * width), BF16), wp_sem=DMA(()),
        xs=pltpu.VMEM((2, TILE, width), F32), x_sem=DMA((2,)),
        dxs=pltpu.VMEM((2, TILE, width), F32), dx_sem=DMA((2,)),
        con_stage=pltpu.VMEM((CHUNK_SLOTS, sides, 2, 4 * piece, width), BF16),
        stage=pltpu.VMEM((2, half, 2, piece, 2 * width), BF16),
        small_part=pltpu.VMEM((total, 1, lanes), F32), small_in=pltpu.VMEM((total, 1, lanes), F32),
        small_send=DMA((total - 1,)), small_recv=DMA((total - 1,)),
    )
    for name, side_first in STREAMS:
        fields = stream_scratch(rows, depths, sides, side_first, shapes[name])
        scratch.update({name + "_" + f: s for f, s in zip(STREAM_FIELDS, fields)})
    names = ("start",) + tuple(operands) + tuple(outs) + tuple(scratch)
    whole_vmem = pl.BlockSpec(memory_space=pltpu.VMEM)
    return pl.pallas_call(
        functools.partial(finish_kernel, mesh_shape, sizes, names),
        out_shape=[jax.ShapeDtypeStruct(s, F32) for s in outs.values()],
        in_specs=[smem()] + [whole_vmem if n in in_vmem else in_hbm() for n in operands],
        out_specs=[in_hbm()] + [whole_vmem] * 5,
        scratch_shapes=list(scratch.values()),
        compiler_params=pltpu.CompilerParams(collective_id=2, has_side_effects=True, vmem_limit_bytes=63 * 2**20),
        name="finish",
    )(start, *operands.values())


def pack(vectors, total):
    joined = jnp.concatenate([v.reshape(total, -1) for v in vectors], 1)
    fill = -joined.shape[1] % 128
    return jnp.pad(joined, ((0, 0), (0, fill)))[:, None]


def unpack(packed, sizes):
    flat = packed.reshape(-1, packed.shape[-1])
    out, at = [], 0
    for size in sizes:
        out.append(flat[:, at : at + size].reshape(-1))
        at += size
    return out


def per_device(
    mesh_shape,
    hidden,
    cotangent,
    lengths,
    thought_start,
    first_gain,
    first_bias,
    project_weight,
    project_bias,
    output_weight,
    output_bias,
    second_gain,
    second_bias,
    expand_weight,
    expand_bias,
    contract_weight,
    contract_bias,
):
    _, seq, width = hidden.shape
    total = mesh_shape["dp"] * mesh_shape["fsdp"]
    vectors = (
        first_gain,
        first_bias,
        project_bias,
        output_bias,
        second_gain,
        second_bias,
        expand_bias,
        contract_bias,
    )
    sizes = [v.shape[0] for v in vectors]
    full = gather_all(
        mesh_shape,
        (pack(vectors, 1)[0], project_weight, output_weight, expand_weight, contract_weight),
    )
    Wp, Wo, We, Wc = (w.reshape(-1, w.shape[-1]) for w in full[1:])

    x, mixed, normed, vec = think(thought_start, hidden[0], full[0], sizes, (Wp, Wo, We, Wc))
    context, log_total = attend(mixed)
    final, resid, normed_two, active, dz, df, dh, dctx, sums = feed(
        lengths, context, x, cotangent[0], (Wo, We, Wc), vec
    )
    dh, dctx, dz, df, sums = reflect(
        thought_start, x, mixed, resid, context, log_total, vec, (Wp, Wc, We, Wo), dh, dctx, dz, df, sums
    )
    if width // total % 8 == 0:
        operands = dict(
            dz=dz, normed=normed_two, context=context, first_normed=normed, logs=log_total, vec=vec, sums=sums,
            active=active, df=df, dh=dh, mixed=mixed, dctx=dctx, x=x, wp=Wp,
        )
        hidden_grad, dWc, dWe, dWo, dWp, small = finish(mesh_shape, sizes, thought_start, operands)
        dg1, db1, dbp, dbo, dg2, db2, dbe, dbc = unpack(small, sizes)
        return (final[None], hidden_grad[None], dg1, db1, dWp, dbp, dWo, dbo, dg2, db2, dWe, dbe, dWc, dbc)
    dq, dk, dv = attend_back(mixed, dctx, log_total)
    g1 = vec[0:1, :width]
    dy = dh.astype(BF16)
    x_hat, x_inv = norm_parts(x)
    dmixed = jnp.concatenate([dq, dk, dv], 1)
    da = dot_nt(dmixed, Wp)
    dx = dh + norm_back(da, x_hat, x_inv, g1)
    position = iota((seq, 1), 0)
    is_thought = (position >= thought_start[0]) & (position < thought_start[0] + THOUGHTS)
    hidden_grad = jnp.where(is_thought, 0.0, dx)

    def column_sum(value):
        return jnp.sum(value, axis=0, dtype=F32)

    column = column_sum(dmixed)
    small = (
        column_sum(da * x_hat),
        column_sum(da),
        jnp.concatenate([column[:width], column[2 * width :]]),
        column_sum(dy),
        sums[0],
        sums[1],
        column_sum(df),
        column_sum(dz),
    )
    large = (
        dot_tn(normed, dmixed),
        dot_tn(context, dy),
        dot_tn(normed_two, df),
        dot_tn(active, dz),
    )
    parts = [pack(small, total)]
    for grad in large:
        parts.append(grad.astype(BF16).reshape(total, grad.shape[0] // total, grad.shape[1]))
    small, dWp, dWo, dWe, dWc = scatter_all(mesh_shape, parts)
    dg1, db1, dbp, dbo, dg2, db2, dbe, dbc = unpack(small, sizes)
    return (final[None], hidden_grad[None], dg1, db1, dWp, dbp, dWo, dbo, dg2, db2, dWe, dbe, dWc, dbc)


def solution(mesh):
    rows = P(AXES, None, None)
    flat = P(AXES)
    square = P(AXES, None)
    specs = (flat, flat, square, flat, square, flat, flat, flat, square, flat, square, flat)
    return jax.shard_map(
        functools.partial(per_device, dict(mesh.shape)),
        mesh=mesh,
        in_specs=(rows, rows, flat, flat) + specs,
        out_specs=(rows, rows) + specs,
        check_vma=False,
    )
```

```python
import functools

import jax
import jax.numpy as jnp
from jax import lax
from jax.experimental import pallas as pl
from jax.experimental.pallas import tpu as pltpu
from jax.sharding import PartitionSpec as P

HEADS = 12
THOUGHTS = 3
PREFIX = 384
TILE = 256

EPSILON = 1e-05
NEG_FILL = -1e30
F32 = jnp.float32
BF16 = jnp.bfloat16
VMEM_LIMIT = 62 * 2**20


AXES = ("dp", "fsdp")
ANY = pl.BlockSpec(memory_space=pl.ANY)
DMA = pltpu.SemaphoreType.DMA


class Place:
    def __init__(self, rows, depths, sides):
        self.rows, self.depths, self.sides = rows, depths, sides
        self.row = lax.axis_index("dp")
        flat = lax.axis_index("fsdp")
        self.depth = flat // (sides * 2)
        self.side = flat // 2 % sides
        self.core = flat % 2

    def index(self, row, depth, side, core):
        return row * (self.depths * self.sides * 2) + (depth * self.sides + side) * 2 + core

    def device(self, row, depth, side, core):
        return {"dp": row, "fsdp": (depth * self.sides + side) * 2 + core}


def gather_kernel(rows, depths, sides, count, *refs):
    shards, fulls = refs[:count], refs[count : 2 * count]
    send_sem, recv_sem, pair_send, pair_recv, own_sem = refs[2 * count :]
    at = Place(rows, depths, sides)
    dev = dict(device_id_type=pl.DeviceIdType.MESH)

    barrier = pltpu.get_barrier_semaphore()
    peers = []
    for k in range(1, depths):
        peers.append(at.device(at.row, (at.depth + k) % depths, at.side, at.core))
    for k in range(1, sides):
        peers.append(at.device(at.row, at.depth, (at.side + k) % sides, at.core))
    for k in range(1, rows):
        peers.append(at.device((at.row + k) % rows, at.depth, at.side, at.core))
    peers.append(at.device(at.row, at.depth, at.side, 1 - at.core))
    for peer in peers:
        pl.semaphore_signal(barrier, inc=1, device_id=peer, **dev)
    pl.semaphore_wait(barrier, len(peers))

    def run(core):
        sends = []

        def index(row, depth, side):
            return at.index(row, depth, side, core)

        def send(w, source, shard, peer, slot):
            copy = pltpu.make_async_remote_copy(
                src_ref=source,
                dst_ref=fulls[w].at[shard],
                send_sem=send_sem.at[w, slot],
                recv_sem=recv_sem.at[w, shard],
                device_id=peer,
                **dev,
            )
            copy.start()
            sends.append(copy)

        def arrive(w, shard):
            pltpu.make_async_remote_copy(
                src_ref=fulls[w].at[shard],
                dst_ref=fulls[w].at[shard],
                send_sem=send_sem.at[w, 0],
                recv_sem=recv_sem.at[w, shard],
                device_id=peers[0],
                **dev,
            ).wait_recv()

        def to_pair(w, source, shard):
            copy = pltpu.make_async_remote_copy(
                src_ref=source,
                dst_ref=fulls[w].at[shard],
                send_sem=pair_send.at[w, shard // 2],
                recv_sem=pair_recv.at[w, shard // 2],
                device_id=at.device(at.row, at.depth, at.side, 1 - core),
                **dev,
            )
            copy.start()
            sends.append(copy)

        slots = [0] * count

        def slot(w):
            slots[w] += 1
            return slots[w] - 1

        second_size, third_size = (sides, rows) if core == 0 else (rows, sides)

        def spot(second, third):
            return (third, second) if core == 0 else (second, third)

        mine = (at.side, at.row) if core == 0 else (at.row, at.side)

        def forward_second(w, source, depth):
            row, side = spot(*mine)
            for k in range(1, second_size):
                r, s = spot((mine[0] + k) % second_size, mine[1])
                send(w, source, index(row, depth, side), at.device(r, at.depth, s, core), slot(w))

        def forward_third(w, source, depth, second):
            row, side = spot(second, mine[1])
            for k in range(1, third_size):
                r, s = spot(mine[0], (mine[1] + k) % third_size)
                send(w, source, index(row, depth, side), at.device(r, at.depth, s, core), slot(w))

        own = []
        for w in range(count):
            me = index(at.row, at.depth, at.side)
            for k in range(1, depths):
                send(w, shards[w], me, at.device(at.row, (at.depth + k) % depths, at.side, core), slot(w))
            forward_second(w, shards[w], at.depth)
            forward_third(w, shards[w], at.depth, mine[0])
            to_pair(w, shards[w], me)
            copy = pltpu.make_async_copy(shards[w], fulls[w].at[me], own_sem.at[w])
            copy.start()
            own.append(copy)

        def stage_one(w):
            for k in range(1, depths):
                depth = (at.depth - k) % depths
                shard = index(at.row, depth, at.side)
                arrive(w, shard)
                forward_second(w, fulls[w].at[shard], depth)
                forward_third(w, fulls[w].at[shard], depth, mine[0])
                to_pair(w, fulls[w].at[shard], shard)

        def stage_two(w):
            for k in range(1, second_size):
                second = (mine[0] - k) % second_size
                for d in range(depths):
                    depth = (at.depth - d) % depths
                    shard = index(spot(second, mine[1])[0], depth, spot(second, mine[1])[1])
                    arrive(w, shard)
                    forward_third(w, fulls[w].at[shard], depth, second)
                    to_pair(w, fulls[w].at[shard], shard)

        def stage_three(w):
            for k in range(1, third_size):
                third = (mine[1] - k) % third_size
                for s in range(second_size):
                    second = (mine[0] - s) % second_size
                    for d in range(depths):
                        depth = (at.depth - d) % depths
                        row, side = spot(second, third)
                        shard = index(row, depth, side)
                        arrive(w, shard)
                        to_pair(w, fulls[w].at[shard], shard)

        for step in range(count + 2):
            if step < count:
                stage_one(step)
            if 0 <= step - 1 < count:
                stage_two(step - 1)
            if 0 <= step - 2 < count:
                stage_three(step - 2)

        for w in range(count):
            for row in range(rows):
                for depth in range(depths):
                    for side in range(sides):
                        shard = at.index(row, depth, side, 1 - core)
                        pltpu.make_async_remote_copy(
                            src_ref=fulls[w].at[shard],
                            dst_ref=fulls[w].at[shard],
                            send_sem=pair_send.at[w, shard // 2],
                            recv_sem=pair_recv.at[w, shard // 2],
                            device_id=peers[0],
                            **dev,
                        ).wait_recv()
        for copy in own:
            copy.wait()
        for copy in sends:
            copy.wait_send()

    for core in range(2):

        @pl.when(at.core == core)
        def _():
            run(core)


def gather_all(mesh_shape, shards, collective_id=0):
    rows, inner = mesh_shape["dp"], mesh_shape["fsdp"]
    depths = 4
    sides = inner // (2 * depths)
    total = rows * inner
    count = len(shards)
    sent = (depths - 1) + depths * (max(rows, sides) - 1) + depths * sides * (rows - 1) + depths * rows * (sides - 1)
    return pl.pallas_call(
        functools.partial(gather_kernel, rows, depths, sides, count),
        out_shape=[jax.ShapeDtypeStruct((total,) + s.shape, s.dtype) for s in shards],
        in_specs=[ANY] * count,
        out_specs=[ANY] * count,
        scratch_shapes=[
            DMA((count, sent)),
            DMA((count, total)),
            DMA((count, total // 2)),
            DMA((count, total // 2)),
            DMA((count,)),
        ],
        compiler_params=pltpu.CompilerParams(collective_id=collective_id, has_side_effects=True),
        name="gather_weights",
    )(*shards)


def scatter_kernel(rows, depths, sides, count, *refs):
    parts, outs = refs[:count], refs[count : 2 * count]
    scratch = refs[2 * count :]
    held, pair, third_in, second_in, depth_in = (scratch[i * count : (i + 1) * count] for i in range(5))
    (own_sem, pair_send, pair_recv, third_send, third_recv, second_send, second_recv, depth_send, depth_recv) = scratch[
        5 * count :
    ]
    at = Place(rows, depths, sides)
    dev = dict(device_id_type=pl.DeviceIdType.MESH)

    barrier = pltpu.get_barrier_semaphore()
    peers = []
    for k in range(1, depths):
        peers.append(at.device(at.row, (at.depth + k) % depths, at.side, at.core))
    for k in range(1, sides):
        peers.append(at.device(at.row, at.depth, (at.side + k) % sides, at.core))
    for k in range(1, rows):
        peers.append(at.device((at.row + k) % rows, at.depth, at.side, at.core))
    peers.append(at.device(at.row, at.depth, at.side, 1 - at.core))
    for peer in peers:
        pl.semaphore_signal(barrier, inc=1, device_id=peer, **dev)
    pl.semaphore_wait(barrier, len(peers))

    def run(core):
        second_size, third_size = (sides, rows) if core == 0 else (rows, sides)
        my_second, my_third = (at.side, at.row) if core == 0 else (at.row, at.side)

        def unit(second, third, depth):
            row, side = (third, second) if core == 0 else (second, third)
            return (row * depths + depth) * sides + side

        def device(second, third, depth):
            row, side = (third, second) if core == 0 else (second, third)
            return at.device(row, depth, side, core)

        def remote(source, target, send, recv, peer):
            return pltpu.make_async_remote_copy(
                src_ref=source, dst_ref=target, send_sem=send, recv_sem=recv, device_id=peer, **dev
            )

        sibling = at.device(at.row, at.depth, at.side, 1 - core)

        def pair_copy(w, u):
            return remote(
                parts[w].at[u, 1 - core], pair[w].at[u], pair_send.at[w], pair_recv.at[w, u], sibling
            )

        def own_copy(w):
            return pltpu.make_async_copy(parts[w].at[:, core], held[w], own_sem.at[w])

        def third_copy(w, u, k, q, peer):
            return remote(
                held[w].at[u],
                third_in[w].at[k - 1, q],
                third_send.at[w, k - 1, q],
                third_recv.at[w, k - 1, q],
                peer,
            )

        def second_copy(w, u, k, q, peer):
            return remote(
                held[w].at[u],
                second_in[w].at[k - 1, q],
                second_send.at[w, k - 1, q],
                second_recv.at[w, k - 1, q],
                peer,
            )

        def depth_copy(w, u, k, peer):
            return remote(
                held[w].at[u], depth_in[w].at[k - 1], depth_send.at[w, k - 1], depth_recv.at[w, k - 1], peer
            )

        def loop(size, body):
            lax.fori_loop(0, size, lambda i, c: (body(i), c)[1], 0)

        def each_unit(visit):
            other_second, other_third = third_size, second_size
            far = my_second
            for k in list(range(1, other_third)) + [0]:
                def inner(q, k=k):
                    second, third = q // depths, (far + k) % other_third
                    row, side = (second, third) if core == 0 else (third, second)
                    visit((row * depths + q % depths) * sides + side)
                loop(other_second * depths, inner)

        for w in range(count):
            each_unit(lambda u, w=w: pair_copy(w, u).start())
            own_copy(w).start()

        def add_pair(w, u):
            pair_copy(w, u).wait_recv()
            held[w][u] = held[w][u] + pair[w][u]

        def stage_third(w):
            own_copy(w).wait()
            for k in list(range(1, third_size)) + [0]:
                third = (my_third + k) % third_size

                def inner(q, k=k, third=third):
                    second, depth = q // depths, q % depths
                    u = unit(second, third, depth)
                    add_pair(w, u)
                    if k:
                        third_copy(w, u, k, q, device(my_second, third, at.depth)).start()

                loop(second_size * depths, inner)

        def stage_second(w):
            for k in list(range(1, second_size)) + [0]:
                second = (my_second + k) % second_size

                def inner(depth, k=k, second=second):
                    u = unit(second, my_third, depth)
                    for j in range(1, third_size):
                        third_copy(w, u, j, second * depths + depth, sibling).wait_recv()
                        held[w][u] = held[w][u] + third_in[w][j - 1, second * depths + depth]
                    if k:
                        second_copy(w, u, k, depth, device(second, my_third, at.depth)).start()

                loop(depths, inner)

        def stage_depth(w):
            for k in list(range(1, depths)) + [0]:
                depth = (at.depth + k) % depths
                u = unit(my_second, my_third, depth)
                for j in range(1, second_size):
                    second_copy(w, u, j, depth, sibling).wait_recv()
                    held[w][u] = held[w][u] + second_in[w][j - 1, depth]
                if k:
                    depth_copy(w, u, k, device(my_second, my_third, depth)).start()

        def stage_last(w):
            u = unit(my_second, my_third, at.depth)
            total = held[w][u].astype(jnp.float32)
            for k in range(1, depths):
                depth_copy(w, u, k, sibling).wait_recv()
                total = total + depth_in[w][k - 1].astype(jnp.float32)
            outs[w][...] = total

        for step in range(count + 3):
            for lag, stage in enumerate((stage_third, stage_second, stage_depth, stage_last)):
                if 0 <= step - lag < count:
                    stage(step - lag)

        for w in range(count):
            remote(pair[w], pair[w], pair_send.at[w], pair_recv.at[w, 0], sibling).wait_send()
            for k in range(1, third_size):
                loop(second_size * depths, lambda q, w=w, k=k: third_copy(w, 0, k, q, sibling).wait_send())
            for k in range(1, second_size):
                loop(depths, lambda q, w=w, k=k: second_copy(w, 0, k, q, sibling).wait_send())
            for k in range(1, depths):
                depth_copy(w, 0, k, sibling).wait_send()

    for core in range(2):

        @pl.when(at.core == core)
        def _():
            run(core)


def scatter_all(mesh_shape, parts, collective_id=1):
    rows, inner = mesh_shape["dp"], mesh_shape["fsdp"]
    depths = 4
    sides = inner // (2 * depths)
    total = rows * inner
    half = total // 2
    count = len(parts)
    if rows == sides:
        thirds, seconds = (rows - 1, sides * depths), (sides - 1, depths)
    else:
        wide = max(rows, sides)
        thirds, seconds = (wide - 1, wide * depths), (wide - 1, depths)
    scratch = []
    for lead in ((half,), (half,), thirds, seconds, (depths - 1,)):
        scratch += [pltpu.VMEM(lead + p.shape[1:], p.dtype) for p in parts]
    parts = [p.reshape((half, 2) + p.shape[1:]) for p in parts]
    sems = [
        (), (), (half,), thirds, thirds, seconds, seconds, (depths - 1,), (depths - 1,),
    ]
    return pl.pallas_call(
        functools.partial(scatter_kernel, rows, depths, sides, count),
        out_shape=[jax.ShapeDtypeStruct(p.shape[2:], jnp.float32) for p in parts],
        in_specs=[ANY] * count,
        out_specs=[pl.BlockSpec(memory_space=pltpu.VMEM)] * count,
        scratch_shapes=scratch + [DMA((count,) + s) for s in sems],
        compiler_params=pltpu.CompilerParams(
            collective_id=collective_id, has_side_effects=True, vmem_limit_bytes=60 * 2**20
        ),
        name="scatter_grads",
    )(*parts)


def dot(left, right):
    return jnp.dot(left, right, preferred_element_type=F32)


def dot_nt(left, right):
    return lax.dot_general(left, right, (((1,), (1,)), ((), ())), preferred_element_type=F32)


def dot_tn(left, right):
    return lax.dot_general(left, right, (((0,), (0,)), ((), ())), preferred_element_type=F32)


def norm_parts(value):
    center = value - jnp.mean(value, axis=-1, keepdims=True)
    inv = lax.rsqrt(jnp.mean(center * center, axis=-1, keepdims=True) + EPSILON)
    return center * inv, inv


def norm_back(grad, hat, inv, gain):
    scaled = grad * gain
    return inv * (
        scaled
        - jnp.mean(scaled, axis=-1, keepdims=True)
        - hat * jnp.mean(scaled * hat, axis=-1, keepdims=True)
    )


GELU_ROOT = 0.7978845608028654


def gelu_parts(value):
    square = value * value
    inner = jnp.tanh(GELU_ROOT * value * (1.0 + 0.044715 * square))
    half = 0.5 * (1.0 + inner)
    slope = half + 0.5 * value * (1.0 - inner * inner) * (GELU_ROOT + 3 * 0.044715 * GELU_ROOT * square)
    return value * half, slope


def iota(shape, axis):
    return lax.broadcasted_iota(jnp.int32, shape, axis)


def wide(row):
    return jnp.broadcast_to(row, (16, row.shape[1])).astype(BF16)


def head_mask(width):
    return iota((16, width), 1) // (width // HEADS) == iota((16, width), 0)


def spread(row, mask):
    return jnp.where(mask, jnp.broadcast_to(row.astype(F32), mask.shape), 0.0).astype(BF16)


def collect(rows, mask):
    return jnp.sum(jnp.where(mask, rows, 0.0), axis=0, keepdims=True)


def row_softmax(spread_query, keys, place):
    score = dot_nt(spread_query, keys) * 0.125
    score = jnp.where(iota(score.shape, 1) <= place, score, NEG_FILL)
    expo = jnp.exp(score - jnp.max(score, axis=-1, keepdims=True))
    return expo / jnp.sum(expo, axis=-1, keepdims=True)


def pick_rows(first, array):
    chosen = iota((16, array.shape[0]), 1) == first + iota((16, array.shape[0]), 0)
    return dot(chosen.astype(F32).astype(BF16), array)


VECTORS = ("g1", "b1", "bp", "bo", "g2", "b2", "be", "bc")


class Vectors:
    def __init__(self, ref, width):
        self.ref, self.width = ref, width
        self.sizes = dict(bp=3 * width, be=4 * width)

    def __getattr__(self, name):
        return self.ref[VECTORS.index(name) : VECTORS.index(name) + 1, : self.sizes.get(name, self.width)]


def spread_vectors(pieces, sizes, width, vec_ref):
    count, offset = pieces.shape[0], 0
    vec_ref[...] = jnp.zeros_like(vec_ref)
    for row, (name, size) in enumerate(zip(VECTORS, sizes)):
        low, high = offset // 128 * 128, -(-(offset + size) // 128) * 128
        length = count * size
        lane = iota((1, length), 1)
        pick = iota((high - low, length), 0) == lane % size + (offset - low)
        tiled = dot(pieces[:, low:high], pick.astype(F32).astype(BF16))
        line = jnp.sum(jnp.where(iota((count, length), 0) == lane // size, tiled, 0.0), axis=0, keepdims=True)
        if name == "bp":
            vec_ref[row : row + 1, :width] = line[:, :width]
            vec_ref[row : row + 1, 2 * width : 3 * width] = line[:, width:]
        else:
            vec_ref[row : row + 1, :length] = line
        offset += size


def fetch(sources, targets, sems):
    copies = [pltpu.make_async_copy(s, t, sems.at[i]) for i, (s, t) in enumerate(zip(sources, targets))]
    for copy in copies:
        copy.start()
    return copies


def aligned(place):
    return pl.multiple_of(place // 16 * 16, 16)


def project_kernel(sizes, hidden_ref, pieces_ref, wp_ref, mixed_ref, normed_ref, vec_ref):
    seq, width = hidden_ref.shape
    spread_vectors(pieces_ref[:, 0, :], sizes, width, vec_ref)
    vec = Vectors(vec_ref, width)
    for at in range(0, seq, TILE):
        part = slice(at, at + TILE)
        normed = (norm_parts(hidden_ref[part].astype(F32))[0] * vec.g1 + vec.b1).astype(BF16)
        normed_ref[part] = normed
        mixed_ref[part] = (dot(normed, wp_ref[...]) + vec.bp).astype(BF16)


def smem():
    return pl.BlockSpec(memory_space=pltpu.SMEM)


def whole(array):
    return pl.BlockSpec(array.shape, lambda *_: (0,) * array.ndim, pipeline_mode=pl.Buffered(1))


def params(semantics=("arbitrary",)):
    return pltpu.CompilerParams(dimension_semantics=semantics, vmem_limit_bytes=VMEM_LIMIT)


def in_hbm():
    return pl.BlockSpec(memory_space=pl.ANY)


def project(hidden, pieces, sizes, weight):
    seq, width = hidden.shape
    outs = [
        jax.ShapeDtypeStruct((seq, 3 * width), BF16),
        jax.ShapeDtypeStruct((seq, width), BF16),
        jax.ShapeDtypeStruct((8, 4 * width), F32),
    ]
    return pl.pallas_call(
        functools.partial(project_kernel, sizes),
        grid=(1,),
        out_shape=outs,
        in_specs=[whole(hidden), whole(pieces), whole(weight)],
        out_specs=[whole(o) for o in outs],
        compiler_params=params(),
        name="project",
    )(hidden, pieces, weight)


def pair_spec(seq, offset, lanes=128):
    return pl.BlockSpec((seq, lanes), lambda i: (0, offset + i))


def attend_back_kernel(query_ref, key_ref, value_ref, up_ref, log_ref, dq_ref, dk_ref, dv_ref, dk_sum, dv_sum):
    seq, lanes = query_ref.shape
    half = lanes // 2
    first_head = iota((TILE, lanes), 1) < half
    keys_t = key_ref[...].T
    for start in reversed(range(0, seq, TILE)):
        stop = start + TILE
        query = query_ref[start:stop].astype(F32) * 0.125
        upstream = up_ref[start:stop].astype(F32)
        outs = []
        for head in range(2):
            own = first_head if head == 0 else jnp.logical_not(first_head)
            masked = jnp.where(own, query, 0.0).astype(BF16)
            up_masked = jnp.where(own, upstream, 0.0).astype(BF16)
            score = dot_nt(key_ref[:stop], masked)
            hidden = iota((TILE, TILE), 0) > iota((TILE, TILE), 1)
            last = jnp.where(hidden, NEG_FILL, score[start:])
            score = jnp.concatenate([score[:start], last], 0) if start else last
            prob = jnp.exp(score - log_ref[head : head + 1, start:stop])
            prob_grad = dot_nt(value_ref[:stop], up_masked)
            inner = jnp.sum(prob * prob_grad, axis=0, keepdims=True)
            score_grad = (prob * (prob_grad - inner)).astype(BF16)
            dv = dot(prob.astype(BF16), up_masked)
            dk = dot(score_grad, masked)
            if stop == seq and head == 0:
                dv_sum[...] = dv
                dk_sum[...] = dk
            else:
                dv_sum[:stop] += dv
                dk_sum[:stop] += dk
            outs.append(dot(keys_t[:, :stop], score_grad)[head * half : (head + 1) * half])
        dq_ref[start:stop] = (jnp.concatenate(outs, 0).T * 0.125).astype(BF16)
    dk_ref[...] = dk_sum[...].astype(BF16)
    dv_ref[...] = dv_sum[...].astype(BF16)


def attend_back(mixed, upstream, log_total):
    seq, width = upstream.shape
    pairs = HEADS // 2
    out = jax.ShapeDtypeStruct((seq, width), BF16)
    return pl.pallas_call(
        attend_back_kernel,
        grid=(pairs,),
        out_shape=[out, out, out],
        in_specs=[
            pair_spec(seq, 0),
            pair_spec(seq, pairs),
            pair_spec(seq, 2 * pairs),
            pair_spec(seq, 0),
            pl.BlockSpec((None, 2, seq), lambda i: (i, 0, 0)),
        ],
        out_specs=[pair_spec(seq, 0)] * 3,
        scratch_shapes=[pltpu.VMEM((seq, 128), F32), pltpu.VMEM((seq, 128), F32)],
        compiler_params=params(),
        name="attend_back",
    )(mixed, mixed, mixed, upstream, log_total)


def tall(row):
    return jnp.concatenate([jnp.broadcast_to(row[i : i + 1], (16, row.shape[1])) for i in range(THOUGHTS)], 0)


def middle_kernel(
    start_ref, length_ref, hidden_ref, cot_ref, vec_ref,
    mixed_hbm, normed_hbm, wo_hbm, we_hbm, wc_hbm, wp_hbm,
    mixed_out, normed_out, x_out, context_out, log_ref, final_out, normed_two_out, active_out, dz_out, df_out,
    dh_out, dctx_out, sums_ref,
    mixed_ref, x_ref, context_ref, resid_ref, dh_ref, dctx_ref, dz_ref, normed_two_ref,
    wo_ref, we_ref, wc_ref, wp_ref, final_ref, active_ref, df_ref, edge_normed, edge_df,
    weight_sems, mixed_sems, tile_sems, out_sems, edge_sems,
):
    seq, width = hidden_ref.shape
    inner = we_ref.shape[1]
    copy = pltpu.make_async_copy
    first_rows = copy(mixed_hbm.at[:PREFIX], mixed_ref.at[:PREFIX], mixed_sems.at[0])
    first_rows.start()
    sources, targets = (wo_hbm, we_hbm, wc_hbm, wp_hbm), (wo_ref, we_ref, wc_ref, wp_ref)
    weights = fetch(sources, targets, weight_sems)
    other_rows = copy(mixed_hbm.at[PREFIX:], mixed_ref.at[PREFIX:], mixed_sems.at[1])
    other_rows.start()
    start = start_ref[0]
    base = aligned(start - 1)
    edge = pl.ds(base, 32)
    edge_row = base + iota((32, 1), 0)
    load_edge = copy(normed_hbm.at[edge], edge_normed, edge_sems.at[0])
    load_edge.start()
    vec = Vectors(vec_ref, width)
    mask = head_mask(width)
    queries, keys, values = (mixed_ref.at[:, i * width : (i + 1) * width] for i in range(3))
    first_keys, first_values = keys.at[:PREFIX], values.at[:PREFIX]
    for at in range(0, seq, TILE):
        x_ref[at : at + TILE] = hidden_ref[at : at + TILE].astype(F32)

    x_row = x_ref[pl.ds(start - 1, 1), :]
    first_rows.wait()
    query = pick_rows(start - 1, queries[:PREFIX])[0:1]
    load_edge.wait()
    for step in range(THOUGHTS):
        place = start - 1 + step
        prob = row_softmax(spread(query, mask), first_keys[...], place)
        context = collect(dot(prob.astype(BF16), first_values[...]), mask)
        if step == 0:
            weights[0].wait()
        resid = x_row + (dot(wide(context), wo_ref[...])[0:1] + vec.bo)
        normed = norm_parts(resid)[0] * vec.g2 + vec.b2
        if step == 0:
            weights[1].wait()
        pre = dot(wide(normed), we_ref[...])[0:1] + vec.be
        active = gelu_parts(pre)[0]
        if step == 0:
            weights[2].wait()
        x_row = resid + (dot(wide(active), wc_ref[...])[0:1] + vec.bc)
        normed = norm_parts(x_row)[0] * vec.g1 + vec.b1
        if step == 0:
            weights[3].wait()
        mixed_row = dot(wide(normed), wp_ref[...])[0:1] + vec.bp
        query = mixed_row[:, :width].astype(BF16)
        x_ref[pl.ds(place + 1, 1), :] = x_row
        window = pl.ds(aligned(place + 1), 16)
        here = aligned(place + 1) + iota((16, 1), 0) == place + 1
        mixed_ref[window, :] = jnp.where(here, mixed_row, mixed_ref[window, :].astype(F32)).astype(BF16)
        edge_normed[...] = jnp.where(edge_row == place + 1, normed, edge_normed[...].astype(F32)).astype(BF16)
    other_rows.wait()
    pending = [
        copy(mixed_ref.at[edge], mixed_out.at[edge], edge_sems.at[0]),
        copy(edge_normed, normed_out.at[edge], edge_sems.at[1]),
        copy(x_ref, x_out, out_sems.at[0]),
    ]
    for c in pending:
        c.start()

    half, block = 64, seq // 2
    first_head = iota((block, 128), 1) < half
    later = iota((block, block), 0) > iota((block, block), 1)
    for pair in range(HEADS // 2):
        columns = slice(pair * 128, pair * 128 + 128)
        values_t = values[:, columns].T
        for at in range(0, seq, block):
            stop = at + block
            query = queries[at:stop, columns].astype(F32) * 0.125
            scores = []
            for head in range(2):
                own = first_head if head == 0 else jnp.logical_not(first_head)
                score = dot_nt(keys[:stop, columns], jnp.where(own, query, 0.0).astype(BF16))
                last = jnp.where(later, NEG_FILL, score[at:])
                scores.append(jnp.concatenate([score[:at], last], 0) if at else last)
            peaks = [jnp.max(score, axis=0, keepdims=True) for score in scores]
            expos = [jnp.exp(score - peak) for score, peak in zip(scores, peaks)]
            totals = [jnp.sum(expo, axis=0, keepdims=True) for expo in expos]
            outs = []
            for head in range(2):
                out = dot(values_t[:, :stop], expos[head].astype(BF16)) * (1.0 / totals[head])
                outs.append(out[head * half : (head + 1) * half])
                log_ref[pair, head : head + 1, at:stop] = peaks[head] + jnp.log(totals[head])
            context_ref[at:stop, columns] = jnp.concatenate(outs, 0).T.astype(BF16)
    pending.append(copy(context_ref, context_out, out_sems.at[1]))
    pending[-1].start()

    sums_ref[...] = jnp.zeros_like(sums_ref)
    tiles = (final_ref, active_ref, df_ref)
    tile_outs = (final_out, active_out, df_out)

    def tile_copies(i):
        slot = i % 2
        rows = pl.ds(i * TILE, TILE)
        return [copy(t.at[slot], o.at[rows], tile_sems.at[slot, n]) for n, (t, o) in enumerate(zip(tiles, tile_outs))]

    for i in range(seq // TILE):
        slot = i % 2
        rows = slice(i * TILE, i * TILE + TILE)
        if i >= 2:
            for c in tile_copies(i - 2):
                c.wait()
        valid = i * TILE + iota((TILE, 1), 0) < length_ref[0]
        resid = x_ref[rows] + (dot(context_ref[rows], wo_ref[...]) + vec.bo)
        resid_ref[rows] = resid
        hat, inv = norm_parts(resid)
        normed = (hat * vec.g2 + vec.b2).astype(BF16)
        normed_two_ref[rows] = normed
        dout = jnp.where(valid, cot_ref[rows].astype(F32), 0.0)
        dz = dout.astype(BF16)
        dz_ref[rows] = dz
        total = jnp.zeros((TILE, width), F32)
        dc = jnp.zeros((TILE, width), F32)
        for at in range(0, inner, width):
            part = slice(at, at + width)
            value, slope = gelu_parts(dot(normed, we_ref[:, part]) + vec.be[:, part])
            value = value.astype(BF16)
            active_ref[slot, :, part] = value
            total = total + dot(value, wc_ref[part])
            df = (dot_nt(dz, wc_ref[part]) * slope).astype(BF16)
            df_ref[slot, :, part] = df
            dc = dc + dot_nt(df, we_ref[:, part])
        final_ref[slot] = jnp.where(valid, resid + (total + vec.bc), 0.0)
        dh = dout + norm_back(dc, hat, inv, vec.g2)
        dh_ref[rows] = dh
        dctx_ref[rows] = dot_nt(dh.astype(BF16), wo_ref[...]).astype(BF16)
        sums_ref[0:1] += jnp.sum(dc * hat, axis=0, keepdims=True)
        sums_ref[1:2] += jnp.sum(dc, axis=0, keepdims=True)
        for c in tile_copies(i):
            c.start()
    pending.append(copy(normed_two_ref, normed_two_out, out_sems.at[2]))
    pending[-1].start()

    masks = jnp.concatenate([mask] * THOUGHTS, 0)

    def split(rows):
        picked = jnp.where(masks, rows, 0.0)
        return jnp.concatenate(
            [jnp.sum(picked[16 * i : 16 * i + 16], axis=0, keepdims=True) for i in range(THOUGHTS)], 0
        )

    def spread_all(rows):
        return jnp.where(masks, tall(rows), 0.0).astype(BF16)

    behind = iota((16, seq), 1)
    logs = jnp.concatenate([log_ref[i] for i in range(HEADS // 2)] + [jnp.zeros((4, seq), F32)], 0)
    ones = mask.astype(F32).astype(BF16)
    delta = []
    for at in range(0, seq, TILE):
        product = dctx_ref[at : at + TILE].astype(F32) * context_ref[at : at + TILE].astype(F32)
        high = product.astype(BF16)
        delta.append(dot_nt(ones, high) + dot_nt(ones, (product - high.astype(F32)).astype(BF16)))
    delta = jnp.concatenate(delta, 1)
    key_rows = spread_all(pick_rows(start, first_keys[...]))
    value_rows = spread_all(pick_rows(start, first_values[...]))
    score = dot_nt(key_rows, queries[...])
    prob_grad = dot_nt(value_rows, dctx_ref[...])
    probs, grads = [], []
    for i in range(THOUGHTS):
        part = slice(16 * i, 16 * i + 16)
        prob = jnp.where(behind >= start + i, jnp.exp(0.125 * score[part] - logs), 0.0)
        probs.append(prob.astype(BF16))
        grads.append((prob * (prob_grad[part] - delta)).astype(BF16))
    main_dk = split(dot(jnp.concatenate(grads, 0), queries[...])) * 0.125
    main_dv = split(dot(jnp.concatenate(probs, 0), dctx_ref[...]))

    def row_back(query, up, place):
        score = dot_nt(query, first_keys[...]) * 0.125
        score = jnp.where(iota(score.shape, 1) <= place, score, NEG_FILL)
        expo = jnp.exp(score - jnp.max(score, axis=-1, keepdims=True))
        prob = expo / jnp.sum(expo, axis=-1, keepdims=True)
        prob_grad = dot_nt(up, first_values[...])
        grad = (prob * (prob_grad - jnp.sum(prob * prob_grad, axis=-1, keepdims=True))).astype(BF16)
        return prob.astype(BF16), grad, dot(grad, first_keys[...]) * 0.125

    places = start + iota((16 * THOUGHTS, 1), 0) // 16
    up = spread_all(pick_rows(start, dctx_ref[:PREFIX]))
    main_dq = split(row_back(spread_all(pick_rows(start, queries[:PREFIX])), up, places)[2])
    query_rows = pick_rows(start - 1, queries[:PREFIX])
    rows = [start - 1 + step for step in range(THOUGHTS)]
    resid = jnp.concatenate([resid_ref[pl.ds(p, 1), :] for p in rows] + [jnp.zeros((13, width), F32)], 0)
    resid_hat, resid_inv = norm_parts(resid)
    normed = (resid_hat * vec.g2 + vec.b2).astype(BF16)
    slopes = gelu_parts(dot(normed, we_ref[...]) + vec.be)[1]
    for i in range(seq // TILE - 2, seq // TILE):
        for c in tile_copies(i):
            c.wait()
    load_edge = copy(df_out.at[edge], edge_df, edge_sems.at[2])
    load_edge.start()
    scores, spreads, probs, ups, df_rows = [], [], [], [], []
    dq_add = jnp.zeros((1, width), F32)
    for step in reversed(range(THOUGHTS)):
        place = rows[step]
        dq_row = main_dq[step : step + 1] + dq_add
        dk_row, dv_row = main_dk[step : step + 1], main_dv[step : step + 1]
        for score, query, prob, up in zip(scores, spreads, probs, ups):
            chosen = iota(score.shape, 1) == place + 1
            share = jnp.sum(jnp.where(chosen, score.astype(F32), 0.0), axis=1, keepdims=True)
            dk_row = dk_row + 0.125 * jnp.sum(share * query.astype(F32), axis=0, keepdims=True)
            share = jnp.sum(jnp.where(chosen, prob.astype(F32), 0.0), axis=1, keepdims=True)
            dv_row = dv_row + jnp.sum(share * up.astype(F32), axis=0, keepdims=True)
        x_hat, x_inv = norm_parts(x_ref[pl.ds(place + 1, 1), :])
        da = dot_nt(wide(jnp.concatenate([dq_row, dk_row, dv_row], 1)), wp_ref[...])
        dz = dh_ref[pl.ds(place + 1, 1), :] + norm_back(da[0:1], x_hat, x_inv, vec.g1)
        df = dot_nt(wide(dz), wc_ref[...])[0:1] * slopes[step : step + 1]
        dc = dot_nt(wide(df), we_ref[...])[0:1]
        hat, inv = resid_hat[step : step + 1], resid_inv[step : step + 1]
        dh = dz + norm_back(dc, hat, inv, vec.g2)
        sums_ref[0:1] += dc * hat
        sums_ref[1:2] += dc
        dctx = dot_nt(wide(dh), wo_ref[...])[0:1]
        query, up = spread(query_rows[step : step + 1], mask), spread(dctx, mask)
        if step:
            prob, score, dq = row_back(query, up, place)
            dq_add = collect(dq, mask)
            scores.append(score)
            spreads.append(query)
            probs.append(prob)
            ups.append(up)
        dh_ref[pl.ds(place, 1), :] += dh
        df_rows.append(df)
        for target, row in ((dz_ref, dz), (dctx_ref, dctx)):
            row = jnp.where(edge_row == place, row, 0.0)
            target[edge, :] = (target[edge, :].astype(F32) + row).astype(BF16)
    load_edge.wait()
    added = sum(jnp.where(edge_row == p, df, 0.0) for p, df in zip(reversed(rows), df_rows))
    edge_df[...] = (edge_df[...].astype(F32) + added).astype(BF16)
    last = [
        copy(edge_df, df_out.at[edge], edge_sems.at[2]),
        copy(dz_ref, dz_out, out_sems.at[3]),
        copy(dctx_ref, dctx_out, out_sems.at[4]),
        copy(dh_ref, dh_out, out_sems.at[5]),
    ]
    for c in last:
        c.start()
    for c in pending + last:
        c.wait()


def middle(start, length, hidden, cotangent, vec, mixed, normed, weights):
    seq, width = hidden.shape
    inner = weights[1].shape[1]
    shape = jax.ShapeDtypeStruct
    flat, pairs = (seq, width), (HEADS // 2, 2, seq)
    outs = [
        (mixed.shape, BF16), (flat, BF16), (flat, F32), (flat, BF16), (pairs, F32), (flat, F32), (flat, BF16),
        ((seq, inner), BF16), (flat, BF16), ((seq, inner), BF16), (flat, F32), (flat, BF16), ((8, width), F32),
    ]
    whole_vmem = pl.BlockSpec(memory_space=pltpu.VMEM)
    out_specs = [whole_vmem if i in (4, 12) else in_hbm() for i in range(len(outs))]
    kept = [
        (mixed.shape, BF16), (flat, F32), (flat, BF16), (flat, F32), (flat, F32), (flat, BF16), (flat, BF16), (flat, BF16),
    ]
    tiles = [((2, TILE, width), F32), ((2, TILE, inner), BF16), ((2, TILE, inner), BF16)]
    edges = [((32, width), BF16), ((32, inner), BF16)]
    buffers = kept + [(w.shape, w.dtype) for w in weights] + tiles + edges
    return pl.pallas_call(
        middle_kernel,
        out_shape=[shape(*o) for o in outs],
        in_specs=[smem(), smem()] + [whole_vmem] * 3 + [in_hbm()] * (2 + len(weights)),
        out_specs=out_specs,
        scratch_shapes=[pltpu.VMEM(*b) for b in buffers]
        + [DMA((4,)), DMA((2,)), DMA((2, 3)), DMA((6,)), DMA((3,))],
        input_output_aliases={5: 0, 6: 1},
        compiler_params=pltpu.CompilerParams(vmem_limit_bytes=VMEM_LIMIT),
        name="middle",
    )(start, length, hidden, cotangent, vec, mixed, normed, *weights)


class Refs:
    def __init__(self, names, refs):
        self.__dict__.update(zip(names, refs))


MESH = dict(device_id_type=pl.DeviceIdType.MESH)


class Stream:
    def __init__(self, at, side_first, name, refs):
        self.at, self.side_first = at, side_first
        for field in STREAM_FIELDS:
            setattr(self, field, getattr(refs, field + str(name)))
        self.sizes = (at.rows, at.sides) if side_first else (at.sides, at.rows)
        self.mine = (at.row, at.side) if side_first else (at.side, at.row)
        self.sent = []

    def spot(self, second, third):
        return (second, third) if self.side_first else (third, second)

    def unit(self, second, third, depth):
        row, side = self.spot(second, third)
        return (row * self.at.depths + depth) * self.at.sides + side

    def remote(self, source, target, send, recv, peer):
        return pltpu.make_async_remote_copy(
            src_ref=source, dst_ref=target, send_sem=send, recv_sem=recv, device_id=peer, **MESH
        )

    def sibling(self):
        return self.at.device(self.at.row, self.at.depth, self.at.side, 1 - self.at.core)

    def pair_copy(self, u, source):
        return self.remote(source, self.pair.at[u], self.pair_send.at[u], self.pair_recv.at[u], self.sibling())

    def third_copy(self, u, k, q):
        peer = self.at.device(*self.place(self.mine[0], (self.mine[1] + k) % self.sizes[1], self.at.depth))
        return self.remote(
            self.held.at[u], self.third.at[k - 1, q], self.third_send.at[k - 1, q], self.third_recv.at[k - 1, q], peer
        )

    def second_copy(self, u, k, depth):
        peer = self.at.device(*self.place((self.mine[0] + k) % self.sizes[0], self.mine[1], self.at.depth))
        return self.remote(
            self.held.at[u],
            self.second.at[k - 1, depth],
            self.second_send.at[k - 1, depth],
            self.second_recv.at[k - 1, depth],
            peer,
        )

    def depth_copy(self, u, k):
        peer = self.at.device(*self.place(*self.mine, (self.at.depth + k) % self.at.depths))
        return self.remote(
            self.held.at[u], self.depth.at[k - 1], self.depth_send.at[k - 1], self.depth_recv.at[k - 1], peer
        )

    def place(self, second, third, depth):
        row, side = self.spot(second, third)
        return row, depth, side, self.at.core

    def third_step(self, k, j, d, source):
        depths = self.at.depths
        second, depth = (self.mine[0] + j) % self.sizes[0], (self.at.depth + d) % depths
        q = second * depths + depth
        u = self.unit(second, (self.mine[1] + k) % self.sizes[1], depth)
        own = source(u)
        self.pair_copy(u, own).wait_recv()
        self.held[u] = own[...] + self.pair[u]
        if k:
            self.third_copy(u, k, q).start()

    def second_step(self, d):
        depth = (self.at.depth + d) % self.at.depths
        for k in list(range(1, self.sizes[0])) + [0]:
            second = (self.mine[0] + k) % self.sizes[0]
            u = self.unit(second, self.mine[1], depth)
            q = second * self.at.depths + depth
            for j in range(1, self.sizes[1]):
                self.third_copy(u, j, q).wait_recv()
                self.held[u] = self.held[u] + self.third[j - 1, q]
            if k:
                self.second_copy(u, k, depth).start()

    def depth_step(self, k):
        depth = (self.at.depth + k) % self.at.depths
        u = self.unit(*self.mine, depth)
        for j in range(1, self.sizes[0]):
            self.second_copy(u, j, depth).wait_recv()
            self.held[u] = self.held[u] + self.second[j - 1, depth]
        if k:
            self.depth_copy(u, k).start()

    def total(self):
        u = self.unit(*self.mine, self.at.depth)
        total = self.held[u].astype(F32)
        for k in range(1, self.at.depths):
            self.depth_copy(u, k).wait_recv()
            total = total + self.depth[k - 1].astype(F32)
        return total

    def drain(self):
        count = self.sizes[0] * self.at.depths
        for k in range(1, self.sizes[1]):
            loop(count, lambda q, k=k: self.third_copy(0, k, q).wait_send())
        for k in range(1, self.sizes[0]):
            loop(self.at.depths, lambda d, k=k: self.second_copy(0, k, d).wait_send())
        for k in range(1, self.at.depths):
            self.depth_copy(0, k).wait_send()


def loop(size, body):
    lax.fori_loop(0, size, lambda i, c: (body(i), c)[1], 0)


STREAM_FIELDS = (
    "held", "pair", "third", "second", "depth",
    "pair_send", "pair_recv", "third_send", "third_recv", "second_send", "second_recv", "depth_send", "depth_recv",
)


def stream_scratch(rows, depths, sides, side_first, shape):
    second, third = (rows, sides) if side_first else (sides, rows)
    half = rows * depths * sides
    leads = ((half,), (half,), (third - 1, second * depths), (second - 1, depths), (depths - 1,))
    buffers = [pltpu.VMEM(lead + shape, BF16) for lead in leads]
    sems = [DMA((half,)), DMA((half,))] + [DMA(lead) for lead in leads[2:] for _ in range(2)]
    return buffers + sems


CON, EX0, EX1, OUT, PR0, PR1 = range(6)
SIDE_FIRST = (False, True, True, False, True, False)


FIRST_PAIRS = 4
CHUNK_SLOTS = 4
CHUNK, SQUARE, ATTN, ROWS, SMALL, THIRD, SECOND, DEPTH = range(8)
SCHEDULE = (
    (CHUNK, 1, 1), (CHUNK, 1, 3), (SQUARE, EX0), (THIRD, CON, 1, 1), (THIRD, CON, 1, 3), (CHUNK, 0, 1),
    (THIRD, EX0, 1, 0), (THIRD, EX0, 1, 1), (ATTN, 0, 0), (THIRD, EX0, 0, 0), (THIRD, EX0, 0, 1), (ATTN, 0, 1),
    (THIRD, CON, 0, 1), (CHUNK, 1, 2), (CHUNK, 0, 3), (ATTN, 0, 2), (SECOND, CON, 1), (THIRD, CON, 1, 2),
    (SQUARE, EX1), (THIRD, CON, 0, 3), (SECOND, EX0, 0), (SECOND, EX0, 1), (CHUNK, 1, 0), (THIRD, EX1, 1, 0),
    (THIRD, EX1, 1, 1), (SECOND, CON, 3), (SECOND, EX0, 2), (ATTN, 0, 3), (THIRD, EX1, 0, 0), (SECOND, EX0, 3),
    (ATTN, 1, 0), (THIRD, EX1, 0, 1), (THIRD, CON, 1, 0), (ATTN, 1, 1), (DEPTH, CON, 1), (ATTN, 1, 2), (ATTN, 1, 3),
    (ATTN, 2, 0), (ATTN, 2, 1), (DEPTH, EX0, 0), (ATTN, 2, 2), (ATTN, 2, 3), (DEPTH, EX0, 1), (ATTN, 3, 0),
    (DEPTH, EX0, 2), (ATTN, 3, 1), (ATTN, 3, 2), (SECOND, EX1, 0), (DEPTH, EX0, 3), (ATTN, 3, 3), (SQUARE, PR0),
    (SECOND, EX1, 1), (SECOND, EX1, 2), (SECOND, EX1, 3), (ATTN, 4, 0), (THIRD, PR0, 1, 0), (THIRD, PR0, 1, 1),
    (DEPTH, CON, 3), (THIRD, PR0, 0, 0), (DEPTH, EX1, 0), (SQUARE, OUT), (THIRD, PR0, 0, 1), (DEPTH, EX1, 1),
    (THIRD, OUT, 1, 0), (DEPTH, EX1, 2), (THIRD, OUT, 1, 1), (DEPTH, EX1, 3), (THIRD, OUT, 0, 0), (CHUNK, 0, 2),
    (THIRD, OUT, 0, 1), (ATTN, 4, 1), (ATTN, 4, 2), (THIRD, CON, 0, 2), (SECOND, CON, 2), (CHUNK, 0, 0),
    (SECOND, OUT, 0), (SECOND, PR0, 0), (ATTN, 4, 3), (SECOND, OUT, 1), (SECOND, PR0, 1), (ATTN, 5, 0),
    (THIRD, CON, 0, 0), (SECOND, CON, 0), (SECOND, OUT, 2), (SECOND, OUT, 3), (SECOND, PR0, 2), (ATTN, 5, 1),
    (SECOND, PR0, 3), (DEPTH, PR0, 0), (ATTN, 5, 2), (ATTN, 5, 3), (DEPTH, PR0, 1), (SQUARE, PR1), (DEPTH, CON, 2),
    (DEPTH, OUT, 1), (THIRD, PR1, 1, 0), (THIRD, PR1, 1, 1), (THIRD, PR1, 0, 0), (DEPTH, OUT, 0), (DEPTH, PR0, 2),
    (DEPTH, PR0, 3), (THIRD, PR1, 0, 1), (ROWS, 0), (DEPTH, CON, 0), (ROWS, 1), (DEPTH, OUT, 2), (SECOND, PR1, 0),
    (DEPTH, OUT, 3), (ROWS, 2), (SECOND, PR1, 1), (SECOND, PR1, 2), (SECOND, PR1, 3), (DEPTH, PR1, 0), (ROWS, 3),
    (DEPTH, PR1, 1), (SMALL,), (DEPTH, PR1, 2), (DEPTH, PR1, 3),
)


def finish_kernel(mesh_shape, sizes, names, *refs):
    r = Refs(names, refs)
    rows, inner = mesh_shape["dp"], mesh_shape["fsdp"]
    depths = 4
    sides = inner // (2 * depths)
    total = rows * inner
    half = total // 2
    at = Place(rows, depths, sides)
    seq, width = r.dz.shape
    groups = (FIRST_PAIRS * 128, width - FIRST_PAIRS * 128)
    core = at.core
    me = at.row * inner + lax.axis_index("fsdp")
    piece = width // total
    vec = Vectors(r.vec, width)

    copies = {}

    def load(key, source, target, sem):
        copies[key] = pltpu.make_async_copy(source, target, sem)
        copies[key].start()

    def ready(key):
        copies.pop(key).wait()

    chunks = [step[1:] for step in SCHEDULE if step[0] == CHUNK]
    span = sides * 2 * piece * 4

    def load_active(i):
        k, d = chunks[i]
        first = ((at.row + k) % rows * depths + (at.depth + d) % depths) * span
        columns = pl.ds(pl.multiple_of(first, 128), span)
        load(("act", i), r.active.at[:, columns], r.act.at[i % 2], r.act_sem.at[i % 2])

    load_active(0)
    load_active(1)
    load("normed", r.normed, r.normedv, r.in_sem.at[0])
    load("df0", r.df.at[:, : 2 * width], r.dfs.at[0], r.df_sem.at[0])
    load("df1", r.df.at[:, 2 * width :], r.dfs.at[1], r.df_sem.at[1])
    load("dh", r.dh, r.dhv, r.dh_sem)
    load("context", r.context, r.contextv, r.in_sem.at[1])
    load("first", r.first_normed, r.firstv, r.in_sem.at[2])
    load("wp", r.wp, r.wpv, r.wp_sem)

    def load_pair(p):
        slot = p % 2
        for i in range(3):
            columns = pl.ds(i * width + p * 128, 128)
            load(("pair", p, i), r.mixed.at[:, columns], r.qkv.at[slot, i], r.qkv_sem.at[slot, i])
        load(("pair", p, 3), r.dctx.at[:, pl.ds(p * 128, 128)], r.qkv.at[slot, 3], r.qkv_sem.at[slot, 3])

    load_pair(0)

    barrier = pltpu.get_barrier_semaphore()

    def other(k):
        index = (me + k) % total
        return {"dp": index // inner, "fsdp": index % inner}

    loop(total - 1, lambda i: pl.semaphore_signal(barrier, inc=1, device_id=other(i + 1), **MESH))
    pl.semaphore_wait(barrier, total - 1)

    streams = {name: Stream(at, side_first, name, r) for name, side_first in enumerate(SIDE_FIRST)}
    con = streams[CON]
    ones = jnp.ones((16, seq), BF16)
    sums = {}

    def chunk(k, d):
        i = chunks.index((k, d))
        ready(("act", i))
        slot = i % CHUNK_SLOTS
        if i >= CHUNK_SLOTS:
            con_sent(i - CHUNK_SLOTS)
        grad = dot_tn(r.act[i % 2], r.dz[...])
        if i + 2 < len(chunks):
            load_active(i + 2)
        r.con_stage[slot] = grad.reshape(sides, 2, 4 * piece, width).astype(BF16)
        for side in range(sides):
            con.pair_copy(con_unit(i, side), r.con_stage.at[slot, side, 1 - core]).start()

    def con_unit(i, side):
        k, d = chunks[i]
        return ((at.row + k) % rows * depths + (at.depth + d) % depths) * sides + side

    def con_sent(i):
        for side in range(sides):
            con.pair_copy(con_unit(i, side), r.con_stage.at[i % CHUNK_SLOTS, side, 1 - core]).wait_send()

    def con_third(k, d):
        slot = chunks.index((k, d)) % CHUNK_SLOTS
        for j in list(range(1, sides)) + [0]:
            side = (at.side + j) % sides
            con.third_step(k, j, d, lambda u: r.con_stage.at[slot, side, core])

    slots = {}

    def square(name, left, right):
        columns = right.shape[1]
        slot = len(slots) % 2
        previous = [n for n, s in slots.items() if s == slot]
        if previous:
            stage_sent(previous[-1])
        slots[name] = slot
        quarter = width // 4
        for part in range(4):
            grad = dot_tn(left[:, part * quarter : (part + 1) * quarter], right[...])
            target = r.stage.at[slot, part * half // 4 : (part + 1) * half // 4, :, :, :columns]
            target[...] = grad.reshape(half // 4, 2, piece, columns).astype(BF16)
        stream = streams[name]
        for k in list(range(1, stream.sizes[1])) + [0]:
            for j in list(range(1, stream.sizes[0])) + [0]:

                def start(d, k=k, j=j):
                    second, third = ((m + n) % z for m, n, z in zip(stream.mine, (j, k), stream.sizes))
                    u = stream.unit(second, third, (at.depth + d) % depths)
                    stream.pair_copy(u, stage_at(name, u, 1 - core, columns)).start()

                loop(depths, start)

    def stage_at(name, u, which, columns):
        return r.stage.at[slots[name], u, which, :, :columns]

    def columns_of(name):
        return streams[name].held.shape[-1]

    def stage_sent(name):
        stream = streams[name]
        loop(half, lambda u: stream.pair_copy(u, stage_at(name, u, 1 - core, columns_of(name))).wait_send())

    def square_third(name, k, j):
        stream = streams[name]
        source = lambda u: stage_at(name, u, core, columns_of(name))
        loop(depths, lambda d: stream.third_step(k, j, d, source))

    def expand(e):
        if e == 0:
            ready("normed")
        ready("df%d" % e)
        square(EX0 + e, r.normedv, r.dfs.at[e])
        sums["be%d" % e] = dot(ones, r.dfs[e])[0:1]

    def output():
        ready("dh")
        ready("context")
        r.dy[...] = r.dhv[...].astype(BF16)
        square(OUT, r.contextv, r.dy)
        sums["bo"] = dot(ones, r.dy[...])[0:1]
        sums["bc"] = dot(ones, r.dz[...])[0:1]

    later = iota((TILE, TILE), 0) > iota((TILE, TILE), 1)
    later = jnp.concatenate([later, later], 1)
    first_head = iota((TILE, 128), 1) < 64

    def two(value):
        parts = [jnp.where(first_head, value, 0.0), jnp.where(first_head, 0.0, value)]
        return jnp.concatenate(parts, 0).astype(BF16)

    def attend_block(p, n):
        block = seq // TILE - 1 - n
        slot = p % 2
        if n == 0:
            for i in range(4):
                ready(("pair", p, i))
            if p + 1 < HEADS // 2:
                load_pair(p + 1)
            r.keys_t[...] = r.qkv[slot, 1].T
        query_ref, key_ref, value_ref, up_ref = (r.qkv.at[slot, i] for i in range(4))
        start, stop = block * TILE, block * TILE + TILE
        query = two(query_ref[start:stop].astype(F32) * 0.125)
        upstream = two(up_ref[start:stop].astype(F32))
        score = dot_nt(key_ref[:stop], query)
        edge = jnp.where(later, NEG_FILL, score[start:])
        score = jnp.concatenate([score[:start], edge], 0) if start else edge
        logs = jnp.concatenate([r.logs[p, 0:1, start:stop], r.logs[p, 1:2, start:stop]], 1)
        prob = jnp.exp(score - logs)
        prob_grad = dot_nt(value_ref[:stop], upstream)
        mean = jnp.sum(prob * prob_grad, axis=0, keepdims=True)
        score_grad = (prob * (prob_grad - mean)).astype(BF16)
        dv = dot(prob.astype(BF16), upstream)
        dk = dot(score_grad, query)
        if n == 0:
            r.dv_sum[...] = dv
            r.dk_sum[...] = dk
        else:
            r.dv_sum[:stop] += dv
            r.dk_sum[:stop] += dk
        out = dot(r.keys_t[:, :stop], score_grad)
        out = jnp.concatenate([out[:64, :TILE], out[64:, TILE:]], 0)
        g = int(p >= FIRST_PAIRS)
        target, group = r.dfs.at[g], groups[g]
        column = (p - g * FIRST_PAIRS) * 128
        target[start:stop, column : column + 128] = (out.T * 0.125).astype(BF16)
        if block == 0:
            target[:, group + column : group + column + 128] = r.dk_sum[...].astype(BF16)
            target[:, 2 * group + column : 2 * group + column + 128] = r.dv_sum[...].astype(BF16)

    def project_grad(g):
        if g == 0:
            ready("first")
        right = r.dfs.at[g, :, : 3 * groups[g]]
        square(PR0 + g, r.firstv, right)
        sums["bp%d" % g] = dot(ones, right[...])[0:1]

    def project_columns(g, n):
        first = n * width + g * groups[0]
        return slice(first, first + groups[g])

    def load_tile(i):
        load(("x", i), r.x.at[pl.ds(i * TILE, TILE)], r.xs.at[i % 2], r.x_sem.at[i % 2])

    def tile(i):
        if i == 0:
            ready("wp")
            load_tile(0)
            load_tile(1)
        ready(("x", i))
        part = slice(i * TILE, i * TILE + TILE)
        da = jnp.zeros((TILE, width), F32)
        for g in range(2):
            for n in range(3):
                da = da + dot_nt(r.dfs[g, part, n * groups[g] : (n + 1) * groups[g]], r.wpv[:, project_columns(g, n)])
        hat, inv = norm_parts(r.xs[i % 2])
        if i + 2 < seq // TILE:
            load_tile(i + 2)
        position = i * TILE + iota((TILE, 1), 0)
        kept = (position < r.start[0]) | (position >= r.start[0] + THOUGHTS)
        if i >= 2:
            ready(("dx", i - 2))
        r.dxs[i % 2] = jnp.where(kept, r.dhv[part] + norm_back(da, hat, inv, vec.g1), 0.0)
        load(("dx", i), r.dxs.at[i % 2], r.hidden_grad.at[pl.ds(i * TILE, TILE)], r.dx_sem.at[i % 2])
        gain, bias = jnp.sum(da * hat, axis=0, keepdims=True), jnp.sum(da, axis=0, keepdims=True)
        sums["g1"] = gain if i == 0 else sums["g1"] + gain
        sums["b1"] = bias if i == 0 else sums["b1"] + bias

    def small_start():
        group_of = lambda n: jnp.concatenate(
            [sums["bp%d" % g][:, n * groups[g] : (n + 1) * groups[g]] for g in range(2)], 1
        )
        lines = dict(
            g1=sums["g1"], b1=sums["b1"], bp=jnp.concatenate([group_of(0), group_of(2)], 1), bo=sums["bo"],
            g2=r.sums[0:1], b2=r.sums[1:2], be=jnp.concatenate([sums["be0"], sums["be1"]], 1), bc=sums["bc"],
        )
        offset = 0
        r.small_part[...] = jnp.zeros_like(r.small_part)
        for name, size in zip(VECTORS, sizes):
            low, high = offset // 128 * 128, -(-(offset + size) // 128) * 128
            length = total * size
            lane = iota((1, length), 1)
            pick = (iota((high - low, length), 0) == lane % size + (offset - low)).astype(F32).astype(BF16)
            rest = jnp.where(iota((total, length), 0) == lane // size, lines[name], 0.0)
            pieces = jnp.zeros((total, high - low), F32)
            for _ in range(2):
                rounded = rest.astype(BF16)
                pieces = pieces + dot_nt(rounded, pick)
                rest = rest - rounded.astype(F32)
            r.small_part[:, 0, low:high] += pieces
            offset += size
        loop(total - 1, lambda i: small_copy(i + 1).start())

    def small_copy(k):
        return pltpu.make_async_remote_copy(
            src_ref=r.small_part.at[(me + k) % total],
            dst_ref=r.small_in.at[k - 1],
            send_sem=r.small_send.at[k - 1],
            recv_sem=r.small_recv.at[k - 1],
            device_id=other(k),
            **MESH,
        )

    def small_end():
        loop(total - 1, lambda i: small_copy(i + 1).wait_recv())
        received = r.small_in[...]
        r.small_out[...] = r.small_part[me] + jnp.sum(received[: total - 1], axis=0)

    def work(kind, *what):
        if kind == CHUNK:
            chunk(*what)
        elif kind == ATTN:
            attend_block(*what)
        elif kind == ROWS:
            tile(*what)
        elif kind == SMALL:
            small_start()
        elif kind == SQUARE:
            name = what[0]
            if name == OUT:
                output()
            elif name in (EX0, EX1):
                expand(name - EX0)
            else:
                project_grad(name - PR0)
        elif kind == THIRD:
            name, k, j = what
            if name == CON:
                con_third(k, j)
            else:
                square_third(name, k, 1 - j)
        elif kind == SECOND:
            streams[what[0]].second_step(what[1])
        else:
            streams[what[0]].depth_step(what[1])

    for step in SCHEDULE:
        work(*step)
    r.contract_out[...] = con.total()
    r.expand_out[:, : 2 * width] = streams[EX0].total()
    r.expand_out[:, 2 * width :] = streams[EX1].total()
    r.output_out[...] = streams[OUT].total()
    for g in range(2):
        grad = streams[PR0 + g].total()
        for n in range(3):
            r.project_out[:, project_columns(g, n)] = grad[:, n * groups[g] : (n + 1) * groups[g]]
    small_end()
    ready(("dx", 2))
    ready(("dx", 3))
    for i in range(len(chunks) - CHUNK_SLOTS, len(chunks)):
        con_sent(i)
    for name in list(slots)[-2:]:
        stage_sent(name)
    for stream in streams.values():
        stream.drain()
    loop(total - 1, lambda i: small_copy(i + 1).wait_send())


def finish(mesh_shape, sizes, start, operands):
    rows, inner = mesh_shape["dp"], mesh_shape["fsdp"]
    depths = 4
    sides = inner // (2 * depths)
    total = rows * inner
    half = total // 2
    seq, width = operands["dz"].shape
    piece = width // total
    lanes = -(-sum(sizes) // 128) * 128
    in_vmem = ("dz", "logs", "vec", "sums")
    outs = dict(
        hidden_grad=(seq, width),
        contract_out=(4 * piece, width),
        expand_out=(piece, 4 * width),
        output_out=(piece, width),
        project_out=(piece, 3 * width),
        small_out=(1, lanes),
    )
    shapes = (
        (4 * piece, width), (piece, 2 * width), (piece, 2 * width), (piece, width),
        (piece, 3 * FIRST_PAIRS * 128), (piece, 3 * (width - FIRST_PAIRS * 128)),
    )
    span = sides * 2 * piece * 4
    scratch = dict(
        act=pltpu.VMEM((2, seq, span), BF16), act_sem=DMA((2,)),
        dfs=pltpu.VMEM((2, seq, 2 * width), BF16), df_sem=DMA((2,)),
        dhv=pltpu.VMEM((seq, width), F32), dh_sem=DMA(()),
        normedv=pltpu.VMEM((seq, width), BF16), contextv=pltpu.VMEM((seq, width), BF16),
        firstv=pltpu.VMEM((seq, width), BF16), in_sem=DMA((3,)),
        dy=pltpu.VMEM((seq, width), BF16),
        qkv=pltpu.VMEM((2, 4, seq, 128), BF16), qkv_sem=DMA((2, 4)),
        keys_t=pltpu.VMEM((128, seq), BF16),
        dk_sum=pltpu.VMEM((seq, 128), F32), dv_sum=pltpu.VMEM((seq, 128), F32),
        wpv=pltpu.VMEM((width, 3 * width), BF16), wp_sem=DMA(()),
        xs=pltpu.VMEM((2, TILE, width), F32), x_sem=DMA((2,)),
        dxs=pltpu.VMEM((2, TILE, width), F32), dx_sem=DMA((2,)),
        con_stage=pltpu.VMEM((CHUNK_SLOTS, sides, 2, 4 * piece, width), BF16),
        stage=pltpu.VMEM((2, half, 2, piece, 2 * width), BF16),
        small_part=pltpu.VMEM((total, 1, lanes), F32), small_in=pltpu.VMEM((total, 1, lanes), F32),
        small_send=DMA((total - 1,)), small_recv=DMA((total - 1,)),
    )
    for name, side_first in enumerate(SIDE_FIRST):
        fields = stream_scratch(rows, depths, sides, side_first, shapes[name])
        scratch.update({f + str(name): s for f, s in zip(STREAM_FIELDS, fields)})
    names = ("start",) + tuple(operands) + tuple(outs) + tuple(scratch)
    whole_vmem = pl.BlockSpec(memory_space=pltpu.VMEM)
    return pl.pallas_call(
        functools.partial(finish_kernel, mesh_shape, sizes, names),
        out_shape=[jax.ShapeDtypeStruct(s, F32) for s in outs.values()],
        in_specs=[smem()] + [whole_vmem if n in in_vmem else in_hbm() for n in operands],
        out_specs=[in_hbm()] + [whole_vmem] * 5,
        scratch_shapes=list(scratch.values()),
        compiler_params=pltpu.CompilerParams(collective_id=2, has_side_effects=True, vmem_limit_bytes=63 * 2**20),
        name="finish",
    )(start, *operands.values())


def deliver_kernel(sizes, *refs):
    count = (len(refs) - len(sizes) + 1) // 2
    sources, small, targets = refs[: count - 1], refs[count - 1], refs[count:]
    for source, target in zip(sources, targets):
        target[...] = source[...]
    offset = 0
    for size, target in zip(sizes, targets[len(sources) :]):
        target[...] = small[0, offset : offset + size]
        offset += size


def deliver(sizes, *arrays):
    seq, width = arrays[0].shape
    first = lambda i: (0, 0)
    rows = pl.BlockSpec((TILE, width), lambda i: (i, 0))
    fixed = [pl.BlockSpec(a.shape, first) for a in arrays[1:]]
    vectors = [jax.ShapeDtypeStruct((size,), F32) for size in sizes]
    return pl.pallas_call(
        functools.partial(deliver_kernel, sizes),
        grid=(seq // TILE,),
        out_shape=[jax.ShapeDtypeStruct(a.shape, F32) for a in arrays[:-1]] + vectors,
        in_specs=[rows] + fixed,
        out_specs=[rows] + fixed[:-1] + [pl.BlockSpec(v.shape, lambda i: (0,)) for v in vectors],
        compiler_params=params(),
        name="deliver",
    )(*arrays)


def pack(vectors, total):
    joined = jnp.concatenate([v.reshape(total, -1) for v in vectors], 1)
    fill = -joined.shape[1] % 128
    return jnp.pad(joined, ((0, 0), (0, fill)))[:, None]


def unpack(packed, sizes):
    flat = packed.reshape(-1, packed.shape[-1])
    out, at = [], 0
    for size in sizes:
        out.append(flat[:, at : at + size].reshape(-1))
        at += size
    return out


def per_device(
    mesh_shape,
    hidden,
    cotangent,
    lengths,
    thought_start,
    first_gain,
    first_bias,
    project_weight,
    project_bias,
    output_weight,
    output_bias,
    second_gain,
    second_bias,
    expand_weight,
    expand_bias,
    contract_weight,
    contract_bias,
):
    _, seq, width = hidden.shape
    total = mesh_shape["dp"] * mesh_shape["fsdp"]
    vectors = (
        first_gain,
        first_bias,
        project_bias,
        output_bias,
        second_gain,
        second_bias,
        expand_bias,
        contract_bias,
    )
    sizes = [v.shape[0] for v in vectors]
    full = gather_all(
        mesh_shape,
        (pack(vectors, 1)[0], project_weight, output_weight, expand_weight, contract_weight),
    )
    Wp, Wo, We, Wc = (w.reshape(-1, w.shape[-1]) for w in full[1:])

    mixed, normed, vec = project(hidden[0], full[0], sizes, Wp)
    (
        mixed, normed, x, context, log_total, final, normed_two, active, dz, df, dh, dctx, sums,
    ) = middle(thought_start, lengths, hidden[0], cotangent[0], vec, mixed, normed, (Wo, We, Wc, Wp))
    if width // total % 8 == 0:
        operands = dict(
            dz=dz, normed=normed_two, context=context, first_normed=normed, logs=log_total, vec=vec, sums=sums,
            active=active, df=df, dh=dh, mixed=mixed, dctx=dctx, x=x, wp=Wp,
        )
        hidden_grad, dWc, dWe, dWo, dWp, *small = deliver(sizes, *finish(mesh_shape, sizes, thought_start, operands))
        dg1, db1, dbp, dbo, dg2, db2, dbe, dbc = small
        return (final[None], hidden_grad[None], dg1, db1, dWp, dbp, dWo, dbo, dg2, db2, dWe, dbe, dWc, dbc)
    dq, dk, dv = attend_back(mixed, dctx, log_total)
    g1 = vec[0:1, :width]
    dy = dh.astype(BF16)
    x_hat, x_inv = norm_parts(x)
    dmixed = jnp.concatenate([dq, dk, dv], 1)
    da = dot_nt(dmixed, Wp)
    dx = dh + norm_back(da, x_hat, x_inv, g1)
    position = iota((seq, 1), 0)
    is_thought = (position >= thought_start[0]) & (position < thought_start[0] + THOUGHTS)
    hidden_grad = jnp.where(is_thought, 0.0, dx)

    def column_sum(value):
        return jnp.sum(value, axis=0, dtype=F32)

    column = column_sum(dmixed)
    small = (
        column_sum(da * x_hat),
        column_sum(da),
        jnp.concatenate([column[:width], column[2 * width :]]),
        column_sum(dy),
        sums[0],
        sums[1],
        column_sum(df),
        column_sum(dz),
    )
    large = (
        dot_tn(normed, dmixed),
        dot_tn(context, dy),
        dot_tn(normed_two, df),
        dot_tn(active, dz),
    )
    parts = [pack(small, total)]
    for grad in large:
        parts.append(grad.astype(BF16).reshape(total, grad.shape[0] // total, grad.shape[1]))
    small, dWp, dWo, dWe, dWc = scatter_all(mesh_shape, parts)
    dg1, db1, dbp, dbo, dg2, db2, dbe, dbc = unpack(small, sizes)
    return (final[None], hidden_grad[None], dg1, db1, dWp, dbp, dWo, dbo, dg2, db2, dWe, dbe, dWc, dbc)


def solution(mesh):
    rows = P(AXES, None, None)
    flat = P(AXES)
    square = P(AXES, None)
    specs = (flat, flat, square, flat, square, flat, flat, flat, square, flat, square, flat)
    return jax.shard_map(
        functools.partial(per_device, dict(mesh.shape)),
        mesh=mesh,
        in_specs=(rows, rows, flat, flat) + specs,
        out_specs=(rows, rows) + specs,
        check_vma=False,
    )
```

```python
import functools

import jax
import jax.numpy as jnp
from jax import lax
from jax.experimental import pallas as pl
from jax.experimental.pallas import tpu as pltpu
from jax.sharding import PartitionSpec as P

HEADS = 12
THOUGHTS = 3
PREFIX = 384
TILE = 256

EPSILON = 1e-05
NEG_FILL = -1e30
F32 = jnp.float32
BF16 = jnp.bfloat16
VMEM_LIMIT = 62 * 2**20


AXES = ("dp", "fsdp")
ANY = pl.BlockSpec(memory_space=pl.ANY)
DMA = pltpu.SemaphoreType.DMA


class Place:
    def __init__(self, rows, depths, sides):
        self.rows, self.depths, self.sides = rows, depths, sides
        self.row = lax.axis_index("dp")
        flat = lax.axis_index("fsdp")
        self.depth = flat // (sides * 2)
        self.side = flat // 2 % sides
        self.core = flat % 2

    def index(self, row, depth, side, core):
        return row * (self.depths * self.sides * 2) + (depth * self.sides + side) * 2 + core

    def device(self, row, depth, side, core):
        return {"dp": row, "fsdp": (depth * self.sides + side) * 2 + core}


def gather_kernel(rows, depths, sides, count, *refs):
    shards, fulls = refs[:count], refs[count : 2 * count]
    send_sem, recv_sem, pair_send, pair_recv, own_sem = refs[2 * count :]
    at = Place(rows, depths, sides)
    dev = dict(device_id_type=pl.DeviceIdType.MESH)

    barrier = pltpu.get_barrier_semaphore()
    peers = []
    for k in range(1, depths):
        peers.append(at.device(at.row, (at.depth + k) % depths, at.side, at.core))
    for k in range(1, sides):
        peers.append(at.device(at.row, at.depth, (at.side + k) % sides, at.core))
    for k in range(1, rows):
        peers.append(at.device((at.row + k) % rows, at.depth, at.side, at.core))
    peers.append(at.device(at.row, at.depth, at.side, 1 - at.core))
    for peer in peers:
        pl.semaphore_signal(barrier, inc=1, device_id=peer, **dev)
    pl.semaphore_wait(barrier, len(peers))

    def run(core):
        sends = []

        def index(row, depth, side):
            return at.index(row, depth, side, core)

        def send(w, source, shard, peer, slot):
            copy = pltpu.make_async_remote_copy(
                src_ref=source,
                dst_ref=fulls[w].at[shard],
                send_sem=send_sem.at[w, slot],
                recv_sem=recv_sem.at[w, shard],
                device_id=peer,
                **dev,
            )
            copy.start()
            sends.append(copy)

        def arrive(w, shard):
            pltpu.make_async_remote_copy(
                src_ref=fulls[w].at[shard],
                dst_ref=fulls[w].at[shard],
                send_sem=send_sem.at[w, 0],
                recv_sem=recv_sem.at[w, shard],
                device_id=peers[0],
                **dev,
            ).wait_recv()

        def to_pair(w, source, shard):
            copy = pltpu.make_async_remote_copy(
                src_ref=source,
                dst_ref=fulls[w].at[shard],
                send_sem=pair_send.at[w, shard // 2],
                recv_sem=pair_recv.at[w, shard // 2],
                device_id=at.device(at.row, at.depth, at.side, 1 - core),
                **dev,
            )
            copy.start()
            sends.append(copy)

        slots = [0] * count

        def slot(w):
            slots[w] += 1
            return slots[w] - 1

        second_size, third_size = (sides, rows) if core == 0 else (rows, sides)

        def spot(second, third):
            return (third, second) if core == 0 else (second, third)

        mine = (at.side, at.row) if core == 0 else (at.row, at.side)

        def forward_second(w, source, depth):
            row, side = spot(*mine)
            for k in range(1, second_size):
                r, s = spot((mine[0] + k) % second_size, mine[1])
                send(w, source, index(row, depth, side), at.device(r, at.depth, s, core), slot(w))

        def forward_third(w, source, depth, second):
            row, side = spot(second, mine[1])
            for k in range(1, third_size):
                r, s = spot(mine[0], (mine[1] + k) % third_size)
                send(w, source, index(row, depth, side), at.device(r, at.depth, s, core), slot(w))

        own = []
        for w in range(count):
            me = index(at.row, at.depth, at.side)
            for k in range(1, depths):
                send(w, shards[w], me, at.device(at.row, (at.depth + k) % depths, at.side, core), slot(w))
            forward_second(w, shards[w], at.depth)
            forward_third(w, shards[w], at.depth, mine[0])
            to_pair(w, shards[w], me)
            copy = pltpu.make_async_copy(shards[w], fulls[w].at[me], own_sem.at[w])
            copy.start()
            own.append(copy)

        def stage_one(w):
            for k in range(1, depths):
                depth = (at.depth - k) % depths
                shard = index(at.row, depth, at.side)
                arrive(w, shard)
                forward_second(w, fulls[w].at[shard], depth)
                forward_third(w, fulls[w].at[shard], depth, mine[0])
                to_pair(w, fulls[w].at[shard], shard)

        def stage_two(w):
            for k in range(1, second_size):
                second = (mine[0] - k) % second_size
                for d in range(depths):
                    depth = (at.depth - d) % depths
                    shard = index(spot(second, mine[1])[0], depth, spot(second, mine[1])[1])
                    arrive(w, shard)
                    forward_third(w, fulls[w].at[shard], depth, second)
                    to_pair(w, fulls[w].at[shard], shard)

        def stage_three(w):
            for k in range(1, third_size):
                third = (mine[1] - k) % third_size
                for s in range(second_size):
                    second = (mine[0] - s) % second_size
                    for d in range(depths):
                        depth = (at.depth - d) % depths
                        row, side = spot(second, third)
                        shard = index(row, depth, side)
                        arrive(w, shard)
                        to_pair(w, fulls[w].at[shard], shard)

        for step in range(count + 2):
            if step < count:
                stage_one(step)
            if 0 <= step - 1 < count:
                stage_two(step - 1)
            if 0 <= step - 2 < count:
                stage_three(step - 2)

        for w in range(count):
            for row in range(rows):
                for depth in range(depths):
                    for side in range(sides):
                        shard = at.index(row, depth, side, 1 - core)
                        pltpu.make_async_remote_copy(
                            src_ref=fulls[w].at[shard],
                            dst_ref=fulls[w].at[shard],
                            send_sem=pair_send.at[w, shard // 2],
                            recv_sem=pair_recv.at[w, shard // 2],
                            device_id=peers[0],
                            **dev,
                        ).wait_recv()
        for copy in own:
            copy.wait()
        for copy in sends:
            copy.wait_send()

    for core in range(2):

        @pl.when(at.core == core)
        def _():
            run(core)


def gather_all(mesh_shape, shards, collective_id=0):
    rows, inner = mesh_shape["dp"], mesh_shape["fsdp"]
    depths = 4
    sides = inner // (2 * depths)
    total = rows * inner
    count = len(shards)
    sent = (depths - 1) + depths * (max(rows, sides) - 1) + depths * sides * (rows - 1) + depths * rows * (sides - 1)
    return pl.pallas_call(
        functools.partial(gather_kernel, rows, depths, sides, count),
        out_shape=[jax.ShapeDtypeStruct((total,) + s.shape, s.dtype) for s in shards],
        in_specs=[ANY] * count,
        out_specs=[ANY] * count,
        scratch_shapes=[
            DMA((count, sent)),
            DMA((count, total)),
            DMA((count, total // 2)),
            DMA((count, total // 2)),
            DMA((count,)),
        ],
        compiler_params=pltpu.CompilerParams(collective_id=collective_id, has_side_effects=True),
        name="gather_weights",
    )(*shards)


def scatter_kernel(rows, depths, sides, count, *refs):
    parts, outs = refs[:count], refs[count : 2 * count]
    scratch = refs[2 * count :]
    held, pair, third_in, second_in, depth_in = (scratch[i * count : (i + 1) * count] for i in range(5))
    (own_sem, pair_send, pair_recv, third_send, third_recv, second_send, second_recv, depth_send, depth_recv) = scratch[
        5 * count :
    ]
    at = Place(rows, depths, sides)
    dev = dict(device_id_type=pl.DeviceIdType.MESH)

    barrier = pltpu.get_barrier_semaphore()
    peers = []
    for k in range(1, depths):
        peers.append(at.device(at.row, (at.depth + k) % depths, at.side, at.core))
    for k in range(1, sides):
        peers.append(at.device(at.row, at.depth, (at.side + k) % sides, at.core))
    for k in range(1, rows):
        peers.append(at.device((at.row + k) % rows, at.depth, at.side, at.core))
    peers.append(at.device(at.row, at.depth, at.side, 1 - at.core))
    for peer in peers:
        pl.semaphore_signal(barrier, inc=1, device_id=peer, **dev)
    pl.semaphore_wait(barrier, len(peers))

    def run(core):
        second_size, third_size = (sides, rows) if core == 0 else (rows, sides)
        my_second, my_third = (at.side, at.row) if core == 0 else (at.row, at.side)

        def unit(second, third, depth):
            row, side = (third, second) if core == 0 else (second, third)
            return (row * depths + depth) * sides + side

        def device(second, third, depth):
            row, side = (third, second) if core == 0 else (second, third)
            return at.device(row, depth, side, core)

        def remote(source, target, send, recv, peer):
            return pltpu.make_async_remote_copy(
                src_ref=source, dst_ref=target, send_sem=send, recv_sem=recv, device_id=peer, **dev
            )

        sibling = at.device(at.row, at.depth, at.side, 1 - core)

        def pair_copy(w, u):
            return remote(
                parts[w].at[u, 1 - core], pair[w].at[u], pair_send.at[w], pair_recv.at[w, u], sibling
            )

        def own_copy(w):
            return pltpu.make_async_copy(parts[w].at[:, core], held[w], own_sem.at[w])

        def third_copy(w, u, k, q, peer):
            return remote(
                held[w].at[u],
                third_in[w].at[k - 1, q],
                third_send.at[w, k - 1, q],
                third_recv.at[w, k - 1, q],
                peer,
            )

        def second_copy(w, u, k, q, peer):
            return remote(
                held[w].at[u],
                second_in[w].at[k - 1, q],
                second_send.at[w, k - 1, q],
                second_recv.at[w, k - 1, q],
                peer,
            )

        def depth_copy(w, u, k, peer):
            return remote(
                held[w].at[u], depth_in[w].at[k - 1], depth_send.at[w, k - 1], depth_recv.at[w, k - 1], peer
            )

        def loop(size, body):
            lax.fori_loop(0, size, lambda i, c: (body(i), c)[1], 0)

        def each_unit(visit):
            other_second, other_third = third_size, second_size
            far = my_second
            for k in list(range(1, other_third)) + [0]:
                def inner(q, k=k):
                    second, third = q // depths, (far + k) % other_third
                    row, side = (second, third) if core == 0 else (third, second)
                    visit((row * depths + q % depths) * sides + side)
                loop(other_second * depths, inner)

        for w in range(count):
            each_unit(lambda u, w=w: pair_copy(w, u).start())
            own_copy(w).start()

        def add_pair(w, u):
            pair_copy(w, u).wait_recv()
            held[w][u] = held[w][u] + pair[w][u]

        def stage_third(w):
            own_copy(w).wait()
            for k in list(range(1, third_size)) + [0]:
                third = (my_third + k) % third_size

                def inner(q, k=k, third=third):
                    second, depth = q // depths, q % depths
                    u = unit(second, third, depth)
                    add_pair(w, u)
                    if k:
                        third_copy(w, u, k, q, device(my_second, third, at.depth)).start()

                loop(second_size * depths, inner)

        def stage_second(w):
            for k in list(range(1, second_size)) + [0]:
                second = (my_second + k) % second_size

                def inner(depth, k=k, second=second):
                    u = unit(second, my_third, depth)
                    for j in range(1, third_size):
                        third_copy(w, u, j, second * depths + depth, sibling).wait_recv()
                        held[w][u] = held[w][u] + third_in[w][j - 1, second * depths + depth]
                    if k:
                        second_copy(w, u, k, depth, device(second, my_third, at.depth)).start()

                loop(depths, inner)

        def stage_depth(w):
            for k in list(range(1, depths)) + [0]:
                depth = (at.depth + k) % depths
                u = unit(my_second, my_third, depth)
                for j in range(1, second_size):
                    second_copy(w, u, j, depth, sibling).wait_recv()
                    held[w][u] = held[w][u] + second_in[w][j - 1, depth]
                if k:
                    depth_copy(w, u, k, device(my_second, my_third, depth)).start()

        def stage_last(w):
            u = unit(my_second, my_third, at.depth)
            total = held[w][u].astype(jnp.float32)
            for k in range(1, depths):
                depth_copy(w, u, k, sibling).wait_recv()
                total = total + depth_in[w][k - 1].astype(jnp.float32)
            outs[w][...] = total

        for step in range(count + 3):
            for lag, stage in enumerate((stage_third, stage_second, stage_depth, stage_last)):
                if 0 <= step - lag < count:
                    stage(step - lag)

        for w in range(count):
            remote(pair[w], pair[w], pair_send.at[w], pair_recv.at[w, 0], sibling).wait_send()
            for k in range(1, third_size):
                loop(second_size * depths, lambda q, w=w, k=k: third_copy(w, 0, k, q, sibling).wait_send())
            for k in range(1, second_size):
                loop(depths, lambda q, w=w, k=k: second_copy(w, 0, k, q, sibling).wait_send())
            for k in range(1, depths):
                depth_copy(w, 0, k, sibling).wait_send()

    for core in range(2):

        @pl.when(at.core == core)
        def _():
            run(core)


def scatter_all(mesh_shape, parts, collective_id=1):
    rows, inner = mesh_shape["dp"], mesh_shape["fsdp"]
    depths = 4
    sides = inner // (2 * depths)
    total = rows * inner
    half = total // 2
    count = len(parts)
    if rows == sides:
        thirds, seconds = (rows - 1, sides * depths), (sides - 1, depths)
    else:
        wide = max(rows, sides)
        thirds, seconds = (wide - 1, wide * depths), (wide - 1, depths)
    scratch = []
    for lead in ((half,), (half,), thirds, seconds, (depths - 1,)):
        scratch += [pltpu.VMEM(lead + p.shape[1:], p.dtype) for p in parts]
    parts = [p.reshape((half, 2) + p.shape[1:]) for p in parts]
    sems = [
        (), (), (half,), thirds, thirds, seconds, seconds, (depths - 1,), (depths - 1,),
    ]
    return pl.pallas_call(
        functools.partial(scatter_kernel, rows, depths, sides, count),
        out_shape=[jax.ShapeDtypeStruct(p.shape[2:], jnp.float32) for p in parts],
        in_specs=[ANY] * count,
        out_specs=[pl.BlockSpec(memory_space=pltpu.VMEM)] * count,
        scratch_shapes=scratch + [DMA((count,) + s) for s in sems],
        compiler_params=pltpu.CompilerParams(
            collective_id=collective_id, has_side_effects=True, vmem_limit_bytes=60 * 2**20
        ),
        name="scatter_grads",
    )(*parts)


def dot(left, right):
    return jnp.dot(left, right, preferred_element_type=F32)


def dot_nt(left, right):
    return lax.dot_general(left, right, (((1,), (1,)), ((), ())), preferred_element_type=F32)


def dot_tn(left, right):
    return lax.dot_general(left, right, (((0,), (0,)), ((), ())), preferred_element_type=F32)


def norm_parts(value):
    center = value - jnp.mean(value, axis=-1, keepdims=True)
    inv = lax.rsqrt(jnp.mean(center * center, axis=-1, keepdims=True) + EPSILON)
    return center * inv, inv


def norm_back(grad, hat, inv, gain):
    scaled = grad * gain
    return inv * (
        scaled
        - jnp.mean(scaled, axis=-1, keepdims=True)
        - hat * jnp.mean(scaled * hat, axis=-1, keepdims=True)
    )


GELU_ROOT = 0.7978845608028654


def gelu_parts(value):
    square = value * value
    inner = jnp.tanh(GELU_ROOT * value * (1.0 + 0.044715 * square))
    half = 0.5 * (1.0 + inner)
    slope = half + 0.5 * value * (1.0 - inner * inner) * (GELU_ROOT + 3 * 0.044715 * GELU_ROOT * square)
    return value * half, slope


def iota(shape, axis):
    return lax.broadcasted_iota(jnp.int32, shape, axis)


def wide(row):
    return jnp.broadcast_to(row, (16, row.shape[1])).astype(BF16)


def head_mask(width):
    return iota((16, width), 1) // (width // HEADS) == iota((16, width), 0)


def spread(row, mask):
    return jnp.where(mask, jnp.broadcast_to(row.astype(F32), mask.shape), 0.0).astype(BF16)


def collect(rows, mask):
    return jnp.sum(jnp.where(mask, rows, 0.0), axis=0, keepdims=True)


def row_softmax(spread_query, keys, place):
    score = dot_nt(spread_query, keys) * 0.125
    score = jnp.where(iota(score.shape, 1) <= place, score, NEG_FILL)
    expo = jnp.exp(score - jnp.max(score, axis=-1, keepdims=True))
    return expo / jnp.sum(expo, axis=-1, keepdims=True)


def pick_rows(first, array):
    chosen = iota((16, array.shape[0]), 1) == first + iota((16, array.shape[0]), 0)
    return dot(chosen.astype(F32).astype(BF16), array)


VECTORS = ("g1", "b1", "bp", "bo", "g2", "b2", "be", "bc")


class Vectors:
    def __init__(self, ref, width):
        self.ref, self.width = ref, width
        self.sizes = dict(bp=3 * width, be=4 * width)

    def __getattr__(self, name):
        return self.ref[VECTORS.index(name) : VECTORS.index(name) + 1, : self.sizes.get(name, self.width)]


def spread_vectors(pieces, sizes, width, vec_ref):
    count, offset = pieces.shape[0], 0
    vec_ref[...] = jnp.zeros_like(vec_ref)
    for row, (name, size) in enumerate(zip(VECTORS, sizes)):
        low, high = offset // 128 * 128, -(-(offset + size) // 128) * 128
        length = count * size
        lane = iota((1, length), 1)
        pick = iota((high - low, length), 0) == lane % size + (offset - low)
        tiled = dot(pieces[:, low:high], pick.astype(F32).astype(BF16))
        line = jnp.sum(jnp.where(iota((count, length), 0) == lane // size, tiled, 0.0), axis=0, keepdims=True)
        if name == "bp":
            vec_ref[row : row + 1, :width] = line[:, :width]
            vec_ref[row : row + 1, 2 * width : 3 * width] = line[:, width:]
        else:
            vec_ref[row : row + 1, :length] = line
        offset += size


def fetch(sources, targets, sems):
    copies = [pltpu.make_async_copy(s, t, sems.at[i]) for i, (s, t) in enumerate(zip(sources, targets))]
    for copy in copies:
        copy.start()
    return copies


def aligned(place):
    return pl.multiple_of(place // 16 * 16, 16)


def project_kernel(sizes, hidden_ref, pieces_ref, wp_ref, mixed_ref, normed_ref, vec_ref):
    seq, width = hidden_ref.shape
    spread_vectors(pieces_ref[:, 0, :], sizes, width, vec_ref)
    vec = Vectors(vec_ref, width)
    for at in range(0, seq, TILE):
        part = slice(at, at + TILE)
        normed = (norm_parts(hidden_ref[part].astype(F32))[0] * vec.g1 + vec.b1).astype(BF16)
        normed_ref[part] = normed
        mixed_ref[part] = (dot(normed, wp_ref[...]) + vec.bp).astype(BF16)


def smem():
    return pl.BlockSpec(memory_space=pltpu.SMEM)


def whole(array):
    return pl.BlockSpec(array.shape, lambda *_: (0,) * array.ndim, pipeline_mode=pl.Buffered(1))


def params(semantics=("arbitrary",)):
    return pltpu.CompilerParams(dimension_semantics=semantics, vmem_limit_bytes=VMEM_LIMIT)


def in_hbm():
    return pl.BlockSpec(memory_space=pl.ANY)


def project(hidden, pieces, sizes, weight):
    seq, width = hidden.shape
    outs = [
        jax.ShapeDtypeStruct((seq, 3 * width), BF16),
        jax.ShapeDtypeStruct((seq, width), BF16),
        jax.ShapeDtypeStruct((8, 4 * width), F32),
    ]
    return pl.pallas_call(
        functools.partial(project_kernel, sizes),
        grid=(1,),
        out_shape=outs,
        in_specs=[whole(hidden), whole(pieces), whole(weight)],
        out_specs=[whole(o) for o in outs],
        compiler_params=params(),
        name="project",
    )(hidden, pieces, weight)


def pair_spec(seq, offset, lanes=128):
    return pl.BlockSpec((seq, lanes), lambda i: (0, offset + i))


def attend_back_kernel(query_ref, key_ref, value_ref, up_ref, log_ref, dq_ref, dk_ref, dv_ref, dk_sum, dv_sum):
    seq, lanes = query_ref.shape
    half = lanes // 2
    first_head = iota((TILE, lanes), 1) < half
    keys_t = key_ref[...].T
    for start in reversed(range(0, seq, TILE)):
        stop = start + TILE
        query = query_ref[start:stop].astype(F32) * 0.125
        upstream = up_ref[start:stop].astype(F32)
        outs = []
        for head in range(2):
            own = first_head if head == 0 else jnp.logical_not(first_head)
            masked = jnp.where(own, query, 0.0).astype(BF16)
            up_masked = jnp.where(own, upstream, 0.0).astype(BF16)
            score = dot_nt(key_ref[:stop], masked)
            hidden = iota((TILE, TILE), 0) > iota((TILE, TILE), 1)
            last = jnp.where(hidden, NEG_FILL, score[start:])
            score = jnp.concatenate([score[:start], last], 0) if start else last
            prob = jnp.exp(score - log_ref[head : head + 1, start:stop])
            prob_grad = dot_nt(value_ref[:stop], up_masked)
            inner = jnp.sum(prob * prob_grad, axis=0, keepdims=True)
            score_grad = (prob * (prob_grad - inner)).astype(BF16)
            dv = dot(prob.astype(BF16), up_masked)
            dk = dot(score_grad, masked)
            if stop == seq and head == 0:
                dv_sum[...] = dv
                dk_sum[...] = dk
            else:
                dv_sum[:stop] += dv
                dk_sum[:stop] += dk
            outs.append(dot(keys_t[:, :stop], score_grad)[head * half : (head + 1) * half])
        dq_ref[start:stop] = (jnp.concatenate(outs, 0).T * 0.125).astype(BF16)
    dk_ref[...] = dk_sum[...].astype(BF16)
    dv_ref[...] = dv_sum[...].astype(BF16)


def attend_back(mixed, upstream, log_total):
    seq, width = upstream.shape
    pairs = HEADS // 2
    out = jax.ShapeDtypeStruct((seq, width), BF16)
    return pl.pallas_call(
        attend_back_kernel,
        grid=(pairs,),
        out_shape=[out, out, out],
        in_specs=[
            pair_spec(seq, 0),
            pair_spec(seq, pairs),
            pair_spec(seq, 2 * pairs),
            pair_spec(seq, 0),
            pl.BlockSpec((None, 2, seq), lambda i: (i, 0, 0)),
        ],
        out_specs=[pair_spec(seq, 0)] * 3,
        scratch_shapes=[pltpu.VMEM((seq, 128), F32), pltpu.VMEM((seq, 128), F32)],
        compiler_params=params(),
        name="attend_back",
    )(mixed, mixed, mixed, upstream, log_total)


def tall(row):
    return jnp.concatenate([jnp.broadcast_to(row[i : i + 1], (16, row.shape[1])) for i in range(THOUGHTS)], 0)


def middle_kernel(
    start_ref, length_ref, hidden_ref, cot_ref, vec_ref,
    mixed_hbm, normed_hbm, wo_hbm, we_hbm, wc_hbm, wp_hbm,
    mixed_out, normed_out, x_out, context_out, log_ref, final_out, normed_two_out, active_out, dz_out, df_out,
    dh_out, dctx_out, sums_ref,
    mixed_ref, x_ref, context_ref, resid_ref, dh_ref, dctx_ref, dz_ref, normed_two_ref,
    wo_ref, we_ref, wc_ref, wp_ref, final_ref, active_ref, df_ref, edge_normed, edge_df,
    weight_sems, mixed_sems, tile_sems, out_sems, edge_sems,
):
    seq, width = hidden_ref.shape
    inner = we_ref.shape[1]
    copy = pltpu.make_async_copy
    first_rows = copy(mixed_hbm.at[:PREFIX], mixed_ref.at[:PREFIX], mixed_sems.at[0])
    first_rows.start()
    sources, targets = (wo_hbm, we_hbm, wc_hbm, wp_hbm), (wo_ref, we_ref, wc_ref, wp_ref)
    weights = fetch(sources, targets, weight_sems)
    other_rows = copy(mixed_hbm.at[PREFIX:], mixed_ref.at[PREFIX:], mixed_sems.at[1])
    other_rows.start()
    start = start_ref[0]
    base = aligned(start - 1)
    edge = pl.ds(base, 32)
    edge_row = base + iota((32, 1), 0)
    load_edge = copy(normed_hbm.at[edge], edge_normed, edge_sems.at[0])
    load_edge.start()
    vec = Vectors(vec_ref, width)
    mask = head_mask(width)
    queries, keys, values = (mixed_ref.at[:, i * width : (i + 1) * width] for i in range(3))
    first_keys, first_values = keys.at[:PREFIX], values.at[:PREFIX]
    for at in range(0, seq, TILE):
        x_ref[at : at + TILE] = hidden_ref[at : at + TILE].astype(F32)

    x_row = x_ref[pl.ds(start - 1, 1), :]
    first_rows.wait()
    query = pick_rows(start - 1, queries[:PREFIX])[0:1]
    load_edge.wait()
    for step in range(THOUGHTS):
        place = start - 1 + step
        prob = row_softmax(spread(query, mask), first_keys[...], place)
        context = collect(dot(prob.astype(BF16), first_values[...]), mask)
        if step == 0:
            weights[0].wait()
        resid = x_row + (dot(wide(context), wo_ref[...])[0:1] + vec.bo)
        normed = norm_parts(resid)[0] * vec.g2 + vec.b2
        if step == 0:
            weights[1].wait()
        pre = dot(wide(normed), we_ref[...])[0:1] + vec.be
        active = gelu_parts(pre)[0]
        if step == 0:
            weights[2].wait()
        x_row = resid + (dot(wide(active), wc_ref[...])[0:1] + vec.bc)
        normed = norm_parts(x_row)[0] * vec.g1 + vec.b1
        if step == 0:
            weights[3].wait()
        mixed_row = dot(wide(normed), wp_ref[...])[0:1] + vec.bp
        query = mixed_row[:, :width].astype(BF16)
        x_ref[pl.ds(place + 1, 1), :] = x_row
        window = pl.ds(aligned(place + 1), 16)
        here = aligned(place + 1) + iota((16, 1), 0) == place + 1
        mixed_ref[window, :] = jnp.where(here, mixed_row, mixed_ref[window, :].astype(F32)).astype(BF16)
        edge_normed[...] = jnp.where(edge_row == place + 1, normed, edge_normed[...].astype(F32)).astype(BF16)
    other_rows.wait()
    pending = [
        copy(mixed_ref.at[edge], mixed_out.at[edge], edge_sems.at[0]),
        copy(edge_normed, normed_out.at[edge], edge_sems.at[1]),
        copy(x_ref, x_out, out_sems.at[0]),
    ]
    for c in pending:
        c.start()

    half, block = 64, seq // 2
    first_head = iota((block, 128), 1) < half
    later = iota((block, block), 0) > iota((block, block), 1)
    for pair in range(HEADS // 2):
        columns = slice(pair * 128, pair * 128 + 128)
        values_t = values[:, columns].T
        for at in range(0, seq, block):
            stop = at + block
            query = queries[at:stop, columns].astype(F32) * 0.125
            scores = []
            for head in range(2):
                own = first_head if head == 0 else jnp.logical_not(first_head)
                score = dot_nt(keys[:stop, columns], jnp.where(own, query, 0.0).astype(BF16))
                last = jnp.where(later, NEG_FILL, score[at:])
                scores.append(jnp.concatenate([score[:at], last], 0) if at else last)
            peaks = [jnp.max(score, axis=0, keepdims=True) for score in scores]
            expos = [jnp.exp(score - peak) for score, peak in zip(scores, peaks)]
            totals = [jnp.sum(expo, axis=0, keepdims=True) for expo in expos]
            outs = []
            for head in range(2):
                out = dot(values_t[:, :stop], expos[head].astype(BF16)) * (1.0 / totals[head])
                outs.append(out[head * half : (head + 1) * half])
                log_ref[pair, head : head + 1, at:stop] = peaks[head] + jnp.log(totals[head])
            context_ref[at:stop, columns] = jnp.concatenate(outs, 0).T.astype(BF16)
    pending.append(copy(context_ref, context_out, out_sems.at[1]))
    pending[-1].start()

    sums_ref[...] = jnp.zeros_like(sums_ref)
    tiles = (final_ref, active_ref, df_ref)
    tile_outs = (final_out, active_out, df_out)

    def tile_copies(i):
        slot = i % 2
        rows = pl.ds(i * TILE, TILE)
        return [copy(t.at[slot], o.at[rows], tile_sems.at[slot, n]) for n, (t, o) in enumerate(zip(tiles, tile_outs))]

    for i in range(seq // TILE):
        slot = i % 2
        rows = slice(i * TILE, i * TILE + TILE)
        if i >= 2:
            for c in tile_copies(i - 2):
                c.wait()
        valid = i * TILE + iota((TILE, 1), 0) < length_ref[0]
        resid = x_ref[rows] + (dot(context_ref[rows], wo_ref[...]) + vec.bo)
        resid_ref[rows] = resid
        hat, inv = norm_parts(resid)
        normed = (hat * vec.g2 + vec.b2).astype(BF16)
        normed_two_ref[rows] = normed
        dout = jnp.where(valid, cot_ref[rows].astype(F32), 0.0)
        dz = dout.astype(BF16)
        dz_ref[rows] = dz
        total = jnp.zeros((TILE, width), F32)
        dc = jnp.zeros((TILE, width), F32)
        for at in range(0, inner, width):
            part = slice(at, at + width)
            value, slope = gelu_parts(dot(normed, we_ref[:, part]) + vec.be[:, part])
            value = value.astype(BF16)
            active_ref[slot, :, part] = value
            total = total + dot(value, wc_ref[part])
            df = (dot_nt(dz, wc_ref[part]) * slope).astype(BF16)
            df_ref[slot, :, part] = df
            dc = dc + dot_nt(df, we_ref[:, part])
        final_ref[slot] = jnp.where(valid, resid + (total + vec.bc), 0.0)
        dh = dout + norm_back(dc, hat, inv, vec.g2)
        dh_ref[rows] = dh
        dctx_ref[rows] = dot_nt(dh.astype(BF16), wo_ref[...]).astype(BF16)
        sums_ref[0:1] += jnp.sum(dc * hat, axis=0, keepdims=True)
        sums_ref[1:2] += jnp.sum(dc, axis=0, keepdims=True)
        for c in tile_copies(i):
            c.start()
    pending.append(copy(normed_two_ref, normed_two_out, out_sems.at[2]))
    pending[-1].start()

    masks = jnp.concatenate([mask] * THOUGHTS, 0)

    def split(rows):
        picked = jnp.where(masks, rows, 0.0)
        return jnp.concatenate(
            [jnp.sum(picked[16 * i : 16 * i + 16], axis=0, keepdims=True) for i in range(THOUGHTS)], 0
        )

    def spread_all(rows):
        return jnp.where(masks, tall(rows), 0.0).astype(BF16)

    behind = iota((16, seq), 1)
    logs = jnp.concatenate([log_ref[i] for i in range(HEADS // 2)] + [jnp.zeros((4, seq), F32)], 0)
    ones = mask.astype(F32).astype(BF16)
    delta = []
    for at in range(0, seq, TILE):
        product = dctx_ref[at : at + TILE].astype(F32) * context_ref[at : at + TILE].astype(F32)
        high = product.astype(BF16)
        delta.append(dot_nt(ones, high) + dot_nt(ones, (product - high.astype(F32)).astype(BF16)))
    delta = jnp.concatenate(delta, 1)
    key_rows = spread_all(pick_rows(start, first_keys[...]))
    value_rows = spread_all(pick_rows(start, first_values[...]))
    score = dot_nt(key_rows, queries[...])
    prob_grad = dot_nt(value_rows, dctx_ref[...])
    probs, grads = [], []
    for i in range(THOUGHTS):
        part = slice(16 * i, 16 * i + 16)
        prob = jnp.where(behind >= start + i, jnp.exp(0.125 * score[part] - logs), 0.0)
        probs.append(prob.astype(BF16))
        grads.append((prob * (prob_grad[part] - delta)).astype(BF16))
    main_dk = split(dot(jnp.concatenate(grads, 0), queries[...])) * 0.125
    main_dv = split(dot(jnp.concatenate(probs, 0), dctx_ref[...]))

    def row_back(query, up, place):
        score = dot_nt(query, first_keys[...]) * 0.125
        score = jnp.where(iota(score.shape, 1) <= place, score, NEG_FILL)
        expo = jnp.exp(score - jnp.max(score, axis=-1, keepdims=True))
        prob = expo / jnp.sum(expo, axis=-1, keepdims=True)
        prob_grad = dot_nt(up, first_values[...])
        grad = (prob * (prob_grad - jnp.sum(prob * prob_grad, axis=-1, keepdims=True))).astype(BF16)
        return prob.astype(BF16), grad, dot(grad, first_keys[...]) * 0.125

    places = start + iota((16 * THOUGHTS, 1), 0) // 16
    up = spread_all(pick_rows(start, dctx_ref[:PREFIX]))
    main_dq = split(row_back(spread_all(pick_rows(start, queries[:PREFIX])), up, places)[2])
    query_rows = pick_rows(start - 1, queries[:PREFIX])
    rows = [start - 1 + step for step in range(THOUGHTS)]
    resid = jnp.concatenate([resid_ref[pl.ds(p, 1), :] for p in rows] + [jnp.zeros((13, width), F32)], 0)
    resid_hat, resid_inv = norm_parts(resid)
    normed = (resid_hat * vec.g2 + vec.b2).astype(BF16)
    slopes = gelu_parts(dot(normed, we_ref[...]) + vec.be)[1]
    for i in range(seq // TILE - 2, seq // TILE):
        for c in tile_copies(i):
            c.wait()
    load_edge = copy(df_out.at[edge], edge_df, edge_sems.at[2])
    load_edge.start()
    scores, spreads, probs, ups, df_rows = [], [], [], [], []
    dq_add = jnp.zeros((1, width), F32)
    for step in reversed(range(THOUGHTS)):
        place = rows[step]
        dq_row = main_dq[step : step + 1] + dq_add
        dk_row, dv_row = main_dk[step : step + 1], main_dv[step : step + 1]
        for score, query, prob, up in zip(scores, spreads, probs, ups):
            chosen = iota(score.shape, 1) == place + 1
            share = jnp.sum(jnp.where(chosen, score.astype(F32), 0.0), axis=1, keepdims=True)
            dk_row = dk_row + 0.125 * jnp.sum(share * query.astype(F32), axis=0, keepdims=True)
            share = jnp.sum(jnp.where(chosen, prob.astype(F32), 0.0), axis=1, keepdims=True)
            dv_row = dv_row + jnp.sum(share * up.astype(F32), axis=0, keepdims=True)
        x_hat, x_inv = norm_parts(x_ref[pl.ds(place + 1, 1), :])
        da = dot_nt(wide(jnp.concatenate([dq_row, dk_row, dv_row], 1)), wp_ref[...])
        dz = dh_ref[pl.ds(place + 1, 1), :] + norm_back(da[0:1], x_hat, x_inv, vec.g1)
        df = dot_nt(wide(dz), wc_ref[...])[0:1] * slopes[step : step + 1]
        dc = dot_nt(wide(df), we_ref[...])[0:1]
        hat, inv = resid_hat[step : step + 1], resid_inv[step : step + 1]
        dh = dz + norm_back(dc, hat, inv, vec.g2)
        sums_ref[0:1] += dc * hat
        sums_ref[1:2] += dc
        dctx = dot_nt(wide(dh), wo_ref[...])[0:1]
        query, up = spread(query_rows[step : step + 1], mask), spread(dctx, mask)
        if step:
            prob, score, dq = row_back(query, up, place)
            dq_add = collect(dq, mask)
            scores.append(score)
            spreads.append(query)
            probs.append(prob)
            ups.append(up)
        dh_ref[pl.ds(place, 1), :] += dh
        df_rows.append(df)
        for target, row in ((dz_ref, dz), (dctx_ref, dctx)):
            row = jnp.where(edge_row == place, row, 0.0)
            target[edge, :] = (target[edge, :].astype(F32) + row).astype(BF16)
    load_edge.wait()
    added = sum(jnp.where(edge_row == p, df, 0.0) for p, df in zip(reversed(rows), df_rows))
    edge_df[...] = (edge_df[...].astype(F32) + added).astype(BF16)
    last = [
        copy(edge_df, df_out.at[edge], edge_sems.at[2]),
        copy(dz_ref, dz_out, out_sems.at[3]),
        copy(dctx_ref, dctx_out, out_sems.at[4]),
        copy(dh_ref, dh_out, out_sems.at[5]),
    ]
    for c in last:
        c.start()
    for c in pending + last:
        c.wait()


def middle(start, length, hidden, cotangent, vec, mixed, normed, weights):
    seq, width = hidden.shape
    inner = weights[1].shape[1]
    shape = jax.ShapeDtypeStruct
    flat, pairs = (seq, width), (HEADS // 2, 2, seq)
    outs = [
        (mixed.shape, BF16), (flat, BF16), (flat, F32), (flat, BF16), (pairs, F32), (flat, F32), (flat, BF16),
        ((seq, inner), BF16), (flat, BF16), ((seq, inner), BF16), (flat, F32), (flat, BF16), ((8, width), F32),
    ]
    whole_vmem = pl.BlockSpec(memory_space=pltpu.VMEM)
    out_specs = [whole_vmem if i in (4, 12) else in_hbm() for i in range(len(outs))]
    kept = [
        (mixed.shape, BF16), (flat, F32), (flat, BF16), (flat, F32), (flat, F32), (flat, BF16), (flat, BF16), (flat, BF16),
    ]
    tiles = [((2, TILE, width), F32), ((2, TILE, inner), BF16), ((2, TILE, inner), BF16)]
    edges = [((32, width), BF16), ((32, inner), BF16)]
    buffers = kept + [(w.shape, w.dtype) for w in weights] + tiles + edges
    return pl.pallas_call(
        middle_kernel,
        out_shape=[shape(*o) for o in outs],
        in_specs=[smem(), smem()] + [whole_vmem] * 3 + [in_hbm()] * (2 + len(weights)),
        out_specs=out_specs,
        scratch_shapes=[pltpu.VMEM(*b) for b in buffers]
        + [DMA((4,)), DMA((2,)), DMA((2, 3)), DMA((6,)), DMA((3,))],
        input_output_aliases={5: 0, 6: 1},
        compiler_params=pltpu.CompilerParams(vmem_limit_bytes=VMEM_LIMIT),
        name="middle",
    )(start, length, hidden, cotangent, vec, mixed, normed, *weights)


class Refs:
    def __init__(self, names, refs):
        self.__dict__.update(zip(names, refs))


MESH = dict(device_id_type=pl.DeviceIdType.MESH)


class Stream:
    def __init__(self, at, side_first, name, refs):
        self.at, self.side_first = at, side_first
        for field in STREAM_FIELDS:
            setattr(self, field, getattr(refs, field + str(name)))
        self.sizes = (at.rows, at.sides) if side_first else (at.sides, at.rows)
        self.mine = (at.row, at.side) if side_first else (at.side, at.row)
        self.sent = []

    def spot(self, second, third):
        return (second, third) if self.side_first else (third, second)

    def unit(self, second, third, depth):
        row, side = self.spot(second, third)
        return (row * self.at.depths + depth) * self.at.sides + side

    def remote(self, source, target, send, recv, peer):
        return pltpu.make_async_remote_copy(
            src_ref=source, dst_ref=target, send_sem=send, recv_sem=recv, device_id=peer, **MESH
        )

    def sibling(self):
        return self.at.device(self.at.row, self.at.depth, self.at.side, 1 - self.at.core)

    def pair_copy(self, u, source):
        return self.remote(source, self.pair.at[u], self.pair_send.at[u], self.pair_recv.at[u], self.sibling())

    def third_copy(self, u, k, q):
        peer = self.at.device(*self.place(self.mine[0], (self.mine[1] + k) % self.sizes[1], self.at.depth))
        return self.remote(
            self.held.at[u], self.third.at[k - 1, q], self.third_send.at[k - 1, q], self.third_recv.at[k - 1, q], peer
        )

    def second_copy(self, u, k, depth):
        peer = self.at.device(*self.place((self.mine[0] + k) % self.sizes[0], self.mine[1], self.at.depth))
        return self.remote(
            self.held.at[u],
            self.second.at[k - 1, depth],
            self.second_send.at[k - 1, depth],
            self.second_recv.at[k - 1, depth],
            peer,
        )

    def depth_copy(self, u, k):
        peer = self.at.device(*self.place(*self.mine, (self.at.depth + k) % self.at.depths))
        return self.remote(
            self.held.at[u], self.depth.at[k - 1], self.depth_send.at[k - 1], self.depth_recv.at[k - 1], peer
        )

    def place(self, second, third, depth):
        row, side = self.spot(second, third)
        return row, depth, side, self.at.core

    def third_step(self, k, j, d, source):
        depths = self.at.depths
        second, depth = (self.mine[0] + j) % self.sizes[0], (self.at.depth + d) % depths
        q = second * depths + depth
        u = self.unit(second, (self.mine[1] + k) % self.sizes[1], depth)
        own = source(u)
        self.pair_copy(u, own).wait_recv()
        self.held[u] = own[...] + self.pair[u]
        if k:
            self.third_copy(u, k, q).start()

    def second_step(self, d):
        depth = (self.at.depth + d) % self.at.depths
        for k in list(range(1, self.sizes[0])) + [0]:
            second = (self.mine[0] + k) % self.sizes[0]
            u = self.unit(second, self.mine[1], depth)
            q = second * self.at.depths + depth
            for j in range(1, self.sizes[1]):
                self.third_copy(u, j, q).wait_recv()
                self.held[u] = self.held[u] + self.third[j - 1, q]
            if k:
                self.second_copy(u, k, depth).start()

    def depth_step(self, k):
        depth = (self.at.depth + k) % self.at.depths
        u = self.unit(*self.mine, depth)
        for j in range(1, self.sizes[0]):
            self.second_copy(u, j, depth).wait_recv()
            self.held[u] = self.held[u] + self.second[j - 1, depth]
        if k:
            self.depth_copy(u, k).start()

    def total(self):
        u = self.unit(*self.mine, self.at.depth)
        total = self.held[u].astype(F32)
        for k in range(1, self.at.depths):
            self.depth_copy(u, k).wait_recv()
            total = total + self.depth[k - 1].astype(F32)
        return total

    def drain(self):
        count = self.sizes[0] * self.at.depths
        for k in range(1, self.sizes[1]):
            loop(count, lambda q, k=k: self.third_copy(0, k, q).wait_send())
        for k in range(1, self.sizes[0]):
            loop(self.at.depths, lambda d, k=k: self.second_copy(0, k, d).wait_send())
        for k in range(1, self.at.depths):
            self.depth_copy(0, k).wait_send()


def loop(size, body):
    lax.fori_loop(0, size, lambda i, c: (body(i), c)[1], 0)


class Spread:
    def __init__(self, at, axes, source, full, send, recv, pair_recv):
        self.at, self.axes, self.source, self.full = at, axes, source, full
        self.send_sem, self.recv_sem, self.pair_recv = send, recv, pair_recv
        self.sizes = [(at.rows, at.depths, at.sides)[a] for a in axes]
        self.mine = [(at.row, at.depth, at.side)[a] for a in axes]

    def spot(self, steps):
        where = [0, 0, 0]
        for axis, mine, size, step in zip(self.axes, self.mine, self.sizes, steps):
            where[axis] = (mine - step) % size
        return where

    def unit(self, steps):
        row, depth, side = self.spot(steps)
        return (row * self.at.depths + depth) * self.at.sides + side

    def copy(self, steps, source, recv, peer):
        return pltpu.make_async_remote_copy(
            src_ref=source,
            dst_ref=self.full(2 * self.unit(steps) + self.at.core),
            send_sem=self.send_sem,
            recv_sem=recv.at[self.unit(steps)],
            device_id=peer,
            **MESH,
        )

    def forward(self, level, steps):
        at = self.at
        source = self.full(2 * self.unit(steps) + at.core) if level else self.source
        for axis in range(level, 3):
            for k in range(1, self.sizes[axis]):
                row, depth, side = self.spot([-k if i == axis else 0 for i in range(3)])
                self.copy(steps, source, self.recv_sem, at.device(row, depth, side, at.core)).start()
        sibling = at.device(at.row, at.depth, at.side, 1 - at.core)
        self.copy(steps, source, self.pair_recv, sibling).start()

    def arrive(self, level, steps):
        unit = self.full(2 * self.unit(steps) + self.at.core)
        self.copy(steps, unit, self.recv_sem, self.at.device(*self.spot([0, 0, 0]), self.at.core)).wait_recv()
        self.forward(level, steps)

    def siblings(self, count):
        def wait(u):
            unit = self.full(2 * u + 1 - self.at.core)
            pltpu.make_async_remote_copy(
                src_ref=unit, dst_ref=unit, send_sem=self.send_sem, recv_sem=self.pair_recv.at[u],
                device_id=self.at.device(*self.spot([0, 0, 0]), 1 - self.at.core), **MESH,
            ).wait_recv()

        loop(count, wait)

    def drain(self, total):
        every = self.full(pl.ds(0, total - 1))
        pltpu.make_async_remote_copy(
            src_ref=every, dst_ref=every, send_sem=self.send_sem, recv_sem=self.recv_sem.at[0],
            device_id=self.at.device(*self.spot([0, 0, 0]), 1 - self.at.core), **MESH,
        ).wait_send()


PARTS = (
    (0, None, (1, 2, 0)),
    (1, None, (1, 2, 0)),
    (4, None, (1, 0, 2)),
    (3, 1, (1, 2, 0)),
    (2, None, (1, 2, 0)),
    (3, 0, (1, 0, 2)),
)
GATHER_ORDER = (
    (1, 0, 1), (1, 0, 2), (1, 0, 3), (2, 0, 1, 0), (3, 0, 1, 0, 0), (2, 1, 1, 0), (3, 1, 1, 0, 0), (1, 1, 1),
    (3, 2, 1, 0, 0), (2, 2, 1, 0), (1, 1, 2), (2, 3, 1, 0), (3, 3, 1, 0, 0), (2, 4, 1, 0), (3, 4, 1, 0, 0),
    (1, 1, 3), (2, 0, 1, 1), (2, 0, 1, 2), (2, 0, 1, 3), (2, 5, 1, 0), (3, 0, 1, 0, 1), (3, 0, 1, 0, 2),
    (3, 0, 1, 0, 3), (3, 0, 1, 1, 0), (3, 5, 1, 0, 0), (2, 1, 1, 1), (3, 1, 1, 1, 0), (1, 2, 1), (3, 1, 1, 0, 1),
    (3, 2, 1, 1, 0), (3, 1, 1, 0, 2), (2, 1, 1, 2), (1, 2, 2), (3, 3, 1, 1, 0), (3, 4, 1, 1, 0), (2, 1, 1, 3),
    (3, 5, 1, 1, 0), (3, 0, 1, 1, 1), (1, 2, 3), (3, 0, 1, 1, 2), (3, 0, 1, 1, 3), (3, 1, 1, 0, 3), (1, 3, 1),
    (3, 1, 1, 1, 1), (3, 2, 1, 0, 1), (4,), (1, 3, 2), (2, 2, 1, 1), (3, 2, 1, 0, 2), (1, 3, 3), (1, 4, 1),
    (3, 1, 1, 1, 2), (1, 4, 2), (3, 2, 1, 0, 3), (1, 4, 3), (2, 3, 1, 1), (2, 2, 1, 2), (1, 5, 1), (2, 3, 1, 2),
    (3, 1, 1, 1, 3), (1, 5, 2), (5,), (1, 5, 3), (2, 2, 1, 3), (3, 2, 1, 1, 1), (6, 0), (2, 3, 1, 3), (2, 4, 1, 1),
    (2, 4, 1, 2), (3, 3, 1, 0, 1), (6, 1), (2, 4, 1, 3), (3, 3, 1, 0, 2), (6, 2), (3, 3, 1, 0, 3), (3, 2, 1, 1, 2),
    (3, 4, 1, 0, 1), (3, 4, 1, 0, 2), (6, 3), (3, 4, 1, 0, 3), (3, 5, 1, 0, 1), (3, 3, 1, 1, 1), (3, 5, 1, 0, 2),
    (2, 5, 1, 1), (3, 5, 1, 0, 3), (3, 3, 1, 1, 2), (2, 5, 1, 2), (3, 2, 1, 1, 3), (2, 5, 1, 3), (3, 5, 1, 1, 1),
    (3, 3, 1, 1, 3), (3, 5, 1, 1, 2), (3, 4, 1, 1, 1), (3, 4, 1, 1, 2), (3, 5, 1, 1, 3), (3, 4, 1, 1, 3),
)


def gather_project_kernel(mesh_shape, sizes, *refs):
    shards, hidden_ref = refs[:5], refs[5]
    fulls, (mixed_ref, normed_ref, vec_ref) = refs[6:11], refs[11:14]
    pieces_ref, rows_ref, wp_ref, send_sem, recv_sem, pair_recv, own_sem, load_sem = refs[14:]
    rows, inner = mesh_shape["dp"], mesh_shape["fsdp"]
    depths = 4
    sides = inner // (2 * depths)
    total = rows * inner
    at = Place(rows, depths, sides)
    me = at.row * inner + lax.axis_index("fsdp")
    width = hidden_ref.shape[1]
    piece = width // total

    barrier = pltpu.get_barrier_semaphore()
    peers = [at.device(at.row, (at.depth + k) % depths, at.side, at.core) for k in range(1, depths)]
    peers += [at.device(at.row, at.depth, (at.side + k) % sides, at.core) for k in range(1, sides)]
    peers += [at.device((at.row + k) % rows, at.depth, at.side, at.core) for k in range(1, rows)]
    peers.append(at.device(at.row, at.depth, at.side, 1 - at.core))
    for peer in peers:
        pl.semaphore_signal(barrier, inc=1, device_id=peer, **MESH)
    pl.semaphore_wait(barrier, len(peers))

    parts, own = [], []
    for i, (w, part, axes) in enumerate(PARTS):
        source, full = shards[w], fulls[w].at
        if part is None:
            target = lambda s, full=full: full[s]
        else:
            half = shards[w].shape[1] // 2
            columns = slice(part * half, part * half + half)
            source = source.at[:, columns]
            target = lambda s, full=full, columns=columns: full[s, :, columns]
        parts.append(Spread(at, axes, source, target, send_sem.at[i], recv_sem.at[i], pair_recv.at[i]))
        own.append(pltpu.make_async_copy(source, target(me), own_sem.at[i]))
        parts[-1].forward(0, (0, 0, 0))
        own[-1].start()

    waited = set()

    def whole_part(w):
        for i, (source, _, _) in enumerate(PARTS):
            if source == w:
                parts[i].siblings(total // 2)
                own[i].wait()
                waited.add(i)

    def load(source, target):
        copy = pltpu.make_async_copy(source, target, load_sem)
        copy.start()
        copy.wait()

    vec = Vectors(vec_ref, width)
    for code, *what in GATHER_ORDER:
        if code <= 3:
            part, *steps = what
            parts[part].arrive(code, (steps[::-1] + [0, 0])[:3])
        elif code == 4:
            whole_part(0)
            load(fulls[0], pieces_ref)
            spread_vectors(pieces_ref[:, 0, :], sizes, width, vec_ref)
        elif code == 5:
            whole_part(1)
            load(fulls[1], rows_ref)

            def join(pair):
                two = rows_ref[pl.ds(2 * pair, 2)].astype(F32).reshape(2 * piece, 3 * width)
                wp_ref[pl.ds(pl.multiple_of(2 * piece * pair, 2 * piece), 2 * piece)] = two.astype(BF16)

            loop(total // 2, join)
        else:
            tile = slice(what[0] * TILE, what[0] * TILE + TILE)
            normed = (norm_parts(hidden_ref[tile].astype(F32))[0] * vec.g1 + vec.b1).astype(BF16)
            normed_ref[tile] = normed
            mixed_ref[tile] = (dot(normed, wp_ref[...]) + vec.bp).astype(BF16)
    for i, part in enumerate(parts):
        if i not in waited:
            part.siblings(total // 2)
            own[i].wait()
        part.drain(total)


def gather_project(mesh_shape, sizes, hidden, shards):
    total = mesh_shape["dp"] * mesh_shape["fsdp"]
    seq, width = hidden.shape
    count = len(PARTS)
    shape = jax.ShapeDtypeStruct
    outs = [shape((total,) + s.shape, s.dtype) for s in shards]
    outs += [shape((seq, 3 * width), BF16), shape((seq, width), BF16), shape((8, 4 * width), F32)]
    whole_vmem = pl.BlockSpec(memory_space=pltpu.VMEM)
    return pl.pallas_call(
        functools.partial(gather_project_kernel, mesh_shape, sizes),
        out_shape=outs,
        in_specs=[in_hbm()] * 5 + [whole_vmem],
        out_specs=[in_hbm()] * 5 + [whole_vmem] * 3,
        scratch_shapes=[
            pltpu.VMEM(outs[0].shape, BF16),
            pltpu.VMEM(outs[1].shape, BF16),
            pltpu.VMEM((width, 3 * width), BF16),
            DMA((count,)), DMA((count, total // 2)), DMA((count, total // 2)), DMA((count,)), DMA(()),
        ],
        compiler_params=pltpu.CompilerParams(collective_id=3, has_side_effects=True, vmem_limit_bytes=VMEM_LIMIT),
        name="gather_project",
    )(*shards, hidden)


STREAM_FIELDS = (
    "held", "pair", "third", "second", "depth",
    "pair_send", "pair_recv", "third_send", "third_recv", "second_send", "second_recv", "depth_send", "depth_recv",
)


def stream_scratch(rows, depths, sides, side_first, shape):
    second, third = (rows, sides) if side_first else (sides, rows)
    half = rows * depths * sides
    leads = ((half,), (half,), (third - 1, second * depths), (second - 1, depths), (depths - 1,))
    buffers = [pltpu.VMEM(lead + shape, BF16) for lead in leads]
    sems = [DMA((half,)), DMA((half,))] + [DMA(lead) for lead in leads[2:] for _ in range(2)]
    return buffers + sems


CON, EX0, EX1, OUT, PR0, PR1 = range(6)
SIDE_FIRST = (False, True, True, False, True, False)


FIRST_PAIRS = 4
CHUNK_SLOTS = 4
CHUNK, SQUARE, ATTN, ROWS, SMALL, THIRD, SECOND, DEPTH = range(8)
SCHEDULE = (
    (CHUNK, 1, 1), (CHUNK, 1, 3), (SQUARE, EX0), (THIRD, CON, 1, 1), (THIRD, CON, 1, 3), (CHUNK, 0, 1),
    (THIRD, EX0, 1, 0), (THIRD, EX0, 1, 1), (ATTN, 0, 0), (THIRD, EX0, 0, 0), (THIRD, EX0, 0, 1), (ATTN, 0, 1),
    (THIRD, CON, 0, 1), (CHUNK, 1, 2), (CHUNK, 0, 3), (ATTN, 0, 2), (SECOND, CON, 1), (THIRD, CON, 1, 2),
    (SQUARE, EX1), (THIRD, CON, 0, 3), (SECOND, EX0, 0), (SECOND, EX0, 1), (CHUNK, 1, 0), (THIRD, EX1, 1, 0),
    (THIRD, EX1, 1, 1), (SECOND, CON, 3), (SECOND, EX0, 2), (ATTN, 0, 3), (THIRD, EX1, 0, 0), (SECOND, EX0, 3),
    (ATTN, 1, 0), (THIRD, EX1, 0, 1), (THIRD, CON, 1, 0), (ATTN, 1, 1), (DEPTH, CON, 1), (ATTN, 1, 2), (ATTN, 1, 3),
    (ATTN, 2, 0), (ATTN, 2, 1), (DEPTH, EX0, 0), (ATTN, 2, 2), (ATTN, 2, 3), (DEPTH, EX0, 1), (ATTN, 3, 0),
    (DEPTH, EX0, 2), (ATTN, 3, 1), (ATTN, 3, 2), (SECOND, EX1, 0), (DEPTH, EX0, 3), (ATTN, 3, 3), (SQUARE, PR0),
    (SECOND, EX1, 1), (SECOND, EX1, 2), (SECOND, EX1, 3), (ATTN, 4, 0), (THIRD, PR0, 1, 0), (THIRD, PR0, 1, 1),
    (DEPTH, CON, 3), (THIRD, PR0, 0, 0), (DEPTH, EX1, 0), (SQUARE, OUT), (THIRD, PR0, 0, 1), (DEPTH, EX1, 1),
    (THIRD, OUT, 1, 0), (DEPTH, EX1, 2), (THIRD, OUT, 1, 1), (DEPTH, EX1, 3), (THIRD, OUT, 0, 0), (CHUNK, 0, 2),
    (THIRD, OUT, 0, 1), (ATTN, 4, 1), (ATTN, 4, 2), (THIRD, CON, 0, 2), (SECOND, CON, 2), (CHUNK, 0, 0),
    (SECOND, OUT, 0), (SECOND, PR0, 0), (ATTN, 4, 3), (SECOND, OUT, 1), (SECOND, PR0, 1), (ATTN, 5, 0),
    (THIRD, CON, 0, 0), (SECOND, CON, 0), (SECOND, OUT, 2), (SECOND, OUT, 3), (SECOND, PR0, 2), (ATTN, 5, 1),
    (SECOND, PR0, 3), (DEPTH, PR0, 0), (ATTN, 5, 2), (ATTN, 5, 3), (DEPTH, PR0, 1), (SQUARE, PR1), (DEPTH, CON, 2),
    (DEPTH, OUT, 1), (THIRD, PR1, 1, 0), (THIRD, PR1, 1, 1), (THIRD, PR1, 0, 0), (DEPTH, OUT, 0), (DEPTH, PR0, 2),
    (DEPTH, PR0, 3), (THIRD, PR1, 0, 1), (ROWS, 0), (DEPTH, CON, 0), (ROWS, 1), (DEPTH, OUT, 2), (SECOND, PR1, 0),
    (DEPTH, OUT, 3), (ROWS, 2), (SECOND, PR1, 1), (SECOND, PR1, 2), (SECOND, PR1, 3), (DEPTH, PR1, 0), (ROWS, 3),
    (DEPTH, PR1, 1), (SMALL,), (DEPTH, PR1, 2), (DEPTH, PR1, 3),
)


def finish_kernel(mesh_shape, sizes, names, *refs):
    r = Refs(names, refs)
    rows, inner = mesh_shape["dp"], mesh_shape["fsdp"]
    depths = 4
    sides = inner // (2 * depths)
    total = rows * inner
    half = total // 2
    at = Place(rows, depths, sides)
    seq, width = r.dz.shape
    groups = (FIRST_PAIRS * 128, width - FIRST_PAIRS * 128)
    core = at.core
    me = at.row * inner + lax.axis_index("fsdp")
    piece = width // total
    vec = Vectors(r.vec, width)

    copies = {}

    def load(key, source, target, sem):
        copies[key] = pltpu.make_async_copy(source, target, sem)
        copies[key].start()

    def ready(key):
        copies.pop(key).wait()

    chunks = [step[1:] for step in SCHEDULE if step[0] == CHUNK]
    span = sides * 2 * piece * 4

    def load_active(i):
        k, d = chunks[i]
        first = ((at.row + k) % rows * depths + (at.depth + d) % depths) * span
        columns = pl.ds(pl.multiple_of(first, 128), span)
        load(("act", i), r.active.at[:, columns], r.act.at[i % 2], r.act_sem.at[i % 2])

    load_active(0)
    load_active(1)
    load("normed", r.normed, r.normedv, r.in_sem.at[0])
    load("df0", r.df.at[:, : 2 * width], r.dfs.at[0], r.df_sem.at[0])
    load("df1", r.df.at[:, 2 * width :], r.dfs.at[1], r.df_sem.at[1])
    load("dh", r.dh, r.dhv, r.dh_sem)
    load("context", r.context, r.contextv, r.in_sem.at[1])
    load("first", r.first_normed, r.firstv, r.in_sem.at[2])
    load("wp", r.wp, r.wpv, r.wp_sem)

    def load_pair(p):
        slot = p % 2
        for i in range(3):
            columns = pl.ds(i * width + p * 128, 128)
            load(("pair", p, i), r.mixed.at[:, columns], r.qkv.at[slot, i], r.qkv_sem.at[slot, i])
        load(("pair", p, 3), r.dctx.at[:, pl.ds(p * 128, 128)], r.qkv.at[slot, 3], r.qkv_sem.at[slot, 3])

    load_pair(0)

    barrier = pltpu.get_barrier_semaphore()

    def other(k):
        index = (me + k) % total
        return {"dp": index // inner, "fsdp": index % inner}

    loop(total - 1, lambda i: pl.semaphore_signal(barrier, inc=1, device_id=other(i + 1), **MESH))
    pl.semaphore_wait(barrier, total - 1)

    streams = {name: Stream(at, side_first, name, r) for name, side_first in enumerate(SIDE_FIRST)}
    con = streams[CON]
    ones = jnp.ones((16, seq), BF16)
    sums = {}

    def chunk(k, d):
        i = chunks.index((k, d))
        ready(("act", i))
        slot = i % CHUNK_SLOTS
        if i >= CHUNK_SLOTS:
            con_sent(i - CHUNK_SLOTS)
        grad = dot_tn(r.act[i % 2], r.dz[...])
        if i + 2 < len(chunks):
            load_active(i + 2)
        r.con_stage[slot] = grad.reshape(sides, 2, 4 * piece, width).astype(BF16)
        for side in range(sides):
            con.pair_copy(con_unit(i, side), r.con_stage.at[slot, side, 1 - core]).start()

    def con_unit(i, side):
        k, d = chunks[i]
        return ((at.row + k) % rows * depths + (at.depth + d) % depths) * sides + side

    def con_sent(i):
        for side in range(sides):
            con.pair_copy(con_unit(i, side), r.con_stage.at[i % CHUNK_SLOTS, side, 1 - core]).wait_send()

    def con_third(k, d):
        slot = chunks.index((k, d)) % CHUNK_SLOTS
        for j in list(range(1, sides)) + [0]:
            side = (at.side + j) % sides
            con.third_step(k, j, d, lambda u: r.con_stage.at[slot, side, core])

    slots = {}

    def square(name, left, right):
        columns = right.shape[1]
        slot = len(slots) % 2
        previous = [n for n, s in slots.items() if s == slot]
        if previous:
            stage_sent(previous[-1])
        slots[name] = slot
        quarter = width // 4
        for part in range(4):
            grad = dot_tn(left[:, part * quarter : (part + 1) * quarter], right[...])
            target = r.stage.at[slot, part * half // 4 : (part + 1) * half // 4, :, :, :columns]
            target[...] = grad.reshape(half // 4, 2, piece, columns).astype(BF16)
        stream = streams[name]
        for k in list(range(1, stream.sizes[1])) + [0]:
            for j in list(range(1, stream.sizes[0])) + [0]:

                def start(d, k=k, j=j):
                    second, third = ((m + n) % z for m, n, z in zip(stream.mine, (j, k), stream.sizes))
                    u = stream.unit(second, third, (at.depth + d) % depths)
                    stream.pair_copy(u, stage_at(name, u, 1 - core, columns)).start()

                loop(depths, start)

    def stage_at(name, u, which, columns):
        return r.stage.at[slots[name], u, which, :, :columns]

    def columns_of(name):
        return streams[name].held.shape[-1]

    def stage_sent(name):
        stream = streams[name]
        loop(half, lambda u: stream.pair_copy(u, stage_at(name, u, 1 - core, columns_of(name))).wait_send())

    def square_third(name, k, j):
        stream = streams[name]
        source = lambda u: stage_at(name, u, core, columns_of(name))
        loop(depths, lambda d: stream.third_step(k, j, d, source))

    def expand(e):
        if e == 0:
            ready("normed")
        ready("df%d" % e)
        square(EX0 + e, r.normedv, r.dfs.at[e])
        sums["be%d" % e] = dot(ones, r.dfs[e])[0:1]

    def output():
        ready("dh")
        ready("context")
        r.dy[...] = r.dhv[...].astype(BF16)
        square(OUT, r.contextv, r.dy)
        sums["bo"] = dot(ones, r.dy[...])[0:1]
        sums["bc"] = dot(ones, r.dz[...])[0:1]

    later = iota((TILE, TILE), 0) > iota((TILE, TILE), 1)
    later = jnp.concatenate([later, later], 1)
    first_head = iota((TILE, 128), 1) < 64

    def two(value):
        parts = [jnp.where(first_head, value, 0.0), jnp.where(first_head, 0.0, value)]
        return jnp.concatenate(parts, 0).astype(BF16)

    def attend_block(p, n):
        block = seq // TILE - 1 - n
        slot = p % 2
        if n == 0:
            for i in range(4):
                ready(("pair", p, i))
            if p + 1 < HEADS // 2:
                load_pair(p + 1)
            r.keys_t[...] = r.qkv[slot, 1].T
        query_ref, key_ref, value_ref, up_ref = (r.qkv.at[slot, i] for i in range(4))
        start, stop = block * TILE, block * TILE + TILE
        query = two(query_ref[start:stop].astype(F32) * 0.125)
        upstream = two(up_ref[start:stop].astype(F32))
        score = dot_nt(key_ref[:stop], query)
        edge = jnp.where(later, NEG_FILL, score[start:])
        score = jnp.concatenate([score[:start], edge], 0) if start else edge
        logs = jnp.concatenate([r.logs[p, 0:1, start:stop], r.logs[p, 1:2, start:stop]], 1)
        prob = jnp.exp(score - logs)
        prob_grad = dot_nt(value_ref[:stop], upstream)
        mean = jnp.sum(prob * prob_grad, axis=0, keepdims=True)
        score_grad = (prob * (prob_grad - mean)).astype(BF16)
        dv = dot(prob.astype(BF16), upstream)
        dk = dot(score_grad, query)
        if n == 0:
            r.dv_sum[...] = dv
            r.dk_sum[...] = dk
        else:
            r.dv_sum[:stop] += dv
            r.dk_sum[:stop] += dk
        out = dot(r.keys_t[:, :stop], score_grad)
        out = jnp.concatenate([out[:64, :TILE], out[64:, TILE:]], 0)
        g = int(p >= FIRST_PAIRS)
        target, group = r.dfs.at[g], groups[g]
        column = (p - g * FIRST_PAIRS) * 128
        target[start:stop, column : column + 128] = (out.T * 0.125).astype(BF16)
        if block == 0:
            target[:, group + column : group + column + 128] = r.dk_sum[...].astype(BF16)
            target[:, 2 * group + column : 2 * group + column + 128] = r.dv_sum[...].astype(BF16)

    def project_grad(g):
        if g == 0:
            ready("first")
        right = r.dfs.at[g, :, : 3 * groups[g]]
        square(PR0 + g, r.firstv, right)
        sums["bp%d" % g] = dot(ones, right[...])[0:1]

    def project_columns(g, n):
        first = n * width + g * groups[0]
        return slice(first, first + groups[g])

    def load_tile(i):
        load(("x", i), r.x.at[pl.ds(i * TILE, TILE)], r.xs.at[i % 2], r.x_sem.at[i % 2])

    def tile(i):
        if i == 0:
            ready("wp")
            load_tile(0)
            load_tile(1)
        ready(("x", i))
        part = slice(i * TILE, i * TILE + TILE)
        da = jnp.zeros((TILE, width), F32)
        for g in range(2):
            for n in range(3):
                da = da + dot_nt(r.dfs[g, part, n * groups[g] : (n + 1) * groups[g]], r.wpv[:, project_columns(g, n)])
        hat, inv = norm_parts(r.xs[i % 2])
        if i + 2 < seq // TILE:
            load_tile(i + 2)
        position = i * TILE + iota((TILE, 1), 0)
        kept = (position < r.start[0]) | (position >= r.start[0] + THOUGHTS)
        if i >= 2:
            ready(("dx", i - 2))
        r.dxs[i % 2] = jnp.where(kept, r.dhv[part] + norm_back(da, hat, inv, vec.g1), 0.0)
        load(("dx", i), r.dxs.at[i % 2], r.hidden_grad.at[pl.ds(i * TILE, TILE)], r.dx_sem.at[i % 2])
        gain, bias = jnp.sum(da * hat, axis=0, keepdims=True), jnp.sum(da, axis=0, keepdims=True)
        sums["g1"] = gain if i == 0 else sums["g1"] + gain
        sums["b1"] = bias if i == 0 else sums["b1"] + bias

    def small_start():
        group_of = lambda n: jnp.concatenate(
            [sums["bp%d" % g][:, n * groups[g] : (n + 1) * groups[g]] for g in range(2)], 1
        )
        lines = dict(
            g1=sums["g1"], b1=sums["b1"], bp=jnp.concatenate([group_of(0), group_of(2)], 1), bo=sums["bo"],
            g2=r.sums[0:1], b2=r.sums[1:2], be=jnp.concatenate([sums["be0"], sums["be1"]], 1), bc=sums["bc"],
        )
        offset = 0
        r.small_part[...] = jnp.zeros_like(r.small_part)
        for name, size in zip(VECTORS, sizes):
            low, high = offset // 128 * 128, -(-(offset + size) // 128) * 128
            length = total * size
            lane = iota((1, length), 1)
            pick = (iota((high - low, length), 0) == lane % size + (offset - low)).astype(F32).astype(BF16)
            rest = jnp.where(iota((total, length), 0) == lane // size, lines[name], 0.0)
            pieces = jnp.zeros((total, high - low), F32)
            for _ in range(2):
                rounded = rest.astype(BF16)
                pieces = pieces + dot_nt(rounded, pick)
                rest = rest - rounded.astype(F32)
            r.small_part[:, 0, low:high] += pieces
            offset += size
        loop(total - 1, lambda i: small_copy(i + 1).start())

    def small_copy(k):
        return pltpu.make_async_remote_copy(
            src_ref=r.small_part.at[(me + k) % total],
            dst_ref=r.small_in.at[k - 1],
            send_sem=r.small_send.at[k - 1],
            recv_sem=r.small_recv.at[k - 1],
            device_id=other(k),
            **MESH,
        )

    def small_end():
        loop(total - 1, lambda i: small_copy(i + 1).wait_recv())
        received = r.small_in[...]
        r.small_out[...] = r.small_part[me] + jnp.sum(received[: total - 1], axis=0)

    def work(kind, *what):
        if kind == CHUNK:
            chunk(*what)
        elif kind == ATTN:
            attend_block(*what)
        elif kind == ROWS:
            tile(*what)
        elif kind == SMALL:
            small_start()
        elif kind == SQUARE:
            name = what[0]
            if name == OUT:
                output()
            elif name in (EX0, EX1):
                expand(name - EX0)
            else:
                project_grad(name - PR0)
        elif kind == THIRD:
            name, k, j = what
            if name == CON:
                con_third(k, j)
            else:
                square_third(name, k, 1 - j)
        elif kind == SECOND:
            streams[what[0]].second_step(what[1])
        else:
            streams[what[0]].depth_step(what[1])

    for step in SCHEDULE:
        work(*step)
    r.contract_out[...] = con.total()
    r.expand_out[:, : 2 * width] = streams[EX0].total()
    r.expand_out[:, 2 * width :] = streams[EX1].total()
    r.output_out[...] = streams[OUT].total()
    for g in range(2):
        grad = streams[PR0 + g].total()
        for n in range(3):
            r.project_out[:, project_columns(g, n)] = grad[:, n * groups[g] : (n + 1) * groups[g]]
    small_end()
    ready(("dx", 2))
    ready(("dx", 3))
    for i in range(len(chunks) - CHUNK_SLOTS, len(chunks)):
        con_sent(i)
    for name in list(slots)[-2:]:
        stage_sent(name)
    for stream in streams.values():
        stream.drain()
    loop(total - 1, lambda i: small_copy(i + 1).wait_send())


def finish(mesh_shape, sizes, start, operands):
    rows, inner = mesh_shape["dp"], mesh_shape["fsdp"]
    depths = 4
    sides = inner // (2 * depths)
    total = rows * inner
    half = total // 2
    seq, width = operands["dz"].shape
    piece = width // total
    lanes = -(-sum(sizes) // 128) * 128
    in_vmem = ("dz", "logs", "vec", "sums")
    outs = dict(
        hidden_grad=(seq, width),
        contract_out=(4 * piece, width),
        expand_out=(piece, 4 * width),
        output_out=(piece, width),
        project_out=(piece, 3 * width),
        small_out=(1, lanes),
    )
    shapes = (
        (4 * piece, width), (piece, 2 * width), (piece, 2 * width), (piece, width),
        (piece, 3 * FIRST_PAIRS * 128), (piece, 3 * (width - FIRST_PAIRS * 128)),
    )
    span = sides * 2 * piece * 4
    scratch = dict(
        act=pltpu.VMEM((2, seq, span), BF16), act_sem=DMA((2,)),
        dfs=pltpu.VMEM((2, seq, 2 * width), BF16), df_sem=DMA((2,)),
        dhv=pltpu.VMEM((seq, width), F32), dh_sem=DMA(()),
        normedv=pltpu.VMEM((seq, width), BF16), contextv=pltpu.VMEM((seq, width), BF16),
        firstv=pltpu.VMEM((seq, width), BF16), in_sem=DMA((3,)),
        dy=pltpu.VMEM((seq, width), BF16),
        qkv=pltpu.VMEM((2, 4, seq, 128), BF16), qkv_sem=DMA((2, 4)),
        keys_t=pltpu.VMEM((128, seq), BF16),
        dk_sum=pltpu.VMEM((seq, 128), F32), dv_sum=pltpu.VMEM((seq, 128), F32),
        wpv=pltpu.VMEM((width, 3 * width), BF16), wp_sem=DMA(()),
        xs=pltpu.VMEM((2, TILE, width), F32), x_sem=DMA((2,)),
        dxs=pltpu.VMEM((2, TILE, width), F32), dx_sem=DMA((2,)),
        con_stage=pltpu.VMEM((CHUNK_SLOTS, sides, 2, 4 * piece, width), BF16),
        stage=pltpu.VMEM((2, half, 2, piece, 2 * width), BF16),
        small_part=pltpu.VMEM((total, 1, lanes), F32), small_in=pltpu.VMEM((total, 1, lanes), F32),
        small_send=DMA((total - 1,)), small_recv=DMA((total - 1,)),
    )
    for name, side_first in enumerate(SIDE_FIRST):
        fields = stream_scratch(rows, depths, sides, side_first, shapes[name])
        scratch.update({f + str(name): s for f, s in zip(STREAM_FIELDS, fields)})
    names = ("start",) + tuple(operands) + tuple(outs) + tuple(scratch)
    whole_vmem = pl.BlockSpec(memory_space=pltpu.VMEM)
    return pl.pallas_call(
        functools.partial(finish_kernel, mesh_shape, sizes, names),
        out_shape=[jax.ShapeDtypeStruct(s, F32) for s in outs.values()],
        in_specs=[smem()] + [whole_vmem if n in in_vmem else in_hbm() for n in operands],
        out_specs=[in_hbm()] + [whole_vmem] * 5,
        scratch_shapes=list(scratch.values()),
        compiler_params=pltpu.CompilerParams(collective_id=2, has_side_effects=True, vmem_limit_bytes=63 * 2**20),
        name="finish",
    )(start, *operands.values())


def deliver_kernel(sizes, *refs):
    count = (len(refs) - len(sizes) + 1) // 2
    sources, small, targets = refs[: count - 1], refs[count - 1], refs[count:]
    for source, target in zip(sources, targets):
        target[...] = source[...]
    offset = 0
    for size, target in zip(sizes, targets[len(sources) :]):
        target[...] = small[0, offset : offset + size]
        offset += size


def deliver(sizes, *arrays):
    seq, width = arrays[0].shape
    first = lambda i: (0, 0)
    rows = pl.BlockSpec((TILE, width), lambda i: (i, 0))
    fixed = [pl.BlockSpec(a.shape, first) for a in arrays[1:]]
    vectors = [jax.ShapeDtypeStruct((size,), F32) for size in sizes]
    return pl.pallas_call(
        functools.partial(deliver_kernel, sizes),
        grid=(seq // TILE,),
        out_shape=[jax.ShapeDtypeStruct(a.shape, F32) for a in arrays[:-1]] + vectors,
        in_specs=[rows] + fixed,
        out_specs=[rows] + fixed[:-1] + [pl.BlockSpec(v.shape, lambda i: (0,)) for v in vectors],
        compiler_params=params(),
        name="deliver",
    )(*arrays)


def pack(vectors, total):
    joined = jnp.concatenate([v.reshape(total, -1) for v in vectors], 1)
    fill = -joined.shape[1] % 128
    return jnp.pad(joined, ((0, 0), (0, fill)))[:, None]


def unpack(packed, sizes):
    flat = packed.reshape(-1, packed.shape[-1])
    out, at = [], 0
    for size in sizes:
        out.append(flat[:, at : at + size].reshape(-1))
        at += size
    return out


def per_device(
    mesh_shape,
    hidden,
    cotangent,
    lengths,
    thought_start,
    first_gain,
    first_bias,
    project_weight,
    project_bias,
    output_weight,
    output_bias,
    second_gain,
    second_bias,
    expand_weight,
    expand_bias,
    contract_weight,
    contract_bias,
):
    _, seq, width = hidden.shape
    total = mesh_shape["dp"] * mesh_shape["fsdp"]
    vectors = (
        first_gain,
        first_bias,
        project_bias,
        output_bias,
        second_gain,
        second_bias,
        expand_bias,
        contract_bias,
    )
    sizes = [v.shape[0] for v in vectors]
    shards = (pack(vectors, 1)[0], project_weight, output_weight, expand_weight, contract_weight)
    whole_tiles = width // total % 8 == 0
    if whole_tiles:
        *full, mixed, normed, vec = gather_project(mesh_shape, sizes, hidden[0], shards)
    else:
        full = gather_all(mesh_shape, shards)
    Wp, Wo, We, Wc = (w.reshape(-1, w.shape[-1]) for w in full[1:])
    if not whole_tiles:
        mixed, normed, vec = project(hidden[0], full[0], sizes, Wp)
    (
        mixed, normed, x, context, log_total, final, normed_two, active, dz, df, dh, dctx, sums,
    ) = middle(thought_start, lengths, hidden[0], cotangent[0], vec, mixed, normed, (Wo, We, Wc, Wp))
    if whole_tiles:
        operands = dict(
            dz=dz, normed=normed_two, context=context, first_normed=normed, logs=log_total, vec=vec, sums=sums,
            active=active, df=df, dh=dh, mixed=mixed, dctx=dctx, x=x, wp=Wp,
        )
        hidden_grad, dWc, dWe, dWo, dWp, *small = deliver(sizes, *finish(mesh_shape, sizes, thought_start, operands))
        dg1, db1, dbp, dbo, dg2, db2, dbe, dbc = small
        return (final[None], hidden_grad[None], dg1, db1, dWp, dbp, dWo, dbo, dg2, db2, dWe, dbe, dWc, dbc)
    dq, dk, dv = attend_back(mixed, dctx, log_total)
    g1 = vec[0:1, :width]
    dy = dh.astype(BF16)
    x_hat, x_inv = norm_parts(x)
    dmixed = jnp.concatenate([dq, dk, dv], 1)
    da = dot_nt(dmixed, Wp)
    dx = dh + norm_back(da, x_hat, x_inv, g1)
    position = iota((seq, 1), 0)
    is_thought = (position >= thought_start[0]) & (position < thought_start[0] + THOUGHTS)
    hidden_grad = jnp.where(is_thought, 0.0, dx)

    def column_sum(value):
        return jnp.sum(value, axis=0, dtype=F32)

    column = column_sum(dmixed)
    small = (
        column_sum(da * x_hat),
        column_sum(da),
        jnp.concatenate([column[:width], column[2 * width :]]),
        column_sum(dy),
        sums[0],
        sums[1],
        column_sum(df),
        column_sum(dz),
    )
    large = (
        dot_tn(normed, dmixed),
        dot_tn(context, dy),
        dot_tn(normed_two, df),
        dot_tn(active, dz),
    )
    parts = [pack(small, total)]
    for grad in large:
        parts.append(grad.astype(BF16).reshape(total, grad.shape[0] // total, grad.shape[1]))
    small, dWp, dWo, dWe, dWc = scatter_all(mesh_shape, parts)
    dg1, db1, dbp, dbo, dg2, db2, dbe, dbc = unpack(small, sizes)
    return (final[None], hidden_grad[None], dg1, db1, dWp, dbp, dWo, dbo, dg2, db2, dWe, dbe, dWc, dbc)


def solution(mesh):
    rows = P(AXES, None, None)
    flat = P(AXES)
    square = P(AXES, None)
    specs = (flat, flat, square, flat, square, flat, flat, flat, square, flat, square, flat)
    return jax.shard_map(
        functools.partial(per_device, dict(mesh.shape)),
        mesh=mesh,
        in_specs=(rows, rows, flat, flat) + specs,
        out_specs=(rows, rows) + specs,
        check_vma=False,
    )
```

```python
import functools

import jax
import jax.numpy as jnp
from jax import lax
from jax.experimental import pallas as pl
from jax.experimental.pallas import tpu as pltpu
from jax.sharding import PartitionSpec as P

HEADS = 12
THOUGHTS = 3
PREFIX = 384
TILE = 256

EPSILON = 1e-05
NEG_FILL = -1e30
F32 = jnp.float32
BF16 = jnp.bfloat16
VMEM_LIMIT = 62 * 2**20


AXES = ("dp", "fsdp")
ANY = pl.BlockSpec(memory_space=pl.ANY)
DMA = pltpu.SemaphoreType.DMA


class Place:
    def __init__(self, rows, depths, sides):
        self.rows, self.depths, self.sides = rows, depths, sides
        self.row = lax.axis_index("dp")
        flat = lax.axis_index("fsdp")
        self.depth = flat // (sides * 2)
        self.side = flat // 2 % sides
        self.core = flat % 2

    def index(self, row, depth, side, core):
        return row * (self.depths * self.sides * 2) + (depth * self.sides + side) * 2 + core

    def device(self, row, depth, side, core):
        return {"dp": row, "fsdp": (depth * self.sides + side) * 2 + core}


def gather_kernel(rows, depths, sides, count, *refs):
    shards, fulls = refs[:count], refs[count : 2 * count]
    send_sem, recv_sem, pair_send, pair_recv, own_sem = refs[2 * count :]
    at = Place(rows, depths, sides)
    dev = dict(device_id_type=pl.DeviceIdType.MESH)

    barrier = pltpu.get_barrier_semaphore()
    peers = []
    for k in range(1, depths):
        peers.append(at.device(at.row, (at.depth + k) % depths, at.side, at.core))
    for k in range(1, sides):
        peers.append(at.device(at.row, at.depth, (at.side + k) % sides, at.core))
    for k in range(1, rows):
        peers.append(at.device((at.row + k) % rows, at.depth, at.side, at.core))
    peers.append(at.device(at.row, at.depth, at.side, 1 - at.core))
    for peer in peers:
        pl.semaphore_signal(barrier, inc=1, device_id=peer, **dev)
    pl.semaphore_wait(barrier, len(peers))

    def run(core):
        sends = []

        def index(row, depth, side):
            return at.index(row, depth, side, core)

        def send(w, source, shard, peer, slot):
            copy = pltpu.make_async_remote_copy(
                src_ref=source,
                dst_ref=fulls[w].at[shard],
                send_sem=send_sem.at[w, slot],
                recv_sem=recv_sem.at[w, shard],
                device_id=peer,
                **dev,
            )
            copy.start()
            sends.append(copy)

        def arrive(w, shard):
            pltpu.make_async_remote_copy(
                src_ref=fulls[w].at[shard],
                dst_ref=fulls[w].at[shard],
                send_sem=send_sem.at[w, 0],
                recv_sem=recv_sem.at[w, shard],
                device_id=peers[0],
                **dev,
            ).wait_recv()

        def to_pair(w, source, shard):
            copy = pltpu.make_async_remote_copy(
                src_ref=source,
                dst_ref=fulls[w].at[shard],
                send_sem=pair_send.at[w, shard // 2],
                recv_sem=pair_recv.at[w, shard // 2],
                device_id=at.device(at.row, at.depth, at.side, 1 - core),
                **dev,
            )
            copy.start()
            sends.append(copy)

        slots = [0] * count

        def slot(w):
            slots[w] += 1
            return slots[w] - 1

        second_size, third_size = (sides, rows) if core == 0 else (rows, sides)

        def spot(second, third):
            return (third, second) if core == 0 else (second, third)

        mine = (at.side, at.row) if core == 0 else (at.row, at.side)

        def forward_second(w, source, depth):
            row, side = spot(*mine)
            for k in range(1, second_size):
                r, s = spot((mine[0] + k) % second_size, mine[1])
                send(w, source, index(row, depth, side), at.device(r, at.depth, s, core), slot(w))

        def forward_third(w, source, depth, second):
            row, side = spot(second, mine[1])
            for k in range(1, third_size):
                r, s = spot(mine[0], (mine[1] + k) % third_size)
                send(w, source, index(row, depth, side), at.device(r, at.depth, s, core), slot(w))

        own = []
        for w in range(count):
            me = index(at.row, at.depth, at.side)
            for k in range(1, depths):
                send(w, shards[w], me, at.device(at.row, (at.depth + k) % depths, at.side, core), slot(w))
            forward_second(w, shards[w], at.depth)
            forward_third(w, shards[w], at.depth, mine[0])
            to_pair(w, shards[w], me)
            copy = pltpu.make_async_copy(shards[w], fulls[w].at[me], own_sem.at[w])
            copy.start()
            own.append(copy)

        def stage_one(w):
            for k in range(1, depths):
                depth = (at.depth - k) % depths
                shard = index(at.row, depth, at.side)
                arrive(w, shard)
                forward_second(w, fulls[w].at[shard], depth)
                forward_third(w, fulls[w].at[shard], depth, mine[0])
                to_pair(w, fulls[w].at[shard], shard)

        def stage_two(w):
            for k in range(1, second_size):
                second = (mine[0] - k) % second_size
                for d in range(depths):
                    depth = (at.depth - d) % depths
                    shard = index(spot(second, mine[1])[0], depth, spot(second, mine[1])[1])
                    arrive(w, shard)
                    forward_third(w, fulls[w].at[shard], depth, second)
                    to_pair(w, fulls[w].at[shard], shard)

        def stage_three(w):
            for k in range(1, third_size):
                third = (mine[1] - k) % third_size
                for s in range(second_size):
                    second = (mine[0] - s) % second_size
                    for d in range(depths):
                        depth = (at.depth - d) % depths
                        row, side = spot(second, third)
                        shard = index(row, depth, side)
                        arrive(w, shard)
                        to_pair(w, fulls[w].at[shard], shard)

        for step in range(count + 2):
            if step < count:
                stage_one(step)
            if 0 <= step - 1 < count:
                stage_two(step - 1)
            if 0 <= step - 2 < count:
                stage_three(step - 2)

        for w in range(count):
            for row in range(rows):
                for depth in range(depths):
                    for side in range(sides):
                        shard = at.index(row, depth, side, 1 - core)
                        pltpu.make_async_remote_copy(
                            src_ref=fulls[w].at[shard],
                            dst_ref=fulls[w].at[shard],
                            send_sem=pair_send.at[w, shard // 2],
                            recv_sem=pair_recv.at[w, shard // 2],
                            device_id=peers[0],
                            **dev,
                        ).wait_recv()
        for copy in own:
            copy.wait()
        for copy in sends:
            copy.wait_send()

    for core in range(2):

        @pl.when(at.core == core)
        def _():
            run(core)


def gather_all(mesh_shape, shards, collective_id=0):
    rows, inner = mesh_shape["dp"], mesh_shape["fsdp"]
    depths = 4
    sides = inner // (2 * depths)
    total = rows * inner
    count = len(shards)
    sent = (depths - 1) + depths * (max(rows, sides) - 1) + depths * sides * (rows - 1) + depths * rows * (sides - 1)
    return pl.pallas_call(
        functools.partial(gather_kernel, rows, depths, sides, count),
        out_shape=[jax.ShapeDtypeStruct((total,) + s.shape, s.dtype) for s in shards],
        in_specs=[ANY] * count,
        out_specs=[ANY] * count,
        scratch_shapes=[
            DMA((count, sent)),
            DMA((count, total)),
            DMA((count, total // 2)),
            DMA((count, total // 2)),
            DMA((count,)),
        ],
        compiler_params=pltpu.CompilerParams(collective_id=collective_id, has_side_effects=True),
        name="gather_weights",
    )(*shards)


def scatter_kernel(rows, depths, sides, count, *refs):
    parts, outs = refs[:count], refs[count : 2 * count]
    scratch = refs[2 * count :]
    held, pair, third_in, second_in, depth_in = (scratch[i * count : (i + 1) * count] for i in range(5))
    (own_sem, pair_send, pair_recv, third_send, third_recv, second_send, second_recv, depth_send, depth_recv) = scratch[
        5 * count :
    ]
    at = Place(rows, depths, sides)
    dev = dict(device_id_type=pl.DeviceIdType.MESH)

    barrier = pltpu.get_barrier_semaphore()
    peers = []
    for k in range(1, depths):
        peers.append(at.device(at.row, (at.depth + k) % depths, at.side, at.core))
    for k in range(1, sides):
        peers.append(at.device(at.row, at.depth, (at.side + k) % sides, at.core))
    for k in range(1, rows):
        peers.append(at.device((at.row + k) % rows, at.depth, at.side, at.core))
    peers.append(at.device(at.row, at.depth, at.side, 1 - at.core))
    for peer in peers:
        pl.semaphore_signal(barrier, inc=1, device_id=peer, **dev)
    pl.semaphore_wait(barrier, len(peers))

    def run(core):
        second_size, third_size = (sides, rows) if core == 0 else (rows, sides)
        my_second, my_third = (at.side, at.row) if core == 0 else (at.row, at.side)

        def unit(second, third, depth):
            row, side = (third, second) if core == 0 else (second, third)
            return (row * depths + depth) * sides + side

        def device(second, third, depth):
            row, side = (third, second) if core == 0 else (second, third)
            return at.device(row, depth, side, core)

        def remote(source, target, send, recv, peer):
            return pltpu.make_async_remote_copy(
                src_ref=source, dst_ref=target, send_sem=send, recv_sem=recv, device_id=peer, **dev
            )

        sibling = at.device(at.row, at.depth, at.side, 1 - core)

        def pair_copy(w, u):
            return remote(
                parts[w].at[u, 1 - core], pair[w].at[u], pair_send.at[w], pair_recv.at[w, u], sibling
            )

        def own_copy(w):
            return pltpu.make_async_copy(parts[w].at[:, core], held[w], own_sem.at[w])

        def third_copy(w, u, k, q, peer):
            return remote(
                held[w].at[u],
                third_in[w].at[k - 1, q],
                third_send.at[w, k - 1, q],
                third_recv.at[w, k - 1, q],
                peer,
            )

        def second_copy(w, u, k, q, peer):
            return remote(
                held[w].at[u],
                second_in[w].at[k - 1, q],
                second_send.at[w, k - 1, q],
                second_recv.at[w, k - 1, q],
                peer,
            )

        def depth_copy(w, u, k, peer):
            return remote(
                held[w].at[u], depth_in[w].at[k - 1], depth_send.at[w, k - 1], depth_recv.at[w, k - 1], peer
            )

        def loop(size, body):
            lax.fori_loop(0, size, lambda i, c: (body(i), c)[1], 0)

        def each_unit(visit):
            other_second, other_third = third_size, second_size
            far = my_second
            for k in list(range(1, other_third)) + [0]:
                def inner(q, k=k):
                    second, third = q // depths, (far + k) % other_third
                    row, side = (second, third) if core == 0 else (third, second)
                    visit((row * depths + q % depths) * sides + side)
                loop(other_second * depths, inner)

        for w in range(count):
            each_unit(lambda u, w=w: pair_copy(w, u).start())
            own_copy(w).start()

        def add_pair(w, u):
            pair_copy(w, u).wait_recv()
            held[w][u] = held[w][u] + pair[w][u]

        def stage_third(w):
            own_copy(w).wait()
            for k in list(range(1, third_size)) + [0]:
                third = (my_third + k) % third_size

                def inner(q, k=k, third=third):
                    second, depth = q // depths, q % depths
                    u = unit(second, third, depth)
                    add_pair(w, u)
                    if k:
                        third_copy(w, u, k, q, device(my_second, third, at.depth)).start()

                loop(second_size * depths, inner)

        def stage_second(w):
            for k in list(range(1, second_size)) + [0]:
                second = (my_second + k) % second_size

                def inner(depth, k=k, second=second):
                    u = unit(second, my_third, depth)
                    for j in range(1, third_size):
                        third_copy(w, u, j, second * depths + depth, sibling).wait_recv()
                        held[w][u] = held[w][u] + third_in[w][j - 1, second * depths + depth]
                    if k:
                        second_copy(w, u, k, depth, device(second, my_third, at.depth)).start()

                loop(depths, inner)

        def stage_depth(w):
            for k in list(range(1, depths)) + [0]:
                depth = (at.depth + k) % depths
                u = unit(my_second, my_third, depth)
                for j in range(1, second_size):
                    second_copy(w, u, j, depth, sibling).wait_recv()
                    held[w][u] = held[w][u] + second_in[w][j - 1, depth]
                if k:
                    depth_copy(w, u, k, device(my_second, my_third, depth)).start()

        def stage_last(w):
            u = unit(my_second, my_third, at.depth)
            total = held[w][u].astype(jnp.float32)
            for k in range(1, depths):
                depth_copy(w, u, k, sibling).wait_recv()
                total = total + depth_in[w][k - 1].astype(jnp.float32)
            outs[w][...] = total

        for step in range(count + 3):
            for lag, stage in enumerate((stage_third, stage_second, stage_depth, stage_last)):
                if 0 <= step - lag < count:
                    stage(step - lag)

        for w in range(count):
            remote(pair[w], pair[w], pair_send.at[w], pair_recv.at[w, 0], sibling).wait_send()
            for k in range(1, third_size):
                loop(second_size * depths, lambda q, w=w, k=k: third_copy(w, 0, k, q, sibling).wait_send())
            for k in range(1, second_size):
                loop(depths, lambda q, w=w, k=k: second_copy(w, 0, k, q, sibling).wait_send())
            for k in range(1, depths):
                depth_copy(w, 0, k, sibling).wait_send()

    for core in range(2):

        @pl.when(at.core == core)
        def _():
            run(core)


def scatter_all(mesh_shape, parts, collective_id=1):
    rows, inner = mesh_shape["dp"], mesh_shape["fsdp"]
    depths = 4
    sides = inner // (2 * depths)
    total = rows * inner
    half = total // 2
    count = len(parts)
    if rows == sides:
        thirds, seconds = (rows - 1, sides * depths), (sides - 1, depths)
    else:
        wide = max(rows, sides)
        thirds, seconds = (wide - 1, wide * depths), (wide - 1, depths)
    scratch = []
    for lead in ((half,), (half,), thirds, seconds, (depths - 1,)):
        scratch += [pltpu.VMEM(lead + p.shape[1:], p.dtype) for p in parts]
    parts = [p.reshape((half, 2) + p.shape[1:]) for p in parts]
    sems = [
        (), (), (half,), thirds, thirds, seconds, seconds, (depths - 1,), (depths - 1,),
    ]
    return pl.pallas_call(
        functools.partial(scatter_kernel, rows, depths, sides, count),
        out_shape=[jax.ShapeDtypeStruct(p.shape[2:], jnp.float32) for p in parts],
        in_specs=[ANY] * count,
        out_specs=[pl.BlockSpec(memory_space=pltpu.VMEM)] * count,
        scratch_shapes=scratch + [DMA((count,) + s) for s in sems],
        compiler_params=pltpu.CompilerParams(
            collective_id=collective_id, has_side_effects=True, vmem_limit_bytes=60 * 2**20
        ),
        name="scatter_grads",
    )(*parts)


def dot(left, right):
    return jnp.dot(left, right, preferred_element_type=F32)


def dot_nt(left, right):
    return lax.dot_general(left, right, (((1,), (1,)), ((), ())), preferred_element_type=F32)


def dot_tn(left, right):
    return lax.dot_general(left, right, (((0,), (0,)), ((), ())), preferred_element_type=F32)


def norm_parts(value):
    center = value - jnp.mean(value, axis=-1, keepdims=True)
    inv = lax.rsqrt(jnp.mean(center * center, axis=-1, keepdims=True) + EPSILON)
    return center * inv, inv


def norm_back(grad, hat, inv, gain):
    scaled = grad * gain
    return inv * (
        scaled
        - jnp.mean(scaled, axis=-1, keepdims=True)
        - hat * jnp.mean(scaled * hat, axis=-1, keepdims=True)
    )


GELU_ROOT = 0.7978845608028654


def gelu_parts(value):
    square = value * value
    inner = jnp.tanh(GELU_ROOT * value * (1.0 + 0.044715 * square))
    half = 0.5 * (1.0 + inner)
    slope = half + 0.5 * value * (1.0 - inner * inner) * (GELU_ROOT + 3 * 0.044715 * GELU_ROOT * square)
    return value * half, slope


def iota(shape, axis):
    return lax.broadcasted_iota(jnp.int32, shape, axis)


def wide(row):
    return jnp.broadcast_to(row, (16, row.shape[1])).astype(BF16)


def head_mask(width):
    return iota((16, width), 1) // (width // HEADS) == iota((16, width), 0)


def spread(row, mask):
    return jnp.where(mask, jnp.broadcast_to(row.astype(F32), mask.shape), 0.0).astype(BF16)


def collect(rows, mask):
    return jnp.sum(jnp.where(mask, rows, 0.0), axis=0, keepdims=True)


def row_softmax(spread_query, keys, place):
    score = dot_nt(spread_query, keys) * 0.125
    score = jnp.where(iota(score.shape, 1) <= place, score, NEG_FILL)
    expo = jnp.exp(score - jnp.max(score, axis=-1, keepdims=True))
    return expo / jnp.sum(expo, axis=-1, keepdims=True)


def pick_rows(first, array):
    chosen = iota((16, array.shape[0]), 1) == first + iota((16, array.shape[0]), 0)
    return dot(chosen.astype(F32).astype(BF16), array)


VECTORS = ("g1", "b1", "bp", "bo", "g2", "b2", "be", "bc")


class Vectors:
    def __init__(self, ref, width):
        self.ref, self.width = ref, width
        self.sizes = dict(bp=3 * width, be=4 * width)

    def __getattr__(self, name):
        return self.ref[VECTORS.index(name) : VECTORS.index(name) + 1, : self.sizes.get(name, self.width)]


def spread_vectors(pieces, sizes, width, vec_ref):
    count, offset = pieces.shape[0], 0
    vec_ref[...] = jnp.zeros_like(vec_ref)
    for row, (name, size) in enumerate(zip(VECTORS, sizes)):
        low, high = offset // 128 * 128, -(-(offset + size) // 128) * 128
        length = count * size
        lane = iota((1, length), 1)
        pick = iota((high - low, length), 0) == lane % size + (offset - low)
        tiled = dot(pieces[:, low:high], pick.astype(F32).astype(BF16))
        line = jnp.sum(jnp.where(iota((count, length), 0) == lane // size, tiled, 0.0), axis=0, keepdims=True)
        if name == "bp":
            vec_ref[row : row + 1, :width] = line[:, :width]
            vec_ref[row : row + 1, 2 * width : 3 * width] = line[:, width:]
        else:
            vec_ref[row : row + 1, :length] = line
        offset += size


def fetch(sources, targets, sems):
    copies = [pltpu.make_async_copy(s, t, sems.at[i]) for i, (s, t) in enumerate(zip(sources, targets))]
    for copy in copies:
        copy.start()
    return copies


def aligned(place):
    return pl.multiple_of(place // 16 * 16, 16)


def project_kernel(sizes, hidden_ref, pieces_ref, wp_ref, mixed_ref, normed_ref, vec_ref):
    seq, width = hidden_ref.shape
    spread_vectors(pieces_ref[:, 0, :], sizes, width, vec_ref)
    vec = Vectors(vec_ref, width)
    for at in range(0, seq, TILE):
        part = slice(at, at + TILE)
        normed = (norm_parts(hidden_ref[part].astype(F32))[0] * vec.g1 + vec.b1).astype(BF16)
        normed_ref[part] = normed
        mixed_ref[part] = (dot(normed, wp_ref[...]) + vec.bp).astype(BF16)


def smem():
    return pl.BlockSpec(memory_space=pltpu.SMEM)


def whole(array):
    return pl.BlockSpec(array.shape, lambda *_: (0,) * array.ndim, pipeline_mode=pl.Buffered(1))


def params(semantics=("arbitrary",)):
    return pltpu.CompilerParams(dimension_semantics=semantics, vmem_limit_bytes=VMEM_LIMIT)


def in_hbm():
    return pl.BlockSpec(memory_space=pl.ANY)


def project(hidden, pieces, sizes, weight):
    seq, width = hidden.shape
    outs = [
        jax.ShapeDtypeStruct((seq, 3 * width), BF16),
        jax.ShapeDtypeStruct((seq, width), BF16),
        jax.ShapeDtypeStruct((8, 4 * width), F32),
    ]
    return pl.pallas_call(
        functools.partial(project_kernel, sizes),
        grid=(1,),
        out_shape=outs,
        in_specs=[whole(hidden), whole(pieces), whole(weight)],
        out_specs=[whole(o) for o in outs],
        compiler_params=params(),
        name="project",
    )(hidden, pieces, weight)


def pair_spec(seq, offset, lanes=128):
    return pl.BlockSpec((seq, lanes), lambda i: (0, offset + i))


def attend_back_kernel(query_ref, key_ref, value_ref, up_ref, log_ref, dq_ref, dk_ref, dv_ref, dk_sum, dv_sum):
    seq, lanes = query_ref.shape
    half = lanes // 2
    first_head = iota((TILE, lanes), 1) < half
    keys_t = key_ref[...].T
    for start in reversed(range(0, seq, TILE)):
        stop = start + TILE
        query = query_ref[start:stop].astype(F32) * 0.125
        upstream = up_ref[start:stop].astype(F32)
        outs = []
        for head in range(2):
            own = first_head if head == 0 else jnp.logical_not(first_head)
            masked = jnp.where(own, query, 0.0).astype(BF16)
            up_masked = jnp.where(own, upstream, 0.0).astype(BF16)
            score = dot_nt(key_ref[:stop], masked)
            hidden = iota((TILE, TILE), 0) > iota((TILE, TILE), 1)
            last = jnp.where(hidden, NEG_FILL, score[start:])
            score = jnp.concatenate([score[:start], last], 0) if start else last
            prob = jnp.exp(score - log_ref[head : head + 1, start:stop])
            prob_grad = dot_nt(value_ref[:stop], up_masked)
            inner = jnp.sum(prob * prob_grad, axis=0, keepdims=True)
            score_grad = (prob * (prob_grad - inner)).astype(BF16)
            dv = dot(prob.astype(BF16), up_masked)
            dk = dot(score_grad, masked)
            if stop == seq and head == 0:
                dv_sum[...] = dv
                dk_sum[...] = dk
            else:
                dv_sum[:stop] += dv
                dk_sum[:stop] += dk
            outs.append(dot(keys_t[:, :stop], score_grad)[head * half : (head + 1) * half])
        dq_ref[start:stop] = (jnp.concatenate(outs, 0).T * 0.125).astype(BF16)
    dk_ref[...] = dk_sum[...].astype(BF16)
    dv_ref[...] = dv_sum[...].astype(BF16)


def attend_back(mixed, upstream, log_total):
    seq, width = upstream.shape
    pairs = HEADS // 2
    out = jax.ShapeDtypeStruct((seq, width), BF16)
    return pl.pallas_call(
        attend_back_kernel,
        grid=(pairs,),
        out_shape=[out, out, out],
        in_specs=[
            pair_spec(seq, 0),
            pair_spec(seq, pairs),
            pair_spec(seq, 2 * pairs),
            pair_spec(seq, 0),
            pl.BlockSpec((None, 2, seq), lambda i: (i, 0, 0)),
        ],
        out_specs=[pair_spec(seq, 0)] * 3,
        scratch_shapes=[pltpu.VMEM((seq, 128), F32), pltpu.VMEM((seq, 128), F32)],
        compiler_params=params(),
        name="attend_back",
    )(mixed, mixed, mixed, upstream, log_total)


def tall(row):
    return jnp.concatenate([jnp.broadcast_to(row[i : i + 1], (16, row.shape[1])) for i in range(THOUGHTS)], 0)


def middle_kernel(
    start_ref, length_ref, hidden_ref, cot_ref, vec_ref,
    mixed_hbm, normed_hbm, wo_hbm, we_hbm, wc_hbm, wp_hbm,
    mixed_out, normed_out, x_out, context_out, log_ref, final_out, normed_two_out, active_out, dz_out, df_out,
    dh_out, dctx_out, sums_ref,
    mixed_ref, x_ref, context_ref, resid_ref, dh_ref, dctx_ref, dz_ref, normed_two_ref,
    wo_ref, we_ref, wc_ref, wp_ref, final_ref, active_ref, df_ref, edge_normed, edge_df,
    weight_sems, mixed_sems, tile_sems, out_sems, edge_sems,
):
    seq, width = hidden_ref.shape
    inner = we_ref.shape[1]
    copy = pltpu.make_async_copy
    first_rows = copy(mixed_hbm.at[:PREFIX], mixed_ref.at[:PREFIX], mixed_sems.at[0])
    first_rows.start()
    sources, targets = (wo_hbm, we_hbm, wc_hbm, wp_hbm), (wo_ref, we_ref, wc_ref, wp_ref)
    weights = fetch(sources, targets, weight_sems)
    other_rows = copy(mixed_hbm.at[PREFIX:], mixed_ref.at[PREFIX:], mixed_sems.at[1])
    other_rows.start()
    start = start_ref[0]
    base = aligned(start - 1)
    edge = pl.ds(base, 32)
    edge_row = base + iota((32, 1), 0)
    load_edge = copy(normed_hbm.at[edge], edge_normed, edge_sems.at[0])
    load_edge.start()
    vec = Vectors(vec_ref, width)
    mask = head_mask(width)
    queries, keys, values = (mixed_ref.at[:, i * width : (i + 1) * width] for i in range(3))
    first_keys, first_values = keys.at[:PREFIX], values.at[:PREFIX]
    for at in range(0, seq, TILE):
        x_ref[at : at + TILE] = hidden_ref[at : at + TILE].astype(F32)

    x_row = x_ref[pl.ds(start - 1, 1), :]
    first_rows.wait()
    query = pick_rows(start - 1, queries[:PREFIX])[0:1]
    load_edge.wait()
    for step in range(THOUGHTS):
        place = start - 1 + step
        prob = row_softmax(spread(query, mask), first_keys[...], place)
        context = collect(dot(prob.astype(BF16), first_values[...]), mask)
        if step == 0:
            weights[0].wait()
        resid = x_row + (dot(wide(context), wo_ref[...])[0:1] + vec.bo)
        normed = norm_parts(resid)[0] * vec.g2 + vec.b2
        if step == 0:
            weights[1].wait()
        pre = dot(wide(normed), we_ref[...])[0:1] + vec.be
        active = gelu_parts(pre)[0]
        if step == 0:
            weights[2].wait()
        x_row = resid + (dot(wide(active), wc_ref[...])[0:1] + vec.bc)
        normed = norm_parts(x_row)[0] * vec.g1 + vec.b1
        if step == 0:
            weights[3].wait()
        mixed_row = dot(wide(normed), wp_ref[...])[0:1] + vec.bp
        query = mixed_row[:, :width].astype(BF16)
        x_ref[pl.ds(place + 1, 1), :] = x_row
        window = pl.ds(aligned(place + 1), 16)
        here = aligned(place + 1) + iota((16, 1), 0) == place + 1
        mixed_ref[window, :] = jnp.where(here, mixed_row, mixed_ref[window, :].astype(F32)).astype(BF16)
        edge_normed[...] = jnp.where(edge_row == place + 1, normed, edge_normed[...].astype(F32)).astype(BF16)
    other_rows.wait()
    pending = [
        copy(mixed_ref.at[edge], mixed_out.at[edge], edge_sems.at[0]),
        copy(edge_normed, normed_out.at[edge], edge_sems.at[1]),
        copy(x_ref, x_out, out_sems.at[0]),
    ]
    for c in pending:
        c.start()

    half, block = 64, seq // 2
    first_head = iota((block, 128), 1) < half
    later = iota((block, block), 0) > iota((block, block), 1)
    for pair in range(HEADS // 2):
        columns = slice(pair * 128, pair * 128 + 128)
        values_t = values[:, columns].T
        for at in range(0, seq, block):
            stop = at + block
            query = queries[at:stop, columns].astype(F32) * 0.125
            scores = []
            for head in range(2):
                own = first_head if head == 0 else jnp.logical_not(first_head)
                score = dot_nt(keys[:stop, columns], jnp.where(own, query, 0.0).astype(BF16))
                last = jnp.where(later, NEG_FILL, score[at:])
                scores.append(jnp.concatenate([score[:at], last], 0) if at else last)
            peaks = [jnp.max(score, axis=0, keepdims=True) for score in scores]
            expos = [jnp.exp(score - peak) for score, peak in zip(scores, peaks)]
            totals = [jnp.sum(expo, axis=0, keepdims=True) for expo in expos]
            outs = []
            for head in range(2):
                out = dot(values_t[:, :stop], expos[head].astype(BF16)) * (1.0 / totals[head])
                outs.append(out[head * half : (head + 1) * half])
                log_ref[pair, head : head + 1, at:stop] = peaks[head] + jnp.log(totals[head])
            context_ref[at:stop, columns] = jnp.concatenate(outs, 0).T.astype(BF16)
    pending.append(copy(context_ref, context_out, out_sems.at[1]))
    pending[-1].start()

    sums_ref[...] = jnp.zeros_like(sums_ref)
    tiles = (final_ref, active_ref, df_ref)
    tile_outs = (final_out, active_out, df_out)

    def tile_copies(i):
        slot = i % 2
        rows = pl.ds(i * TILE, TILE)
        return [copy(t.at[slot], o.at[rows], tile_sems.at[slot, n]) for n, (t, o) in enumerate(zip(tiles, tile_outs))]

    for i in range(seq // TILE):
        slot = i % 2
        rows = slice(i * TILE, i * TILE + TILE)
        if i >= 2:
            for c in tile_copies(i - 2):
                c.wait()
        valid = i * TILE + iota((TILE, 1), 0) < length_ref[0]
        resid = x_ref[rows] + (dot(context_ref[rows], wo_ref[...]) + vec.bo)
        resid_ref[rows] = resid
        hat, inv = norm_parts(resid)
        normed = (hat * vec.g2 + vec.b2).astype(BF16)
        normed_two_ref[rows] = normed
        dout = jnp.where(valid, cot_ref[rows].astype(F32), 0.0)
        dz = dout.astype(BF16)
        dz_ref[rows] = dz
        total = jnp.zeros((TILE, width), F32)
        dc = jnp.zeros((TILE, width), F32)
        for at in range(0, inner, width):
            part = slice(at, at + width)
            value, slope = gelu_parts(dot(normed, we_ref[:, part]) + vec.be[:, part])
            value = value.astype(BF16)
            active_ref[slot, :, part] = value
            total = total + dot(value, wc_ref[part])
            df = (dot_nt(dz, wc_ref[part]) * slope).astype(BF16)
            df_ref[slot, :, part] = df
            dc = dc + dot_nt(df, we_ref[:, part])
        final_ref[slot] = jnp.where(valid, resid + (total + vec.bc), 0.0)
        dh = dout + norm_back(dc, hat, inv, vec.g2)
        dh_ref[rows] = dh
        dctx_ref[rows] = dot_nt(dh.astype(BF16), wo_ref[...]).astype(BF16)
        sums_ref[0:1] += jnp.sum(dc * hat, axis=0, keepdims=True)
        sums_ref[1:2] += jnp.sum(dc, axis=0, keepdims=True)
        for c in tile_copies(i):
            c.start()
    pending.append(copy(normed_two_ref, normed_two_out, out_sems.at[2]))
    pending[-1].start()

    masks = jnp.concatenate([mask] * THOUGHTS, 0)

    def split(rows):
        picked = jnp.where(masks, rows, 0.0)
        return jnp.concatenate(
            [jnp.sum(picked[16 * i : 16 * i + 16], axis=0, keepdims=True) for i in range(THOUGHTS)], 0
        )

    def spread_all(rows):
        return jnp.where(masks, tall(rows), 0.0).astype(BF16)

    behind = iota((16, seq), 1)
    logs = jnp.concatenate([log_ref[i] for i in range(HEADS // 2)] + [jnp.zeros((4, seq), F32)], 0)
    ones = mask.astype(F32).astype(BF16)
    delta = []
    for at in range(0, seq, TILE):
        product = dctx_ref[at : at + TILE].astype(F32) * context_ref[at : at + TILE].astype(F32)
        high = product.astype(BF16)
        delta.append(dot_nt(ones, high) + dot_nt(ones, (product - high.astype(F32)).astype(BF16)))
    delta = jnp.concatenate(delta, 1)
    key_rows = spread_all(pick_rows(start, first_keys[...]))
    value_rows = spread_all(pick_rows(start, first_values[...]))
    score = dot_nt(key_rows, queries[...])
    prob_grad = dot_nt(value_rows, dctx_ref[...])
    probs, grads = [], []
    for i in range(THOUGHTS):
        part = slice(16 * i, 16 * i + 16)
        prob = jnp.where(behind >= start + i, jnp.exp(0.125 * score[part] - logs), 0.0)
        probs.append(prob.astype(BF16))
        grads.append((prob * (prob_grad[part] - delta)).astype(BF16))
    main_dk = split(dot(jnp.concatenate(grads, 0), queries[...])) * 0.125
    main_dv = split(dot(jnp.concatenate(probs, 0), dctx_ref[...]))

    def row_back(query, up, place):
        score = dot_nt(query, first_keys[...]) * 0.125
        score = jnp.where(iota(score.shape, 1) <= place, score, NEG_FILL)
        expo = jnp.exp(score - jnp.max(score, axis=-1, keepdims=True))
        prob = expo / jnp.sum(expo, axis=-1, keepdims=True)
        prob_grad = dot_nt(up, first_values[...])
        grad = (prob * (prob_grad - jnp.sum(prob * prob_grad, axis=-1, keepdims=True))).astype(BF16)
        return prob.astype(BF16), grad, dot(grad, first_keys[...]) * 0.125

    places = start + iota((16 * THOUGHTS, 1), 0) // 16
    up = spread_all(pick_rows(start, dctx_ref[:PREFIX]))
    main_dq = split(row_back(spread_all(pick_rows(start, queries[:PREFIX])), up, places)[2])
    query_rows = pick_rows(start - 1, queries[:PREFIX])
    rows = [start - 1 + step for step in range(THOUGHTS)]
    resid = jnp.concatenate([resid_ref[pl.ds(p, 1), :] for p in rows] + [jnp.zeros((13, width), F32)], 0)
    resid_hat, resid_inv = norm_parts(resid)
    normed = (resid_hat * vec.g2 + vec.b2).astype(BF16)
    slopes = gelu_parts(dot(normed, we_ref[...]) + vec.be)[1]
    for i in range(seq // TILE - 2, seq // TILE):
        for c in tile_copies(i):
            c.wait()
    load_edge = copy(df_out.at[edge], edge_df, edge_sems.at[2])
    load_edge.start()
    scores, spreads, probs, ups, df_rows = [], [], [], [], []
    dq_add = jnp.zeros((1, width), F32)
    for step in reversed(range(THOUGHTS)):
        place = rows[step]
        dq_row = main_dq[step : step + 1] + dq_add
        dk_row, dv_row = main_dk[step : step + 1], main_dv[step : step + 1]
        for score, query, prob, up in zip(scores, spreads, probs, ups):
            chosen = iota(score.shape, 1) == place + 1
            share = jnp.sum(jnp.where(chosen, score.astype(F32), 0.0), axis=1, keepdims=True)
            dk_row = dk_row + 0.125 * jnp.sum(share * query.astype(F32), axis=0, keepdims=True)
            share = jnp.sum(jnp.where(chosen, prob.astype(F32), 0.0), axis=1, keepdims=True)
            dv_row = dv_row + jnp.sum(share * up.astype(F32), axis=0, keepdims=True)
        x_hat, x_inv = norm_parts(x_ref[pl.ds(place + 1, 1), :])
        da = dot_nt(wide(jnp.concatenate([dq_row, dk_row, dv_row], 1)), wp_ref[...])
        dz = dh_ref[pl.ds(place + 1, 1), :] + norm_back(da[0:1], x_hat, x_inv, vec.g1)
        df = dot_nt(wide(dz), wc_ref[...])[0:1] * slopes[step : step + 1]
        dc = dot_nt(wide(df), we_ref[...])[0:1]
        hat, inv = resid_hat[step : step + 1], resid_inv[step : step + 1]
        dh = dz + norm_back(dc, hat, inv, vec.g2)
        sums_ref[0:1] += dc * hat
        sums_ref[1:2] += dc
        dctx = dot_nt(wide(dh), wo_ref[...])[0:1]
        query, up = spread(query_rows[step : step + 1], mask), spread(dctx, mask)
        if step:
            prob, score, dq = row_back(query, up, place)
            dq_add = collect(dq, mask)
            scores.append(score)
            spreads.append(query)
            probs.append(prob)
            ups.append(up)
        dh_ref[pl.ds(place, 1), :] += dh
        df_rows.append(df)
        for target, row in ((dz_ref, dz), (dctx_ref, dctx)):
            row = jnp.where(edge_row == place, row, 0.0)
            target[edge, :] = (target[edge, :].astype(F32) + row).astype(BF16)
    load_edge.wait()
    added = sum(jnp.where(edge_row == p, df, 0.0) for p, df in zip(reversed(rows), df_rows))
    edge_df[...] = (edge_df[...].astype(F32) + added).astype(BF16)
    last = [
        copy(edge_df, df_out.at[edge], edge_sems.at[2]),
        copy(dz_ref, dz_out, out_sems.at[3]),
        copy(dctx_ref, dctx_out, out_sems.at[4]),
        copy(dh_ref, dh_out, out_sems.at[5]),
    ]
    for c in last:
        c.start()
    for c in pending + last:
        c.wait()


def middle(start, length, hidden, cotangent, vec, mixed, normed, weights):
    seq, width = hidden.shape
    inner = weights[1].shape[1]
    shape = jax.ShapeDtypeStruct
    flat, pairs = (seq, width), (HEADS // 2, 2, seq)
    outs = [
        (mixed.shape, BF16), (flat, BF16), (flat, F32), (flat, BF16), (pairs, F32), (flat, F32), (flat, BF16),
        ((seq, inner), BF16), (flat, BF16), ((seq, inner), BF16), (flat, F32), (flat, BF16), ((8, width), F32),
    ]
    whole_vmem = pl.BlockSpec(memory_space=pltpu.VMEM)
    out_specs = [whole_vmem if i in (4, 12) else in_hbm() for i in range(len(outs))]
    kept = [
        (mixed.shape, BF16), (flat, F32), (flat, BF16), (flat, F32), (flat, F32), (flat, BF16), (flat, BF16), (flat, BF16),
    ]
    tiles = [((2, TILE, width), F32), ((2, TILE, inner), BF16), ((2, TILE, inner), BF16)]
    edges = [((32, width), BF16), ((32, inner), BF16)]
    buffers = kept + [(w.shape, w.dtype) for w in weights] + tiles + edges
    return pl.pallas_call(
        middle_kernel,
        out_shape=[shape(*o) for o in outs],
        in_specs=[smem(), smem()] + [whole_vmem] * 3 + [in_hbm()] * (2 + len(weights)),
        out_specs=out_specs,
        scratch_shapes=[pltpu.VMEM(*b) for b in buffers]
        + [DMA((4,)), DMA((2,)), DMA((2, 3)), DMA((6,)), DMA((3,))],
        input_output_aliases={5: 0, 6: 1},
        compiler_params=pltpu.CompilerParams(vmem_limit_bytes=VMEM_LIMIT),
        name="middle",
    )(start, length, hidden, cotangent, vec, mixed, normed, *weights)


class Refs:
    def __init__(self, names, refs):
        self.__dict__.update(zip(names, refs))


MESH = dict(device_id_type=pl.DeviceIdType.MESH)


class Stream:
    def __init__(self, at, side_first, name, refs):
        self.at, self.side_first = at, side_first
        for field in STREAM_FIELDS:
            setattr(self, field, getattr(refs, field + str(name)))
        self.sizes = (at.rows, at.sides) if side_first else (at.sides, at.rows)
        self.mine = (at.row, at.side) if side_first else (at.side, at.row)
        self.sent = []

    def spot(self, second, third):
        return (second, third) if self.side_first else (third, second)

    def unit(self, second, third, depth):
        row, side = self.spot(second, third)
        return (row * self.at.depths + depth) * self.at.sides + side

    def remote(self, source, target, send, recv, peer):
        return pltpu.make_async_remote_copy(
            src_ref=source, dst_ref=target, send_sem=send, recv_sem=recv, device_id=peer, **MESH
        )

    def sibling(self):
        return self.at.device(self.at.row, self.at.depth, self.at.side, 1 - self.at.core)

    def pair_copy(self, u, source):
        return self.remote(source, self.pair.at[u], self.pair_send.at[u], self.pair_recv.at[u], self.sibling())

    def third_copy(self, u, k, q):
        peer = self.at.device(*self.place(self.mine[0], (self.mine[1] + k) % self.sizes[1], self.at.depth))
        return self.remote(
            self.held.at[u], self.third.at[k - 1, q], self.third_send.at[k - 1, q], self.third_recv.at[k - 1, q], peer
        )

    def second_copy(self, u, k, depth):
        peer = self.at.device(*self.place((self.mine[0] + k) % self.sizes[0], self.mine[1], self.at.depth))
        return self.remote(
            self.held.at[u],
            self.second.at[k - 1, depth],
            self.second_send.at[k - 1, depth],
            self.second_recv.at[k - 1, depth],
            peer,
        )

    def depth_copy(self, u, k):
        peer = self.at.device(*self.place(*self.mine, (self.at.depth + k) % self.at.depths))
        return self.remote(
            self.held.at[u], self.depth.at[k - 1], self.depth_send.at[k - 1], self.depth_recv.at[k - 1], peer
        )

    def place(self, second, third, depth):
        row, side = self.spot(second, third)
        return row, depth, side, self.at.core

    def third_step(self, k, j, d, source):
        depths = self.at.depths
        second, depth = (self.mine[0] + j) % self.sizes[0], (self.at.depth + d) % depths
        q = second * depths + depth
        u = self.unit(second, (self.mine[1] + k) % self.sizes[1], depth)
        own = source(u)
        self.pair_copy(u, own).wait_recv()
        self.held[u] = own[...] + self.pair[u]
        if k:
            self.third_copy(u, k, q).start()

    def second_step(self, d):
        depth = (self.at.depth + d) % self.at.depths
        for k in list(range(1, self.sizes[0])) + [0]:
            second = (self.mine[0] + k) % self.sizes[0]
            u = self.unit(second, self.mine[1], depth)
            q = second * self.at.depths + depth
            for j in range(1, self.sizes[1]):
                self.third_copy(u, j, q).wait_recv()
                self.held[u] = self.held[u] + self.third[j - 1, q]
            if k:
                self.second_copy(u, k, depth).start()

    def depth_step(self, k):
        depth = (self.at.depth + k) % self.at.depths
        u = self.unit(*self.mine, depth)
        for j in range(1, self.sizes[0]):
            self.second_copy(u, j, depth).wait_recv()
            self.held[u] = self.held[u] + self.second[j - 1, depth]
        if k:
            self.depth_copy(u, k).start()

    def total(self):
        u = self.unit(*self.mine, self.at.depth)
        total = self.held[u].astype(F32)
        for k in range(1, self.at.depths):
            self.depth_copy(u, k).wait_recv()
            total = total + self.depth[k - 1].astype(F32)
        return total

    def drain(self):
        count = self.sizes[0] * self.at.depths
        for k in range(1, self.sizes[1]):
            loop(count, lambda q, k=k: self.third_copy(0, k, q).wait_send())
        for k in range(1, self.sizes[0]):
            loop(self.at.depths, lambda d, k=k: self.second_copy(0, k, d).wait_send())
        for k in range(1, self.at.depths):
            self.depth_copy(0, k).wait_send()


def loop(size, body):
    lax.fori_loop(0, size, lambda i, c: (body(i), c)[1], 0)


class Spread:
    def __init__(self, at, axes, source, full, send, recv, pair_recv):
        self.at, self.axes, self.source, self.full = at, axes, source, full
        self.send_sem, self.recv_sem, self.pair_recv = send, recv, pair_recv
        self.sizes = [(at.rows, at.depths, at.sides)[a] for a in axes]
        self.mine = [(at.row, at.depth, at.side)[a] for a in axes]

    def spot(self, steps):
        where = [0, 0, 0]
        for axis, mine, size, step in zip(self.axes, self.mine, self.sizes, steps):
            where[axis] = (mine - step) % size
        return where

    def unit(self, steps):
        row, depth, side = self.spot(steps)
        return (row * self.at.depths + depth) * self.at.sides + side

    def copy(self, steps, source, recv, peer):
        return pltpu.make_async_remote_copy(
            src_ref=source,
            dst_ref=self.full(2 * self.unit(steps) + self.at.core),
            send_sem=self.send_sem,
            recv_sem=recv.at[self.unit(steps)],
            device_id=peer,
            **MESH,
        )

    def forward(self, level, steps):
        at = self.at
        source = self.full(2 * self.unit(steps) + at.core) if level else self.source
        for axis in range(level, 3):
            for k in range(1, self.sizes[axis]):
                row, depth, side = self.spot([-k if i == axis else 0 for i in range(3)])
                self.copy(steps, source, self.recv_sem, at.device(row, depth, side, at.core)).start()
        sibling = at.device(at.row, at.depth, at.side, 1 - at.core)
        self.copy(steps, source, self.pair_recv, sibling).start()

    def arrive(self, level, steps):
        unit = self.full(2 * self.unit(steps) + self.at.core)
        self.copy(steps, unit, self.recv_sem, self.at.device(*self.spot([0, 0, 0]), self.at.core)).wait_recv()
        self.forward(level, steps)

    def siblings(self, count):
        def wait(u):
            unit = self.full(2 * u + 1 - self.at.core)
            pltpu.make_async_remote_copy(
                src_ref=unit, dst_ref=unit, send_sem=self.send_sem, recv_sem=self.pair_recv.at[u],
                device_id=self.at.device(*self.spot([0, 0, 0]), 1 - self.at.core), **MESH,
            ).wait_recv()

        loop(count, wait)

    def drain(self, total):
        every = self.full(pl.ds(0, total - 1))
        pltpu.make_async_remote_copy(
            src_ref=every, dst_ref=every, send_sem=self.send_sem, recv_sem=self.recv_sem.at[0],
            device_id=self.at.device(*self.spot([0, 0, 0]), 1 - self.at.core), **MESH,
        ).wait_send()


PARTS = (
    (0, None, (1, 2, 0)),
    (1, None, (1, 2, 0)),
    (4, None, (1, 0, 2)),
    (3, 1, (1, 2, 0)),
    (2, None, (1, 2, 0)),
    (3, 0, (1, 0, 2)),
)
GATHER_ORDER = (
    (1, 0, 1), (1, 0, 2), (1, 0, 3), (2, 0, 1, 0), (3, 0, 1, 0, 0), (2, 1, 1, 0), (3, 1, 1, 0, 0), (1, 1, 1),
    (3, 2, 1, 0, 0), (2, 2, 1, 0), (1, 1, 2), (2, 3, 1, 0), (3, 3, 1, 0, 0), (2, 4, 1, 0), (3, 4, 1, 0, 0),
    (1, 1, 3), (2, 0, 1, 1), (2, 0, 1, 2), (2, 0, 1, 3), (2, 5, 1, 0), (3, 0, 1, 0, 1), (3, 0, 1, 0, 2),
    (3, 0, 1, 0, 3), (3, 0, 1, 1, 0), (3, 5, 1, 0, 0), (2, 1, 1, 1), (3, 1, 1, 1, 0), (1, 2, 1), (3, 1, 1, 0, 1),
    (3, 2, 1, 1, 0), (3, 1, 1, 0, 2), (2, 1, 1, 2), (1, 2, 2), (3, 3, 1, 1, 0), (3, 4, 1, 1, 0), (2, 1, 1, 3),
    (3, 5, 1, 1, 0), (3, 0, 1, 1, 1), (1, 2, 3), (3, 0, 1, 1, 2), (3, 0, 1, 1, 3), (3, 1, 1, 0, 3), (1, 3, 1),
    (3, 1, 1, 1, 1), (3, 2, 1, 0, 1), (4,), (1, 3, 2), (2, 2, 1, 1), (3, 2, 1, 0, 2), (1, 3, 3), (1, 4, 1),
    (3, 1, 1, 1, 2), (1, 4, 2), (3, 2, 1, 0, 3), (1, 4, 3), (2, 3, 1, 1), (2, 2, 1, 2), (1, 5, 1), (2, 3, 1, 2),
    (3, 1, 1, 1, 3), (1, 5, 2), (5,), (1, 5, 3), (2, 2, 1, 3), (3, 2, 1, 1, 1), (6, 0), (2, 3, 1, 3), (2, 4, 1, 1),
    (2, 4, 1, 2), (3, 3, 1, 0, 1), (6, 1), (2, 4, 1, 3), (3, 3, 1, 0, 2), (6, 2), (3, 3, 1, 0, 3), (3, 2, 1, 1, 2),
    (3, 4, 1, 0, 1), (3, 4, 1, 0, 2), (6, 3), (3, 4, 1, 0, 3), (3, 5, 1, 0, 1), (3, 3, 1, 1, 1), (3, 5, 1, 0, 2),
    (2, 5, 1, 1), (3, 5, 1, 0, 3), (3, 3, 1, 1, 2), (2, 5, 1, 2), (3, 2, 1, 1, 3), (2, 5, 1, 3), (3, 5, 1, 1, 1),
    (3, 3, 1, 1, 3), (3, 5, 1, 1, 2), (3, 4, 1, 1, 1), (3, 4, 1, 1, 2), (3, 5, 1, 1, 3), (3, 4, 1, 1, 3),
)


def gather_project_kernel(mesh_shape, sizes, *refs):
    shards, hidden_ref = refs[:5], refs[5]
    fulls, (mixed_ref, normed_ref, vec_ref) = refs[6:11], refs[11:14]
    pieces_ref, rows_ref, wp_ref, send_sem, recv_sem, pair_recv, own_sem, load_sem = refs[14:]
    rows, inner = mesh_shape["dp"], mesh_shape["fsdp"]
    depths = 4
    sides = inner // (2 * depths)
    total = rows * inner
    at = Place(rows, depths, sides)
    me = at.row * inner + lax.axis_index("fsdp")
    width = hidden_ref.shape[1]
    piece = width // total

    barrier = pltpu.get_barrier_semaphore()
    peers = [at.device(at.row, (at.depth + k) % depths, at.side, at.core) for k in range(1, depths)]
    peers += [at.device(at.row, at.depth, (at.side + k) % sides, at.core) for k in range(1, sides)]
    peers += [at.device((at.row + k) % rows, at.depth, at.side, at.core) for k in range(1, rows)]
    peers.append(at.device(at.row, at.depth, at.side, 1 - at.core))
    for peer in peers:
        pl.semaphore_signal(barrier, inc=1, device_id=peer, **MESH)
    pl.semaphore_wait(barrier, len(peers))

    parts, own = [], []
    for i, (w, part, axes) in enumerate(PARTS):
        source, full = shards[w], fulls[w].at
        if part is None:
            target = lambda s, full=full: full[s]
        else:
            half = shards[w].shape[1] // 2
            columns = slice(part * half, part * half + half)
            source = source.at[:, columns]
            target = lambda s, full=full, columns=columns: full[s, :, columns]
        parts.append(Spread(at, axes, source, target, send_sem.at[i], recv_sem.at[i], pair_recv.at[i]))
        own.append(pltpu.make_async_copy(source, target(me), own_sem.at[i]))
        parts[-1].forward(0, (0, 0, 0))
        own[-1].start()

    waited = set()

    def whole_part(w):
        for i, (source, _, _) in enumerate(PARTS):
            if source == w:
                parts[i].siblings(total // 2)
                own[i].wait()
                waited.add(i)

    def load(source, target):
        copy = pltpu.make_async_copy(source, target, load_sem)
        copy.start()
        copy.wait()

    vec = Vectors(vec_ref, width)
    for code, *what in GATHER_ORDER:
        if code <= 3:
            part, *steps = what
            parts[part].arrive(code, (steps[::-1] + [0, 0])[:3])
        elif code == 4:
            whole_part(0)
            load(fulls[0], pieces_ref)
            spread_vectors(pieces_ref[:, 0, :], sizes, width, vec_ref)
        elif code == 5:
            whole_part(1)
            load(fulls[1], rows_ref)

            def join(pair):
                two = rows_ref[pl.ds(2 * pair, 2)].astype(F32).reshape(2 * piece, 3 * width)
                wp_ref[pl.ds(pl.multiple_of(2 * piece * pair, 2 * piece), 2 * piece)] = two.astype(BF16)

            loop(total // 2, join)
        else:
            tile = slice(what[0] * TILE, what[0] * TILE + TILE)
            normed = (norm_parts(hidden_ref[tile].astype(F32))[0] * vec.g1 + vec.b1).astype(BF16)
            normed_ref[tile] = normed
            mixed_ref[tile] = (dot(normed, wp_ref[...]) + vec.bp).astype(BF16)
    for i, part in enumerate(parts):
        if i not in waited:
            part.siblings(total // 2)
            own[i].wait()
        part.drain(total)


def gather_project(mesh_shape, sizes, hidden, shards):
    total = mesh_shape["dp"] * mesh_shape["fsdp"]
    seq, width = hidden.shape
    count = len(PARTS)
    shape = jax.ShapeDtypeStruct
    outs = [shape((total,) + s.shape, s.dtype) for s in shards]
    outs += [shape((seq, 3 * width), BF16), shape((seq, width), BF16), shape((8, 4 * width), F32)]
    whole_vmem = pl.BlockSpec(memory_space=pltpu.VMEM)
    return pl.pallas_call(
        functools.partial(gather_project_kernel, mesh_shape, sizes),
        out_shape=outs,
        in_specs=[in_hbm()] * 5 + [whole_vmem],
        out_specs=[in_hbm()] * 5 + [whole_vmem] * 3,
        scratch_shapes=[
            pltpu.VMEM(outs[0].shape, BF16),
            pltpu.VMEM(outs[1].shape, BF16),
            pltpu.VMEM((width, 3 * width), BF16),
            DMA((count,)), DMA((count, total // 2)), DMA((count, total // 2)), DMA((count,)), DMA(()),
        ],
        compiler_params=pltpu.CompilerParams(collective_id=3, has_side_effects=True, vmem_limit_bytes=VMEM_LIMIT),
        name="gather_project",
    )(*shards, hidden)


STREAM_FIELDS = (
    "held", "pair", "third", "second", "depth",
    "pair_send", "pair_recv", "third_send", "third_recv", "second_send", "second_recv", "depth_send", "depth_recv",
)


def stream_scratch(rows, depths, sides, side_first, shape):
    second, third = (rows, sides) if side_first else (sides, rows)
    half = rows * depths * sides
    leads = ((half,), (half,), (third - 1, second * depths), (second - 1, depths), (depths - 1,))
    buffers = [pltpu.VMEM(lead + shape, BF16) for lead in leads]
    sems = [DMA((half,)), DMA((half,))] + [DMA(lead) for lead in leads[2:] for _ in range(2)]
    return buffers + sems


CON, EX0, EX1, OUT, PR0, PR1 = range(6)
SIDE_FIRST = (False, True, True, False, True, False)


FIRST_PAIRS = 4
CHUNK_SLOTS = 4
CHUNK, SQUARE, ATTN, ROWS, SMALL, THIRD, SECOND, DEPTH = range(8)
SCHEDULE = (
    (CHUNK, 1, 2), (SQUARE, EX0), (THIRD, CON, 1, 2), (CHUNK, 1, 3), (THIRD, EX0, 1, 0), (SQUARE, EX1),
    (THIRD, CON, 1, 3), (THIRD, EX0, 1, 1), (THIRD, EX1, 1, 0), (THIRD, EX0, 0, 0), (THIRD, EX0, 0, 1), (ATTN, 0, 0),
    (THIRD, EX1, 1, 1), (THIRD, EX1, 0, 0), (ATTN, 0, 1), (THIRD, EX1, 0, 1), (ATTN, 0, 2), (SQUARE, OUT),
    (SECOND, EX0, 0), (SECOND, EX0, 1), (THIRD, OUT, 1, 0), (CHUNK, 1, 1), (THIRD, OUT, 1, 1), (THIRD, OUT, 0, 0),
    (THIRD, OUT, 0, 1), (SECOND, EX0, 2), (ATTN, 0, 3), (CHUNK, 0, 2), (THIRD, CON, 1, 1), (SECOND, EX0, 3),
    (DEPTH, EX0, 0), (ATTN, 1, 0), (THIRD, CON, 0, 2), (SECOND, CON, 2), (DEPTH, EX0, 1), (ATTN, 1, 1), (ATTN, 1, 2),
    (ATTN, 1, 3), (ATTN, 2, 0), (SECOND, OUT, 0), (ATTN, 2, 1), (SECOND, OUT, 1), (SECOND, OUT, 2), (SECOND, EX1, 0),
    (ATTN, 2, 2), (SECOND, OUT, 3), (ATTN, 2, 3), (SECOND, EX1, 1), (ATTN, 3, 0), (SECOND, EX1, 2), (DEPTH, EX0, 2),
    (ATTN, 3, 1), (CHUNK, 0, 3), (SECOND, EX1, 3), (ATTN, 3, 2), (CHUNK, 1, 0), (THIRD, CON, 0, 3), (SECOND, CON, 3),
    (ATTN, 3, 3), (DEPTH, CON, 2), (SQUARE, PR0), (THIRD, CON, 1, 0), (DEPTH, EX0, 3), (DEPTH, EX1, 0),
    (DEPTH, OUT, 1), (DEPTH, OUT, 2), (DEPTH, OUT, 3), (THIRD, PR0, 1, 0), (DEPTH, OUT, 0), (ATTN, 4, 0),
    (THIRD, PR0, 1, 1), (THIRD, PR0, 0, 0), (DEPTH, CON, 3), (DEPTH, EX1, 1), (DEPTH, EX1, 2), (ATTN, 4, 1),
    (THIRD, PR0, 0, 1), (DEPTH, EX1, 3), (CHUNK, 0, 1), (ATTN, 4, 2), (ATTN, 4, 3), (CHUNK, 0, 0),
    (THIRD, CON, 0, 1), (SECOND, CON, 1), (ATTN, 5, 0), (THIRD, CON, 0, 0), (ATTN, 5, 1), (SECOND, CON, 0),
    (SECOND, PR0, 0), (ATTN, 5, 2), (ATTN, 5, 3), (SECOND, PR0, 1), (SQUARE, PR1), (SECOND, PR0, 2), (DEPTH, PR0, 0),
    (THIRD, PR1, 1, 0), (SECOND, PR0, 3), (THIRD, PR1, 1, 1), (ROWS, 0), (THIRD, PR1, 0, 0), (THIRD, PR1, 0, 1),
    (DEPTH, PR0, 1), (ROWS, 1), (DEPTH, CON, 1), (DEPTH, PR0, 2), (ROWS, 2), (ROWS, 3), (DEPTH, CON, 0), (SMALL,),
    (SECOND, PR1, 0), (DEPTH, PR0, 3), (SECOND, PR1, 1), (SECOND, PR1, 2), (SECOND, PR1, 3), (DEPTH, PR1, 0),
    (DEPTH, PR1, 1), (DEPTH, PR1, 2), (DEPTH, PR1, 3),
)


def finish_kernel(mesh_shape, sizes, names, *refs):
    r = Refs(names, refs)
    rows, inner = mesh_shape["dp"], mesh_shape["fsdp"]
    depths = 4
    sides = inner // (2 * depths)
    total = rows * inner
    half = total // 2
    at = Place(rows, depths, sides)
    seq, width = r.dz.shape
    groups = (FIRST_PAIRS * 128, width - FIRST_PAIRS * 128)
    core = at.core
    me = at.row * inner + lax.axis_index("fsdp")
    piece = width // total
    vec = Vectors(r.vec, width)

    copies = {}

    def load(key, source, target, sem):
        copies[key] = pltpu.make_async_copy(source, target, sem)
        copies[key].start()

    def ready(key):
        copies.pop(key).wait()

    chunks = [step[1:] for step in SCHEDULE if step[0] == CHUNK]
    span = sides * 2 * piece * 4

    def load_active(i):
        k, d = chunks[i]
        first = ((at.row + k) % rows * depths + (at.depth + d) % depths) * span
        columns = pl.ds(pl.multiple_of(first, 128), span)
        load(("act", i), r.active.at[:, columns], r.act.at[i % 2], r.act_sem.at[i % 2])

    load_active(0)
    load_active(1)
    load("normed", r.normed, r.normedv, r.in_sem.at[0])
    load("df0", r.df.at[:, : 2 * width], r.dfs.at[0], r.df_sem.at[0])
    load("df1", r.df.at[:, 2 * width :], r.dfs.at[1], r.df_sem.at[1])
    load("dh", r.dh, r.dhv, r.dh_sem)
    load("context", r.context, r.contextv, r.in_sem.at[1])
    load("first", r.first_normed, r.firstv, r.in_sem.at[2])
    load("wp", r.wp, r.wpv, r.wp_sem)

    def load_pair(p):
        slot = p % 2
        for i in range(3):
            columns = pl.ds(i * width + p * 128, 128)
            load(("pair", p, i), r.mixed.at[:, columns], r.qkv.at[slot, i], r.qkv_sem.at[slot, i])
        load(("pair", p, 3), r.dctx.at[:, pl.ds(p * 128, 128)], r.qkv.at[slot, 3], r.qkv_sem.at[slot, 3])

    load_pair(0)

    barrier = pltpu.get_barrier_semaphore()

    def other(k):
        index = (me + k) % total
        return {"dp": index // inner, "fsdp": index % inner}

    loop(total - 1, lambda i: pl.semaphore_signal(barrier, inc=1, device_id=other(i + 1), **MESH))
    pl.semaphore_wait(barrier, total - 1)

    streams = {name: Stream(at, side_first, name, r) for name, side_first in enumerate(SIDE_FIRST)}
    con = streams[CON]
    ones = jnp.ones((16, seq), BF16)
    sums = {}

    def chunk(k, d):
        i = chunks.index((k, d))
        ready(("act", i))
        slot = i % CHUNK_SLOTS
        if i >= CHUNK_SLOTS:
            con_sent(i - CHUNK_SLOTS)
        grad = dot_tn(r.act[i % 2], r.dz[...])
        if i + 2 < len(chunks):
            load_active(i + 2)
        r.con_stage[slot] = grad.reshape(sides, 2, 4 * piece, width).astype(BF16)
        for side in range(sides):
            con.pair_copy(con_unit(i, side), r.con_stage.at[slot, side, 1 - core]).start()

    def con_unit(i, side):
        k, d = chunks[i]
        return ((at.row + k) % rows * depths + (at.depth + d) % depths) * sides + side

    def con_sent(i):
        for side in range(sides):
            con.pair_copy(con_unit(i, side), r.con_stage.at[i % CHUNK_SLOTS, side, 1 - core]).wait_send()

    def con_third(k, d):
        slot = chunks.index((k, d)) % CHUNK_SLOTS
        for j in list(range(1, sides)) + [0]:
            side = (at.side + j) % sides
            con.third_step(k, j, d, lambda u: r.con_stage.at[slot, side, core])

    slots = {}

    def square(name, left, right):
        columns = right.shape[1]
        slot = len(slots) % 2
        previous = [n for n, s in slots.items() if s == slot]
        if previous:
            stage_sent(previous[-1])
        slots[name] = slot
        quarter = width // 4
        for part in range(4):
            grad = dot_tn(left[:, part * quarter : (part + 1) * quarter], right[...])
            target = r.stage.at[slot, part * half // 4 : (part + 1) * half // 4, :, :, :columns]
            target[...] = grad.reshape(half // 4, 2, piece, columns).astype(BF16)
        stream = streams[name]
        for k in list(range(1, stream.sizes[1])) + [0]:
            for j in list(range(1, stream.sizes[0])) + [0]:

                def start(d, k=k, j=j):
                    second, third = ((m + n) % z for m, n, z in zip(stream.mine, (j, k), stream.sizes))
                    u = stream.unit(second, third, (at.depth + d) % depths)
                    stream.pair_copy(u, stage_at(name, u, 1 - core, columns)).start()

                loop(depths, start)

    def stage_at(name, u, which, columns):
        return r.stage.at[slots[name], u, which, :, :columns]

    def columns_of(name):
        return streams[name].held.shape[-1]

    def stage_sent(name):
        stream = streams[name]
        loop(half, lambda u: stream.pair_copy(u, stage_at(name, u, 1 - core, columns_of(name))).wait_send())

    def square_third(name, k, j):
        stream = streams[name]
        source = lambda u: stage_at(name, u, core, columns_of(name))
        loop(depths, lambda d: stream.third_step(k, j, d, source))

    def expand(e):
        if e == 0:
            ready("normed")
        ready("df%d" % e)
        square(EX0 + e, r.normedv, r.dfs.at[e])
        sums["be%d" % e] = dot(ones, r.dfs[e])[0:1]

    def output():
        ready("dh")
        ready("context")
        r.dy[...] = r.dhv[...].astype(BF16)
        square(OUT, r.contextv, r.dy)
        sums["bo"] = dot(ones, r.dy[...])[0:1]
        sums["bc"] = dot(ones, r.dz[...])[0:1]

    later = iota((TILE, TILE), 0) > iota((TILE, TILE), 1)
    later = jnp.concatenate([later, later], 1)
    first_head = iota((TILE, 128), 1) < 64

    def two(value):
        parts = [jnp.where(first_head, value, 0.0), jnp.where(first_head, 0.0, value)]
        return jnp.concatenate(parts, 0).astype(BF16)

    def attend_block(p, n):
        block = seq // TILE - 1 - n
        slot = p % 2
        if n == 0:
            for i in range(4):
                ready(("pair", p, i))
            if p + 1 < HEADS // 2:
                load_pair(p + 1)
            r.keys_t[...] = r.qkv[slot, 1].T
        query_ref, key_ref, value_ref, up_ref = (r.qkv.at[slot, i] for i in range(4))
        start, stop = block * TILE, block * TILE + TILE
        query = two(query_ref[start:stop].astype(F32) * 0.125)
        upstream = two(up_ref[start:stop].astype(F32))
        score = dot_nt(key_ref[:stop], query)
        edge = jnp.where(later, NEG_FILL, score[start:])
        score = jnp.concatenate([score[:start], edge], 0) if start else edge
        logs = jnp.concatenate([r.logs[p, 0:1, start:stop], r.logs[p, 1:2, start:stop]], 1)
        prob = jnp.exp(score - logs)
        prob_grad = dot_nt(value_ref[:stop], upstream)
        mean = jnp.sum(prob * prob_grad, axis=0, keepdims=True)
        score_grad = (prob * (prob_grad - mean)).astype(BF16)
        dv = dot(prob.astype(BF16), upstream)
        dk = dot(score_grad, query)
        if n == 0:
            r.dv_sum[...] = dv
            r.dk_sum[...] = dk
        else:
            r.dv_sum[:stop] += dv
            r.dk_sum[:stop] += dk
        out = dot(r.keys_t[:, :stop], score_grad)
        out = jnp.concatenate([out[:64, :TILE], out[64:, TILE:]], 0)
        g = int(p >= FIRST_PAIRS)
        target, group = r.dfs.at[g], groups[g]
        column = (p - g * FIRST_PAIRS) * 128
        target[start:stop, column : column + 128] = (out.T * 0.125).astype(BF16)
        if block == 0:
            target[:, group + column : group + column + 128] = r.dk_sum[...].astype(BF16)
            target[:, 2 * group + column : 2 * group + column + 128] = r.dv_sum[...].astype(BF16)

    def project_grad(g):
        if g == 0:
            ready("first")
        right = r.dfs.at[g, :, : 3 * groups[g]]
        square(PR0 + g, r.firstv, right)
        sums["bp%d" % g] = dot(ones, right[...])[0:1]

    def project_columns(g, n):
        first = n * width + g * groups[0]
        return slice(first, first + groups[g])

    def load_tile(i):
        load(("x", i), r.x.at[pl.ds(i * TILE, TILE)], r.xs.at[i % 2], r.x_sem.at[i % 2])

    def tile(i):
        if i == 0:
            ready("wp")
            load_tile(0)
            load_tile(1)
        ready(("x", i))
        part = slice(i * TILE, i * TILE + TILE)
        da = jnp.zeros((TILE, width), F32)
        for g in range(2):
            for n in range(3):
                da = da + dot_nt(r.dfs[g, part, n * groups[g] : (n + 1) * groups[g]], r.wpv[:, project_columns(g, n)])
        hat, inv = norm_parts(r.xs[i % 2])
        if i + 2 < seq // TILE:
            load_tile(i + 2)
        position = i * TILE + iota((TILE, 1), 0)
        kept = (position < r.start[0]) | (position >= r.start[0] + THOUGHTS)
        if i >= 2:
            ready(("dx", i - 2))
        r.dxs[i % 2] = jnp.where(kept, r.dhv[part] + norm_back(da, hat, inv, vec.g1), 0.0)
        load(("dx", i), r.dxs.at[i % 2], r.hidden_grad.at[pl.ds(i * TILE, TILE)], r.dx_sem.at[i % 2])
        gain, bias = jnp.sum(da * hat, axis=0, keepdims=True), jnp.sum(da, axis=0, keepdims=True)
        sums["g1"] = gain if i == 0 else sums["g1"] + gain
        sums["b1"] = bias if i == 0 else sums["b1"] + bias

    def small_start():
        group_of = lambda n: jnp.concatenate(
            [sums["bp%d" % g][:, n * groups[g] : (n + 1) * groups[g]] for g in range(2)], 1
        )
        lines = dict(
            g1=sums["g1"], b1=sums["b1"], bp=jnp.concatenate([group_of(0), group_of(2)], 1), bo=sums["bo"],
            g2=r.sums[0:1], b2=r.sums[1:2], be=jnp.concatenate([sums["be0"], sums["be1"]], 1), bc=sums["bc"],
        )
        offset = 0
        r.small_part[...] = jnp.zeros_like(r.small_part)
        for name, size in zip(VECTORS, sizes):
            low, high = offset // 128 * 128, -(-(offset + size) // 128) * 128
            length = total * size
            lane = iota((1, length), 1)
            pick = (iota((high - low, length), 0) == lane % size + (offset - low)).astype(F32).astype(BF16)
            rest = jnp.where(iota((total, length), 0) == lane // size, lines[name], 0.0)
            pieces = jnp.zeros((total, high - low), F32)
            for _ in range(2):
                rounded = rest.astype(BF16)
                pieces = pieces + dot_nt(rounded, pick)
                rest = rest - rounded.astype(F32)
            r.small_part[:, 0, low:high] += pieces
            offset += size
        loop(total - 1, lambda i: small_copy(i + 1).start())

    def small_copy(k):
        return pltpu.make_async_remote_copy(
            src_ref=r.small_part.at[(me + k) % total],
            dst_ref=r.small_in.at[k - 1],
            send_sem=r.small_send.at[k - 1],
            recv_sem=r.small_recv.at[k - 1],
            device_id=other(k),
            **MESH,
        )

    def small_end():
        loop(total - 1, lambda i: small_copy(i + 1).wait_recv())
        received = r.small_in[...]
        r.small_out[...] = r.small_part[me] + jnp.sum(received[: total - 1], axis=0)

    def work(kind, *what):
        if kind == CHUNK:
            chunk(*what)
        elif kind == ATTN:
            attend_block(*what)
        elif kind == ROWS:
            tile(*what)
        elif kind == SMALL:
            small_start()
        elif kind == SQUARE:
            name = what[0]
            if name == OUT:
                output()
            elif name in (EX0, EX1):
                expand(name - EX0)
            else:
                project_grad(name - PR0)
        elif kind == THIRD:
            name, k, j = what
            if name == CON:
                con_third(k, j)
            else:
                square_third(name, k, 1 - j)
        elif kind == SECOND:
            streams[what[0]].second_step(what[1])
        else:
            streams[what[0]].depth_step(what[1])

    for step in SCHEDULE:
        work(*step)
    r.contract_out[...] = con.total()
    r.expand_out[:, : 2 * width] = streams[EX0].total()
    r.expand_out[:, 2 * width :] = streams[EX1].total()
    r.output_out[...] = streams[OUT].total()
    for g in range(2):
        grad = streams[PR0 + g].total()
        for n in range(3):
            r.project_out[:, project_columns(g, n)] = grad[:, n * groups[g] : (n + 1) * groups[g]]
    small_end()
    ready(("dx", 2))
    ready(("dx", 3))
    for i in range(len(chunks) - CHUNK_SLOTS, len(chunks)):
        con_sent(i)
    for name in list(slots)[-2:]:
        stage_sent(name)
    for stream in streams.values():
        stream.drain()
    loop(total - 1, lambda i: small_copy(i + 1).wait_send())


def finish(mesh_shape, sizes, start, operands):
    rows, inner = mesh_shape["dp"], mesh_shape["fsdp"]
    depths = 4
    sides = inner // (2 * depths)
    total = rows * inner
    half = total // 2
    seq, width = operands["dz"].shape
    piece = width // total
    lanes = -(-sum(sizes) // 128) * 128
    in_vmem = ("dz", "logs", "vec", "sums")
    outs = dict(
        hidden_grad=(seq, width),
        contract_out=(4 * piece, width),
        expand_out=(piece, 4 * width),
        output_out=(piece, width),
        project_out=(piece, 3 * width),
        small_out=(1, lanes),
    )
    shapes = (
        (4 * piece, width), (piece, 2 * width), (piece, 2 * width), (piece, width),
        (piece, 3 * FIRST_PAIRS * 128), (piece, 3 * (width - FIRST_PAIRS * 128)),
    )
    span = sides * 2 * piece * 4
    scratch = dict(
        act=pltpu.VMEM((2, seq, span), BF16), act_sem=DMA((2,)),
        dfs=pltpu.VMEM((2, seq, 2 * width), BF16), df_sem=DMA((2,)),
        dhv=pltpu.VMEM((seq, width), F32), dh_sem=DMA(()),
        normedv=pltpu.VMEM((seq, width), BF16), contextv=pltpu.VMEM((seq, width), BF16),
        firstv=pltpu.VMEM((seq, width), BF16), in_sem=DMA((3,)),
        dy=pltpu.VMEM((seq, width), BF16),
        qkv=pltpu.VMEM((2, 4, seq, 128), BF16), qkv_sem=DMA((2, 4)),
        keys_t=pltpu.VMEM((128, seq), BF16),
        dk_sum=pltpu.VMEM((seq, 128), F32), dv_sum=pltpu.VMEM((seq, 128), F32),
        wpv=pltpu.VMEM((width, 3 * width), BF16), wp_sem=DMA(()),
        xs=pltpu.VMEM((2, TILE, width), F32), x_sem=DMA((2,)),
        dxs=pltpu.VMEM((2, TILE, width), F32), dx_sem=DMA((2,)),
        con_stage=pltpu.VMEM((CHUNK_SLOTS, sides, 2, 4 * piece, width), BF16),
        stage=pltpu.VMEM((2, half, 2, piece, 2 * width), BF16),
        small_part=pltpu.VMEM((total, 1, lanes), F32), small_in=pltpu.VMEM((total, 1, lanes), F32),
        small_send=DMA((total - 1,)), small_recv=DMA((total - 1,)),
    )
    for name, side_first in enumerate(SIDE_FIRST):
        fields = stream_scratch(rows, depths, sides, side_first, shapes[name])
        scratch.update({f + str(name): s for f, s in zip(STREAM_FIELDS, fields)})
    names = ("start",) + tuple(operands) + tuple(outs) + tuple(scratch)
    whole_vmem = pl.BlockSpec(memory_space=pltpu.VMEM)
    return pl.pallas_call(
        functools.partial(finish_kernel, mesh_shape, sizes, names),
        out_shape=[jax.ShapeDtypeStruct(s, F32) for s in outs.values()],
        in_specs=[smem()] + [whole_vmem if n in in_vmem else in_hbm() for n in operands],
        out_specs=[in_hbm()] + [whole_vmem] * 5,
        scratch_shapes=list(scratch.values()),
        compiler_params=pltpu.CompilerParams(collective_id=2, has_side_effects=True, vmem_limit_bytes=63 * 2**20),
        name="finish",
    )(start, *operands.values())


def deliver_kernel(sizes, *refs):
    count = (len(refs) - len(sizes) + 1) // 2
    sources, small, targets = refs[: count - 1], refs[count - 1], refs[count:]
    for source, target in zip(sources, targets):
        target[...] = source[...]
    offset = 0
    for size, target in zip(sizes, targets[len(sources) :]):
        target[...] = small[0, offset : offset + size]
        offset += size


def deliver(sizes, *arrays):
    seq, width = arrays[0].shape
    first = lambda i: (0, 0)
    rows = pl.BlockSpec((TILE, width), lambda i: (i, 0))
    fixed = [pl.BlockSpec(a.shape, first) for a in arrays[1:]]
    vectors = [jax.ShapeDtypeStruct((size,), F32) for size in sizes]
    return pl.pallas_call(
        functools.partial(deliver_kernel, sizes),
        grid=(seq // TILE,),
        out_shape=[jax.ShapeDtypeStruct(a.shape, F32) for a in arrays[:-1]] + vectors,
        in_specs=[rows] + fixed,
        out_specs=[rows] + fixed[:-1] + [pl.BlockSpec(v.shape, lambda i: (0,)) for v in vectors],
        compiler_params=params(),
        name="deliver",
    )(*arrays)


def pack(vectors, total):
    joined = jnp.concatenate([v.reshape(total, -1) for v in vectors], 1)
    fill = -joined.shape[1] % 128
    return jnp.pad(joined, ((0, 0), (0, fill)))[:, None]


def unpack(packed, sizes):
    flat = packed.reshape(-1, packed.shape[-1])
    out, at = [], 0
    for size in sizes:
        out.append(flat[:, at : at + size].reshape(-1))
        at += size
    return out


def per_device(
    mesh_shape,
    hidden,
    cotangent,
    lengths,
    thought_start,
    first_gain,
    first_bias,
    project_weight,
    project_bias,
    output_weight,
    output_bias,
    second_gain,
    second_bias,
    expand_weight,
    expand_bias,
    contract_weight,
    contract_bias,
):
    _, seq, width = hidden.shape
    total = mesh_shape["dp"] * mesh_shape["fsdp"]
    vectors = (
        first_gain,
        first_bias,
        project_bias,
        output_bias,
        second_gain,
        second_bias,
        expand_bias,
        contract_bias,
    )
    sizes = [v.shape[0] for v in vectors]
    shards = (pack(vectors, 1)[0], project_weight, output_weight, expand_weight, contract_weight)
    whole_tiles = width // total % 8 == 0
    if whole_tiles:
        *full, mixed, normed, vec = gather_project(mesh_shape, sizes, hidden[0], shards)
    else:
        full = gather_all(mesh_shape, shards)
    Wp, Wo, We, Wc = (w.reshape(-1, w.shape[-1]) for w in full[1:])
    if not whole_tiles:
        mixed, normed, vec = project(hidden[0], full[0], sizes, Wp)
    (
        mixed, normed, x, context, log_total, final, normed_two, active, dz, df, dh, dctx, sums,
    ) = middle(thought_start, lengths, hidden[0], cotangent[0], vec, mixed, normed, (Wo, We, Wc, Wp))
    if whole_tiles:
        operands = dict(
            dz=dz, normed=normed_two, context=context, first_normed=normed, logs=log_total, vec=vec, sums=sums,
            active=active, df=df, dh=dh, mixed=mixed, dctx=dctx, x=x, wp=Wp,
        )
        hidden_grad, dWc, dWe, dWo, dWp, *small = deliver(sizes, *finish(mesh_shape, sizes, thought_start, operands))
        dg1, db1, dbp, dbo, dg2, db2, dbe, dbc = small
        return (final[None], hidden_grad[None], dg1, db1, dWp, dbp, dWo, dbo, dg2, db2, dWe, dbe, dWc, dbc)
    dq, dk, dv = attend_back(mixed, dctx, log_total)
    g1 = vec[0:1, :width]
    dy = dh.astype(BF16)
    x_hat, x_inv = norm_parts(x)
    dmixed = jnp.concatenate([dq, dk, dv], 1)
    da = dot_nt(dmixed, Wp)
    dx = dh + norm_back(da, x_hat, x_inv, g1)
    position = iota((seq, 1), 0)
    is_thought = (position >= thought_start[0]) & (position < thought_start[0] + THOUGHTS)
    hidden_grad = jnp.where(is_thought, 0.0, dx)

    def column_sum(value):
        return jnp.sum(value, axis=0, dtype=F32)

    column = column_sum(dmixed)
    small = (
        column_sum(da * x_hat),
        column_sum(da),
        jnp.concatenate([column[:width], column[2 * width :]]),
        column_sum(dy),
        sums[0],
        sums[1],
        column_sum(df),
        column_sum(dz),
    )
    large = (
        dot_tn(normed, dmixed),
        dot_tn(context, dy),
        dot_tn(normed_two, df),
        dot_tn(active, dz),
    )
    parts = [pack(small, total)]
    for grad in large:
        parts.append(grad.astype(BF16).reshape(total, grad.shape[0] // total, grad.shape[1]))
    small, dWp, dWo, dWe, dWc = scatter_all(mesh_shape, parts)
    dg1, db1, dbp, dbo, dg2, db2, dbe, dbc = unpack(small, sizes)
    return (final[None], hidden_grad[None], dg1, db1, dWp, dbp, dWo, dbo, dg2, db2, dWe, dbe, dWc, dbc)


def solution(mesh):
    rows = P(AXES, None, None)
    flat = P(AXES)
    square = P(AXES, None)
    specs = (flat, flat, square, flat, square, flat, flat, flat, square, flat, square, flat)
    return jax.shard_map(
        functools.partial(per_device, dict(mesh.shape)),
        mesh=mesh,
        in_specs=(rows, rows, flat, flat) + specs,
        out_specs=(rows, rows) + specs,
        check_vma=False,
    )
```
